32 devices in a mesh: expert: 8 (over y, x, core), shard: 4 (over z).
Axes of the slice: x: 2, y: 2, z: 4, core: 2. Of those that a mesh axis runs over, the one named last changes fastest.
Arguments:
- block_input: float32 [64, 65, 768], P(('expert', 'shard')), may hold values from -6 to 6
- image_live: int32 [64], P(('expert', 'shard')), may hold values from 0 to 1, as said below
- expert_routes: int32 [64, 65, 2], P(('expert', 'shard')), may hold values from 0 to 7, all different within a row; in each aligned block of 130 rows (0 to 129, 130 to 259, ..., all dimensions but the last counted through in order) at most 49 rows name the same one
- first_gain: bfloat16 [768], P('shard'), may hold values from 0.5 to 1.5
- first_shift: bfloat16 [768], P('shard'), may hold values from -3 to 3
- qkv_weight: bfloat16 [768, 2304], P('shard'), may hold values from -0.21875 to 0.21875
- query_value_bias: bfloat16 [1536], P('shard'), may hold values from -2 to 2
- attn_out_weight: bfloat16 [768, 768], P('shard'), may hold values from -0.4375 to 0.4375
- attn_out_bias: bfloat16 [768], P('shard'), may hold values from -3 to 3
- second_gain: bfloat16 [768], P('shard'), may hold values from 0.5 to 1.5
- second_shift: bfloat16 [768], P('shard'), may hold values from -3 to 3
- router_weight: bfloat16 [768, 8], P('shard'), may hold values from -0.28867513 to 0.28867513
- expert_in_weight: bfloat16 [8, 768, 3072], P('expert', None, 'shard'), may hold values from -0.21875 to 0.21875
- expert_in_bias: bfloat16 [8, 3072], P('expert', 'shard'), may hold values from -3 to 3
- expert_out_weight: bfloat16 [8, 3072, 768], P('expert', None, 'shard'), may hold values from -1.75 to 1.75
- expert_out_bias: bfloat16 [8, 768], P('expert', 'shard'), may hold values from -5 to 5
- output_grad: float32 [64, 65, 768], P(('expert', 'shard')), may hold values from -6 to 6
Outputs:
- block_output: float32 [64, 65, 768], P(('expert', 'shard'))
- input_grad: float32 [64, 65, 768], P(('expert', 'shard'))
- first_gain_grad: float32 [768], P('shard')
- first_shift_grad: float32 [768], P('shard')
- qkv_weight_grad: float32 [768, 2304], P('shard')
- query_value_bias_grad: float32 [1536], P('shard')
- attn_out_weight_grad: float32 [768, 768], P('shard')
- attn_out_bias_grad: float32 [768], P('shard')
- second_gain_grad: float32 [768], P('shard')
- second_shift_grad: float32 [768], P('shard')
- router_weight_grad: float32 [768, 8], P('shard')
- expert_in_weight_grad: float32 [8, 768, 3072], P('expert', None, 'shard')
- expert_in_bias_grad: float32 [8, 3072], P('expert', 'shard')
- expert_out_weight_grad: float32 [8, 3072, 768], P('expert', None, 'shard')
- expert_out_bias_grad: float32 [8, 768], P('expert', 'shard')
The draws below stay inside these ranges and needn't reach their ends.
Inputs may be any that keep to these rules, and one draw needn't show every extreme that they name: `expert_routes`: each token names two different experts; among the rows of the image slots i with i // 2 equal, no expert is named more than 49 times, a bound that some block reaches. image_live[i] is 1 wherever i is a multiple of 2.
All inputs are finite; a program needn't handle non-finite values.
Results may differ from the reference program's by a relative error of at most 0.023.
Values may be sent and summed in bfloat16 or wider, within the bound.
A program may use at most 128 MiB of HBM per device.

```python
import math
import jax
import jax.numpy as jnp
import numpy as np
from jax import lax

D = 768
HEADS = 12
HEAD_DIM = 64
FF = 3072
SEQ = 65
IMG_DEV = 2
EXPERTS = 8
CAP = 49
IMAGES = 64


def draw_image_live(key, part):
    coin = jax.random.randint(key, (IMAGES,), 0, 4)
    first_slot = jnp.arange(IMAGES, dtype=jnp.int32) % IMG_DEV == 0
    return jnp.where(first_slot, 1, jnp.minimum(coin, 1)).astype(jnp.int32)


def draw_query_value_bias(key, part):
    noise = jnp.clip(jax.random.normal(key, (2 * D,), jnp.float32), -4.0, 4.0)
    return (noise * 0.5).astype(jnp.bfloat16)


def draw_router_weight(key, part):
    noise = jnp.clip(jax.random.normal(key, (D, EXPERTS), jnp.float32), -4.0, 4.0) * (2.0 / math.sqrt(D))
    return noise.astype(jnp.bfloat16)


def levels(key, dims, split, smallest, top_value):
    gain = 1.0
    for axis_at, parts in split:
        heights = jax.random.uniform(jax.random.fold_in(jax.random.fold_in(key, 6), axis_at), (parts,), jnp.float32, smallest / len(split), top_value / len(split))
        gain = gain * jnp.repeat(jnp.exp(heights), dims[axis_at] // parts).reshape((-1,) + (1,) * (len(dims) - 1 - axis_at))
    return gain


def deal_out(stream_key, own, number, rows, count, top, bound, slope):
    sequence = jax.random.permutation(stream_key, count)
    heavy_load, ordinary = portions_of(count, rows * top, bound, slope, True), portions_of(count, rows * top, bound, slope, False)
    places = jnp.arange(count)

    def named(tallies, rotation):
        used = int((tallies > 0).sum())
        fixed = max(1, used // 4)
        moved = fixed + (places - fixed + rotation * (used - fixed)) % max(1, count - fixed)
        return jnp.zeros((count,), jnp.int32).at[sequence[jnp.where(places < fixed, places, moved)]].set(jnp.asarray(tallies, jnp.int32))

    tallies = jnp.where(number % 4 == 0, named(heavy_load, number // 4), named(ordinary, number - number // 4 - 1))
    mixed = jax.random.permutation(jax.random.fold_in(own, 3), count)
    donor, taker = mixed[0:count // 2 * 2:2], mixed[1:count // 2 * 2:2]
    room = jnp.minimum(tallies[donor] - 1, bound - tallies[taker]) // 2
    room = jnp.where((donor == sequence[0]) | (taker == sequence[0]) | (tallies[taker] == 0), 0, jnp.maximum(room, 0))
    moved = jax.random.randint(jax.random.fold_in(own, 4), (count // 2,), 0, 1 << 20) % (room + 1)
    tallies = tallies.at[donor].add(-moved).at[taker].add(moved)
    labels = jnp.searchsorted(jnp.cumsum(tallies), jnp.arange(rows * top), side="right").astype(jnp.int32)
    grid = labels.reshape(top, rows).T
    grid = grid[jax.random.permutation(jax.random.fold_in(own, 1), rows)]
    rotation = jax.random.randint(jax.random.fold_in(own, 2), (rows, 1), 0, top)
    return jnp.take_along_axis(grid, (jnp.arange(top)[None, :] + rotation) % top, axis=1)


def portions_of(amount, total, reach, lean, full):
    loads = [(1 << 20) // math.isqrt(standing ** lean) + 1 for standing in range(1, amount + 1)]
    largest = reach if full else min(reach, max(-(-total // amount), total * loads[0] // sum(loads)))
    least = 1 if total - largest >= amount - 1 else 0
    counts, spare = [largest] + [least] * (amount - 1), total - largest - least * (amount - 1)
    while spare > 0:
        free = [i for i in range(1, amount) if counts[i] < largest] or [i for i in range(1, amount) if counts[i] < reach]
        pool, remaining = sum([loads[i] for i in free]), spare
        for i in free:
            addition = min(reach - counts[i], max(1, remaining * loads[i] // pool), spare)
            counts[i] = counts[i] + addition
            spare = spare - addition
    return np.array(counts)


def bell_draw(rng, extent, scale, most, cuts=(), kind=jnp.bfloat16):
    values = jax.random.normal(rng, extent, jnp.float32) * scale
    if len(cuts) > 0:
        values = levels(rng, extent, cuts, -0.22, 0.18) * values
    return jnp.clip(values, min=-most, max=most).astype(kind)


def setup_inputs(seed: int = 0) -> dict:
    key_of = jax.random.split(jax.random.key(seed), 18)
    block_input = bell_draw(key_of[0], (IMAGES, SEQ, D), 1.0, 6.0, ((0, 32),), jnp.float32)
    image_live = draw_image_live(jax.random.fold_in(key_of[17], 71), 0)
    expert_routes_keys = jax.random.split(jax.random.fold_in(key_of[2], 1), IMAGES * SEQ // (IMG_DEV * SEQ))
    expert_routes_turns = jax.random.permutation(jax.random.fold_in(key_of[2], 3), IMAGES * SEQ // (IMG_DEV * SEQ))
    expert_routes = jax.vmap(lambda own, number: deal_out(jax.random.fold_in(key_of[2], 2), own, number, IMG_DEV * SEQ, EXPERTS, 2, CAP, 1))(expert_routes_keys, expert_routes_turns).reshape((IMAGES, SEQ, 2))
    first_gain = jnp.clip(1.0 + 0.1 * jax.random.normal(key_of[3], (D,), jnp.float32), 0.5, 1.5).astype(jnp.bfloat16)
    first_shift = bell_draw(key_of[4], (D,), 0.5, 3.0, ((0, 4),))
    qkv_weight = bell_draw(key_of[5], (D, 3 * D), D ** -0.5, 0.21875, ((0, 4),))
    query_value_bias = draw_query_value_bias(jax.random.fold_in(key_of[17], 71), 0)
    attn_out_weight = bell_draw(key_of[7], (D, D), (D // 4) ** -0.5, 0.4375, ((0, 4),))
    attn_out_bias = bell_draw(key_of[8], (D,), 0.5, 3.0, ((0, 4),))
    second_gain = jnp.clip(1.0 + 0.1 * jax.random.normal(key_of[9], (D,), jnp.float32), 0.5, 1.5).astype(jnp.bfloat16)
    second_shift = bell_draw(key_of[10], (D,), 0.5, 3.0, ((0, 4),))
    router_weight = draw_router_weight(jax.random.fold_in(key_of[17], 71), 0)
    expert_in_weight = bell_draw(key_of[12], (EXPERTS, D, FF), D ** -0.5, 0.21875, ((0, 8), (2, 4)))
    expert_in_bias = bell_draw(key_of[13], (EXPERTS, FF), 0.5, 3.0, ((0, 8), (1, 4)))
    expert_out_weight = bell_draw(key_of[14], (EXPERTS, FF, D), (FF // 256 + 1) ** -0.5, 1.75, ((0, 8), (2, 4)))
    expert_out_bias = bell_draw(key_of[15], (EXPERTS, D), 1.0, 5.0, ((0, 8), (1, 4)))
    output_grad = bell_draw(key_of[16], (IMAGES, SEQ, D), 1.0, 6.0, ((0, 32),), jnp.float32)
    return {"block_input": block_input, "image_live": image_live, "expert_routes": expert_routes, "first_gain": first_gain, "first_shift": first_shift, "qkv_weight": qkv_weight, "query_value_bias": query_value_bias, "attn_out_weight": attn_out_weight, "attn_out_bias": attn_out_bias, "second_gain": second_gain, "second_shift": second_shift, "router_weight": router_weight, "expert_in_weight": expert_in_weight, "expert_in_bias": expert_in_bias, "expert_out_weight": expert_out_weight, "expert_out_bias": expert_out_bias, "output_grad": output_grad}


EPSILON = 1e-06
PRECISE = lax.Precision.HIGHEST
HALF_ROOT = 0.7071067811865476
DENSITY = 0.3989422804014327

def as_float(array_in):
    return array_in.astype(jnp.float32)

def contract_rows(left_side, right_side):
    return lax.dot_general(left_side, right_side, (((0,), (0,)), ((), ())), preferred_element_type=jnp.float32)

def contract_cols(left_side, right_side):
    return lax.dot_general(left_side, right_side, (((1,), (1,)), ((), ())), preferred_element_type=jnp.float32)

def precise_rows(left_side, right_side):
    return lax.dot_general(left_side, right_side, (((0,), (0,)), ((), ())), precision=PRECISE, preferred_element_type=jnp.float32)

def precise_cols(left_side, right_side):
    return lax.dot_general(left_side, right_side, (((1,), (1,)), ((), ())), precision=PRECISE, preferred_element_type=jnp.float32)

def layer_norm(values_in, gain_vec, shift_vec):
    center = values_in - lax.optimization_barrier(jnp.mean(values_in, axis=-1, keepdims=True))
    inv_std = lax.rsqrt(lax.optimization_barrier(jnp.mean(center * center, axis=-1, keepdims=True)) + EPSILON)
    normed = center * inv_std
    return (normed * as_float(gain_vec) + as_float(shift_vec), normed, inv_std)

def norm_back(upstream, normed, inv_std, gain_vec):
    scaled = upstream * as_float(gain_vec)
    return inv_std * (scaled - lax.optimization_barrier(jnp.mean(scaled, axis=-1, keepdims=True)) - normed * lax.optimization_barrier(jnp.mean(scaled * normed, axis=-1, keepdims=True)))

def gelu_parts(pre_act):
    normal_cdf = 0.5 * (1.0 + jax.scipy.special.erf(pre_act * HALF_ROOT))
    return (pre_act * normal_cdf, normal_cdf + pre_act * DENSITY * jnp.exp(-0.5 * pre_act * pre_act))

def route_tables(expert_routes, image_live, expert_count, capacity):
    row_count = expert_routes.shape[0] * expert_routes.shape[1]
    flat_routes = expert_routes.reshape(2 * row_count)
    live_rows = jnp.repeat(image_live, expert_routes.shape[1])
    alive_pairs = jnp.repeat(live_rows, 2)
    chosen = (flat_routes[:, None] == jnp.arange(expert_count, dtype=jnp.int32)[None, :]).astype(jnp.int32)
    live_hits = chosen * alive_pairs[:, None]
    position = lax.optimization_barrier(jnp.sum((jnp.cumsum(live_hits, axis=0, dtype=jnp.int32) - live_hits) * live_hits, axis=1, dtype=jnp.int32))
    slot_index = flat_routes * capacity + position
    slot_table = ((slot_index[None, :] == jnp.arange(expert_count * capacity, dtype=jnp.int32)[:, None]) & (alive_pairs[None, :] > 0)).astype(jnp.bfloat16)
    return (chosen.reshape(row_count, 2, expert_count), slot_table, live_rows)

def attention_scores(query_rows, key_rows):
    return jnp.einsum('bqhd,bkhd->bhqk', as_float(query_rows), as_float(key_rows)) * (1.0 / math.sqrt(HEAD_DIM))

def forward_device(tokens, image_live, expert_routes, output_grad, params):
    first_gain, first_shift, qkv_weight, query_value_bias, attn_out_weight, attn_out_bias, second_gain, second_shift, router_weight = params
    row_count = IMG_DEV * SEQ
    flat_tokens = tokens.reshape(row_count, D)
    norm_out, normed_one, inv_one = layer_norm(flat_tokens, first_gain, first_shift)
    attn_in = norm_out.astype(jnp.bfloat16)
    bias_row = jnp.concatenate([as_float(query_value_bias[:D]), jnp.zeros((D,), jnp.float32), as_float(query_value_bias[D:])])
    packed = (jnp.dot(attn_in, qkv_weight, preferred_element_type=jnp.float32) + bias_row).astype(jnp.bfloat16).reshape(IMG_DEV, SEQ, 3, HEADS, HEAD_DIM)
    query_rows = packed[:, :, 0]
    key_rows = packed[:, :, 1]
    value_rows = packed[:, :, 2]
    scores = attention_scores(query_rows, key_rows)
    row_max = lax.optimization_barrier(jnp.max(scores, axis=-1, keepdims=True))
    log_total = row_max + jnp.log(lax.optimization_barrier(jnp.sum(jnp.exp(scores - row_max), axis=-1, keepdims=True)))
    weights = jnp.exp(scores - log_total).astype(jnp.bfloat16)
    mixed_heads = jnp.einsum('bhqk,bkhd->bqhd', as_float(weights), as_float(value_rows)).astype(jnp.bfloat16).reshape(row_count, D)
    residual = flat_tokens + jnp.dot(mixed_heads, attn_out_weight, preferred_element_type=jnp.float32) + as_float(attn_out_bias)
    norm_two_out, normed_two, inv_two = layer_norm(residual, second_gain, second_shift)
    expert_in = norm_two_out.astype(jnp.bfloat16)
    logits = jnp.dot(expert_in, router_weight, preferred_element_type=jnp.float32)
    shifted = jnp.exp(logits - lax.optimization_barrier(jnp.max(logits, axis=-1, keepdims=True)))
    gate_probs = shifted / lax.optimization_barrier(jnp.sum(shifted, axis=-1, keepdims=True))
    chosen, slot_table, live_rows = route_tables(expert_routes, image_live, EXPERTS, CAP)
    gate_pick = lax.optimization_barrier(jnp.sum(gate_probs[:, None, :] * as_float(chosen), axis=2))
    upstream = output_grad.reshape(row_count, D) * as_float(live_rows)[:, None]
    send_table = lax.optimization_barrier(jnp.sum(slot_table.reshape(EXPERTS * CAP, row_count, 2), axis=2))
    outgoing = jnp.dot(send_table, expert_in, preferred_element_type=jnp.float32).astype(jnp.bfloat16)
    sent_grad = (gate_pick[:, :, None] * upstream[:, None, :]).astype(jnp.bfloat16).reshape(2 * row_count, D)
    grad_out = jnp.dot(slot_table, sent_grad, preferred_element_type=jnp.float32).astype(jnp.bfloat16)
    kept = (normed_one, inv_one, attn_in, query_rows, key_rows, value_rows, log_total, mixed_heads, residual, normed_two, inv_two, expert_in, gate_probs, chosen, slot_table, gate_pick, upstream, live_rows)
    return (outgoing, grad_out, kept)

def expert_pass(inputs):
    rows_in, grads_in, in_weight, in_bias, out_weight, out_bias = inputs
    pre_act = jnp.dot(rows_in, in_weight, preferred_element_type=jnp.float32) + as_float(in_bias)
    gelu_out, gelu_slope = gelu_parts(pre_act)
    gelu_bf = gelu_out.astype(jnp.bfloat16)
    expert_out = (jnp.dot(gelu_bf, out_weight, preferred_element_type=jnp.float32) + as_float(out_bias)).astype(jnp.bfloat16)
    out_bias_grad = lax.optimization_barrier(jnp.sum(as_float(grads_in), axis=0))
    out_weight_grad = contract_rows(gelu_bf, grads_in)
    pre_grad = contract_cols(grads_in, out_weight) * gelu_slope
    in_bias_grad = lax.optimization_barrier(jnp.sum(pre_grad, axis=0))
    pre_bf = pre_grad.astype(jnp.bfloat16)
    in_weight_grad = contract_rows(rows_in, pre_bf)
    back_rows = contract_cols(pre_bf, in_weight).astype(jnp.bfloat16)
    return (expert_out, back_rows, in_weight_grad, in_bias_grad, out_weight_grad, out_bias_grad)

def backward_device(returned, returned_grad, kept, params):
    first_gain, first_shift, qkv_weight, query_value_bias, attn_out_weight, attn_out_bias, second_gain, second_shift, router_weight = params
    normed_one, inv_one, attn_in, query_rows, key_rows, value_rows, log_total, mixed_heads, residual, normed_two, inv_two, expert_in, gate_probs, chosen, slot_table, gate_pick, upstream, live_rows = kept
    row_count = IMG_DEV * SEQ
    picked = contract_rows(slot_table, returned).reshape(row_count, 2, D)
    live_col = as_float(live_rows)[:, None]
    block_output = residual + live_col * lax.optimization_barrier(jnp.sum(gate_pick[:, :, None] * picked, axis=1))
    gate_grad = lax.optimization_barrier(jnp.sum(upstream[:, None, :] * picked, axis=2))
    full_gate_grad = lax.optimization_barrier(jnp.sum(gate_grad[:, :, None] * as_float(chosen), axis=1))
    logit_grad = gate_probs * (full_gate_grad - lax.optimization_barrier(jnp.sum(gate_probs * full_gate_grad, axis=-1, keepdims=True)))
    router_grad = precise_rows(as_float(expert_in), logit_grad)
    route_grad = lax.optimization_barrier(jnp.sum(contract_rows(slot_table, returned_grad).reshape(row_count, 2, D), axis=1))
    normed_two_grad = route_grad + precise_cols(logit_grad, as_float(router_weight))
    second_gain_grad = lax.optimization_barrier(jnp.sum(normed_two_grad * normed_two, axis=0))
    second_shift_grad = lax.optimization_barrier(jnp.sum(normed_two_grad, axis=0))
    residual_grad = upstream + norm_back(normed_two_grad, normed_two, inv_two, second_gain)
    proj_bias_grad = lax.optimization_barrier(jnp.sum(residual_grad, axis=0))
    residual_bf = residual_grad.astype(jnp.bfloat16)
    proj_grad = contract_rows(mixed_heads, residual_bf)
    mixed_grad = contract_cols(residual_bf, attn_out_weight).astype(jnp.bfloat16).reshape(IMG_DEV, SEQ, HEADS, HEAD_DIM)
    scores = attention_scores(query_rows, key_rows)
    probs = jnp.exp(scores - log_total)
    probs_bf = probs.astype(jnp.bfloat16)
    value_grad = jnp.einsum('bhqk,bqhd->bkhd', as_float(probs_bf), as_float(mixed_grad))
    prob_grad = jnp.einsum('bqhd,bkhd->bhqk', as_float(mixed_grad), as_float(value_rows))
    score_grad = (probs * (prob_grad - lax.optimization_barrier(jnp.sum(probs * prob_grad, axis=-1, keepdims=True))) * (1.0 / math.sqrt(HEAD_DIM))).astype(jnp.bfloat16)
    query_grad = jnp.einsum('bhqk,bkhd->bqhd', as_float(score_grad), as_float(key_rows))
    key_grad = jnp.einsum('bhqk,bqhd->bkhd', as_float(score_grad), as_float(query_rows))
    bias_grad = jnp.concatenate([lax.optimization_barrier(jnp.sum(query_grad.reshape(row_count, D), axis=0)), lax.optimization_barrier(jnp.sum(value_grad.reshape(row_count, D), axis=0))])
    packed_grad = jnp.stack([query_grad, key_grad, value_grad], axis=2).reshape(row_count, 3 * D).astype(jnp.bfloat16)
    qkv_grad = contract_rows(attn_in, packed_grad)
    normed_one_grad = contract_cols(packed_grad, qkv_weight)
    first_gain_grad = lax.optimization_barrier(jnp.sum(normed_one_grad * normed_one, axis=0))
    first_shift_grad = lax.optimization_barrier(jnp.sum(normed_one_grad, axis=0))
    input_grad = residual_grad + norm_back(normed_one_grad, normed_one, inv_one, first_gain)
    grads = (first_gain_grad, first_shift_grad, qkv_grad, bias_grad, proj_grad, proj_bias_grad, second_gain_grad, second_shift_grad, router_grad)
    return ((block_output.reshape(IMG_DEV, SEQ, D), input_grad.reshape(IMG_DEV, SEQ, D)), grads)

def reference(block_input, image_live, expert_routes, first_gain, first_shift, qkv_weight, query_value_bias, attn_out_weight, attn_out_bias, second_gain, second_shift, router_weight, expert_in_weight, expert_in_bias, expert_out_weight, expert_out_bias, output_grad):
    device_count = IMAGES // IMG_DEV
    params = (first_gain, first_shift, qkv_weight, query_value_bias, attn_out_weight, attn_out_bias, second_gain, second_shift, router_weight)

    def front(inputs):
        return forward_device(inputs[0], inputs[1], inputs[2], inputs[3], params)
    outgoing, grad_out, kept = lax.map(front, (block_input.reshape(device_count, IMG_DEV, SEQ, D), image_live.reshape(device_count, IMG_DEV), expert_routes.reshape(device_count, IMG_DEV, SEQ, 2), output_grad.reshape(device_count, IMG_DEV, SEQ, D)))

    def regroup(stacked):
        return stacked.reshape(device_count, EXPERTS, CAP, D).transpose(1, 0, 2, 3).reshape(EXPERTS, device_count * CAP, D)

    def ungroup(stacked):
        return stacked.reshape(EXPERTS, device_count, CAP, D).transpose(1, 0, 2, 3).reshape(device_count, EXPERTS * CAP, D)
    expert_out, back_rows, in_weight_grad, in_bias_grad, out_weight_grad, out_bias_grad = lax.map(expert_pass, (regroup(outgoing), regroup(grad_out), expert_in_weight, expert_in_bias, expert_out_weight, expert_out_bias))

    def back_step(running, inputs):
        outputs, grads = backward_device(inputs[0], inputs[1], inputs[2], params)
        return (jax.tree.map(jnp.add, running, grads), outputs)
    zero_grads = tuple((jnp.zeros(param.shape, jnp.float32) for param in params))
    sums, outputs = lax.scan(back_step, zero_grads, (ungroup(expert_out), ungroup(back_rows), kept))
    block_output = outputs[0].reshape(IMAGES, SEQ, D)
    input_grad = outputs[1].reshape(IMAGES, SEQ, D)
    return (block_output, input_grad, sums[0], sums[1], sums[2], sums[3], sums[4], sums[5], sums[6], sums[7], sums[8], in_weight_grad, in_bias_grad, out_weight_grad, out_bias_grad)
```

```python
import functools
import math

import jax
import jax.numpy as jnp
from jax import lax
from jax.experimental import pallas as pl
from jax.experimental.pallas import tpu as pltpu
from jax.sharding import PartitionSpec as P

HEADS = 12
HEAD_DIM = 64


EPSILON = 1e-06
PRECISE = lax.Precision.HIGHEST
HALF_ROOT = 0.7071067811865476
DENSITY = 0.3989422804014327


def as_float(array_in):
    return array_in.astype(jnp.float32)


def contract_rows(left_side, right_side):
    return lax.dot_general(
        left_side, right_side, (((0,), (0,)), ((), ())), preferred_element_type=jnp.float32
    )


def contract_cols(left_side, right_side):
    return lax.dot_general(
        left_side, right_side, (((1,), (1,)), ((), ())), preferred_element_type=jnp.float32
    )


def precise_rows(left_side, right_side):
    return lax.dot_general(
        left_side,
        right_side,
        (((0,), (0,)), ((), ())),
        precision=PRECISE,
        preferred_element_type=jnp.float32,
    )


def precise_cols(left_side, right_side):
    return lax.dot_general(
        left_side,
        right_side,
        (((1,), (1,)), ((), ())),
        precision=PRECISE,
        preferred_element_type=jnp.float32,
    )


def layer_norm(values_in, gain_vec, shift_vec):
    center = values_in - jnp.mean(values_in, axis=-1, keepdims=True)
    inv_std = lax.rsqrt(jnp.mean(center * center, axis=-1, keepdims=True) + EPSILON)
    normed = center * inv_std
    return (normed * as_float(gain_vec) + as_float(shift_vec), normed, inv_std)


def norm_back(upstream, normed, inv_std, gain_vec):
    scaled = upstream * as_float(gain_vec)
    return inv_std * (
        scaled
        - jnp.mean(scaled, axis=-1, keepdims=True)
        - normed * jnp.mean(scaled * normed, axis=-1, keepdims=True)
    )


def gelu_parts(pre_act):
    normal_cdf = 0.5 * (1.0 + jax.scipy.special.erf(pre_act * HALF_ROOT))
    return (
        pre_act * normal_cdf,
        normal_cdf + pre_act * DENSITY * jnp.exp(-0.5 * pre_act * pre_act),
    )


BIG_VMEM = 56 * 1024 * 1024
VECTORS = 7


def plain_dot(left_side, right_side):
    return jnp.dot(left_side, right_side, preferred_element_type=jnp.float32)


def exact_dot(left_side, right_side):
    return lax.dot_general(
        left_side,
        right_side,
        (((1,), (0,)), ((), ())),
        precision=PRECISE,
        preferred_element_type=jnp.float32,
    )


def round_up(value, step):
    return -(-value // step) * step


def slot_places(route_rows, live_rows, expert_count):
    row_count = route_rows.shape[0]
    flat_routes = route_rows.reshape(2 * row_count)
    alive_pairs = jnp.repeat(live_rows, 2)
    chosen = (flat_routes[:, None] == jnp.arange(expert_count, dtype=jnp.int32)[None, :]).astype(
        jnp.int32
    )
    live_hits = chosen * alive_pairs[:, None]
    earlier = (
        jnp.arange(2 * row_count, dtype=jnp.int32)[:, None]
        > jnp.arange(2 * row_count, dtype=jnp.int32)[None, :]
    ).astype(jnp.bfloat16)
    counted = jnp.dot(earlier, live_hits.astype(jnp.bfloat16), preferred_element_type=jnp.float32)
    position = jnp.sum(counted * as_float(live_hits), axis=1)
    route_code = jnp.where(alive_pairs > 0, flat_routes, -1).astype(jnp.float32)
    return route_code.reshape(row_count, 2), position.reshape(row_count, 2)


class Place:
    def __init__(self, shards, chips):
        self.shards = shards
        self.chips = chips
        self.expert = lax.axis_index("expert")
        self.shard = lax.axis_index("shard")
        self.core = lax.rem(self.expert, 2)
        self.chip = lax.div(self.expert, 2)

    def along(self, step):
        return {
            "expert": self.expert,
            "shard": lax.rem(self.shard + step + self.shards, self.shards),
        }

    def peer(self, step):
        other = lax.rem(self.chip + step + self.chips, self.chips)
        return {"expert": other * 2 + self.core, "shard": self.shard}

    def sibling(self):
        return {"expert": self.chip * 2 + 1 - self.core, "shard": self.shard}

    def plane(self, step):
        count = 2 * self.chips
        return {"expert": lax.rem(self.expert + step, count), "shard": self.shard}

    def greet(self, others):
        barrier = pltpu.get_barrier_semaphore()
        for other in others:
            pl.semaphore_signal(
                barrier, inc=1, device_id=other, device_id_type=pl.DeviceIdType.MESH
            )
        pl.semaphore_wait(barrier, len(others))


def remote(src, dst, send_sem, recv_sem, device):
    return pltpu.make_async_remote_copy(
        src_ref=src,
        dst_ref=dst,
        send_sem=send_sem,
        recv_sem=recv_sem,
        device_id=device,
        device_id_type=pl.DeviceIdType.MESH,
    )


def gather_kernel(
    shards,
    chips,
    qkv_ref,
    proj_ref,
    extra_ref,
    line_ref,
    qkv_out,
    proj_out,
    extra_out,
    line_out,
    here_sem,
    far_send,
    far_recv,
    peer_send,
    peer_recv,
    twin_send,
    twin_recv,
):
    place = Place(shards, chips)
    place.greet(
        [place.along(j) for j in range(1, shards)]
        + [place.peer(i) for i in range(1, chips)]
        + [place.sibling()]
    )
    kinds = ((qkv_ref, qkv_out), (proj_ref, proj_out))

    def cut(kind, chip_step, core):
        source = kinds[kind][0]
        rows = source.shape[0] // chips
        cols = source.shape[1] // 2
        chip = lax.rem(place.chip + chip_step + chips, chips)
        return (
            pl.ds(pl.multiple_of(chip * rows, 16), rows),
            pl.ds(pl.multiple_of(core * cols, 128), cols),
        )

    order = sorted(range(1, shards), key=lambda j: min(j, shards - j))
    sent = []

    def send(copy):
        copy.start()
        sent.append(copy)

    def far_copy(kind, j):
        if kind < 2:
            rows, cols = cut(kind, 0, place.core)
            src = kinds[kind][0].at[rows, cols]
            dst = kinds[kind][1].at[place.shard, rows, cols]
        else:
            src, dst = ((extra_ref, extra_out), (line_ref, line_out))[kind - 2]
            dst = dst.at[place.shard]
        return remote(src, dst, far_send.at[kind, j], far_recv.at[kind, j], place.along(j))

    for kind in (2, 0, 1, 3):
        for j in order:
            send(far_copy(kind, j))
    local = []
    for at, (src, dst) in enumerate(
        ((qkv_ref, qkv_out), (proj_ref, proj_out), (extra_ref, extra_out), (line_ref, line_out))
    ):
        copy = pltpu.make_async_copy(src, dst.at[place.shard], here_sem.at[at])
        copy.start()
        local.append(copy)

    def owner(j):
        return lax.rem(place.shard - j + shards, shards)

    def to_twin(kind, j, i):
        rows, cols = cut(kind, -i, place.core)
        block = kinds[kind][1].at[owner(j), rows, cols]
        return remote(
            block, block, twin_send.at[kind, j, i], twin_recv.at[kind, j, i], place.sibling()
        )

    def to_peer(kind, j, i):
        rows, cols = cut(kind, 0, place.core)
        block = kinds[kind][1].at[owner(j), rows, cols]
        return remote(
            block, block, peer_send.at[kind, j, i], peer_recv.at[kind, j, i], place.peer(i)
        )

    for kind in range(2):
        for j in order:
            far_copy(kind, j).wait_recv()
            for i in range(1, chips):
                send(to_peer(kind, j, i))
            send(to_twin(kind, j, 0))
    for kind in range(2):
        for j in order:
            for i in range(1, chips):
                to_peer(kind, j, i).wait_recv()
                send(to_twin(kind, j, i))
    for kind in range(2):
        for j in order:
            for i in range(chips):
                to_twin(kind, j, i).wait_recv()
    for kind in (2, 3):
        for j in order:
            far_copy(kind, j).wait_recv()
    for copy in sent:
        copy.wait_send()
    for copy in local:
        copy.wait()


def gather_params(fast, shards, chips, qkv, proj, extra, line):
    if not fast:
        return tuple(
            lax.all_gather(each, "shard", axis=0, tiled=False) for each in (qkv, proj, extra, line)
        )
    arrays = (qkv, proj, extra, line)
    dma = pltpu.SemaphoreType.DMA
    return pl.pallas_call(
        functools.partial(gather_kernel, shards, chips),
        out_shape=[jax.ShapeDtypeStruct((shards,) + each.shape, each.dtype) for each in arrays],
        in_specs=[pl.BlockSpec(memory_space=pl.ANY)] * 4,
        out_specs=[pl.BlockSpec(memory_space=pl.ANY)] * 4,
        scratch_shapes=[
            dma((4,)),
            dma((4, shards)),
            dma((4, shards)),
            dma((2, shards, chips)),
            dma((2, shards, chips)),
            dma((2, shards, chips)),
            dma((2, shards, chips)),
        ],
        compiler_params=pltpu.CompilerParams(collective_id=1, has_side_effects=True),
        name="gather_params",
    )(*arrays)


def norm_stats(values_in):
    center = values_in - jnp.mean(values_in, axis=-1, keepdims=True)
    inv_std = lax.rsqrt(jnp.mean(center * center, axis=-1, keepdims=True) + EPSILON)
    return center * inv_std, inv_std


def spread_rows(dst, src, image_count, seq_length, stride):
    dst[...] = jnp.zeros_like(dst)
    for image in range(image_count):
        dst[image * stride : image * stride + seq_length, :] = src[image]


def same_image(rows, stride, seq_length):
    row_at = lax.broadcasted_iota(jnp.int32, (rows, rows), 0)
    col_at = lax.broadcasted_iota(jnp.int32, (rows, rows), 1)
    mask = None
    for image in range(rows // stride):
        low = image * stride
        part = (
            (row_at >= low)
            & (row_at < low + stride)
            & (col_at >= low)
            & (col_at < low + seq_length)
        )
        mask = part if mask is None else mask | part
    return mask


def masked_softmax(query_half, keys, mask):
    scores = contract_cols(query_half, keys) * (1.0 / math.sqrt(HEAD_DIM))
    scores = jnp.where(mask, scores, -1e30)
    row_max = jnp.max(scores, axis=-1, keepdims=True)
    log_total = row_max + jnp.log(jnp.sum(jnp.exp(scores - row_max), axis=-1, keepdims=True))
    return jnp.exp(scores - log_total)


def forward_kernel(
    stride,
    expert_count,
    x_ref,
    qkv_ref,
    proj_ref,
    vec_ref,
    bias_ref,
    router_ref,
    packed_ref,
    mixed_ref,
    residual_ref,
    line_ref,
    gates_ref,
    flat_ref,
    attn_ref,
):
    image_count, seq_length, width = x_ref.shape
    rows = flat_ref.shape[0]
    bf16 = jnp.bfloat16
    spread_rows(flat_ref, x_ref, image_count, seq_length, stride)
    normed, _ = norm_stats(flat_ref[...])
    attn_ref[...] = (normed * vec_ref[0:1, :] + vec_ref[1:2, :]).astype(bf16)

    def project(tile, carry):
        cols = pl.ds(pl.multiple_of(tile * width, 128), width)
        packed_ref[:, cols] = (
            plain_dot(attn_ref[...], qkv_ref[:, cols]) + bias_ref[0:1, cols]
        ).astype(bf16)
        return carry

    lax.fori_loop(0, 3, project, 0)
    mask = same_image(rows, stride, seq_length)
    low_lanes = lax.broadcasted_iota(jnp.int32, (rows, 128), 1) < HEAD_DIM

    def attend(pair, carry):
        def part(which):
            return packed_ref[:, pl.ds(pl.multiple_of(which * width + pair * 128, 128), 128)]

        query, key, value = part(0), part(1), part(2)
        zero = jnp.zeros_like(query)
        weights_low = masked_softmax(jnp.where(low_lanes, query, zero), key, mask).astype(bf16)
        weights_high = masked_softmax(jnp.where(low_lanes, zero, query), key, mask).astype(bf16)
        mixed_ref[:, pl.ds(pl.multiple_of(pair * 128, 128), 128)] = jnp.where(
            low_lanes, plain_dot(weights_low, value), plain_dot(weights_high, value)
        ).astype(bf16)
        return carry

    lax.fori_loop(0, HEADS // 2, attend, 0)
    residual = flat_ref[...] + plain_dot(mixed_ref[...], proj_ref[...]) + vec_ref[2:3, :]
    residual_ref[...] = residual
    normed_two, _ = norm_stats(residual)
    expert_in = (normed_two * vec_ref[3:4, :] + vec_ref[4:5, :]).astype(bf16)
    line_ref[...] = expert_in
    logits = contract_cols(expert_in, router_ref[...])
    lanes = lax.broadcasted_iota(jnp.int32, logits.shape, 1)
    logits = jnp.where(lanes < expert_count, logits, -1e30)
    shifted = jnp.exp(logits - jnp.max(logits, axis=-1, keepdims=True))
    gates_ref[...] = shifted / jnp.sum(shifted, axis=-1, keepdims=True)


def backward_kernel(
    stride,
    live_ref,
    x_ref,
    up_ref,
    route_ref,
    packed_ref,
    mixed_ref,
    residual_ref,
    expert_ref,
    gates_ref,
    summed_ref,
    back_ref,
    qkv_ref,
    proj_ref,
    vec_ref,
    router_ref,
    block_ref,
    grad_ref,
    weight_ref,
    extra_ref,
    flat_ref,
    upstream_ref,
    attn_t_ref,
    mixed_grad_ref,
    packed_grad_ref,
    res_grad_ref,
):
    image_count, seq_length, width = x_ref.shape
    rows = flat_ref.shape[0]
    bf16 = jnp.bfloat16
    half = 3 * width // 2
    spread_rows(flat_ref, x_ref, image_count, seq_length, stride)
    upstream_ref[...] = jnp.zeros_like(upstream_ref)
    residual = residual_ref[...]
    block = residual + as_float(summed_ref[:, :width])
    for image in range(image_count):
        live = live_ref[image].astype(jnp.float32)
        here = slice(image * stride, image * stride + seq_length)
        upstream_ref[here, :] = up_ref[image] * live
        block_ref[image] = block[here, :]

    gates = gates_ref[...]
    lanes = lax.broadcasted_iota(jnp.int32, gates.shape, 1)
    gate_grads = as_float(summed_ref[:, width:])
    picked = jnp.zeros_like(gates)
    for route in range(2):
        picked += jnp.where(
            lanes == route_ref[:, route : route + 1], gate_grads[:, route : route + 1], 0.0
        )
    logit_grad = gates * (picked - jnp.sum(gates * picked, axis=-1, keepdims=True))
    router_rows = extra_ref.shape[0] - VECTORS
    extra_ref[VECTORS:, :] = precise_rows(logit_grad, as_float(expert_ref[...]))[
        :router_rows
    ]
    normed_two_grad = as_float(back_ref[...]) + exact_dot(
        logit_grad, as_float(router_ref[...])
    )
    normed_two, inv_two = norm_stats(residual)
    extra_ref[3:4, :] = jnp.sum(normed_two_grad * normed_two, axis=0, keepdims=True)
    extra_ref[4:5, :] = jnp.sum(normed_two_grad, axis=0, keepdims=True)
    residual_grad = upstream_ref[...] + norm_back(
        normed_two_grad, normed_two, inv_two, vec_ref[3:4, :]
    )
    res_grad_ref[...] = residual_grad
    extra_ref[2:3, :] = jnp.sum(residual_grad, axis=0, keepdims=True)
    residual_bf = residual_grad.astype(bf16)
    proj_grad = contract_rows(mixed_ref[...], residual_bf)
    for core in range(2):
        weight_ref[core, :, half:] = proj_grad[
            :, core * (width // 2) : (core + 1) * (width // 2)
        ].astype(bf16)
    mixed_grad_ref[...] = contract_cols(residual_bf, proj_ref[...]).astype(bf16)

    mask = same_image(rows, stride, seq_length)
    low_lanes = lax.broadcasted_iota(jnp.int32, (rows, 128), 1) < HEAD_DIM

    def attend(pair, carry):
        def part(which):
            return pl.ds(pl.multiple_of(which * width + pair * 128, 128), 128)

        query, key, value = (packed_ref[:, part(which)] for which in range(3))
        mixed_grad = mixed_grad_ref[:, part(0)]
        zero = jnp.zeros_like(query)
        totals = [0.0, 0.0, 0.0]
        for high in range(2):

            def only(array_in):
                return jnp.where(low_lanes, zero if high else array_in, array_in if high else zero)

            query_half, mixed_half = only(query), only(mixed_grad)
            probs = masked_softmax(query_half, key, mask)
            prob_grad = contract_cols(mixed_half, value)
            score_grad = (
                probs
                * (prob_grad - jnp.sum(probs * prob_grad, axis=-1, keepdims=True))
                * (1.0 / math.sqrt(HEAD_DIM))
            ).astype(bf16)
            totals[0] += plain_dot(score_grad, only(key))
            totals[1] += contract_rows(score_grad, query_half)
            totals[2] += contract_rows(probs.astype(bf16), mixed_half)
        for which in range(3):
            packed_grad_ref[:, part(which)] = totals[which].astype(bf16)
        extra_ref[5:6, part(0)] = jnp.sum(totals[0], axis=0, keepdims=True)
        extra_ref[6:7, part(0)] = jnp.sum(totals[2], axis=0, keepdims=True)
        return carry

    lax.fori_loop(0, HEADS // 2, attend, 0)

    normed_one, inv_one = norm_stats(flat_ref[...])
    attn_in = normed_one * vec_ref[0:1, :] + vec_ref[1:2, :]
    attn_t_ref[...] = attn_in.T.astype(bf16)
    tile = half // 3

    def weigh(at, carry):
        src = pl.ds(pl.multiple_of(at * tile, 128), tile)
        dst = pl.ds(pl.multiple_of(lax.rem(at, 3) * tile, 128), tile)
        weight_ref[lax.div(at, 3), :, dst] = plain_dot(
            attn_t_ref[...], packed_grad_ref[:, src]
        ).astype(bf16)
        return carry

    lax.fori_loop(0, 6, weigh, 0)
    upstream_ref[...] = jnp.zeros_like(upstream_ref)

    def push_back(at, carry):
        cols = pl.ds(pl.multiple_of(at * width, 128), width)
        upstream_ref[...] += contract_cols(packed_grad_ref[:, cols], qkv_ref[:, cols])
        return carry

    lax.fori_loop(0, 3, push_back, 0)
    normed_one_grad = upstream_ref[...]
    extra_ref[0:1, :] = jnp.sum(normed_one_grad * normed_one, axis=0, keepdims=True)
    extra_ref[1:2, :] = jnp.sum(normed_one_grad, axis=0, keepdims=True)
    input_grad = res_grad_ref[...] + norm_back(
        normed_one_grad, normed_one, inv_one, vec_ref[0:1, :]
    )
    for image in range(image_count):
        grad_ref[image] = input_grad[image * stride : image * stride + seq_length, :]


def reduce_kernel(
    shards,
    chips,
    grads_ref,
    extra_ref,
    qkv_out,
    proj_out,
    extra_out,
    twin_in,
    plane_sum,
    peer_in,
    far_out,
    far_in,
    whole,
    small_in,
    small_out,
    small_far,
    twin_send,
    twin_recv,
    peer_send,
    peer_recv,
    far_send,
    far_recv,
    back_send,
    back_recv,
    last_send,
    last_recv,
    small_send,
    small_recv,
    edge_send,
    edge_recv,
):
    place = Place(shards, chips)
    bf16 = jnp.bfloat16
    core, chip, shard = place.core, place.chip, place.shard
    count = 2 * chips
    place.greet(
        [place.along(j) for j in range(1, shards)]
        + [place.plane(i) for i in range(1, count)]
    )
    sent = []

    def send(copy):
        copy.start()
        sent.append(copy)

    def target(j):
        return lax.rem(shard + 1 + j, shards)

    def to_twin(j):
        return remote(
            grads_ref.at[1 - core, target(j)],
            twin_in.at[j],
            twin_send.at[j],
            twin_recv.at[j],
            place.sibling(),
        )

    def small_copy(i):
        return remote(
            extra_ref, small_in.at[i], small_send.at[i], small_recv.at[i], place.plane(i)
        )

    def peer_copy(j, i):
        return remote(
            plane_sum.at[j, lax.rem(chip + i, chips)],
            peer_in.at[j, i],
            peer_send.at[j, i],
            peer_recv.at[j, i],
            place.peer(i),
        )

    def far_copy(j):
        return remote(
            far_out.at[j], far_in.at[j], far_send.at[j], far_recv.at[j], place.along(1 + j)
        )

    def edge_copy(j):
        return remote(
            small_out, small_far.at[j], edge_send.at[j], edge_recv.at[j], place.along(j)
        )

    def back_copy(i):
        block = whole.at[core, chip]
        return remote(block, block, back_send.at[i], back_recv.at[i], place.peer(i))

    def last_copy(i):
        block = whole.at[core, lax.rem(chip - i + chips, chips)]
        return remote(block, block, last_send.at[i], last_recv.at[i], place.sibling())

    for j in range(shards):
        send(to_twin(j))
    for i in range(1, count):
        send(small_copy(i))
    for j in range(shards):
        to_twin(j).wait_recv()

        def add_twin(at, carry):
            plane_sum[j, at] = (
                as_float(grads_ref[core, target(j), at]) + as_float(twin_in[j, at])
            ).astype(bf16)
            return carry

        lax.fori_loop(0, chips, add_twin, 0)
        for i in range(1, chips):
            send(peer_copy(j, i))
    total = as_float(extra_ref[...])
    for i in range(1, count):
        small_copy(i).wait_recv()
        total += as_float(small_in[i])
    small_out[...] = total.astype(bf16)
    for j in range(1, shards):
        send(edge_copy(j))
    for j in range(shards):
        mine = as_float(plane_sum[j, chip])
        for i in range(1, chips):
            peer_copy(j, i).wait_recv()
            mine += as_float(peer_in[j, i])
        far_out[j] = mine.astype(bf16)
        if j < shards - 1:
            send(far_copy(j))
    mine = as_float(far_out[shards - 1])
    for j in range(shards - 1):
        far_copy(j).wait_recv()
        mine += as_float(far_in[j])
    whole[core, chip] = mine.astype(bf16)
    for i in range(1, chips):
        send(back_copy(i))
    send(last_copy(0))
    total = as_float(small_out[...])
    for j in range(1, shards):
        edge_copy(j).wait_recv()
        total += as_float(small_far[j])
    extra_out[...] = total
    for i in range(1, chips):
        back_copy(i).wait_recv()
        send(last_copy(i))
    for i in range(chips):
        last_copy(i).wait_recv()
    rows = qkv_out.shape[0] // chips
    wide, narrow = qkv_out.shape[1] // 2, proj_out.shape[1] // 2
    for side in range(2):
        for at in range(chips):
            block = as_float(whole[side, at])
            here = slice(at * rows, (at + 1) * rows)
            qkv_out[here, side * wide : (side + 1) * wide] = block[:, :wide]
            proj_out[here, side * narrow : (side + 1) * narrow] = block[:, wide:]
    for copy in sent:
        copy.wait_send()


def reduce_grads(fast, shards, chips, grads, extra):
    _, height, cols = grads.shape
    width = cols // 2
    shard_rows = height // shards
    if not fast:
        wide = 3 * width // 2
        joined = jnp.concatenate(
            [grads[0, :, :wide], grads[1, :, :wide], grads[0, :, wide:], grads[1, :, wide:]],
            axis=1,
        )
        mine = lax.psum_scatter(joined, "shard", scatter_dimension=0, tiled=True)
        mine = as_float(lax.psum(mine, "expert"))
        extra_sum = as_float(lax.psum(extra, ("shard", "expert")))
        return mine[:, : 3 * width], mine[:, 3 * width :], extra_sum
    rows = shard_rows // chips
    bf16, dma = jnp.bfloat16, pltpu.SemaphoreType.DMA
    cut = grads.reshape(2, shards, chips, rows, cols)
    count = 2 * chips
    return pl.pallas_call(
        functools.partial(reduce_kernel, shards, chips),
        out_shape=[
            jax.ShapeDtypeStruct((shard_rows, 3 * width), jnp.float32),
            jax.ShapeDtypeStruct((shard_rows, width), jnp.float32),
            jax.ShapeDtypeStruct(extra.shape, jnp.float32),
        ],
        in_specs=[pl.BlockSpec(memory_space=pltpu.VMEM)] * 2,
        out_specs=[pl.BlockSpec(memory_space=pltpu.VMEM)] * 3,
        scratch_shapes=[
            pltpu.VMEM((shards, chips, rows, cols), bf16),
            pltpu.VMEM((shards, chips, rows, cols), bf16),
            pltpu.VMEM((shards, chips, rows, cols), bf16),
            pltpu.VMEM((shards, rows, cols), bf16),
            pltpu.VMEM((shards, rows, cols), bf16),
            pltpu.VMEM((2, chips, rows, cols), bf16),
            pltpu.VMEM((count,) + extra.shape, bf16),
            pltpu.VMEM(extra.shape, bf16),
            pltpu.VMEM((shards,) + extra.shape, bf16),
            dma((shards,)),
            dma((shards,)),
            dma((shards, chips)),
            dma((shards, chips)),
            dma((shards,)),
            dma((shards,)),
            dma((chips,)),
            dma((chips,)),
            dma((chips,)),
            dma((chips,)),
            dma((count,)),
            dma((count,)),
            dma((shards,)),
            dma((shards,)),
        ],
        compiler_params=pltpu.CompilerParams(
            collective_id=2, has_side_effects=True, vmem_limit_bytes=BIG_VMEM
        ),
        name="reduce_grads",
    )(cut, extra)


def body(
    block_input,
    image_live,
    expert_routes,
    first_gain,
    first_shift,
    qkv_weight,
    query_value_bias,
    attn_out_weight,
    attn_out_bias,
    second_gain,
    second_shift,
    router_weight,
    expert_in_weight,
    expert_in_bias,
    expert_out_weight,
    expert_out_bias,
    output_grad,
):
    image_count, seq_length, width = block_input.shape
    shards = lax.axis_size("shard")
    experts = lax.axis_size("expert")
    chips = experts // 2
    expert_count = router_weight.shape[1]
    my_shard = lax.axis_index("shard")
    shard_rows = first_gain.shape[0]
    stride = round_up(seq_length, 8)
    row_count = image_count * stride
    capacity = (3 * image_count * seq_length + expert_count - 1) // expert_count
    group_rows = round_up(shards * capacity, 16)
    slot_rows = expert_count * group_rows
    bf16 = jnp.bfloat16
    fast = chips == 4 and shard_rows % (16 * chips) == 0

    router_pad = round_up(expert_count, 128)
    extra = jnp.concatenate(
        [
            jnp.stack(
                [
                    first_gain,
                    first_shift,
                    attn_out_bias,
                    second_gain,
                    second_shift,
                    query_value_bias[:shard_rows],
                    query_value_bias[shard_rows:],
                ]
            ),
            router_weight.T,
        ],
        axis=0,
    )
    extra_rows = round_up(VECTORS + expert_count, 16)
    extra = jnp.pad(
        extra,
        ((0, extra_rows - extra.shape[0]), (0, round_up(shard_rows, 128) - shard_rows)),
    )

    tail_rows = stride - seq_length
    live_rows = jnp.repeat(image_live, stride) * jnp.tile(
        (jnp.arange(stride) < seq_length).astype(jnp.int32), image_count
    )
    route_rows = jnp.pad(expert_routes, ((0, 0), (0, tail_rows), (0, 0))).reshape(row_count, 2)
    route_code, position = slot_places(route_rows, live_rows, expert_count)
    up_rows = (
        jnp.pad(output_grad, ((0, 0), (0, tail_rows), (0, 0))).reshape(row_count, width)
        * as_float(live_rows)[:, None]
    )
    notes = jnp.concatenate([route_code.astype(bf16), position.astype(bf16)], axis=1)
    notes = jnp.pad(notes, ((0, 0), (0, 128 - notes.shape[1])))
    up_line = jnp.concatenate([up_rows.astype(bf16), notes], axis=1)

    qkv_all, proj_all, extra_all, line_all = gather_params(
        fast, shards, chips, qkv_weight, attn_out_weight, extra, up_line
    )
    qkv_full = qkv_all.reshape(width, 3 * width)
    proj_full = proj_all.reshape(width, width)
    extra_t = jnp.transpose(extra_all[:, :, :shard_rows], (1, 0, 2))
    vectors = as_float(extra_t[:8]).reshape(8, width)
    query_value = as_float(extra_t[5:7])
    bias_full = jnp.transpose(query_value, (1, 0, 2)).reshape(2 * width)
    bias_row = jnp.concatenate(
        [bias_full[:width], jnp.zeros((width,), jnp.float32), bias_full[width:]]
    )
    bias_row = jnp.pad(bias_row[None], ((0, 7), (0, 0)))
    router_t = jnp.pad(
        extra_t[VECTORS : VECTORS + expert_count].reshape(expert_count, width),
        ((0, router_pad - expert_count), (0, 0)),
    )

    line_rows = shards * row_count
    line = line_all.reshape(line_rows, width + 128)
    line_up = line[:, :width]
    line_notes = as_float(line[:, width : width + 4])
    line_ids = jnp.arange(line_rows, dtype=jnp.int32)[:, None]
    line_slot = (
        line_notes[:, 0:2].astype(jnp.int32) * group_rows
        + (line_ids // row_count) * capacity
        + line_notes[:, 2:4].astype(jnp.int32)
    )
    line_slot = jnp.where(line_notes[:, 0:2] >= 0, line_slot, -1)
    slot_ids = jnp.arange(slot_rows, dtype=jnp.int32)
    table_0 = line_slot[:, 0:1] == slot_ids[None, :]
    table_1 = line_slot[:, 1:2] == slot_ids[None, :]
    send_table = (table_0 | table_1).astype(bf16)
    up_out = contract_rows(send_table, line_up).astype(bf16)
    up_in = lax.all_to_all(up_out, "expert", split_axis=0, concat_axis=0, tiled=True)

    out_slice = lax.all_to_all(
        expert_out_weight[0], "shard", split_axis=0, concat_axis=1, tiled=True
    )
    in_slice = expert_in_weight[0]

    packed, mixed, residual, expert_in, gates = pl.pallas_call(
        functools.partial(forward_kernel, stride, expert_count),
        out_shape=[
            jax.ShapeDtypeStruct((row_count, 3 * width), bf16),
            jax.ShapeDtypeStruct((row_count, width), bf16),
            jax.ShapeDtypeStruct((row_count, width), jnp.float32),
            jax.ShapeDtypeStruct((row_count, width), bf16),
            jax.ShapeDtypeStruct((row_count, router_pad), jnp.float32),
        ],
        in_specs=[pl.BlockSpec(memory_space=pltpu.VMEM)] * 6,
        out_specs=[pl.BlockSpec(memory_space=pltpu.VMEM)] * 5,
        scratch_shapes=[
            pltpu.VMEM((row_count, width), jnp.float32),
            pltpu.VMEM((row_count, width), bf16),
        ],
        compiler_params=pltpu.CompilerParams(vmem_limit_bytes=BIG_VMEM),
        cost_estimate=pl.CostEstimate(
            flops=16 * row_count * width * width,
            bytes_accessed=24 * width * width,
            transcendentals=2 * HEADS * row_count * row_count,
        ),
        name="attention_forward",
    )(block_input, qkv_full, proj_full, vectors, bias_row, router_t)

    chosen = route_rows[:, :, None] == jnp.arange(router_pad, dtype=jnp.int32)[None, None, :]
    gate_pick = jnp.sum(jnp.where(chosen, gates[:, None, :], 0.0), axis=2)
    gate_high = gate_pick.astype(bf16)
    gate_low = (gate_pick - as_float(gate_high)).astype(bf16)
    gate_notes = jnp.concatenate([gate_high, gate_low], axis=1)
    gate_notes = jnp.pad(gate_notes, ((0, 0), (0, 128 - gate_notes.shape[1])))
    sent_line = jnp.concatenate([expert_in, gate_notes], axis=1)
    row_line = lax.all_gather(sent_line, "shard", axis=0, tiled=True)
    line_in = row_line[:, :width]
    gate_line = as_float(row_line[:, width : width + 4])
    line_gate = gate_line[:, 0:2] + gate_line[:, 2:4]
    outgoing = contract_rows(send_table, line_in).astype(bf16)
    slot_gate = jnp.sum(
        jnp.where(table_0, line_gate[:, 0:1], 0.0) + jnp.where(table_1, line_gate[:, 1:2], 0.0),
        axis=0,
    )
    slot_high = slot_gate.astype(bf16)
    slot_low = (slot_gate - as_float(slot_high)).astype(bf16)
    slot_notes = jnp.pad(jnp.stack([slot_high, slot_low], axis=1), ((0, 0), (0, 126)))
    incoming = lax.all_to_all(
        jnp.concatenate([outgoing, slot_notes], axis=1),
        "expert",
        split_axis=0,
        concat_axis=0,
        tiled=True,
    )
    rows_in = incoming[:, :width]
    gate_in = as_float(incoming[:, width : width + 1]) + as_float(
        incoming[:, width + 1 : width + 2]
    )
    grad_in = (as_float(up_in) * gate_in).astype(bf16)

    pre_act = jnp.dot(rows_in, in_slice, preferred_element_type=jnp.float32) + as_float(
        expert_in_bias
    )
    gelu_out, gelu_slope = gelu_parts(pre_act)
    gelu_bf = gelu_out.astype(bf16)
    own_bias = lax.dynamic_update_slice(
        jnp.zeros((1, width), jnp.float32),
        as_float(expert_out_bias),
        (0, my_shard * shard_rows),
    )
    expert_out = (
        jnp.dot(gelu_bf, out_slice, preferred_element_type=jnp.float32) + own_bias
    ).astype(bf16)
    returned = lax.all_to_all(expert_out, "expert", split_axis=0, concat_axis=0, tiled=True)
    pre_grad = contract_cols(grad_in, out_slice) * gelu_slope
    in_bias_part = jnp.sum(pre_grad, axis=0)[None]
    pre_bf = pre_grad.astype(bf16)
    back_rows = contract_cols(pre_bf, in_slice).astype(bf16)
    returned_grad = lax.all_to_all(back_rows, "expert", split_axis=0, concat_axis=0, tiled=True)
    out_weight_grad = contract_rows(gelu_bf, grad_in).astype(bf16)
    out_weight_part = as_float(
        lax.all_to_all(out_weight_grad, "shard", split_axis=1, concat_axis=0, tiled=True)
    )[None]
    in_weight_part = contract_rows(rows_in, pre_bf)[None]
    out_bias_part = lax.dynamic_slice_in_dim(
        jnp.sum(as_float(grad_in), axis=0), my_shard * shard_rows, shard_rows
    )[None]

    out_0 = jnp.dot(table_0.astype(bf16), returned, preferred_element_type=jnp.float32)
    out_1 = jnp.dot(table_1.astype(bf16), returned, preferred_element_type=jnp.float32)
    combined = line_gate[:, 0:1] * out_0 + line_gate[:, 1:2] * out_1
    line_up_wide = as_float(line_up)
    gate_grad_line = jnp.stack(
        [jnp.sum(line_up_wide * out_0, axis=1), jnp.sum(line_up_wide * out_1, axis=1)], axis=1
    )
    summed = lax.psum_scatter(
        jnp.concatenate(
            [
                combined.astype(bf16),
                jnp.pad(gate_grad_line, ((0, 0), (0, 126))).astype(bf16),
            ],
            axis=1,
        ),
        "shard",
        scatter_dimension=0,
        tiled=True,
    )
    back_line = jnp.dot(send_table, returned_grad, preferred_element_type=jnp.float32)
    route_grad = lax.psum_scatter(back_line.astype(bf16), "shard", scatter_dimension=0, tiled=True)

    smem = pl.BlockSpec(memory_space=pltpu.SMEM)
    vmem = pl.BlockSpec(memory_space=pltpu.VMEM)
    wide_rows = pltpu.VMEM((row_count, width), jnp.float32)
    block_output, input_grad, weight_grads, extra_grads = pl.pallas_call(
        functools.partial(backward_kernel, stride),
        out_shape=[
            jax.ShapeDtypeStruct(block_input.shape, jnp.float32),
            jax.ShapeDtypeStruct(block_input.shape, jnp.float32),
            jax.ShapeDtypeStruct((2, width, 2 * width), bf16),
            jax.ShapeDtypeStruct((extra_rows, width), jnp.float32),
        ],
        in_specs=[smem] + [vmem] * 14,
        out_specs=[vmem] * 4,
        scratch_shapes=[
            wide_rows,
            wide_rows,
            pltpu.VMEM((width, row_count), bf16),
            pltpu.VMEM((row_count, width), bf16),
            pltpu.VMEM((row_count, 3 * width), bf16),
            wide_rows,
        ],
        compiler_params=pltpu.CompilerParams(vmem_limit_bytes=BIG_VMEM),
        cost_estimate=pl.CostEstimate(
            flops=32 * row_count * width * width,
            bytes_accessed=48 * width * width,
            transcendentals=2 * HEADS * row_count * row_count,
        ),
        name="attention_backward",
    )(
        image_live,
        block_input,
        output_grad,
        route_rows,
        packed,
        mixed,
        residual,
        expert_in,
        gates,
        summed,
        route_grad,
        qkv_full,
        proj_full,
        vectors,
        router_t,
    )
    qkv_sum, proj_sum, extra_sum = reduce_grads(
        fast, shards, chips, weight_grads, extra_grads.astype(bf16)
    )

    def own(array_in, size, axis=0):
        return lax.dynamic_slice_in_dim(array_in, my_shard * size, size, axis=axis)

    mine = own(extra_sum, shard_rows, axis=1)
    return (
        block_output,
        input_grad,
        mine[0],
        mine[1],
        qkv_sum,
        own(extra_sum[5:7].reshape(2 * width), 2 * shard_rows),
        proj_sum,
        mine[2],
        mine[3],
        mine[4],
        mine[VECTORS : VECTORS + expert_count].T,
        in_weight_part,
        in_bias_part,
        out_weight_part,
        out_bias_part,
    )


def solution(mesh):
    in_specs = (
        P(("expert", "shard"), None, None),
        P(("expert", "shard")),
        P(("expert", "shard"), None, None),
        P("shard"),
        P("shard"),
        P("shard", None),
        P("shard"),
        P("shard", None),
        P("shard"),
        P("shard"),
        P("shard"),
        P("shard", None),
        P("expert", None, "shard"),
        P("expert", "shard"),
        P("expert", None, "shard"),
        P("expert", "shard"),
        P(("expert", "shard"), None, None),
    )
    out_specs = (
        P(("expert", "shard"), None, None),
        P(("expert", "shard"), None, None),
        P("shard"),
        P("shard"),
        P("shard", None),
        P("shard"),
        P("shard", None),
        P("shard"),
        P("shard"),
        P("shard"),
        P("shard", None),
        P("expert", None, "shard"),
        P("expert", "shard"),
        P("expert", None, "shard"),
        P("expert", "shard"),
    )
    return jax.shard_map(body, mesh=mesh, in_specs=in_specs, out_specs=out_specs, check_vma=False)
```

```python
import functools
import math

import jax
import jax.numpy as jnp
from jax import lax
from jax.experimental import pallas as pl
from jax.experimental.pallas import tpu as pltpu
from jax.sharding import PartitionSpec as P

HEADS = 12
HEAD_DIM = 64


EPSILON = 1e-06
PRECISE = lax.Precision.HIGHEST
HALF_ROOT = 0.7071067811865476
DENSITY = 0.3989422804014327


def as_float(array_in):
    return array_in.astype(jnp.float32)


def contract_rows(left_side, right_side):
    return lax.dot_general(
        left_side, right_side, (((0,), (0,)), ((), ())), preferred_element_type=jnp.float32
    )


def contract_cols(left_side, right_side):
    return lax.dot_general(
        left_side, right_side, (((1,), (1,)), ((), ())), preferred_element_type=jnp.float32
    )


def precise_rows(left_side, right_side):
    return lax.dot_general(
        left_side,
        right_side,
        (((0,), (0,)), ((), ())),
        precision=PRECISE,
        preferred_element_type=jnp.float32,
    )


def precise_cols(left_side, right_side):
    return lax.dot_general(
        left_side,
        right_side,
        (((1,), (1,)), ((), ())),
        precision=PRECISE,
        preferred_element_type=jnp.float32,
    )


def layer_norm(values_in, gain_vec, shift_vec):
    center = values_in - jnp.mean(values_in, axis=-1, keepdims=True)
    inv_std = lax.rsqrt(jnp.mean(center * center, axis=-1, keepdims=True) + EPSILON)
    normed = center * inv_std
    return (normed * as_float(gain_vec) + as_float(shift_vec), normed, inv_std)


def norm_back(upstream, normed, inv_std, gain_vec):
    scaled = upstream * as_float(gain_vec)
    return inv_std * (
        scaled
        - jnp.mean(scaled, axis=-1, keepdims=True)
        - normed * jnp.mean(scaled * normed, axis=-1, keepdims=True)
    )


def gelu_parts(pre_act):
    normal_cdf = 0.5 * (1.0 + jax.scipy.special.erf(pre_act * HALF_ROOT))
    return (
        pre_act * normal_cdf,
        normal_cdf + pre_act * DENSITY * jnp.exp(-0.5 * pre_act * pre_act),
    )


BIG_VMEM = 56 * 1024 * 1024
VECTORS = 7


def plain_dot(left_side, right_side):
    return jnp.dot(left_side, right_side, preferred_element_type=jnp.float32)


def exact_dot(left_side, right_side):
    return lax.dot_general(
        left_side,
        right_side,
        (((1,), (0,)), ((), ())),
        precision=PRECISE,
        preferred_element_type=jnp.float32,
    )


def round_up(value, step):
    return -(-value // step) * step


def slot_places(route_rows, live_rows, expert_count):
    row_count = route_rows.shape[0]
    flat_routes = route_rows.reshape(2 * row_count)
    alive_pairs = jnp.repeat(live_rows, 2)
    chosen = (flat_routes[:, None] == jnp.arange(expert_count, dtype=jnp.int32)[None, :]).astype(
        jnp.int32
    )
    live_hits = chosen * alive_pairs[:, None]
    earlier = (
        jnp.arange(2 * row_count, dtype=jnp.int32)[:, None]
        > jnp.arange(2 * row_count, dtype=jnp.int32)[None, :]
    ).astype(jnp.bfloat16)
    counted = jnp.dot(earlier, live_hits.astype(jnp.bfloat16), preferred_element_type=jnp.float32)
    position = jnp.sum(counted * as_float(live_hits), axis=1)
    route_code = jnp.where(alive_pairs > 0, flat_routes, -1).astype(jnp.float32)
    return route_code.reshape(row_count, 2), position.reshape(row_count, 2)


class Place:
    def __init__(self, shards, chips):
        self.shards = shards
        self.chips = chips
        self.expert = lax.axis_index("expert")
        self.shard = lax.axis_index("shard")
        self.core = lax.rem(self.expert, 2)
        self.chip = lax.div(self.expert, 2)

    def along(self, step):
        return {
            "expert": self.expert,
            "shard": lax.rem(self.shard + step + self.shards, self.shards),
        }

    def peer(self, step):
        other = lax.rem(self.chip + step + self.chips, self.chips)
        return {"expert": other * 2 + self.core, "shard": self.shard}

    def sibling(self):
        return {"expert": self.chip * 2 + 1 - self.core, "shard": self.shard}

    def plane(self, step):
        count = 2 * self.chips
        return {"expert": lax.rem(self.expert + step, count), "shard": self.shard}

    def greet(self, others):
        barrier = pltpu.get_barrier_semaphore()
        for other in others:
            pl.semaphore_signal(
                barrier, inc=1, device_id=other, device_id_type=pl.DeviceIdType.MESH
            )
        pl.semaphore_wait(barrier, len(others))


def remote(src, dst, send_sem, recv_sem, device):
    return pltpu.make_async_remote_copy(
        src_ref=src,
        dst_ref=dst,
        send_sem=send_sem,
        recv_sem=recv_sem,
        device_id=device,
        device_id_type=pl.DeviceIdType.MESH,
    )


def gather_kernel(
    shards,
    chips,
    qkv_ref,
    proj_ref,
    extra_ref,
    line_ref,
    qkv_out,
    proj_out,
    extra_out,
    line_out,
    here_sem,
    far_send,
    far_recv,
    peer_send,
    peer_recv,
    twin_send,
    twin_recv,
):
    place = Place(shards, chips)
    place.greet(
        [place.along(j) for j in range(1, shards)]
        + [place.peer(i) for i in range(1, chips)]
        + [place.sibling()]
    )
    kinds = ((qkv_ref, qkv_out), (proj_ref, proj_out))

    def cut(kind, chip_step, core):
        source = kinds[kind][0]
        rows = source.shape[0] // chips
        cols = source.shape[1] // 2
        chip = lax.rem(place.chip + chip_step + chips, chips)
        return (
            pl.ds(pl.multiple_of(chip * rows, 16), rows),
            pl.ds(pl.multiple_of(core * cols, 128), cols),
        )

    order = sorted(range(1, shards), key=lambda j: min(j, shards - j))
    sent = []

    def send(copy):
        copy.start()
        sent.append(copy)

    def far_copy(kind, j):
        if kind < 2:
            rows, cols = cut(kind, 0, place.core)
            src = kinds[kind][0].at[rows, cols]
            dst = kinds[kind][1].at[place.shard, rows, cols]
        else:
            src, dst = ((extra_ref, extra_out), (line_ref, line_out))[kind - 2]
            dst = dst.at[place.shard]
        return remote(src, dst, far_send.at[kind, j], far_recv.at[kind, j], place.along(j))

    for kind in (2, 0, 1, 3):
        for j in order:
            send(far_copy(kind, j))
    local = []
    for at, (src, dst) in enumerate(
        ((qkv_ref, qkv_out), (proj_ref, proj_out), (extra_ref, extra_out), (line_ref, line_out))
    ):
        copy = pltpu.make_async_copy(src, dst.at[place.shard], here_sem.at[at])
        copy.start()
        local.append(copy)

    def owner(j):
        return lax.rem(place.shard - j + shards, shards)

    def to_twin(kind, j, i):
        rows, cols = cut(kind, -i, place.core)
        block = kinds[kind][1].at[owner(j), rows, cols]
        return remote(
            block, block, twin_send.at[kind, j, i], twin_recv.at[kind, j, i], place.sibling()
        )

    def to_peer(kind, j, i):
        rows, cols = cut(kind, 0, place.core)
        block = kinds[kind][1].at[owner(j), rows, cols]
        return remote(
            block, block, peer_send.at[kind, j, i], peer_recv.at[kind, j, i], place.peer(i)
        )

    for kind in range(2):
        for j in order:
            far_copy(kind, j).wait_recv()
            for i in range(1, chips):
                send(to_peer(kind, j, i))
            send(to_twin(kind, j, 0))
    for kind in range(2):
        for j in order:
            for i in range(1, chips):
                to_peer(kind, j, i).wait_recv()
                send(to_twin(kind, j, i))
    for kind in range(2):
        for j in order:
            for i in range(chips):
                to_twin(kind, j, i).wait_recv()
    for kind in (2, 3):
        for j in order:
            far_copy(kind, j).wait_recv()
    for copy in sent:
        copy.wait_send()
    for copy in local:
        copy.wait()


def gather_params(fast, shards, chips, qkv, proj, extra, line):
    if not fast:
        return tuple(
            lax.all_gather(each, "shard", axis=0, tiled=False) for each in (qkv, proj, extra, line)
        )
    arrays = (qkv, proj, extra, line)
    dma = pltpu.SemaphoreType.DMA
    return pl.pallas_call(
        functools.partial(gather_kernel, shards, chips),
        out_shape=[jax.ShapeDtypeStruct((shards,) + each.shape, each.dtype) for each in arrays],
        in_specs=[pl.BlockSpec(memory_space=pl.ANY)] * 4,
        out_specs=[pl.BlockSpec(memory_space=pl.ANY)] * 4,
        scratch_shapes=[
            dma((4,)),
            dma((4, shards)),
            dma((4, shards)),
            dma((2, shards, chips)),
            dma((2, shards, chips)),
            dma((2, shards, chips)),
            dma((2, shards, chips)),
        ],
        compiler_params=pltpu.CompilerParams(collective_id=1, has_side_effects=True),
        name="gather_params",
    )(*arrays)


def norm_stats(values_in):
    center = values_in - jnp.mean(values_in, axis=-1, keepdims=True)
    inv_std = lax.rsqrt(jnp.mean(center * center, axis=-1, keepdims=True) + EPSILON)
    return center * inv_std, inv_std


def spread_rows(dst, src, image_count, seq_length, stride):
    dst[...] = jnp.zeros_like(dst)
    for image in range(image_count):
        dst[image * stride : image * stride + seq_length, :] = src[image]


def same_image(rows, stride, seq_length):
    row_at = lax.broadcasted_iota(jnp.int32, (rows, rows), 0)
    col_at = lax.broadcasted_iota(jnp.int32, (rows, rows), 1)
    mask = None
    for image in range(rows // stride):
        low = image * stride
        part = (
            (row_at >= low)
            & (row_at < low + stride)
            & (col_at >= low)
            & (col_at < low + seq_length)
        )
        mask = part if mask is None else mask | part
    return mask


def masked_softmax(query_half, keys, mask):
    scores = contract_cols(query_half, keys) * (1.0 / math.sqrt(HEAD_DIM))
    scores = jnp.where(mask, scores, -1e30)
    row_max = jnp.max(scores, axis=-1, keepdims=True)
    log_total = row_max + jnp.log(jnp.sum(jnp.exp(scores - row_max), axis=-1, keepdims=True))
    return jnp.exp(scores - log_total)


def forward_kernel(
    stride,
    expert_count,
    x_ref,
    qkv_ref,
    proj_ref,
    vec_ref,
    bias_ref,
    router_ref,
    packed_ref,
    mixed_ref,
    residual_ref,
    line_ref,
    gates_ref,
    flat_ref,
    attn_ref,
):
    image_count, seq_length, width = x_ref.shape
    rows = flat_ref.shape[0]
    bf16 = jnp.bfloat16
    spread_rows(flat_ref, x_ref, image_count, seq_length, stride)
    normed, _ = norm_stats(flat_ref[...])
    attn_ref[...] = (normed * vec_ref[0:1, :] + vec_ref[1:2, :]).astype(bf16)

    def project(tile, carry):
        cols = pl.ds(pl.multiple_of(tile * width, 128), width)
        packed_ref[:, cols] = (
            plain_dot(attn_ref[...], qkv_ref[:, cols]) + bias_ref[0:1, cols]
        ).astype(bf16)
        return carry

    lax.fori_loop(0, 3, project, 0)
    mask = same_image(rows, stride, seq_length)
    low_lanes = lax.broadcasted_iota(jnp.int32, (rows, 128), 1) < HEAD_DIM

    def attend(pair, carry):
        def part(which):
            return packed_ref[:, pl.ds(pl.multiple_of(which * width + pair * 128, 128), 128)]

        query, key, value = part(0), part(1), part(2)
        zero = jnp.zeros_like(query)
        weights_low = masked_softmax(jnp.where(low_lanes, query, zero), key, mask).astype(bf16)
        weights_high = masked_softmax(jnp.where(low_lanes, zero, query), key, mask).astype(bf16)
        mixed_ref[:, pl.ds(pl.multiple_of(pair * 128, 128), 128)] = jnp.where(
            low_lanes, plain_dot(weights_low, value), plain_dot(weights_high, value)
        ).astype(bf16)
        return carry

    lax.fori_loop(0, HEADS // 2, attend, 0)
    residual = flat_ref[...] + plain_dot(mixed_ref[...], proj_ref[...]) + vec_ref[2:3, :]
    residual_ref[...] = residual
    normed_two, _ = norm_stats(residual)
    expert_in = (normed_two * vec_ref[3:4, :] + vec_ref[4:5, :]).astype(bf16)
    line_ref[...] = expert_in
    logits = contract_cols(expert_in, router_ref[...])
    lanes = lax.broadcasted_iota(jnp.int32, logits.shape, 1)
    logits = jnp.where(lanes < expert_count, logits, -1e30)
    shifted = jnp.exp(logits - jnp.max(logits, axis=-1, keepdims=True))
    gates_ref[...] = shifted / jnp.sum(shifted, axis=-1, keepdims=True)


def backward_kernel(
    stride,
    live_ref,
    x_ref,
    up_ref,
    packed_ref,
    mixed_ref,
    residual_ref,
    expert_ref,
    gates_ref,
    summed_ref,
    back_ref,
    qkv_ref,
    proj_ref,
    vec_ref,
    router_ref,
    block_ref,
    grad_ref,
    weight_ref,
    extra_ref,
    flat_ref,
    upstream_ref,
    attn_t_ref,
    mixed_grad_ref,
    packed_grad_ref,
    res_grad_ref,
):
    image_count, seq_length, width = x_ref.shape
    rows = flat_ref.shape[0]
    bf16 = jnp.bfloat16
    half = 3 * width // 2
    spread_rows(flat_ref, x_ref, image_count, seq_length, stride)
    upstream_ref[...] = jnp.zeros_like(upstream_ref)
    residual = residual_ref[...]
    block = residual + as_float(summed_ref[:, :width])
    for image in range(image_count):
        live = live_ref[image].astype(jnp.float32)
        here = slice(image * stride, image * stride + seq_length)
        upstream_ref[here, :] = up_ref[image] * live
        block_ref[image] = block[here, :]

    gates = gates_ref[...]
    picked = as_float(summed_ref[:, width:])
    logit_grad = gates * (picked - jnp.sum(gates * picked, axis=-1, keepdims=True))
    router_rows = extra_ref.shape[0] - VECTORS
    extra_ref[VECTORS:, :] = precise_rows(logit_grad, as_float(expert_ref[...]))[
        :router_rows
    ]
    normed_two_grad = as_float(back_ref[...]) + exact_dot(
        logit_grad, as_float(router_ref[...])
    )
    normed_two, inv_two = norm_stats(residual)
    extra_ref[3:4, :] = jnp.sum(normed_two_grad * normed_two, axis=0, keepdims=True)
    extra_ref[4:5, :] = jnp.sum(normed_two_grad, axis=0, keepdims=True)
    residual_grad = upstream_ref[...] + norm_back(
        normed_two_grad, normed_two, inv_two, vec_ref[3:4, :]
    )
    res_grad_ref[...] = residual_grad
    extra_ref[2:3, :] = jnp.sum(residual_grad, axis=0, keepdims=True)
    residual_bf = residual_grad.astype(bf16)
    proj_grad = contract_rows(mixed_ref[...], residual_bf)
    for core in range(2):
        weight_ref[core, :, half:] = proj_grad[
            :, core * (width // 2) : (core + 1) * (width // 2)
        ].astype(bf16)
    mixed_grad_ref[...] = contract_cols(residual_bf, proj_ref[...]).astype(bf16)

    mask = same_image(rows, stride, seq_length)
    low_lanes = lax.broadcasted_iota(jnp.int32, (rows, 128), 1) < HEAD_DIM

    def attend(pair, carry):
        def part(which):
            return pl.ds(pl.multiple_of(which * width + pair * 128, 128), 128)

        query, key, value = (packed_ref[:, part(which)] for which in range(3))
        mixed_grad = mixed_grad_ref[:, part(0)]
        zero = jnp.zeros_like(query)
        totals = [0.0, 0.0, 0.0]
        for high in range(2):

            def only(array_in):
                return jnp.where(low_lanes, zero if high else array_in, array_in if high else zero)

            query_half, mixed_half = only(query), only(mixed_grad)
            probs = masked_softmax(query_half, key, mask)
            prob_grad = contract_cols(mixed_half, value)
            score_grad = (
                probs
                * (prob_grad - jnp.sum(probs * prob_grad, axis=-1, keepdims=True))
                * (1.0 / math.sqrt(HEAD_DIM))
            ).astype(bf16)
            totals[0] += plain_dot(score_grad, only(key))
            totals[1] += contract_rows(score_grad, query_half)
            totals[2] += contract_rows(probs.astype(bf16), mixed_half)
        for which in range(3):
            packed_grad_ref[:, part(which)] = totals[which].astype(bf16)
        extra_ref[5:6, part(0)] = jnp.sum(totals[0], axis=0, keepdims=True)
        extra_ref[6:7, part(0)] = jnp.sum(totals[2], axis=0, keepdims=True)
        return carry

    lax.fori_loop(0, HEADS // 2, attend, 0)

    normed_one, inv_one = norm_stats(flat_ref[...])
    attn_in = normed_one * vec_ref[0:1, :] + vec_ref[1:2, :]
    attn_t_ref[...] = attn_in.T.astype(bf16)
    tile = half // 3

    def weigh(at, carry):
        src = pl.ds(pl.multiple_of(at * tile, 128), tile)
        dst = pl.ds(pl.multiple_of(lax.rem(at, 3) * tile, 128), tile)
        weight_ref[lax.div(at, 3), :, dst] = plain_dot(
            attn_t_ref[...], packed_grad_ref[:, src]
        ).astype(bf16)
        return carry

    lax.fori_loop(0, 6, weigh, 0)
    upstream_ref[...] = jnp.zeros_like(upstream_ref)

    def push_back(at, carry):
        cols = pl.ds(pl.multiple_of(at * width, 128), width)
        upstream_ref[...] += contract_cols(packed_grad_ref[:, cols], qkv_ref[:, cols])
        return carry

    lax.fori_loop(0, 3, push_back, 0)
    normed_one_grad = upstream_ref[...]
    extra_ref[0:1, :] = jnp.sum(normed_one_grad * normed_one, axis=0, keepdims=True)
    extra_ref[1:2, :] = jnp.sum(normed_one_grad, axis=0, keepdims=True)
    input_grad = res_grad_ref[...] + norm_back(
        normed_one_grad, normed_one, inv_one, vec_ref[0:1, :]
    )
    for image in range(image_count):
        grad_ref[image] = input_grad[image * stride : image * stride + seq_length, :]


def reduce_kernel(
    shards,
    chips,
    grads_ref,
    extra_ref,
    qkv_out,
    proj_out,
    extra_out,
    twin_in,
    plane_sum,
    peer_in,
    far_out,
    far_in,
    whole,
    small_in,
    small_out,
    small_far,
    twin_send,
    twin_recv,
    peer_send,
    peer_recv,
    far_send,
    far_recv,
    back_send,
    back_recv,
    last_send,
    last_recv,
    small_send,
    small_recv,
    edge_send,
    edge_recv,
):
    place = Place(shards, chips)
    bf16 = jnp.bfloat16
    core, chip, shard = place.core, place.chip, place.shard
    count = 2 * chips
    place.greet(
        [place.along(j) for j in range(1, shards)]
        + [place.plane(i) for i in range(1, count)]
    )
    sent = []

    def send(copy):
        copy.start()
        sent.append(copy)

    def target(j):
        return lax.rem(shard + 1 + j, shards)

    def to_twin(j):
        return remote(
            grads_ref.at[1 - core, target(j)],
            twin_in.at[j],
            twin_send.at[j],
            twin_recv.at[j],
            place.sibling(),
        )

    def small_copy(i):
        return remote(
            extra_ref, small_in.at[i], small_send.at[i], small_recv.at[i], place.plane(i)
        )

    def peer_copy(j, i):
        return remote(
            plane_sum.at[j, lax.rem(chip + i, chips)],
            peer_in.at[j, i],
            peer_send.at[j, i],
            peer_recv.at[j, i],
            place.peer(i),
        )

    def far_copy(j):
        return remote(
            far_out.at[j], far_in.at[j], far_send.at[j], far_recv.at[j], place.along(1 + j)
        )

    def edge_copy(j):
        return remote(
            small_out, small_far.at[j], edge_send.at[j], edge_recv.at[j], place.along(j)
        )

    def back_copy(i):
        block = whole.at[core, chip]
        return remote(block, block, back_send.at[i], back_recv.at[i], place.peer(i))

    def last_copy(i):
        block = whole.at[core, lax.rem(chip - i + chips, chips)]
        return remote(block, block, last_send.at[i], last_recv.at[i], place.sibling())

    for j in range(shards):
        send(to_twin(j))
    for i in range(1, count):
        send(small_copy(i))
    for j in range(shards):
        to_twin(j).wait_recv()

        def add_twin(at, carry):
            plane_sum[j, at] = (
                as_float(grads_ref[core, target(j), at]) + as_float(twin_in[j, at])
            ).astype(bf16)
            return carry

        lax.fori_loop(0, chips, add_twin, 0)
        for i in range(1, chips):
            send(peer_copy(j, i))
    total = as_float(extra_ref[...])
    for i in range(1, count):
        small_copy(i).wait_recv()
        total += as_float(small_in[i])
    small_out[...] = total.astype(bf16)
    for j in range(1, shards):
        send(edge_copy(j))
    for j in range(shards):
        mine = as_float(plane_sum[j, chip])
        for i in range(1, chips):
            peer_copy(j, i).wait_recv()
            mine += as_float(peer_in[j, i])
        far_out[j] = mine.astype(bf16)
        if j < shards - 1:
            send(far_copy(j))
    mine = as_float(far_out[shards - 1])
    for j in range(shards - 1):
        far_copy(j).wait_recv()
        mine += as_float(far_in[j])
    whole[core, chip] = mine.astype(bf16)
    for i in range(1, chips):
        send(back_copy(i))
    send(last_copy(0))
    total = as_float(small_out[...])
    for j in range(1, shards):
        edge_copy(j).wait_recv()
        total += as_float(small_far[j])
    extra_out[...] = total
    for i in range(1, chips):
        back_copy(i).wait_recv()
        send(last_copy(i))
    for i in range(chips):
        last_copy(i).wait_recv()
    rows = qkv_out.shape[0] // chips
    wide, narrow = qkv_out.shape[1] // 2, proj_out.shape[1] // 2
    for side in range(2):
        for at in range(chips):
            block = as_float(whole[side, at])
            here = slice(at * rows, (at + 1) * rows)
            qkv_out[here, side * wide : (side + 1) * wide] = block[:, :wide]
            proj_out[here, side * narrow : (side + 1) * narrow] = block[:, wide:]
    for copy in sent:
        copy.wait_send()


def reduce_grads(fast, shards, chips, grads, extra):
    _, height, cols = grads.shape
    width = cols // 2
    shard_rows = height // shards
    if not fast:
        wide = 3 * width // 2
        joined = jnp.concatenate(
            [grads[0, :, :wide], grads[1, :, :wide], grads[0, :, wide:], grads[1, :, wide:]],
            axis=1,
        )
        mine = lax.psum_scatter(joined, "shard", scatter_dimension=0, tiled=True)
        mine = as_float(lax.psum(mine, "expert"))
        extra_sum = as_float(lax.psum(extra, ("shard", "expert")))
        return mine[:, : 3 * width], mine[:, 3 * width :], extra_sum
    rows = shard_rows // chips
    bf16, dma = jnp.bfloat16, pltpu.SemaphoreType.DMA
    cut = grads.reshape(2, shards, chips, rows, cols)
    count = 2 * chips
    return pl.pallas_call(
        functools.partial(reduce_kernel, shards, chips),
        out_shape=[
            jax.ShapeDtypeStruct((shard_rows, 3 * width), jnp.float32),
            jax.ShapeDtypeStruct((shard_rows, width), jnp.float32),
            jax.ShapeDtypeStruct(extra.shape, jnp.float32),
        ],
        in_specs=[pl.BlockSpec(memory_space=pltpu.VMEM)] * 2,
        out_specs=[pl.BlockSpec(memory_space=pltpu.VMEM)] * 3,
        scratch_shapes=[
            pltpu.VMEM((shards, chips, rows, cols), bf16),
            pltpu.VMEM((shards, chips, rows, cols), bf16),
            pltpu.VMEM((shards, chips, rows, cols), bf16),
            pltpu.VMEM((shards, rows, cols), bf16),
            pltpu.VMEM((shards, rows, cols), bf16),
            pltpu.VMEM((2, chips, rows, cols), bf16),
            pltpu.VMEM((count,) + extra.shape, bf16),
            pltpu.VMEM(extra.shape, bf16),
            pltpu.VMEM((shards,) + extra.shape, bf16),
            dma((shards,)),
            dma((shards,)),
            dma((shards, chips)),
            dma((shards, chips)),
            dma((shards,)),
            dma((shards,)),
            dma((chips,)),
            dma((chips,)),
            dma((chips,)),
            dma((chips,)),
            dma((count,)),
            dma((count,)),
            dma((shards,)),
            dma((shards,)),
        ],
        compiler_params=pltpu.CompilerParams(
            collective_id=2, has_side_effects=True, vmem_limit_bytes=BIG_VMEM
        ),
        name="reduce_grads",
    )(cut, extra)


def expert_kernel(
    shards,
    experts,
    capacity,
    expert_count,
    token_ref,
    slot_row_ref,
    slot_col_ref,
    up_ref,
    in_ref,
    out_ref,
    in_bias_ref,
    out_bias_ref,
    router_ref,
    summed_ref,
    route_ref,
    in_grad_ref,
    out_grad_ref,
    in_bias_grad_ref,
    out_bias_grad_ref,
    line,
    outgoing,
    rows_in,
    gelu_all,
    slope_all,
    sent_all,
    pre_all,
    out_rows,
    out_notes,
    back_rows,
    out_in,
    note_in,
    back_in,
    total,
    far_out,
    far_out_in,
    far_back,
    far_back_in,
    line_send,
    line_recv,
    row_send,
    row_recv,
    out_send,
    out_recv,
    note_send,
    note_recv,
    back_send,
    back_recv,
    far_send,
    far_recv,
    last_send,
    last_recv,
):
    place = Place(shards, experts // 2)
    bf16 = jnp.bfloat16
    me, shard = place.expert, place.shard
    row_count, width = token_ref.shape
    group_rows = rows_in.shape[1]
    line_rows = shards * row_count
    first_rows = 2 * capacity // 16 * 16
    second_rows = group_rows - first_rows
    upper = lax.div(shard, 2)
    place.greet(
        [place.along(j) for j in range(1, shards)]
        + [place.plane(i) for i in range(1, experts)]
    )

    def line_copy(j):
        here = pl.ds(pl.multiple_of(shard * row_count, 16), row_count)
        return remote(
            token_ref, line.at[here], line_send.at[j], line_recv.at[j], place.along(j)
        )

    for j in (1, 3, 2):
        line_copy(j).start()
    line[pl.ds(pl.multiple_of(shard * row_count, 16), row_count), :] = token_ref[...]

    def target(i):
        return lax.rem(me + i, experts)

    def origin(i):
        return lax.rem(me - i + experts, experts)

    def row_copy(i, part, start, size):
        here = pl.ds(pl.multiple_of(start, 16), size)
        return remote(
            outgoing.at[target(i), here],
            rows_in.at[me, here],
            row_send.at[i, part],
            row_recv.at[i, part],
            place.plane(i),
        )

    first_start = upper * second_rows
    second_start = (1 - upper) * first_rows
    spans = ((first_start, first_rows), (second_start, second_rows))

    def dispatch(part, line_start, line_size):
        start, size = spans[part]
        here = pl.ds(pl.multiple_of(start, 16), size)
        rows = line[pl.ds(pl.multiple_of(line_start, 16), line_size), :]

        def one(i, carry):
            to = target(i)
            base = to * group_rows + start
            ids = lax.broadcasted_iota(jnp.int32, (size, line_size), 0) + base
            slots = slot_row_ref[part] if part else slot_row_ref[0]
            hit = (ids == slots[0:1, :line_size]) | (ids == slots[1:2, :line_size])
            picked = plain_dot(jnp.where(hit, 1.0, 0.0).astype(bf16), rows).astype(bf16)

            @pl.when(i == 0)
            def _():
                rows_in[me, here, :] = picked

            @pl.when(i > 0)
            def _():
                outgoing[to, here, :] = picked
                row_copy(i, part, start, size).start()

            return carry

        lax.fori_loop(0, experts, one, 0)

    def wait_pair(j):
        line_copy(j).wait_recv()

    even = lax.rem(shard, 2) == 0

    @pl.when(even)
    def _():
        wait_pair(3)

    @pl.when(jnp.logical_not(even))
    def _():
        wait_pair(1)

    dispatch(0, upper * 2 * row_count, 2 * row_count)

    @pl.when(even)
    def _():
        wait_pair(1)

    @pl.when(jnp.logical_not(even))
    def _():
        wait_pair(3)

    wait_pair(2)
    dispatch(1, 0, line_rows)

    def out_copy(i):
        return remote(
            out_rows.at[origin(i)], out_in.at[me], out_send.at[i], out_recv.at[i], place.plane(experts - i)
        )

    def note_copy(i):
        return remote(
            out_notes.at[origin(i)], note_in.at[me], note_send.at[i], note_recv.at[i], place.plane(experts - i)
        )

    def back_copy(i):
        return remote(
            back_rows.at[origin(i)], back_in.at[me], back_send.at[i], back_recv.at[i], place.plane(experts - i)
        )

    def forward(i, carry):
        at = origin(i)

        @pl.when(i > 0)
        def _():
            for part in range(2):
                row_copy(i, part, *spans[part]).wait_recv()

        rows = rows_in[at]
        gelu_out, gelu_slope = gelu_parts(plain_dot(rows, in_ref[...]) + in_bias_ref[0:1, :])
        slope_all[at] = gelu_slope
        gelu_bf = gelu_out.astype(bf16)
        gelu_all[at] = gelu_bf
        logits = contract_cols(rows, router_ref[...])
        lanes = lax.broadcasted_iota(jnp.int32, logits.shape, 1)
        logits = jnp.where(lanes < expert_count, logits, -1e30)
        shifted = jnp.exp(logits - jnp.max(logits, axis=-1, keepdims=True))
        chosen = jnp.sum(jnp.where(lanes == me, shifted, 0.0), axis=-1, keepdims=True)
        gate = chosen / jnp.sum(shifted, axis=-1, keepdims=True)
        upstream = as_float(up_ref[at])
        sent_all[at] = (gate * upstream).astype(bf16)
        expert_out = plain_dot(gelu_bf, out_ref[...]) + out_bias_ref[0:1, :]
        gate_grad = jnp.sum(upstream * expert_out, axis=-1, keepdims=True)
        notes = jnp.broadcast_to(gate_grad, (group_rows, 128)).T[:16].astype(bf16)
        gated = (gate * expert_out).astype(bf16)

        @pl.when(i == 0)
        def _():
            out_in[me] = gated
            note_in[me, :, :group_rows] = notes

        @pl.when(i > 0)
        def _():
            out_rows[at] = gated
            out_notes[at, :, :group_rows] = notes
            out_copy(i).start()
            note_copy(i).start()

        return carry

    out_notes[...] = jnp.zeros_like(out_notes)
    lax.fori_loop(0, experts, forward, 0)
    in_bias_grad_ref[...] = jnp.zeros_like(in_bias_grad_ref)
    out_bias_grad_ref[...] = jnp.zeros_like(out_bias_grad_ref)

    def backward(i, carry):
        at = origin(i)
        sent = sent_all[at]
        out_bias_grad_ref[0:1, :] += jnp.sum(as_float(sent), axis=0, keepdims=True)
        pre_grad = contract_cols(sent, out_ref[...]) * slope_all[at]
        in_bias_grad_ref[0:1, :] += jnp.sum(pre_grad, axis=0, keepdims=True)
        pre_bf = pre_grad.astype(bf16)
        pre_all[at] = pre_bf
        back = contract_cols(pre_bf, in_ref[...]).astype(bf16)

        @pl.when(i == 0)
        def _():
            back_in[me] = back

        @pl.when(i > 0)
        def _():
            back_rows[at] = back
            back_copy(i).start()

        return carry

    lax.fori_loop(0, experts, backward, 0)

    def hits(source):
        ids = lax.broadcasted_iota(jnp.int32, (line_rows, group_rows), 1) + source * group_rows
        hit = (ids == slot_col_ref[:, 0:1]) | (ids == slot_col_ref[:, 1:2])
        return jnp.where(hit, 1.0, 0.0).astype(bf16)

    def collect_out(i, carry):
        at = target(i)

        @pl.when(i > 0)
        def _():
            out_copy(i).wait_recv()
            note_copy(i).wait_recv()

        table = hits(at)
        total[:, :width] += plain_dot(table, out_in[at])
        rows_at = lax.broadcasted_iota(jnp.int32, (128, group_rows), 0)
        note = as_float(note_in[at, 0:1, :group_rows])
        spread = jnp.where(rows_at == at, note, 0.0).astype(bf16)
        total[:, width:] += contract_cols(table, spread)
        return carry

    def far_copy(buffers, sems, j):
        to = lax.rem(shard + j, shards)
        return remote(
            buffers[0].at[to], buffers[1].at[j], sems[0].at[j], sems[1].at[j], place.along(j)
        )

    out_far = ((far_out, far_out_in), (far_send, far_recv))
    back_far = ((far_back, far_back_in), (last_send, last_recv))

    def spread_far(far, cols):
        for at in range(shards):
            far[0][0][at] = total[at * row_count : (at + 1) * row_count, :cols].astype(bf16)
        for j in range(1, shards):
            far_copy(*far, j).start()

    def own_rows(cols):
        return total[pl.ds(pl.multiple_of(shard * row_count, 16), row_count), :cols]

    total[...] = jnp.zeros_like(total)
    lax.fori_loop(0, experts, collect_out, 0)
    spread_far(out_far, width + 128)
    summed_ref[...] = own_rows(width + 128)

    tile = 128
    for left, right, grad in (
        (gelu_all, sent_all, out_grad_ref),
        (rows_in, pre_all, in_grad_ref),
    ):

        def weigh(at, carry, left=left, right=right, grad=grad):
            cols = pl.ds(pl.multiple_of(at * tile, 128), tile)
            lhs = left[:, :, cols].reshape(experts * group_rows, tile)
            rhs = right[...].reshape(experts * group_rows, width)
            grad[cols, :] = contract_rows(lhs, rhs).astype(grad.dtype)
            return carry

        lax.fori_loop(0, left.shape[2] // tile, weigh, 0)

    total[...] = jnp.zeros_like(total)

    def collect_back(i, carry):
        at = target(i)

        @pl.when(i > 0)
        def _():
            back_copy(i).wait_recv()

        total[:, :width] += plain_dot(hits(at), back_in[at])
        return carry

    lax.fori_loop(0, experts, collect_back, 0)
    spread_far(back_far, width)
    for j in range(1, shards):
        far_copy(*out_far, j).wait_recv()
        summed_ref[...] += as_float(far_out_in[j])
    route_ref[...] = own_rows(width)
    for j in range(1, shards):
        far_copy(*back_far, j).wait_recv()
        route_ref[...] += as_float(far_back_in[j])

    for j in range(1, shards):
        line_copy(j).wait_send()
        far_copy(*out_far, j).wait_send()
        far_copy(*back_far, j).wait_send()

    def finish(i, carry):
        for part in range(2):
            row_copy(i, part, *spans[part]).wait_send()
        out_copy(i).wait_send()
        note_copy(i).wait_send()
        back_copy(i).wait_send()
        return carry

    lax.fori_loop(1, experts, finish, 0)


def expert_fast(
    shards, experts, capacity, expert_count, tokens, line_slot, up_in, in_w, out_w, in_b, out_b, router
):
    row_count, width = tokens.shape
    hidden = in_w.shape[1]
    line_rows = shards * row_count
    group_rows = round_up(shards * capacity, 16)
    bf16, dma = jnp.bfloat16, pltpu.SemaphoreType.DMA
    shard = lax.axis_index("shard")
    flat = line_slot.T
    pair = lax.dynamic_slice_in_dim(flat, (shard // 2) * 2 * row_count, 2 * row_count, axis=1)
    slot_rows = jnp.stack([jnp.pad(pair, ((0, 6), (0, line_rows - 2 * row_count))), jnp.pad(flat, ((0, 6), (0, 0)))])
    slot_cols = jnp.pad(line_slot, ((0, 0), (0, 126)))
    in_bias = jnp.pad(in_b, ((0, 7), (0, 0)))
    out_bias = jnp.pad(out_b, ((0, 7), (0, 0)))
    vmem = pl.BlockSpec(memory_space=pltpu.VMEM)

    def block(cols, kind=bf16):
        return pltpu.VMEM((experts, group_rows, cols), kind)

    def pair_sems(*shape):
        return [dma(shape), dma(shape)]

    return pl.pallas_call(
        functools.partial(expert_kernel, shards, experts, capacity, expert_count),
        out_shape=[
            jax.ShapeDtypeStruct((row_count, width + 128), jnp.float32),
            jax.ShapeDtypeStruct((row_count, width), jnp.float32),
            jax.ShapeDtypeStruct((width, hidden), jnp.float32),
            jax.ShapeDtypeStruct((hidden, width), bf16),
            jax.ShapeDtypeStruct((8, hidden), jnp.float32),
            jax.ShapeDtypeStruct((8, width), jnp.float32),
        ],
        in_specs=[vmem] * 9,
        out_specs=[vmem] * 6,
        scratch_shapes=[
            pltpu.VMEM((line_rows, width), bf16),
            block(width),
            block(width),
            block(hidden),
            block(hidden, jnp.float32),
            block(width),
            block(hidden),
            block(width),
            pltpu.VMEM((experts, 16, round_up(group_rows, 128)), bf16),
            block(width),
            block(width),
            pltpu.VMEM((experts, 16, round_up(group_rows, 128)), bf16),
            block(width),
            pltpu.VMEM((line_rows, width + 128), jnp.float32),
            pltpu.VMEM((shards, row_count, width + 128), bf16),
            pltpu.VMEM((shards, row_count, width + 128), bf16),
            pltpu.VMEM((shards, row_count, width), bf16),
            pltpu.VMEM((shards, row_count, width), bf16),
        ]
        + pair_sems(shards)
        + pair_sems(experts, 2)
        + pair_sems(experts)
        + pair_sems(experts)
        + pair_sems(experts)
        + pair_sems(shards)
        + pair_sems(shards),
        compiler_params=pltpu.CompilerParams(
            collective_id=3, has_side_effects=True, vmem_limit_bytes=BIG_VMEM
        ),
        name="expert_pass",
    )(tokens, slot_rows, slot_cols, up_in, in_w, out_w, in_bias, out_bias, router)


def expert_slow(
    tokens, gates, route_rows, tables, line_up, up_in, in_slice, out_slice, in_bias, own_bias
):
    row_count, width = tokens.shape
    bf16 = jnp.bfloat16
    table_0, table_1, send_table = tables
    router_pad = gates.shape[1]
    chosen = route_rows[:, :, None] == jnp.arange(router_pad, dtype=jnp.int32)[None, None, :]
    gate_pick = jnp.sum(jnp.where(chosen, gates[:, None, :], 0.0), axis=2)
    gate_high = gate_pick.astype(bf16)
    gate_low = (gate_pick - as_float(gate_high)).astype(bf16)
    gate_notes = jnp.concatenate([gate_high, gate_low], axis=1)
    gate_notes = jnp.pad(gate_notes, ((0, 0), (0, 128 - gate_notes.shape[1])))
    sent_line = jnp.concatenate([tokens, gate_notes], axis=1)
    row_line = lax.all_gather(sent_line, "shard", axis=0, tiled=True)
    line_in = row_line[:, :width]
    gate_line = as_float(row_line[:, width : width + 4])
    line_gate = gate_line[:, 0:2] + gate_line[:, 2:4]
    outgoing = contract_rows(send_table, line_in).astype(bf16)
    slot_gate = jnp.sum(
        jnp.where(table_0, line_gate[:, 0:1], 0.0) + jnp.where(table_1, line_gate[:, 1:2], 0.0),
        axis=0,
    )
    slot_high = slot_gate.astype(bf16)
    slot_low = (slot_gate - as_float(slot_high)).astype(bf16)
    slot_notes = jnp.pad(jnp.stack([slot_high, slot_low], axis=1), ((0, 0), (0, 126)))
    incoming = lax.all_to_all(
        jnp.concatenate([outgoing, slot_notes], axis=1),
        "expert",
        split_axis=0,
        concat_axis=0,
        tiled=True,
    )
    rows_in = incoming[:, :width]
    gate_in = as_float(incoming[:, width : width + 1]) + as_float(
        incoming[:, width + 1 : width + 2]
    )
    grad_in = (as_float(up_in) * gate_in).astype(bf16)
    pre_act = plain_dot(rows_in, in_slice) + in_bias
    gelu_out, gelu_slope = gelu_parts(pre_act)
    gelu_bf = gelu_out.astype(bf16)
    expert_out = (plain_dot(gelu_bf, out_slice) + own_bias).astype(bf16)
    returned = lax.all_to_all(expert_out, "expert", split_axis=0, concat_axis=0, tiled=True)
    pre_grad = contract_cols(grad_in, out_slice) * gelu_slope
    pre_bf = pre_grad.astype(bf16)
    back_rows = contract_cols(pre_bf, in_slice).astype(bf16)
    returned_grad = lax.all_to_all(back_rows, "expert", split_axis=0, concat_axis=0, tiled=True)
    out_0 = plain_dot(table_0.astype(bf16), returned)
    out_1 = plain_dot(table_1.astype(bf16), returned)
    combined = line_gate[:, 0:1] * out_0 + line_gate[:, 1:2] * out_1
    line_up_wide = as_float(line_up)
    gate_grad_line = jnp.stack(
        [jnp.sum(line_up_wide * out_0, axis=1), jnp.sum(line_up_wide * out_1, axis=1)], axis=1
    )
    joined = jnp.concatenate(
        [combined.astype(bf16), jnp.pad(gate_grad_line, ((0, 0), (0, 126))).astype(bf16)], axis=1
    )
    summed = as_float(lax.psum_scatter(joined, "shard", scatter_dimension=0, tiled=True))
    picked = jnp.sum(
        jnp.where(chosen, summed[:, width : width + 2][:, :, None], 0.0), axis=1
    )
    summed = jnp.concatenate([summed[:, :width], picked], axis=1)
    back_line = plain_dot(send_table, returned_grad)
    route_grad = lax.psum_scatter(back_line.astype(bf16), "shard", scatter_dimension=0, tiled=True)
    return (
        summed,
        route_grad,
        contract_rows(rows_in, pre_bf),
        contract_rows(gelu_bf, grad_in).astype(bf16),
        jnp.sum(pre_grad, axis=0)[None],
        jnp.sum(as_float(grad_in), axis=0)[None],
    )


def body(
    block_input,
    image_live,
    expert_routes,
    first_gain,
    first_shift,
    qkv_weight,
    query_value_bias,
    attn_out_weight,
    attn_out_bias,
    second_gain,
    second_shift,
    router_weight,
    expert_in_weight,
    expert_in_bias,
    expert_out_weight,
    expert_out_bias,
    output_grad,
):
    image_count, seq_length, width = block_input.shape
    shards = lax.axis_size("shard")
    experts = lax.axis_size("expert")
    chips = experts // 2
    expert_count = router_weight.shape[1]
    my_shard = lax.axis_index("shard")
    shard_rows = first_gain.shape[0]
    stride = round_up(seq_length, 8)
    row_count = image_count * stride
    capacity = (3 * image_count * seq_length + expert_count - 1) // expert_count
    group_rows = round_up(shards * capacity, 16)
    slot_rows = expert_count * group_rows
    bf16 = jnp.bfloat16
    fast = chips == 4 and shards == 4 and shard_rows % (16 * chips) == 0

    router_pad = round_up(expert_count, 128)
    extra = jnp.concatenate(
        [
            jnp.stack(
                [
                    first_gain,
                    first_shift,
                    attn_out_bias,
                    second_gain,
                    second_shift,
                    query_value_bias[:shard_rows],
                    query_value_bias[shard_rows:],
                ]
            ),
            router_weight.T,
        ],
        axis=0,
    )
    extra_rows = round_up(VECTORS + expert_count, 16)
    extra = jnp.pad(
        extra,
        ((0, extra_rows - extra.shape[0]), (0, round_up(shard_rows, 128) - shard_rows)),
    )

    tail_rows = stride - seq_length
    live_rows = jnp.repeat(image_live, stride) * jnp.tile(
        (jnp.arange(stride) < seq_length).astype(jnp.int32), image_count
    )
    route_rows = jnp.pad(expert_routes, ((0, 0), (0, tail_rows), (0, 0))).reshape(row_count, 2)
    route_code, position = slot_places(route_rows, live_rows, expert_count)
    up_rows = (
        jnp.pad(output_grad, ((0, 0), (0, tail_rows), (0, 0))).reshape(row_count, width)
        * as_float(live_rows)[:, None]
    )
    notes = jnp.concatenate([route_code.astype(bf16), position.astype(bf16)], axis=1)
    notes = jnp.pad(notes, ((0, 0), (0, 128 - notes.shape[1])))
    up_line = jnp.concatenate([up_rows.astype(bf16), notes], axis=1)

    qkv_all, proj_all, extra_all, line_all = gather_params(
        fast, shards, chips, qkv_weight, attn_out_weight, extra, up_line
    )
    qkv_full = qkv_all.reshape(width, 3 * width)
    proj_full = proj_all.reshape(width, width)
    extra_t = jnp.transpose(extra_all[:, :, :shard_rows], (1, 0, 2))
    vectors = as_float(extra_t[:8]).reshape(8, width)
    query_value = as_float(extra_t[5:7])
    bias_full = jnp.transpose(query_value, (1, 0, 2)).reshape(2 * width)
    bias_row = jnp.concatenate(
        [bias_full[:width], jnp.zeros((width,), jnp.float32), bias_full[width:]]
    )
    bias_row = jnp.pad(bias_row[None], ((0, 7), (0, 0)))
    router_t = jnp.pad(
        extra_t[VECTORS : VECTORS + expert_count].reshape(expert_count, width),
        ((0, router_pad - expert_count), (0, 0)),
    )

    line_rows = shards * row_count
    line = line_all.reshape(line_rows, width + 128)
    line_up = line[:, :width]
    line_notes = as_float(line[:, width : width + 4])
    line_ids = jnp.arange(line_rows, dtype=jnp.int32)[:, None]
    line_slot = (
        line_notes[:, 0:2].astype(jnp.int32) * group_rows
        + (line_ids // row_count) * capacity
        + line_notes[:, 2:4].astype(jnp.int32)
    )
    line_slot = jnp.where(line_notes[:, 0:2] >= 0, line_slot, -1)
    slot_ids = jnp.arange(slot_rows, dtype=jnp.int32)
    table_0 = line_slot[:, 0:1] == slot_ids[None, :]
    table_1 = line_slot[:, 1:2] == slot_ids[None, :]
    send_table = (table_0 | table_1).astype(bf16)
    up_out = contract_rows(send_table, line_up).astype(bf16)
    up_in = lax.all_to_all(up_out, "expert", split_axis=0, concat_axis=0, tiled=True)

    out_slice = lax.all_to_all(
        expert_out_weight[0], "shard", split_axis=0, concat_axis=1, tiled=True
    )
    in_slice = expert_in_weight[0]

    packed, mixed, residual, expert_in, gates = pl.pallas_call(
        functools.partial(forward_kernel, stride, expert_count),
        out_shape=[
            jax.ShapeDtypeStruct((row_count, 3 * width), bf16),
            jax.ShapeDtypeStruct((row_count, width), bf16),
            jax.ShapeDtypeStruct((row_count, width), jnp.float32),
            jax.ShapeDtypeStruct((row_count, width), bf16),
            jax.ShapeDtypeStruct((row_count, router_pad), jnp.float32),
        ],
        in_specs=[pl.BlockSpec(memory_space=pltpu.VMEM)] * 6,
        out_specs=[pl.BlockSpec(memory_space=pltpu.VMEM)] * 5,
        scratch_shapes=[
            pltpu.VMEM((row_count, width), jnp.float32),
            pltpu.VMEM((row_count, width), bf16),
        ],
        compiler_params=pltpu.CompilerParams(vmem_limit_bytes=BIG_VMEM),
        cost_estimate=pl.CostEstimate(
            flops=16 * row_count * width * width,
            bytes_accessed=24 * width * width,
            transcendentals=2 * HEADS * row_count * row_count,
        ),
        name="attention_forward",
    )(block_input, qkv_full, proj_full, vectors, bias_row, router_t)

    own_bias = lax.dynamic_update_slice(
        jnp.zeros((1, width), jnp.float32),
        as_float(expert_out_bias),
        (0, my_shard * shard_rows),
    )
    in_bias = as_float(expert_in_bias)
    if fast:
        results = expert_fast(
            shards,
            experts,
            capacity,
            expert_count,
            expert_in,
            line_slot,
            up_in.reshape(experts, group_rows, width),
            in_slice,
            out_slice,
            in_bias,
            own_bias,
            router_t,
        )
    else:
        results = expert_slow(
            expert_in,
            gates,
            route_rows,
            (table_0, table_1, send_table),
            line_up,
            up_in,
            in_slice,
            out_slice,
            in_bias,
            own_bias,
        )
    summed, route_grad, in_weight_grad, out_weight_grad, in_bias_sum, out_bias_sum = results
    out_weight_part = as_float(
        lax.all_to_all(out_weight_grad, "shard", split_axis=1, concat_axis=0, tiled=True)
    )[None]
    in_weight_part = in_weight_grad[None]
    in_bias_part = in_bias_sum[:1]
    out_bias_part = lax.dynamic_slice_in_dim(
        out_bias_sum[0], my_shard * shard_rows, shard_rows
    )[None]

    smem = pl.BlockSpec(memory_space=pltpu.SMEM)
    vmem = pl.BlockSpec(memory_space=pltpu.VMEM)
    wide_rows = pltpu.VMEM((row_count, width), jnp.float32)
    block_output, input_grad, weight_grads, extra_grads = pl.pallas_call(
        functools.partial(backward_kernel, stride),
        out_shape=[
            jax.ShapeDtypeStruct(block_input.shape, jnp.float32),
            jax.ShapeDtypeStruct(block_input.shape, jnp.float32),
            jax.ShapeDtypeStruct((2, width, 2 * width), bf16),
            jax.ShapeDtypeStruct((extra_rows, width), jnp.float32),
        ],
        in_specs=[smem] + [vmem] * 13,
        out_specs=[vmem] * 4,
        scratch_shapes=[
            wide_rows,
            wide_rows,
            pltpu.VMEM((width, row_count), bf16),
            pltpu.VMEM((row_count, width), bf16),
            pltpu.VMEM((row_count, 3 * width), bf16),
            wide_rows,
        ],
        compiler_params=pltpu.CompilerParams(vmem_limit_bytes=BIG_VMEM),
        cost_estimate=pl.CostEstimate(
            flops=32 * row_count * width * width,
            bytes_accessed=48 * width * width,
            transcendentals=2 * HEADS * row_count * row_count,
        ),
        name="attention_backward",
    )(
        image_live,
        block_input,
        output_grad,
        packed,
        mixed,
        residual,
        expert_in,
        gates,
        summed,
        route_grad,
        qkv_full,
        proj_full,
        vectors,
        router_t,
    )
    qkv_sum, proj_sum, extra_sum = reduce_grads(
        fast, shards, chips, weight_grads, extra_grads.astype(bf16)
    )

    def own(array_in, size, axis=0):
        return lax.dynamic_slice_in_dim(array_in, my_shard * size, size, axis=axis)

    mine = own(extra_sum, shard_rows, axis=1)
    return (
        block_output,
        input_grad,
        mine[0],
        mine[1],
        qkv_sum,
        own(extra_sum[5:7].reshape(2 * width), 2 * shard_rows),
        proj_sum,
        mine[2],
        mine[3],
        mine[4],
        mine[VECTORS : VECTORS + expert_count].T,
        in_weight_part,
        in_bias_part,
        out_weight_part,
        out_bias_part,
    )


def solution(mesh):
    in_specs = (
        P(("expert", "shard"), None, None),
        P(("expert", "shard")),
        P(("expert", "shard"), None, None),
        P("shard"),
        P("shard"),
        P("shard", None),
        P("shard"),
        P("shard", None),
        P("shard"),
        P("shard"),
        P("shard"),
        P("shard", None),
        P("expert", None, "shard"),
        P("expert", "shard"),
        P("expert", None, "shard"),
        P("expert", "shard"),
        P(("expert", "shard"), None, None),
    )
    out_specs = (
        P(("expert", "shard"), None, None),
        P(("expert", "shard"), None, None),
        P("shard"),
        P("shard"),
        P("shard", None),
        P("shard"),
        P("shard", None),
        P("shard"),
        P("shard"),
        P("shard"),
        P("shard", None),
        P("expert", None, "shard"),
        P("expert", "shard"),
        P("expert", None, "shard"),
        P("expert", "shard"),
    )
    return jax.shard_map(body, mesh=mesh, in_specs=in_specs, out_specs=out_specs, check_vma=False)
```

```python
import functools
import math
import types

import jax
import jax.numpy as jnp
from jax import lax
from jax.experimental import pallas as pl
from jax.experimental.pallas import tpu as pltpu
from jax.sharding import PartitionSpec as P

HEADS = 12
HEAD_DIM = 64


EPSILON = 1e-06
PRECISE = lax.Precision.HIGHEST
HALF_ROOT = 0.7071067811865476
DENSITY = 0.3989422804014327


def as_float(array_in):
    return array_in.astype(jnp.float32)


def contract_rows(left_side, right_side):
    return lax.dot_general(
        left_side, right_side, (((0,), (0,)), ((), ())), preferred_element_type=jnp.float32
    )


def contract_cols(left_side, right_side):
    return lax.dot_general(
        left_side, right_side, (((1,), (1,)), ((), ())), preferred_element_type=jnp.float32
    )


def precise_rows(left_side, right_side):
    return lax.dot_general(
        left_side,
        right_side,
        (((0,), (0,)), ((), ())),
        precision=PRECISE,
        preferred_element_type=jnp.float32,
    )


def precise_cols(left_side, right_side):
    return lax.dot_general(
        left_side,
        right_side,
        (((1,), (1,)), ((), ())),
        precision=PRECISE,
        preferred_element_type=jnp.float32,
    )


def layer_norm(values_in, gain_vec, shift_vec):
    center = values_in - jnp.mean(values_in, axis=-1, keepdims=True)
    inv_std = lax.rsqrt(jnp.mean(center * center, axis=-1, keepdims=True) + EPSILON)
    normed = center * inv_std
    return (normed * as_float(gain_vec) + as_float(shift_vec), normed, inv_std)


def norm_back(upstream, normed, inv_std, gain_vec):
    scaled = upstream * as_float(gain_vec)
    return inv_std * (
        scaled
        - jnp.mean(scaled, axis=-1, keepdims=True)
        - normed * jnp.mean(scaled * normed, axis=-1, keepdims=True)
    )


def gelu_parts(pre_act):
    normal_cdf = 0.5 * (1.0 + jax.scipy.special.erf(pre_act * HALF_ROOT))
    return (
        pre_act * normal_cdf,
        normal_cdf + pre_act * DENSITY * jnp.exp(-0.5 * pre_act * pre_act),
    )


BIG_VMEM = 56 * 1024 * 1024
VECTORS = 7


def plain_dot(left_side, right_side):
    return jnp.dot(left_side, right_side, preferred_element_type=jnp.float32)


def exact_dot(left_side, right_side):
    return lax.dot_general(
        left_side,
        right_side,
        (((1,), (0,)), ((), ())),
        precision=PRECISE,
        preferred_element_type=jnp.float32,
    )


def round_up(value, step):
    return -(-value // step) * step


def slot_places(route_rows, live_rows, expert_count):
    row_count = route_rows.shape[0]
    flat_routes = route_rows.reshape(2 * row_count)
    alive_pairs = jnp.repeat(live_rows, 2)
    chosen = (flat_routes[:, None] == jnp.arange(expert_count, dtype=jnp.int32)[None, :]).astype(
        jnp.int32
    )
    live_hits = chosen * alive_pairs[:, None]
    earlier = (
        jnp.arange(2 * row_count, dtype=jnp.int32)[:, None]
        > jnp.arange(2 * row_count, dtype=jnp.int32)[None, :]
    ).astype(jnp.bfloat16)
    counted = jnp.dot(earlier, live_hits.astype(jnp.bfloat16), preferred_element_type=jnp.float32)
    position = jnp.sum(counted * as_float(live_hits), axis=1)
    route_code = jnp.where(alive_pairs > 0, flat_routes, -1).astype(jnp.float32)
    return route_code.reshape(row_count, 2), position.reshape(row_count, 2)


class Place:
    def __init__(self, shards, chips):
        self.shards = shards
        self.chips = chips
        self.expert = lax.axis_index("expert")
        self.shard = lax.axis_index("shard")
        self.core = lax.rem(self.expert, 2)
        self.chip = lax.div(self.expert, 2)

    def along(self, step):
        return {
            "expert": self.expert,
            "shard": lax.rem(self.shard + step + self.shards, self.shards),
        }

    def peer(self, step):
        other = lax.rem(self.chip + step + self.chips, self.chips)
        return {"expert": other * 2 + self.core, "shard": self.shard}

    def sibling(self):
        return {"expert": self.chip * 2 + 1 - self.core, "shard": self.shard}

    def plane(self, step):
        count = 2 * self.chips
        return {"expert": lax.rem(self.expert + step, count), "shard": self.shard}

    def greet(self, others):
        barrier = pltpu.get_barrier_semaphore()
        for other in others:
            pl.semaphore_signal(
                barrier, inc=1, device_id=other, device_id_type=pl.DeviceIdType.MESH
            )
        pl.semaphore_wait(barrier, len(others))


def remote(src, dst, send_sem, recv_sem, device):
    return pltpu.make_async_remote_copy(
        src_ref=src,
        dst_ref=dst,
        send_sem=send_sem,
        recv_sem=recv_sem,
        device_id=device,
        device_id_type=pl.DeviceIdType.MESH,
    )


def norm_stats(values_in):
    center = values_in - jnp.mean(values_in, axis=-1, keepdims=True)
    inv_std = lax.rsqrt(jnp.mean(center * center, axis=-1, keepdims=True) + EPSILON)
    return center * inv_std, inv_std


def spread_rows(dst, src, image_count, seq_length, stride):
    dst[...] = jnp.zeros_like(dst)
    for image in range(image_count):
        dst[image * stride : image * stride + seq_length, :] = src[image]


def same_image(rows, stride, seq_length):
    row_at = lax.broadcasted_iota(jnp.int32, (rows, rows), 0)
    col_at = lax.broadcasted_iota(jnp.int32, (rows, rows), 1)
    mask = None
    for image in range(rows // stride):
        low = image * stride
        part = (
            (row_at >= low)
            & (row_at < low + stride)
            & (col_at >= low)
            & (col_at < low + seq_length)
        )
        mask = part if mask is None else mask | part
    return mask


def masked_softmax(query_half, keys, mask):
    scores = contract_cols(query_half, keys) * (1.0 / math.sqrt(HEAD_DIM))
    scores = jnp.where(mask, scores, -1e30)
    row_max = jnp.max(scores, axis=-1, keepdims=True)
    log_total = row_max + jnp.log(jnp.sum(jnp.exp(scores - row_max), axis=-1, keepdims=True))
    return jnp.exp(scores - log_total)


def forward_kernel(
    stride,
    expert_count,
    x_ref,
    qkv_ref,
    proj_ref,
    vec_ref,
    bias_ref,
    router_ref,
    packed_ref,
    mixed_ref,
    residual_ref,
    line_ref,
    gates_ref,
    flat_ref,
    attn_ref,
):
    image_count, seq_length, width = x_ref.shape
    rows = flat_ref.shape[0]
    bf16 = jnp.bfloat16
    spread_rows(flat_ref, x_ref, image_count, seq_length, stride)
    normed, _ = norm_stats(flat_ref[...])
    attn_ref[...] = (normed * vec_ref[0:1, :] + vec_ref[1:2, :]).astype(bf16)

    def project(tile, carry):
        cols = pl.ds(pl.multiple_of(tile * width, 128), width)
        packed_ref[:, cols] = (
            plain_dot(attn_ref[...], qkv_ref[:, cols]) + bias_ref[0:1, cols]
        ).astype(bf16)
        return carry

    lax.fori_loop(0, 3, project, 0)
    mask = same_image(rows, stride, seq_length)
    low_lanes = lax.broadcasted_iota(jnp.int32, (rows, 128), 1) < HEAD_DIM

    def attend(pair, carry):
        def part(which):
            return packed_ref[:, pl.ds(pl.multiple_of(which * width + pair * 128, 128), 128)]

        query, key, value = part(0), part(1), part(2)
        zero = jnp.zeros_like(query)
        weights_low = masked_softmax(jnp.where(low_lanes, query, zero), key, mask).astype(bf16)
        weights_high = masked_softmax(jnp.where(low_lanes, zero, query), key, mask).astype(bf16)
        mixed_ref[:, pl.ds(pl.multiple_of(pair * 128, 128), 128)] = jnp.where(
            low_lanes, plain_dot(weights_low, value), plain_dot(weights_high, value)
        ).astype(bf16)
        return carry

    lax.fori_loop(0, HEADS // 2, attend, 0)
    residual = flat_ref[...] + plain_dot(mixed_ref[...], proj_ref[...]) + vec_ref[2:3, :]
    residual_ref[...] = residual
    normed_two, _ = norm_stats(residual)
    expert_in = (normed_two * vec_ref[3:4, :] + vec_ref[4:5, :]).astype(bf16)
    line_ref[...] = expert_in
    logits = contract_cols(expert_in, router_ref[...])
    lanes = lax.broadcasted_iota(jnp.int32, logits.shape, 1)
    logits = jnp.where(lanes < expert_count, logits, -1e30)
    shifted = jnp.exp(logits - jnp.max(logits, axis=-1, keepdims=True))
    gates_ref[...] = shifted / jnp.sum(shifted, axis=-1, keepdims=True)


def backward_kernel(
    stride,
    live_ref,
    x_ref,
    up_ref,
    packed_ref,
    mixed_ref,
    residual_ref,
    expert_ref,
    gates_ref,
    summed_ref,
    back_ref,
    qkv_ref,
    proj_ref,
    vec_ref,
    router_ref,
    block_ref,
    grad_ref,
    weight_ref,
    extra_ref,
    flat_ref,
    upstream_ref,
    attn_t_ref,
    mixed_grad_ref,
    packed_grad_ref,
    res_grad_ref,
):
    image_count, seq_length, width = x_ref.shape
    rows = flat_ref.shape[0]
    bf16 = jnp.bfloat16
    half = 3 * width // 2
    spread_rows(flat_ref, x_ref, image_count, seq_length, stride)
    upstream_ref[...] = jnp.zeros_like(upstream_ref)
    residual = residual_ref[...]
    block = residual + as_float(summed_ref[:, :width])
    for image in range(image_count):
        live = live_ref[image].astype(jnp.float32)
        here = slice(image * stride, image * stride + seq_length)
        upstream_ref[here, :] = up_ref[image] * live
        block_ref[image] = block[here, :]

    gates = gates_ref[...]
    picked = as_float(summed_ref[:, width:])
    logit_grad = gates * (picked - jnp.sum(gates * picked, axis=-1, keepdims=True))
    router_rows = extra_ref.shape[0] - VECTORS
    extra_ref[VECTORS:, :] = precise_rows(logit_grad, as_float(expert_ref[...]))[
        :router_rows
    ]
    normed_two_grad = as_float(back_ref[...]) + exact_dot(
        logit_grad, as_float(router_ref[...])
    )
    normed_two, inv_two = norm_stats(residual)
    extra_ref[3:4, :] = jnp.sum(normed_two_grad * normed_two, axis=0, keepdims=True)
    extra_ref[4:5, :] = jnp.sum(normed_two_grad, axis=0, keepdims=True)
    residual_grad = upstream_ref[...] + norm_back(
        normed_two_grad, normed_two, inv_two, vec_ref[3:4, :]
    )
    res_grad_ref[...] = residual_grad
    extra_ref[2:3, :] = jnp.sum(residual_grad, axis=0, keepdims=True)
    residual_bf = residual_grad.astype(bf16)
    proj_grad = contract_rows(mixed_ref[...], residual_bf)
    for core in range(2):
        weight_ref[core, :, half:] = proj_grad[
            :, core * (width // 2) : (core + 1) * (width // 2)
        ].astype(bf16)
    mixed_grad_ref[...] = contract_cols(residual_bf, proj_ref[...]).astype(bf16)

    mask = same_image(rows, stride, seq_length)
    low_lanes = lax.broadcasted_iota(jnp.int32, (rows, 128), 1) < HEAD_DIM

    def attend(pair, carry):
        def part(which):
            return pl.ds(pl.multiple_of(which * width + pair * 128, 128), 128)

        query, key, value = (packed_ref[:, part(which)] for which in range(3))
        mixed_grad = mixed_grad_ref[:, part(0)]
        zero = jnp.zeros_like(query)
        totals = [0.0, 0.0, 0.0]
        for high in range(2):

            def only(array_in):
                return jnp.where(low_lanes, zero if high else array_in, array_in if high else zero)

            query_half, mixed_half = only(query), only(mixed_grad)
            probs = masked_softmax(query_half, key, mask)
            prob_grad = contract_cols(mixed_half, value)
            score_grad = (
                probs
                * (prob_grad - jnp.sum(probs * prob_grad, axis=-1, keepdims=True))
                * (1.0 / math.sqrt(HEAD_DIM))
            ).astype(bf16)
            totals[0] += plain_dot(score_grad, only(key))
            totals[1] += contract_rows(score_grad, query_half)
            totals[2] += contract_rows(probs.astype(bf16), mixed_half)
        for which in range(3):
            packed_grad_ref[:, part(which)] = totals[which].astype(bf16)
        extra_ref[5:6, part(0)] = jnp.sum(totals[0], axis=0, keepdims=True)
        extra_ref[6:7, part(0)] = jnp.sum(totals[2], axis=0, keepdims=True)
        return carry

    lax.fori_loop(0, HEADS // 2, attend, 0)

    normed_one, inv_one = norm_stats(flat_ref[...])
    attn_in = normed_one * vec_ref[0:1, :] + vec_ref[1:2, :]
    attn_t_ref[...] = attn_in.T.astype(bf16)
    tile = half // 3

    def weigh(at, carry):
        src = pl.ds(pl.multiple_of(at * tile, 128), tile)
        dst = pl.ds(pl.multiple_of(lax.rem(at, 3) * tile, 128), tile)
        weight_ref[lax.div(at, 3), :, dst] = plain_dot(
            attn_t_ref[...], packed_grad_ref[:, src]
        ).astype(bf16)
        return carry

    lax.fori_loop(0, 6, weigh, 0)
    upstream_ref[...] = jnp.zeros_like(upstream_ref)

    def push_back(at, carry):
        cols = pl.ds(pl.multiple_of(at * width, 128), width)
        upstream_ref[...] += contract_cols(packed_grad_ref[:, cols], qkv_ref[:, cols])
        return carry

    lax.fori_loop(0, 3, push_back, 0)
    normed_one_grad = upstream_ref[...]
    extra_ref[0:1, :] = jnp.sum(normed_one_grad * normed_one, axis=0, keepdims=True)
    extra_ref[1:2, :] = jnp.sum(normed_one_grad, axis=0, keepdims=True)
    input_grad = res_grad_ref[...] + norm_back(
        normed_one_grad, normed_one, inv_one, vec_ref[0:1, :]
    )
    for image in range(image_count):
        grad_ref[image] = input_grad[image * stride : image * stride + seq_length, :]


def reduce_kernel(
    shards,
    chips,
    grads_ref,
    extra_ref,
    blocks_ref,
    qkv_out,
    proj_out,
    extra_out,
    blocks_out,
    twin_in,
    plane_sum,
    peer_in,
    far_out,
    far_in,
    whole,
    small_in,
    small_out,
    small_far,
    twin_send,
    twin_recv,
    peer_send,
    peer_recv,
    far_send,
    far_recv,
    back_send,
    back_recv,
    last_send,
    last_recv,
    small_send,
    small_recv,
    edge_send,
    edge_recv,
    block_send,
    block_recv,
    block_here,
):
    place = Place(shards, chips)
    bf16 = jnp.bfloat16
    core, chip, shard = place.core, place.chip, place.shard
    count = 2 * chips
    place.greet(
        [place.along(j) for j in range(1, shards)]
        + [place.plane(i) for i in range(1, count)]
    )
    sent = []

    def send(copy):
        copy.start()
        sent.append(copy)

    def target(j):
        return lax.rem(shard + 1 + j, shards)

    def to_twin(j):
        return remote(
            grads_ref.at[1 - core, target(j)],
            twin_in.at[j],
            twin_send.at[j],
            twin_recv.at[j],
            place.sibling(),
        )

    def small_copy(i):
        return remote(
            extra_ref, small_in.at[i], small_send.at[i], small_recv.at[i], place.plane(i)
        )

    def peer_copy(j, i):
        return remote(
            plane_sum.at[j, lax.rem(chip + i, chips)],
            peer_in.at[j, i],
            peer_send.at[j, i],
            peer_recv.at[j, i],
            place.peer(i),
        )

    def far_copy(j):
        return remote(
            far_out.at[j], far_in.at[j], far_send.at[j], far_recv.at[j], place.along(1 + j)
        )

    def edge_copy(j):
        return remote(
            small_out, small_far.at[j], edge_send.at[j], edge_recv.at[j], place.along(j)
        )

    def back_copy(i):
        block = whole.at[core, chip]
        return remote(block, block, back_send.at[i], back_recv.at[i], place.peer(i))

    def last_copy(i):
        block = whole.at[core, lax.rem(chip - i + chips, chips)]
        return remote(block, block, last_send.at[i], last_recv.at[i], place.sibling())

    def block_copy(j):
        to = lax.rem(shard + j, shards)
        return remote(
            blocks_ref.at[to],
            blocks_out.at[shard],
            block_send.at[j],
            block_recv.at[j],
            place.along(j),
        )

    for j in range(shards):
        send(to_twin(j))
    for i in range(1, count):
        send(small_copy(i))
    for j in range(1, shards):
        send(block_copy(j))
    block_local = pltpu.make_async_copy(
        blocks_ref.at[shard], blocks_out.at[shard], block_here.at[0]
    )
    block_local.start()
    for j in range(shards):
        to_twin(j).wait_recv()

        def add_twin(at, carry):
            plane_sum[j, at] = (
                as_float(grads_ref[core, target(j), at]) + as_float(twin_in[j, at])
            ).astype(bf16)
            return carry

        lax.fori_loop(0, chips, add_twin, 0)
        for i in range(1, chips):
            send(peer_copy(j, i))
    total = as_float(extra_ref[...])
    for i in range(1, count):
        small_copy(i).wait_recv()
        total += as_float(small_in[i])
    small_out[...] = total.astype(bf16)
    for j in range(1, shards):
        send(edge_copy(j))
    for j in range(shards):
        mine = as_float(plane_sum[j, chip])
        for i in range(1, chips):
            peer_copy(j, i).wait_recv()
            mine += as_float(peer_in[j, i])
        far_out[j] = mine.astype(bf16)
        if j < shards - 1:
            send(far_copy(j))
    mine = as_float(far_out[shards - 1])
    for j in range(shards - 1):
        far_copy(j).wait_recv()
        mine += as_float(far_in[j])
    whole[core, chip] = mine.astype(bf16)
    for i in range(1, chips):
        send(back_copy(i))
    send(last_copy(0))
    total = as_float(small_out[...])
    for j in range(1, shards):
        edge_copy(j).wait_recv()
        total += as_float(small_far[j])
    extra_out[...] = total
    for i in range(1, chips):
        back_copy(i).wait_recv()
        send(last_copy(i))
    for i in range(chips):
        last_copy(i).wait_recv()
    rows = qkv_out.shape[0] // chips
    wide, narrow = qkv_out.shape[1] // 2, proj_out.shape[1] // 2
    for side in range(2):
        for at in range(chips):
            block = as_float(whole[side, at])
            here = slice(at * rows, (at + 1) * rows)
            qkv_out[here, side * wide : (side + 1) * wide] = block[:, :wide]
            proj_out[here, side * narrow : (side + 1) * narrow] = block[:, wide:]
    block_local.wait()
    for j in range(1, shards):
        block_copy(j).wait_recv()
    for copy in sent:
        copy.wait_send()


def reduce_grads(fast, shards, chips, grads, extra, blocks):
    _, height, cols = grads.shape
    width = cols // 2
    shard_rows = height // shards
    if not fast:
        wide = 3 * width // 2
        joined = jnp.concatenate(
            [grads[0, :, :wide], grads[1, :, :wide], grads[0, :, wide:], grads[1, :, wide:]],
            axis=1,
        )
        mine = lax.psum_scatter(joined, "shard", scatter_dimension=0, tiled=True)
        mine = as_float(lax.psum(mine, "expert"))
        extra_sum = as_float(lax.psum(extra, ("shard", "expert")))
        moved = lax.all_to_all(blocks, "shard", split_axis=0, concat_axis=0, tiled=True)
        return mine[:, : 3 * width], mine[:, 3 * width :], extra_sum, moved
    rows = shard_rows // chips
    bf16, dma = jnp.bfloat16, pltpu.SemaphoreType.DMA
    cut = grads.reshape(2, shards, chips, rows, cols)
    count = 2 * chips
    return pl.pallas_call(
        functools.partial(reduce_kernel, shards, chips),
        out_shape=[
            jax.ShapeDtypeStruct((shard_rows, 3 * width), jnp.float32),
            jax.ShapeDtypeStruct((shard_rows, width), jnp.float32),
            jax.ShapeDtypeStruct(extra.shape, jnp.float32),
            jax.ShapeDtypeStruct(blocks.shape, blocks.dtype),
        ],
        in_specs=[pl.BlockSpec(memory_space=pltpu.VMEM)] * 2
        + [pl.BlockSpec(memory_space=pl.ANY)],
        out_specs=[pl.BlockSpec(memory_space=pltpu.VMEM)] * 3
        + [pl.BlockSpec(memory_space=pl.ANY)],
        scratch_shapes=[
            pltpu.VMEM((shards, chips, rows, cols), bf16),
            pltpu.VMEM((shards, chips, rows, cols), bf16),
            pltpu.VMEM((shards, chips, rows, cols), bf16),
            pltpu.VMEM((shards, rows, cols), bf16),
            pltpu.VMEM((shards, rows, cols), bf16),
            pltpu.VMEM((2, chips, rows, cols), bf16),
            pltpu.VMEM((count,) + extra.shape, bf16),
            pltpu.VMEM(extra.shape, bf16),
            pltpu.VMEM((shards,) + extra.shape, bf16),
            dma((shards,)),
            dma((shards,)),
            dma((shards, chips)),
            dma((shards, chips)),
            dma((shards,)),
            dma((shards,)),
            dma((chips,)),
            dma((chips,)),
            dma((chips,)),
            dma((chips,)),
            dma((count,)),
            dma((count,)),
            dma((shards,)),
            dma((shards,)),
            dma((shards,)),
            dma((shards,)),
            dma((1,)),
        ],
        compiler_params=pltpu.CompilerParams(
            collective_id=2, has_side_effects=True, vmem_limit_bytes=BIG_VMEM
        ),
        name="reduce_grads",
    )(cut, extra, blocks)


def attention_core(stride, expert_count, r):
    rows, width = r.flat.shape
    bf16 = jnp.bfloat16
    mask = same_image(rows, stride, r.x.shape[1])
    low_lanes = lax.broadcasted_iota(jnp.int32, (rows, 128), 1) < HEAD_DIM

    def attend(pair, carry):
        def part(which):
            return r.packed[:, pl.ds(pl.multiple_of(which * width + pair * 128, 128), 128)]

        query, key, value = part(0), part(1), part(2)
        zero = jnp.zeros_like(query)
        weights_low = masked_softmax(jnp.where(low_lanes, query, zero), key, mask).astype(bf16)
        weights_high = masked_softmax(jnp.where(low_lanes, zero, query), key, mask).astype(bf16)
        r.mixed[:, pl.ds(pl.multiple_of(pair * 128, 128), 128)] = jnp.where(
            low_lanes, plain_dot(weights_low, value), plain_dot(weights_high, value)
        ).astype(bf16)
        return carry

    lax.fori_loop(0, HEADS // 2, attend, 0)


def route_core(expert_count, r, proj):
    bf16 = jnp.bfloat16
    residual = r.flat[...] + plain_dot(r.mixed[...], proj) + r.vectors[2:3, :]
    r.residual[...] = residual
    normed_two, _ = norm_stats(residual)
    expert_in = (normed_two * r.vectors[3:4, :] + r.vectors[4:5, :]).astype(bf16)
    r.tokens[...] = expert_in
    r.gates[...] = softmax_gates(expert_in, r.router[...], expert_count)


def softmax_gates(rows, router, expert_count):
    logits = contract_cols(rows, router)
    lanes = lax.broadcasted_iota(jnp.int32, logits.shape, 1)
    logits = jnp.where(lanes < expert_count, logits, -1e30)
    shifted = jnp.exp(logits - jnp.max(logits, axis=-1, keepdims=True))
    return shifted / jnp.sum(shifted, axis=-1, keepdims=True)


FUSED_IN = ("x", "qkv", "proj", "extra", "up", "slots", "in_w", "out_wt", "in_bias", "out_bias")
FUSED_OUT = (
    "qkv_all",
    "proj_all",
    "vectors",
    "router",
    "packed",
    "mixed",
    "residual",
    "tokens",
    "gates",
    "summed",
    "route",
    "in_grad",
    "out_grad",
    "in_bias_grad",
    "out_bias_grad",
)


def fused_kernel(shards, experts, capacity, expert_count, stride, names, *refs):
    r = types.SimpleNamespace(**dict(zip(names, refs)))
    chips = experts // 2
    place = Place(shards, chips)
    bf16 = jnp.bfloat16
    me, shard = place.expert, place.shard
    row_count, width = r.tokens.shape
    group_rows = r.rows_in.shape[1]
    shard_rows = r.qkv.shape[0]
    image_count, seq_length = r.x.shape[:2]
    first_rows = 2 * capacity // 16 * 16
    second_rows = group_rows - first_rows
    upper = lax.div(shard, 2)
    even = lax.rem(shard, 2) == 0
    place.greet(
        [place.along(j) for j in range(1, shards)]
        + [place.plane(i) for i in range(1, experts)]
    )
    order = (1, 3, 2)
    kinds = ((r.qkv, r.qkv_all), (r.proj, r.proj_all))

    def target(i):
        return lax.rem(me + i, experts)

    def origin(i):
        return lax.rem(me - i + experts, experts)

    def owner(j):
        return lax.rem(shard - j + shards, shards)

    def cut(kind, chip_step):
        source = kinds[kind][0]
        rows = source.shape[0] // chips
        cols = source.shape[1] // 2
        chip = lax.rem(place.chip + chip_step + chips, chips)
        return (
            pl.ds(pl.multiple_of(chip * rows, 16), rows),
            pl.ds(pl.multiple_of(place.core * cols, 128), cols),
        )

    def far_copy(kind, j):
        rows, cols = cut(kind, 0)
        return remote(
            kinds[kind][0].at[rows, cols],
            kinds[kind][1].at[shard, rows, cols],
            r.far_s.at[kind, j],
            r.far_r.at[kind, j],
            place.along(j),
        )

    def to_twin(kind, j, i):
        rows, cols = cut(kind, -i)
        block = kinds[kind][1].at[owner(j), rows, cols]
        return remote(
            block, block, r.twin_s.at[kind, j, i], r.twin_r.at[kind, j, i], place.sibling()
        )

    def to_peer(kind, j, i):
        rows, cols = cut(kind, 0)
        block = kinds[kind][1].at[owner(j), rows, cols]
        return remote(
            block, block, r.peer_s.at[kind, j, i], r.peer_r.at[kind, j, i], place.peer(i)
        )

    def small_copy(which, j):
        src, dst = ((r.extra, r.extra_all), (r.slots, r.slots_all))[which]
        return remote(
            src, dst.at[shard], r.small_s.at[which, j], r.small_r.at[which, j], place.along(j)
        )

    def up_line_copy(j):
        return remote(
            r.up, r.up_line.at[shard], r.upline_s.at[j], r.upline_r.at[j], place.along(j)
        )

    for j in order:
        small_copy(0, j).start()
    for kind in range(2):
        for j in order:
            far_copy(kind, j).start()
    for j in order:
        small_copy(1, j).start()
    local = [
        pltpu.make_async_copy(r.qkv, r.qkv_all.at[shard], r.here.at[0]),
        pltpu.make_async_copy(r.proj, r.proj_all.at[shard], r.here.at[1]),
    ]
    for copy in local:
        copy.start()
    r.extra_all[shard] = r.extra[...]
    r.slots_all[shard] = r.slots[...]
    r.up_line[shard] = r.up[...]
    spread_rows(r.flat, r.x, image_count, seq_length, stride)

    for kind in range(2):
        for j in order:
            far_copy(kind, j).wait_recv()
            for i in range(1, chips):
                to_peer(kind, j, i).start()
            to_twin(kind, j, 0).start()
    for j in order:
        up_line_copy(j).start()

    for j in order:
        small_copy(0, j).wait_recv()
    lane_from = lax.broadcasted_iota(jnp.int32, (r.extra.shape[1], width), 0)
    lane_to = lax.broadcasted_iota(jnp.int32, (r.extra.shape[1], width), 1)

    def placed(source, at):
        hit = (lane_to == lane_from + at * shard_rows) & (lane_from < shard_rows)
        return plain_dot(r.extra_all[source], jnp.where(hit, 1.0, 0.0).astype(bf16))

    whole = placed(0, 0)
    for at in range(1, shards):
        whole += placed(at, at)
    r.vectors[...] = whole
    r.router[...] = jnp.zeros_like(r.router)
    r.router[:expert_count, :] = whole[VECTORS : VECTORS + expert_count].astype(bf16)
    biases = []
    for first in (0, shards // 2):
        total = jnp.zeros((1, width), jnp.float32)
        for at in range(shards):
            row = VECTORS - 2 + at % 2
            total += placed(first + at // 2, at)[row : row + 1]
        biases.append(total)
    normed, _ = norm_stats(r.flat[...])
    r.attn[...] = (normed * r.vectors[0:1, :] + r.vectors[1:2, :]).astype(bf16)

    for kind in range(2):
        for j in order:
            for i in range(1, chips):
                to_peer(kind, j, i).wait_recv()
                to_twin(kind, j, i).start()

    for j in order:
        small_copy(1, j).wait_recv()
    for at in range(shards):
        r.slot_col[at * row_count : (at + 1) * row_count, 0:8] = r.slots_all[at].T[:row_count]

    def table(at, base, size):
        ids = (lax.broadcasted_iota(jnp.int32, (size, row_count), 0) + base).astype(jnp.float32)
        slots = r.slots_all[at]
        hit = (ids == slots[0:1, :row_count]) | (ids == slots[1:2, :row_count])
        return jnp.where(hit, 1.0, 0.0).astype(bf16)

    def up_copy(i):
        return remote(
            r.stage_a.at[target(i)], r.up_in.at[me], r.up_s.at[i], r.up_r.at[i], place.plane(i)
        )

    for j in order:
        up_line_copy(j).wait_recv()

    def dispatch_up(i, carry):
        to = target(i)
        picked = plain_dot(table(0, to * group_rows, group_rows), r.up_line[0])
        for at in range(1, shards):
            picked += plain_dot(table(at, to * group_rows, group_rows), r.up_line[at])
        picked = picked.astype(bf16)

        @pl.when(i == 0)
        def _():
            r.up_in[me] = picked

        @pl.when(i > 0)
        def _():
            r.stage_a[to] = picked
            up_copy(i).start()

        return carry

    lax.fori_loop(0, experts, dispatch_up, 0)

    for copy in local:
        copy.wait()
    for j in order:
        for i in range(chips):
            to_twin(0, j, i).wait_recv()

    def project(tile, carry):
        cols = pl.ds(pl.multiple_of(tile * width, 128), width)
        weight = r.qkv_all[:, :, cols].reshape(width, width)
        bias = jnp.where(tile == 0, biases[0], jnp.where(tile == 2, biases[1], 0.0))
        r.packed[:, cols] = (plain_dot(r.attn[...], weight) + bias).astype(bf16)
        return carry

    lax.fori_loop(0, 3, project, 0)
    attention_core(stride, expert_count, r)
    for j in order:
        for i in range(chips):
            to_twin(1, j, i).wait_recv()
    route_core(expert_count, r, r.proj_all[...].reshape(width, width))

    def line_copy(j):
        return remote(
            r.tokens, r.line.at[shard], r.line_s.at[j], r.line_r.at[j], place.along(j)
        )

    hidden = r.in_w.shape[1]

    def weight_copy(j):
        cols = pl.ds(
            pl.multiple_of(lax.rem(shard + j, shards) * hidden, 128), hidden
        )
        rows = pl.ds(pl.multiple_of(shard * shard_rows, 16), shard_rows)
        return remote(
            r.out_wt.at[:, cols],
            r.out_w.at[rows],
            r.weight_s.at[j],
            r.weight_r.at[j],
            place.along(j),
        )

    for j in order:
        line_copy(j).start()
    weight_local = pltpu.make_async_copy(
        r.out_wt.at[:, pl.ds(pl.multiple_of(shard * hidden, 128), hidden)],
        r.out_w.at[pl.ds(pl.multiple_of(shard * shard_rows, 16), shard_rows)],
        r.here.at[2],
    )
    weight_local.start()
    r.line[shard] = r.tokens[...]

    def row_copy(i, part, start, size):
        here = pl.ds(pl.multiple_of(start, 16), size)
        return remote(
            r.stage_b.at[target(i), here],
            r.rows_in.at[me, here],
            r.row_s.at[i, part],
            r.row_r.at[i, part],
            place.plane(i),
        )

    spans = (
        (upper * second_rows, first_rows),
        ((1 - upper) * first_rows, second_rows),
    )

    def dispatch(part, sources):
        start, size = spans[part]
        here = pl.ds(pl.multiple_of(start, 16), size)

        def one(i, carry):
            to = target(i)
            base = to * group_rows + start
            picked = plain_dot(table(sources[0], base, size), r.line[sources[0]])
            for at in sources[1:]:
                picked += plain_dot(table(at, base, size), r.line[at])
            picked = picked.astype(bf16)

            @pl.when(i == 0)
            def _():
                r.rows_in[me, here, :] = picked

            @pl.when(i > 0)
            def _():
                r.stage_b[to, here, :] = picked
                row_copy(i, part, start, size).start()

            return carry

        lax.fori_loop(0, experts, one, 0)

    @pl.when(even)
    def _():
        line_copy(3).wait_recv()

    @pl.when(jnp.logical_not(even))
    def _():
        line_copy(1).wait_recv()

    dispatch(0, (2 * upper, 2 * upper + 1))

    @pl.when(even)
    def _():
        line_copy(1).wait_recv()

    @pl.when(jnp.logical_not(even))
    def _():
        line_copy(3).wait_recv()

    line_copy(2).wait_recv()
    for j in order:
        weight_copy(j).start()
    dispatch(1, tuple(range(shards)))

    def enter(i, carry):
        at = origin(i)

        @pl.when(i > 0)
        def _():
            for part in range(2):
                row_copy(i, part, *spans[part]).wait_recv()

        rows = r.rows_in[at]
        gelu_out, gelu_slope = gelu_parts(plain_dot(rows, r.in_w[...]) + r.in_bias[0:1, :])
        r.slope[at] = gelu_slope
        r.gelu[at] = gelu_out.astype(bf16)
        gates = softmax_gates(rows, r.router[...], expert_count)
        lanes = lax.broadcasted_iota(jnp.int32, gates.shape, 1)
        gate = jnp.sum(jnp.where(lanes == me, gates, 0.0), axis=-1, keepdims=True)
        r.gate_in[at] = jnp.broadcast_to(gate, gates.shape)
        return carry

    lax.fori_loop(0, experts, enter, 0)

    def out_copy(i):
        return remote(
            r.stage_a.at[origin(i)],
            r.out_in.at[me],
            r.out_s.at[i],
            r.out_r.at[i],
            place.plane(experts - i),
        )

    def note_copy(i):
        return remote(
            r.notes.at[origin(i)],
            r.note_in.at[me],
            r.note_s.at[i],
            r.note_r.at[i],
            place.plane(experts - i),
        )

    def back_copy(i):
        return remote(
            r.stage_b.at[origin(i)],
            r.back_in.at[me],
            r.back_s.at[i],
            r.back_r.at[i],
            place.plane(experts - i),
        )

    weight_local.wait()
    for j in order:
        weight_copy(j).wait_recv()

    def drain(i, carry):
        up_copy(i).wait_send()
        for part in range(2):
            row_copy(i, part, *spans[part]).wait_send()
        return carry

    lax.fori_loop(1, experts, drain, 0)
    r.notes[...] = jnp.zeros_like(r.notes)

    def leave(i, carry):
        at = origin(i)

        @pl.when(i > 0)
        def _():
            up_copy(i).wait_recv()

        gate = r.gate_in[at][:, 0:1]
        upstream = as_float(r.up_in[at])
        r.sent[at] = (gate * upstream).astype(bf16)
        expert_out = contract_cols(r.gelu[at], r.out_w[...]) + r.out_bias[0:1, :]
        gate_grad = jnp.sum(upstream * expert_out, axis=-1, keepdims=True)
        notes = jnp.broadcast_to(gate_grad, (group_rows, 128)).T[:16].astype(bf16)
        gated = (gate * expert_out).astype(bf16)

        @pl.when(i == 0)
        def _():
            r.out_in[me] = gated
            r.note_in[me, :, :group_rows] = notes

        @pl.when(i > 0)
        def _():
            r.stage_a[at] = gated
            r.notes[at, :, :group_rows] = notes
            out_copy(i).start()
            note_copy(i).start()

        return carry

    lax.fori_loop(0, experts, leave, 0)
    r.in_bias_grad[...] = jnp.zeros_like(r.in_bias_grad)
    r.out_bias_grad[...] = jnp.zeros_like(r.out_bias_grad)

    def backward(i, carry):
        at = origin(i)
        sent = r.sent[at]
        r.out_bias_grad[0:1, :] += jnp.sum(as_float(sent), axis=0, keepdims=True)
        pre_grad = plain_dot(sent, r.out_w[...]) * r.slope[at]
        r.in_bias_grad[0:1, :] += jnp.sum(pre_grad, axis=0, keepdims=True)
        pre_bf = pre_grad.astype(bf16)
        r.pre[at] = pre_bf
        back = contract_cols(pre_bf, r.in_w[...]).astype(bf16)

        @pl.when(i == 0)
        def _():
            r.back_in[me] = back

        @pl.when(i > 0)
        def _():
            r.stage_b[at] = back
            back_copy(i).start()

        return carry

    lax.fori_loop(0, experts, backward, 0)

    def hits(source):
        ids = lax.broadcasted_iota(jnp.int32, (shards * row_count, group_rows), 1)
        ids = (ids + source * group_rows).astype(jnp.float32)
        hit = (ids == r.slot_col[:, 0:1]) | (ids == r.slot_col[:, 1:2])
        return jnp.where(hit, 1.0, 0.0).astype(bf16)

    def collect_out(i, carry):
        at = target(i)

        @pl.when(i > 0)
        def _():
            out_copy(i).wait_recv()
            note_copy(i).wait_recv()

        chosen = hits(at)
        r.total[:, :width] += plain_dot(chosen, r.out_in[at])
        rows_at = lax.broadcasted_iota(jnp.int32, (128, group_rows), 0)
        note = as_float(r.note_in[at, 0:1, :group_rows])
        r.total[:, width:] += contract_cols(
            chosen, jnp.where(rows_at == at, note, 0.0).astype(bf16)
        )
        return carry

    def sum_copy(which, j):
        src, dst = ((r.far_out, r.far_out_in), (r.far_back, r.far_back_in))[which]
        to = lax.rem(shard + j, shards)
        return remote(
            src.at[to], dst.at[j], r.sum_s.at[which, j], r.sum_r.at[which, j], place.along(j)
        )

    def spread_sums(which, cols):
        far = (r.far_out, r.far_back)[which]
        for at in range(shards):
            far[at] = r.total[at * row_count : (at + 1) * row_count, :cols].astype(bf16)
        for j in order:
            sum_copy(which, j).start()

    def own_rows(cols):
        return r.total[pl.ds(pl.multiple_of(shard * row_count, 16), row_count), :cols]

    r.total[...] = jnp.zeros_like(r.total)
    lax.fori_loop(0, experts, collect_out, 0)
    spread_sums(0, width + 128)
    r.summed[...] = own_rows(width + 128)

    tile = 128
    for left, right, grad in ((r.sent, r.gelu, r.out_grad), (r.rows_in, r.pre, r.in_grad)):

        def weigh(at, carry, left=left, right=right, grad=grad):
            cols = pl.ds(pl.multiple_of(at * tile, 128), tile)
            lhs = left[:, :, cols].reshape(experts * group_rows, tile)
            rhs = right[...].reshape(experts * group_rows, right.shape[2])
            grad[cols, :] = contract_rows(lhs, rhs).astype(grad.dtype)
            return carry

        lax.fori_loop(0, left.shape[2] // tile, weigh, 0)

    r.total[...] = jnp.zeros_like(r.total)

    def collect_back(i, carry):
        at = target(i)

        @pl.when(i > 0)
        def _():
            back_copy(i).wait_recv()

        r.total[:, :width] += plain_dot(hits(at), r.back_in[at])
        return carry

    lax.fori_loop(0, experts, collect_back, 0)
    spread_sums(1, width)
    for j in order:
        sum_copy(0, j).wait_recv()
        r.summed[...] += as_float(r.far_out_in[j])
    r.route[...] = own_rows(width)
    for j in order:
        sum_copy(1, j).wait_recv()
        r.route[...] += as_float(r.far_back_in[j])

    for j in order:
        for which in range(2):
            far_copy(which, j).wait_send()
            small_copy(which, j).wait_send()
            sum_copy(which, j).wait_send()
            for i in range(chips):
                to_twin(which, j, i).wait_send()
                if i:
                    to_peer(which, j, i).wait_send()
        up_line_copy(j).wait_send()
        line_copy(j).wait_send()
        weight_copy(j).wait_send()

    def finish(i, carry):
        out_copy(i).wait_send()
        note_copy(i).wait_send()
        back_copy(i).wait_send()
        return carry

    lax.fori_loop(1, experts, finish, 0)


def fused_pass(shards, experts, capacity, expert_count, stride, inputs):
    x, qkv, proj, extra, up, _, in_w, _, _, _ = inputs
    width, hidden = in_w.shape
    row_count = up.shape[0]
    router_pad = round_up(expert_count, 128)
    group_rows = round_up(shards * capacity, 16)
    lanes = round_up(group_rows, 128)
    chips = experts // 2
    bf16, f32, dma = jnp.bfloat16, jnp.float32, pltpu.SemaphoreType.DMA
    vmem, anywhere = pl.BlockSpec(memory_space=pltpu.VMEM), pl.BlockSpec(memory_space=pl.ANY)

    def shape(dims, kind=bf16):
        return jax.ShapeDtypeStruct(dims, kind)

    outs = (
        shape((shards,) + qkv.shape),
        shape((shards,) + proj.shape),
        shape((extra.shape[0], width), f32),
        shape((router_pad, width)),
        shape((row_count, 3 * width)),
        shape((row_count, width)),
        shape((row_count, width), f32),
        shape((row_count, width)),
        shape((row_count, router_pad), f32),
        shape((row_count, width + 128), f32),
        shape((row_count, width), f32),
        shape((width, hidden), f32),
        shape((width, hidden)),
        shape((8, hidden), f32),
        shape((8, width), f32),
    )
    group = (experts, group_rows)
    scratch = {
        "flat": pltpu.VMEM((row_count, width), f32),
        "attn": pltpu.VMEM((row_count, width), bf16),
        "extra_all": pltpu.VMEM((shards,) + extra.shape, bf16),
        "slots_all": pltpu.VMEM((shards, 8, round_up(row_count, 128)), f32),
        "slot_col": pltpu.VMEM((shards * row_count, 128), f32),
        "up_line": pltpu.VMEM((shards, row_count, width), bf16),
        "line": pltpu.VMEM((shards, row_count, width), bf16),
        "out_w": pltpu.VMEM((width, hidden), bf16),
        "up_in": pltpu.VMEM(group + (width,), bf16),
        "stage_a": pltpu.VMEM(group + (width,), bf16),
        "stage_b": pltpu.VMEM(group + (width,), bf16),
        "rows_in": pltpu.VMEM(group + (width,), bf16),
        "gelu": pltpu.VMEM(group + (hidden,), bf16),
        "slope": pltpu.VMEM(group + (hidden,), f32),
        "gate_in": pltpu.VMEM(group + (128,), f32),
        "sent": pltpu.VMEM(group + (width,), bf16),
        "pre": pltpu.VMEM(group + (hidden,), bf16),
        "out_in": pltpu.VMEM(group + (width,), bf16),
        "back_in": pltpu.VMEM(group + (width,), bf16),
        "notes": pltpu.VMEM((experts, 16, lanes), bf16),
        "note_in": pltpu.VMEM((experts, 16, lanes), bf16),
        "total": pltpu.VMEM((shards * row_count, width + 128), f32),
        "far_out": pltpu.VMEM((shards, row_count, width + 128), bf16),
        "far_out_in": pltpu.VMEM((shards, row_count, width + 128), bf16),
        "far_back": pltpu.VMEM((shards, row_count, width), bf16),
        "far_back_in": pltpu.VMEM((shards, row_count, width), bf16),
        "here": dma((3,)),
    }
    pairs = {
        "far": (2, shards),
        "twin": (2, shards, chips),
        "peer": (2, shards, chips),
        "small": (2, shards),
        "upline": (shards,),
        "up": (experts,),
        "line": (shards,),
        "weight": (shards,),
        "row": (experts, 2),
        "out": (experts,),
        "note": (experts,),
        "back": (experts,),
        "sum": (2, shards),
    }
    for name, dims in pairs.items():
        scratch[name + "_s"] = dma(dims)
        scratch[name + "_r"] = dma(dims)
    names = FUSED_IN + FUSED_OUT + tuple(scratch)
    specs = [anywhere if name in ("qkv", "proj", "out_wt") else vmem for name in FUSED_IN]
    return pl.pallas_call(
        functools.partial(fused_kernel, shards, experts, capacity, expert_count, stride, names),
        out_shape=outs,
        in_specs=specs,
        out_specs=[vmem] * len(outs),
        scratch_shapes=list(scratch.values()),
        compiler_params=pltpu.CompilerParams(
            collective_id=1, has_side_effects=True, vmem_limit_bytes=BIG_VMEM
        ),
        name="front_and_experts",
    )(*inputs)


def expert_slow(
    tokens, gates, route_rows, tables, line_up, up_in, in_slice, out_slice, in_bias, own_bias
):
    row_count, width = tokens.shape
    bf16 = jnp.bfloat16
    table_0, table_1, send_table = tables
    router_pad = gates.shape[1]
    chosen = route_rows[:, :, None] == jnp.arange(router_pad, dtype=jnp.int32)[None, None, :]
    gate_pick = jnp.sum(jnp.where(chosen, gates[:, None, :], 0.0), axis=2)
    gate_high = gate_pick.astype(bf16)
    gate_low = (gate_pick - as_float(gate_high)).astype(bf16)
    gate_notes = jnp.concatenate([gate_high, gate_low], axis=1)
    gate_notes = jnp.pad(gate_notes, ((0, 0), (0, 128 - gate_notes.shape[1])))
    sent_line = jnp.concatenate([tokens, gate_notes], axis=1)
    row_line = lax.all_gather(sent_line, "shard", axis=0, tiled=True)
    line_in = row_line[:, :width]
    gate_line = as_float(row_line[:, width : width + 4])
    line_gate = gate_line[:, 0:2] + gate_line[:, 2:4]
    outgoing = contract_rows(send_table, line_in).astype(bf16)
    slot_gate = jnp.sum(
        jnp.where(table_0, line_gate[:, 0:1], 0.0) + jnp.where(table_1, line_gate[:, 1:2], 0.0),
        axis=0,
    )
    slot_high = slot_gate.astype(bf16)
    slot_low = (slot_gate - as_float(slot_high)).astype(bf16)
    slot_notes = jnp.pad(jnp.stack([slot_high, slot_low], axis=1), ((0, 0), (0, 126)))
    incoming = lax.all_to_all(
        jnp.concatenate([outgoing, slot_notes], axis=1),
        "expert",
        split_axis=0,
        concat_axis=0,
        tiled=True,
    )
    rows_in = incoming[:, :width]
    gate_in = as_float(incoming[:, width : width + 1]) + as_float(
        incoming[:, width + 1 : width + 2]
    )
    grad_in = (as_float(up_in) * gate_in).astype(bf16)
    pre_act = plain_dot(rows_in, in_slice) + in_bias
    gelu_out, gelu_slope = gelu_parts(pre_act)
    gelu_bf = gelu_out.astype(bf16)
    expert_out = (plain_dot(gelu_bf, out_slice) + own_bias).astype(bf16)
    returned = lax.all_to_all(expert_out, "expert", split_axis=0, concat_axis=0, tiled=True)
    pre_grad = contract_cols(grad_in, out_slice) * gelu_slope
    pre_bf = pre_grad.astype(bf16)
    back_rows = contract_cols(pre_bf, in_slice).astype(bf16)
    returned_grad = lax.all_to_all(back_rows, "expert", split_axis=0, concat_axis=0, tiled=True)
    out_0 = plain_dot(table_0.astype(bf16), returned)
    out_1 = plain_dot(table_1.astype(bf16), returned)
    combined = line_gate[:, 0:1] * out_0 + line_gate[:, 1:2] * out_1
    line_up_wide = as_float(line_up)
    gate_grad_line = jnp.stack(
        [jnp.sum(line_up_wide * out_0, axis=1), jnp.sum(line_up_wide * out_1, axis=1)], axis=1
    )
    joined = jnp.concatenate(
        [combined.astype(bf16), jnp.pad(gate_grad_line, ((0, 0), (0, 126))).astype(bf16)], axis=1
    )
    summed = as_float(lax.psum_scatter(joined, "shard", scatter_dimension=0, tiled=True))
    picked = jnp.sum(
        jnp.where(chosen, summed[:, width : width + 2][:, :, None], 0.0), axis=1
    )
    summed = jnp.concatenate([summed[:, :width], picked], axis=1)
    back_line = plain_dot(send_table, returned_grad)
    route_grad = lax.psum_scatter(back_line.astype(bf16), "shard", scatter_dimension=0, tiled=True)
    return (
        summed,
        route_grad,
        contract_rows(rows_in, pre_bf),
        contract_rows(gelu_bf, grad_in).astype(bf16),
        jnp.sum(pre_grad, axis=0)[None],
        jnp.sum(as_float(grad_in), axis=0)[None],
    )


def body(
    block_input,
    image_live,
    expert_routes,
    first_gain,
    first_shift,
    qkv_weight,
    query_value_bias,
    attn_out_weight,
    attn_out_bias,
    second_gain,
    second_shift,
    router_weight,
    expert_in_weight,
    expert_in_bias,
    expert_out_weight,
    expert_out_bias,
    output_grad,
):
    image_count, seq_length, width = block_input.shape
    shards = lax.axis_size("shard")
    experts = lax.axis_size("expert")
    chips = experts // 2
    expert_count = router_weight.shape[1]
    my_shard = lax.axis_index("shard")
    shard_rows = first_gain.shape[0]
    stride = round_up(seq_length, 8)
    row_count = image_count * stride
    capacity = (3 * image_count * seq_length + expert_count - 1) // expert_count
    group_rows = round_up(shards * capacity, 16)
    slot_rows = expert_count * group_rows
    bf16 = jnp.bfloat16
    fast = chips == 4 and shards == 4 and shard_rows % (16 * chips) == 0

    router_pad = round_up(expert_count, 128)
    extra = jnp.concatenate(
        [
            jnp.stack(
                [
                    first_gain,
                    first_shift,
                    attn_out_bias,
                    second_gain,
                    second_shift,
                    query_value_bias[:shard_rows],
                    query_value_bias[shard_rows:],
                ]
            ),
            router_weight.T,
        ],
        axis=0,
    )
    extra_rows = round_up(VECTORS + expert_count, 16)
    extra = jnp.pad(
        extra,
        ((0, extra_rows - extra.shape[0]), (0, round_up(shard_rows, 128) - shard_rows)),
    )

    tail_rows = stride - seq_length
    live_rows = jnp.repeat(image_live, stride) * jnp.tile(
        (jnp.arange(stride) < seq_length).astype(jnp.int32), image_count
    )
    route_rows = jnp.pad(expert_routes, ((0, 0), (0, tail_rows), (0, 0))).reshape(row_count, 2)
    route_code, position = slot_places(route_rows, live_rows, expert_count)
    up_rows = (
        jnp.pad(output_grad, ((0, 0), (0, tail_rows), (0, 0))).reshape(row_count, width)
        * as_float(live_rows)[:, None]
    )
    slot_index = (
        route_code.astype(jnp.int32) * group_rows
        + my_shard * capacity
        + position.astype(jnp.int32)
    )
    slot_index = jnp.where(route_code >= 0, slot_index, -1)
    own_bias = lax.dynamic_update_slice(
        jnp.zeros((1, width), jnp.float32),
        as_float(expert_out_bias),
        (0, my_shard * shard_rows),
    )
    in_bias = as_float(expert_in_bias)
    in_slice = expert_in_weight[0]
    out_slice_t = expert_out_weight[0].T
    if fast:
        slot_rows_f = jnp.pad(
            slot_index.T.astype(jnp.float32),
            ((0, 6), (0, round_up(row_count, 128) - row_count)),
            constant_values=-1.0,
        )
        (
            qkv_full,
            proj_full,
            vectors,
            router_t,
            packed,
            mixed,
            residual,
            expert_in,
            gates,
            summed,
            route_grad,
            in_weight_grad,
            out_weight_grad,
            in_bias_sum,
            out_bias_sum,
        ) = fused_pass(
            shards,
            experts,
            capacity,
            expert_count,
            stride,
            (
                block_input,
                qkv_weight,
                attn_out_weight,
                extra,
                up_rows.astype(bf16),
                slot_rows_f,
                in_slice,
                out_slice_t,
                jnp.pad(in_bias, ((0, 7), (0, 0))),
                jnp.pad(own_bias, ((0, 7), (0, 0))),
            ),
        )
        qkv_full = qkv_full.reshape(width, 3 * width)
        proj_full = proj_full.reshape(width, width)
        vectors = vectors[:8]
    else:
        notes = jnp.concatenate([route_code.astype(bf16), position.astype(bf16)], axis=1)
        notes = jnp.pad(notes, ((0, 0), (0, 128 - notes.shape[1])))
        up_line = jnp.concatenate([up_rows.astype(bf16), notes], axis=1)
        qkv_all, proj_all, extra_all, line_all = (
            lax.all_gather(each, "shard", axis=0, tiled=False)
            for each in (qkv_weight, attn_out_weight, extra, up_line)
        )
        qkv_full = qkv_all.reshape(width, 3 * width)
        proj_full = proj_all.reshape(width, width)
        extra_t = jnp.transpose(extra_all[:, :, :shard_rows], (1, 0, 2))
        vectors = as_float(extra_t[:8]).reshape(8, width)
        query_value = as_float(extra_t[5:7])
        bias_full = jnp.transpose(query_value, (1, 0, 2)).reshape(2 * width)
        bias_row = jnp.concatenate(
            [bias_full[:width], jnp.zeros((width,), jnp.float32), bias_full[width:]]
        )
        bias_row = jnp.pad(bias_row[None], ((0, 7), (0, 0)))
        router_t = jnp.pad(
            extra_t[VECTORS : VECTORS + expert_count].reshape(expert_count, width),
            ((0, router_pad - expert_count), (0, 0)),
        )
        line_rows = shards * row_count
        line = line_all.reshape(line_rows, width + 128)
        line_up = line[:, :width]
        line_notes = as_float(line[:, width : width + 4])
        line_ids = jnp.arange(line_rows, dtype=jnp.int32)[:, None]
        line_slot = (
            line_notes[:, 0:2].astype(jnp.int32) * group_rows
            + (line_ids // row_count) * capacity
            + line_notes[:, 2:4].astype(jnp.int32)
        )
        line_slot = jnp.where(line_notes[:, 0:2] >= 0, line_slot, -1)
        slot_ids = jnp.arange(slot_rows, dtype=jnp.int32)
        table_0 = line_slot[:, 0:1] == slot_ids[None, :]
        table_1 = line_slot[:, 1:2] == slot_ids[None, :]
        send_table = (table_0 | table_1).astype(bf16)
        up_out = contract_rows(send_table, line_up).astype(bf16)
        up_in = lax.all_to_all(up_out, "expert", split_axis=0, concat_axis=0, tiled=True)
        out_slice = lax.all_to_all(
            expert_out_weight[0], "shard", split_axis=0, concat_axis=1, tiled=True
        )
        packed, mixed, residual, expert_in, gates = pl.pallas_call(
            functools.partial(forward_kernel, stride, expert_count),
            out_shape=[
                jax.ShapeDtypeStruct((row_count, 3 * width), bf16),
                jax.ShapeDtypeStruct((row_count, width), bf16),
                jax.ShapeDtypeStruct((row_count, width), jnp.float32),
                jax.ShapeDtypeStruct((row_count, width), bf16),
                jax.ShapeDtypeStruct((row_count, router_pad), jnp.float32),
            ],
            in_specs=[pl.BlockSpec(memory_space=pltpu.VMEM)] * 6,
            out_specs=[pl.BlockSpec(memory_space=pltpu.VMEM)] * 5,
            scratch_shapes=[
                pltpu.VMEM((row_count, width), jnp.float32),
                pltpu.VMEM((row_count, width), bf16),
            ],
            compiler_params=pltpu.CompilerParams(vmem_limit_bytes=BIG_VMEM),
            name="attention_forward",
        )(block_input, qkv_full, proj_full, vectors, bias_row, router_t)
        (
            summed,
            route_grad,
            in_weight_grad,
            out_weight_grad,
            in_bias_sum,
            out_bias_sum,
        ) = expert_slow(
            expert_in,
            gates,
            route_rows,
            (table_0, table_1, send_table),
            line_up,
            up_in,
            in_slice,
            out_slice,
            in_bias,
            own_bias,
        )
        out_weight_grad = out_weight_grad.T
    out_weight_grad = out_weight_grad.reshape(shards, shard_rows, -1)
    in_weight_part = in_weight_grad[None]
    in_bias_part = in_bias_sum[:1]
    out_bias_part = lax.dynamic_slice_in_dim(
        out_bias_sum[0], my_shard * shard_rows, shard_rows
    )[None]

    smem = pl.BlockSpec(memory_space=pltpu.SMEM)
    vmem = pl.BlockSpec(memory_space=pltpu.VMEM)
    wide_rows = pltpu.VMEM((row_count, width), jnp.float32)
    block_output, input_grad, weight_grads, extra_grads = pl.pallas_call(
        functools.partial(backward_kernel, stride),
        out_shape=[
            jax.ShapeDtypeStruct(block_input.shape, jnp.float32),
            jax.ShapeDtypeStruct(block_input.shape, jnp.float32),
            jax.ShapeDtypeStruct((2, width, 2 * width), bf16),
            jax.ShapeDtypeStruct((extra_rows, width), jnp.float32),
        ],
        in_specs=[smem] + [vmem] * 13,
        out_specs=[vmem] * 4,
        scratch_shapes=[
            wide_rows,
            wide_rows,
            pltpu.VMEM((width, row_count), bf16),
            pltpu.VMEM((row_count, width), bf16),
            pltpu.VMEM((row_count, 3 * width), bf16),
            wide_rows,
        ],
        compiler_params=pltpu.CompilerParams(vmem_limit_bytes=BIG_VMEM),
        cost_estimate=pl.CostEstimate(
            flops=32 * row_count * width * width,
            bytes_accessed=48 * width * width,
            transcendentals=2 * HEADS * row_count * row_count,
        ),
        name="attention_backward",
    )(
        image_live,
        block_input,
        output_grad,
        packed,
        mixed,
        residual,
        expert_in,
        gates,
        summed,
        route_grad,
        qkv_full,
        proj_full,
        vectors,
        router_t,
    )
    qkv_sum, proj_sum, extra_sum, out_weight_blocks = reduce_grads(
        fast, shards, chips, weight_grads, extra_grads.astype(bf16), out_weight_grad
    )
    out_weight_part = (
        jnp.transpose(as_float(out_weight_blocks), (0, 2, 1)).reshape(-1, shard_rows)[None]
    )

    def own(array_in, size, axis=0):
        return lax.dynamic_slice_in_dim(array_in, my_shard * size, size, axis=axis)

    mine = own(extra_sum, shard_rows, axis=1)
    return (
        block_output,
        input_grad,
        mine[0],
        mine[1],
        qkv_sum,
        own(extra_sum[5:7].reshape(2 * width), 2 * shard_rows),
        proj_sum,
        mine[2],
        mine[3],
        mine[4],
        mine[VECTORS : VECTORS + expert_count].T,
        in_weight_part,
        in_bias_part,
        out_weight_part,
        out_bias_part,
    )


def solution(mesh):
    in_specs = (
        P(("expert", "shard"), None, None),
        P(("expert", "shard")),
        P(("expert", "shard"), None, None),
        P("shard"),
        P("shard"),
        P("shard", None),
        P("shard"),
        P("shard", None),
        P("shard"),
        P("shard"),
        P("shard"),
        P("shard", None),
        P("expert", None, "shard"),
        P("expert", "shard"),
        P("expert", None, "shard"),
        P("expert", "shard"),
        P(("expert", "shard"), None, None),
    )
    out_specs = (
        P(("expert", "shard"), None, None),
        P(("expert", "shard"), None, None),
        P("shard"),
        P("shard"),
        P("shard", None),
        P("shard"),
        P("shard", None),
        P("shard"),
        P("shard"),
        P("shard"),
        P("shard", None),
        P("expert", None, "shard"),
        P("expert", "shard"),
        P("expert", None, "shard"),
        P("expert", "shard"),
    )
    return jax.shard_map(body, mesh=mesh, in_specs=in_specs, out_specs=out_specs, check_vma=False)
```

```python
import functools
import math
import types

import jax
import jax.numpy as jnp
from jax import lax
from jax.experimental import pallas as pl
from jax.experimental.pallas import tpu as pltpu
from jax.sharding import PartitionSpec as P

HEADS = 12
HEAD_DIM = 64


EPSILON = 1e-06
PRECISE = lax.Precision.HIGHEST
HALF_ROOT = 0.7071067811865476
DENSITY = 0.3989422804014327


def as_float(array_in):
    return array_in.astype(jnp.float32)


def contract_rows(left_side, right_side):
    return lax.dot_general(
        left_side, right_side, (((0,), (0,)), ((), ())), preferred_element_type=jnp.float32
    )


def contract_cols(left_side, right_side):
    return lax.dot_general(
        left_side, right_side, (((1,), (1,)), ((), ())), preferred_element_type=jnp.float32
    )


def precise_rows(left_side, right_side):
    return lax.dot_general(
        left_side,
        right_side,
        (((0,), (0,)), ((), ())),
        precision=PRECISE,
        preferred_element_type=jnp.float32,
    )


def precise_cols(left_side, right_side):
    return lax.dot_general(
        left_side,
        right_side,
        (((1,), (1,)), ((), ())),
        precision=PRECISE,
        preferred_element_type=jnp.float32,
    )


def layer_norm(values_in, gain_vec, shift_vec):
    center = values_in - jnp.mean(values_in, axis=-1, keepdims=True)
    inv_std = lax.rsqrt(jnp.mean(center * center, axis=-1, keepdims=True) + EPSILON)
    normed = center * inv_std
    return (normed * as_float(gain_vec) + as_float(shift_vec), normed, inv_std)


def norm_back(upstream, normed, inv_std, gain_vec):
    scaled = upstream * as_float(gain_vec)
    return inv_std * (
        scaled
        - jnp.mean(scaled, axis=-1, keepdims=True)
        - normed * jnp.mean(scaled * normed, axis=-1, keepdims=True)
    )


def gelu_parts(pre_act):
    normal_cdf = 0.5 * (1.0 + jax.scipy.special.erf(pre_act * HALF_ROOT))
    return (
        pre_act * normal_cdf,
        normal_cdf + pre_act * DENSITY * jnp.exp(-0.5 * pre_act * pre_act),
    )


BIG_VMEM = 56 * 1024 * 1024
VECTORS = 7


def plain_dot(left_side, right_side):
    return jnp.dot(left_side, right_side, preferred_element_type=jnp.float32)


def exact_dot(left_side, right_side):
    return lax.dot_general(
        left_side,
        right_side,
        (((1,), (0,)), ((), ())),
        precision=PRECISE,
        preferred_element_type=jnp.float32,
    )


def round_up(value, step):
    return -(-value // step) * step


def slot_places(route_rows, live_rows, expert_count):
    row_count = route_rows.shape[0]
    flat_routes = route_rows.reshape(2 * row_count)
    alive_pairs = jnp.repeat(live_rows, 2)
    chosen = (flat_routes[:, None] == jnp.arange(expert_count, dtype=jnp.int32)[None, :]).astype(
        jnp.int32
    )
    live_hits = chosen * alive_pairs[:, None]
    earlier = (
        jnp.arange(2 * row_count, dtype=jnp.int32)[:, None]
        > jnp.arange(2 * row_count, dtype=jnp.int32)[None, :]
    ).astype(jnp.bfloat16)
    counted = jnp.dot(earlier, live_hits.astype(jnp.bfloat16), preferred_element_type=jnp.float32)
    position = jnp.sum(counted * as_float(live_hits), axis=1)
    route_code = jnp.where(alive_pairs > 0, flat_routes, -1).astype(jnp.float32)
    return route_code.reshape(row_count, 2), position.reshape(row_count, 2)


class Place:
    def __init__(self, shards, chips):
        self.shards = shards
        self.chips = chips
        self.expert = lax.axis_index("expert")
        self.shard = lax.axis_index("shard")
        self.core = lax.rem(self.expert, 2)
        self.chip = lax.div(self.expert, 2)

    def along(self, step):
        return {
            "expert": self.expert,
            "shard": lax.rem(self.shard + step + self.shards, self.shards),
        }

    def peer(self, step):
        other = lax.rem(self.chip + step + self.chips, self.chips)
        return {"expert": other * 2 + self.core, "shard": self.shard}

    def sibling(self):
        return {"expert": self.chip * 2 + 1 - self.core, "shard": self.shard}

    def plane(self, step):
        count = 2 * self.chips
        return {"expert": lax.rem(self.expert + step, count), "shard": self.shard}

    def greet(self, others):
        barrier = pltpu.get_barrier_semaphore()
        for other in others:
            pl.semaphore_signal(
                barrier, inc=1, device_id=other, device_id_type=pl.DeviceIdType.MESH
            )
        pl.semaphore_wait(barrier, len(others))


def remote(src, dst, send_sem, recv_sem, device):
    return pltpu.make_async_remote_copy(
        src_ref=src,
        dst_ref=dst,
        send_sem=send_sem,
        recv_sem=recv_sem,
        device_id=device,
        device_id_type=pl.DeviceIdType.MESH,
    )


def norm_stats(values_in):
    center = values_in - jnp.mean(values_in, axis=-1, keepdims=True)
    inv_std = lax.rsqrt(jnp.mean(center * center, axis=-1, keepdims=True) + EPSILON)
    return center * inv_std, inv_std


def spread_rows(dst, src, image_count, seq_length, stride):
    dst[...] = jnp.zeros_like(dst)
    for image in range(image_count):
        dst[image * stride : image * stride + seq_length, :] = src[:, image, :]


def same_image(rows, stride, seq_length):
    row_at = lax.broadcasted_iota(jnp.int32, (rows, rows), 0)
    col_at = lax.broadcasted_iota(jnp.int32, (rows, rows), 1)
    mask = None
    for image in range(rows // stride):
        low = image * stride
        part = (
            (row_at >= low)
            & (row_at < low + stride)
            & (col_at >= low)
            & (col_at < low + seq_length)
        )
        mask = part if mask is None else mask | part
    return mask


def masked_softmax(query_half, keys, mask):
    scores = contract_cols(query_half, keys) * (1.0 / math.sqrt(HEAD_DIM))
    scores = jnp.where(mask, scores, -1e30)
    row_max = jnp.max(scores, axis=-1, keepdims=True)
    log_total = row_max + jnp.log(jnp.sum(jnp.exp(scores - row_max), axis=-1, keepdims=True))
    return jnp.exp(scores - log_total)


def forward_kernel(
    stride,
    expert_count,
    x_ref,
    qkv_ref,
    proj_ref,
    vec_ref,
    bias_ref,
    router_ref,
    packed_ref,
    mixed_ref,
    residual_ref,
    line_ref,
    gates_ref,
    flat_ref,
    attn_ref,
):
    seq_length, image_count, width = x_ref.shape
    rows = flat_ref.shape[0]
    bf16 = jnp.bfloat16
    spread_rows(flat_ref, x_ref, image_count, seq_length, stride)
    normed, _ = norm_stats(flat_ref[...])
    attn_ref[...] = (normed * vec_ref[0:1, :] + vec_ref[1:2, :]).astype(bf16)

    def project(tile, carry):
        cols = pl.ds(pl.multiple_of(tile * width, 128), width)
        packed_ref[:, cols] = (
            plain_dot(attn_ref[...], qkv_ref[:, cols]) + bias_ref[0:1, cols]
        ).astype(bf16)
        return carry

    lax.fori_loop(0, 3, project, 0)
    mask = same_image(rows, stride, seq_length)
    low_lanes = lax.broadcasted_iota(jnp.int32, (rows, 128), 1) < HEAD_DIM

    def attend(pair, carry):
        def part(which):
            return packed_ref[:, pl.ds(pl.multiple_of(which * width + pair * 128, 128), 128)]

        query, key, value = part(0), part(1), part(2)
        zero = jnp.zeros_like(query)
        weights_low = masked_softmax(jnp.where(low_lanes, query, zero), key, mask).astype(bf16)
        weights_high = masked_softmax(jnp.where(low_lanes, zero, query), key, mask).astype(bf16)
        mixed_ref[:, pl.ds(pl.multiple_of(pair * 128, 128), 128)] = jnp.where(
            low_lanes, plain_dot(weights_low, value), plain_dot(weights_high, value)
        ).astype(bf16)
        return carry

    lax.fori_loop(0, HEADS // 2, attend, 0)
    residual = flat_ref[...] + plain_dot(mixed_ref[...], proj_ref[...]) + vec_ref[2:3, :]
    residual_ref[...] = residual
    normed_two, _ = norm_stats(residual)
    expert_in = (normed_two * vec_ref[3:4, :] + vec_ref[4:5, :]).astype(bf16)
    line_ref[...] = expert_in
    logits = contract_cols(expert_in, router_ref[...])
    lanes = lax.broadcasted_iota(jnp.int32, logits.shape, 1)
    logits = jnp.where(lanes < expert_count, logits, -1e30)
    shifted = jnp.exp(logits - jnp.max(logits, axis=-1, keepdims=True))
    gates_ref[...] = shifted / jnp.sum(shifted, axis=-1, keepdims=True)


def backward_kernel(
    stride,
    live_ref,
    x_ref,
    up_ref,
    packed_ref,
    mixed_ref,
    residual_ref,
    expert_ref,
    gates_ref,
    summed_ref,
    back_ref,
    qkv_ref,
    proj_ref,
    vec_ref,
    router_ref,
    block_ref,
    grad_ref,
    weight_ref,
    extra_ref,
    flat_ref,
    upstream_ref,
    attn_t_ref,
    mixed_grad_ref,
    packed_grad_ref,
    res_grad_ref,
):
    seq_length, image_count, width = x_ref.shape
    rows = flat_ref.shape[0]
    bf16 = jnp.bfloat16
    half = 3 * width // 2
    spread_rows(flat_ref, x_ref, image_count, seq_length, stride)
    upstream_ref[...] = jnp.zeros_like(upstream_ref)
    residual = residual_ref[...]
    block = residual + as_float(summed_ref[:, :width])
    for image in range(image_count):
        live = live_ref[image].astype(jnp.float32)
        here = slice(image * stride, image * stride + seq_length)
        upstream_ref[here, :] = up_ref[:, image, :] * live
        block_ref[:, image, :] = block[here, :]

    gates = gates_ref[...]
    picked = as_float(summed_ref[:, width:])
    logit_grad = gates * (picked - jnp.sum(gates * picked, axis=-1, keepdims=True))
    router_rows = extra_ref.shape[0] - VECTORS
    extra_ref[VECTORS:, :] = precise_rows(logit_grad, as_float(expert_ref[...]))[
        :router_rows
    ]
    normed_two_grad = as_float(back_ref[...]) + exact_dot(
        logit_grad, as_float(router_ref[...])
    )
    normed_two, inv_two = norm_stats(residual)
    extra_ref[3:4, :] = jnp.sum(normed_two_grad * normed_two, axis=0, keepdims=True)
    extra_ref[4:5, :] = jnp.sum(normed_two_grad, axis=0, keepdims=True)
    residual_grad = upstream_ref[...] + norm_back(
        normed_two_grad, normed_two, inv_two, vec_ref[3:4, :]
    )
    res_grad_ref[...] = residual_grad
    extra_ref[2:3, :] = jnp.sum(residual_grad, axis=0, keepdims=True)
    residual_bf = residual_grad.astype(bf16)
    proj_grad = contract_rows(mixed_ref[...], residual_bf)
    for core in range(2):
        weight_ref[core, :, half:] = proj_grad[
            :, core * (width // 2) : (core + 1) * (width // 2)
        ].astype(bf16)
    mixed_grad_ref[...] = contract_cols(residual_bf, proj_ref[...]).astype(bf16)

    mask = same_image(rows, stride, seq_length)
    low_lanes = lax.broadcasted_iota(jnp.int32, (rows, 128), 1) < HEAD_DIM

    def attend(pair, carry):
        def part(which):
            return pl.ds(pl.multiple_of(which * width + pair * 128, 128), 128)

        query, key, value = (packed_ref[:, part(which)] for which in range(3))
        mixed_grad = mixed_grad_ref[:, part(0)]
        zero = jnp.zeros_like(query)
        totals = [0.0, 0.0, 0.0]
        for high in range(2):

            def only(array_in):
                return jnp.where(low_lanes, zero if high else array_in, array_in if high else zero)

            query_half, mixed_half = only(query), only(mixed_grad)
            probs = masked_softmax(query_half, key, mask)
            prob_grad = contract_cols(mixed_half, value)
            score_grad = (
                probs
                * (prob_grad - jnp.sum(probs * prob_grad, axis=-1, keepdims=True))
                * (1.0 / math.sqrt(HEAD_DIM))
            ).astype(bf16)
            totals[0] += plain_dot(score_grad, only(key))
            totals[1] += contract_rows(score_grad, query_half)
            totals[2] += contract_rows(probs.astype(bf16), mixed_half)
        for which in range(3):
            packed_grad_ref[:, part(which)] = totals[which].astype(bf16)
        extra_ref[5:6, part(0)] = jnp.sum(totals[0], axis=0, keepdims=True)
        extra_ref[6:7, part(0)] = jnp.sum(totals[2], axis=0, keepdims=True)
        return carry

    lax.fori_loop(0, HEADS // 2, attend, 0)

    normed_one, inv_one = norm_stats(flat_ref[...])
    attn_in = normed_one * vec_ref[0:1, :] + vec_ref[1:2, :]
    attn_t_ref[...] = attn_in.T.astype(bf16)
    tile = half // 3

    def weigh(at, carry):
        src = pl.ds(pl.multiple_of(at * tile, 128), tile)
        dst = pl.ds(pl.multiple_of(lax.rem(at, 3) * tile, 128), tile)
        weight_ref[lax.div(at, 3), :, dst] = plain_dot(
            attn_t_ref[...], packed_grad_ref[:, src]
        ).astype(bf16)
        return carry

    lax.fori_loop(0, 6, weigh, 0)
    upstream_ref[...] = jnp.zeros_like(upstream_ref)

    def push_back(at, carry):
        cols = pl.ds(pl.multiple_of(at * width, 128), width)
        upstream_ref[...] += contract_cols(packed_grad_ref[:, cols], qkv_ref[:, cols])
        return carry

    lax.fori_loop(0, 3, push_back, 0)
    normed_one_grad = upstream_ref[...]
    extra_ref[0:1, :] = jnp.sum(normed_one_grad * normed_one, axis=0, keepdims=True)
    extra_ref[1:2, :] = jnp.sum(normed_one_grad, axis=0, keepdims=True)
    input_grad = res_grad_ref[...] + norm_back(
        normed_one_grad, normed_one, inv_one, vec_ref[0:1, :]
    )
    for image in range(image_count):
        grad_ref[:, image, :] = input_grad[image * stride : image * stride + seq_length, :]


def reduce_kernel(
    shards,
    chips,
    grads_ref,
    extra_ref,
    blocks_ref,
    qkv_out,
    proj_out,
    extra_out,
    blocks_out,
    twin_in,
    plane_sum,
    peer_in,
    far_out,
    far_in,
    whole,
    small_in,
    small_out,
    small_far,
    twin_send,
    twin_recv,
    peer_send,
    peer_recv,
    far_send,
    far_recv,
    back_send,
    back_recv,
    last_send,
    last_recv,
    small_send,
    small_recv,
    edge_send,
    edge_recv,
    block_send,
    block_recv,
    block_here,
):
    place = Place(shards, chips)
    bf16 = jnp.bfloat16
    core, chip, shard = place.core, place.chip, place.shard
    count = 2 * chips
    place.greet(
        [place.along(j) for j in range(1, shards)]
        + [place.plane(i) for i in range(1, count)]
    )
    sent = []

    def send(copy):
        copy.start()
        sent.append(copy)

    def target(j):
        return lax.rem(shard + 1 + j, shards)

    def to_twin(j):
        return remote(
            grads_ref.at[1 - core, target(j)],
            twin_in.at[j],
            twin_send.at[j],
            twin_recv.at[j],
            place.sibling(),
        )

    def small_copy(i):
        return remote(
            extra_ref, small_in.at[i], small_send.at[i], small_recv.at[i], place.plane(i)
        )

    def peer_copy(j, i):
        return remote(
            plane_sum.at[j, lax.rem(chip + i, chips)],
            peer_in.at[j, i],
            peer_send.at[j, i],
            peer_recv.at[j, i],
            place.peer(i),
        )

    def far_copy(j):
        return remote(
            far_out.at[j], far_in.at[j], far_send.at[j], far_recv.at[j], place.along(1 + j)
        )

    def edge_copy(j):
        return remote(
            small_out, small_far.at[j], edge_send.at[j], edge_recv.at[j], place.along(j)
        )

    def back_copy(i):
        block = whole.at[core, chip]
        return remote(block, block, back_send.at[i], back_recv.at[i], place.peer(i))

    def last_copy(i):
        block = whole.at[core, lax.rem(chip - i + chips, chips)]
        return remote(block, block, last_send.at[i], last_recv.at[i], place.sibling())

    def block_copy(j):
        to = lax.rem(shard + j, shards)
        return remote(
            blocks_ref.at[to],
            blocks_out.at[shard],
            block_send.at[j],
            block_recv.at[j],
            place.along(j),
        )

    for j in range(shards):
        send(to_twin(j))
    for i in range(1, count):
        send(small_copy(i))
    for j in range(1, shards):
        send(block_copy(j))
    block_local = pltpu.make_async_copy(
        blocks_ref.at[shard], blocks_out.at[shard], block_here.at[0]
    )
    block_local.start()
    for j in range(shards):
        to_twin(j).wait_recv()

        def add_twin(at, carry):
            plane_sum[j, at] = (
                as_float(grads_ref[core, target(j), at]) + as_float(twin_in[j, at])
            ).astype(bf16)
            return carry

        lax.fori_loop(0, chips, add_twin, 0)
        for i in range(1, chips):
            send(peer_copy(j, i))
    total = as_float(extra_ref[...])
    for i in range(1, count):
        small_copy(i).wait_recv()
        total += as_float(small_in[i])
    small_out[...] = total.astype(bf16)
    for j in range(1, shards):
        send(edge_copy(j))
    for j in range(shards):
        mine = as_float(plane_sum[j, chip])
        for i in range(1, chips):
            peer_copy(j, i).wait_recv()
            mine += as_float(peer_in[j, i])
        far_out[j] = mine.astype(bf16)
        if j < shards - 1:
            send(far_copy(j))
    mine = as_float(far_out[shards - 1])
    for j in range(shards - 1):
        far_copy(j).wait_recv()
        mine += as_float(far_in[j])
    whole[core, chip] = mine.astype(bf16)
    for i in range(1, chips):
        send(back_copy(i))
    send(last_copy(0))
    total = as_float(small_out[...])
    for j in range(1, shards):
        edge_copy(j).wait_recv()
        total += as_float(small_far[j])
    extra_out[...] = total
    for i in range(1, chips):
        back_copy(i).wait_recv()
        send(last_copy(i))
    for i in range(chips):
        last_copy(i).wait_recv()
    rows = qkv_out.shape[0] // chips
    wide, narrow = qkv_out.shape[1] // 2, proj_out.shape[1] // 2
    for side in range(2):
        for at in range(chips):
            block = as_float(whole[side, at])
            here = slice(at * rows, (at + 1) * rows)
            qkv_out[here, side * wide : (side + 1) * wide] = block[:, :wide]
            proj_out[here, side * narrow : (side + 1) * narrow] = block[:, wide:]
    block_local.wait()
    for j in range(1, shards):
        block_copy(j).wait_recv()
    for copy in sent:
        copy.wait_send()


def reduce_grads(fast, shards, chips, grads, extra, blocks):
    _, height, cols = grads.shape
    width = cols // 2
    shard_rows = height // shards
    if not fast:
        wide = 3 * width // 2
        joined = jnp.concatenate(
            [grads[0, :, :wide], grads[1, :, :wide], grads[0, :, wide:], grads[1, :, wide:]],
            axis=1,
        )
        mine = lax.psum_scatter(joined, "shard", scatter_dimension=0, tiled=True)
        mine = as_float(lax.psum(mine, "expert"))
        extra_sum = as_float(lax.psum(extra, ("shard", "expert")))
        moved = lax.all_to_all(blocks, "shard", split_axis=0, concat_axis=0, tiled=True)
        return mine[:, : 3 * width], mine[:, 3 * width :], extra_sum, moved
    rows = shard_rows // chips
    bf16, dma = jnp.bfloat16, pltpu.SemaphoreType.DMA
    cut = grads.reshape(2, shards, chips, rows, cols)
    count = 2 * chips
    return pl.pallas_call(
        functools.partial(reduce_kernel, shards, chips),
        out_shape=[
            jax.ShapeDtypeStruct((shard_rows, 3 * width), jnp.float32),
            jax.ShapeDtypeStruct((shard_rows, width), jnp.float32),
            jax.ShapeDtypeStruct(extra.shape, jnp.float32),
            jax.ShapeDtypeStruct(blocks.shape, blocks.dtype),
        ],
        in_specs=[pl.BlockSpec(memory_space=pltpu.VMEM)] * 2
        + [pl.BlockSpec(memory_space=pl.ANY)],
        out_specs=[pl.BlockSpec(memory_space=pltpu.VMEM)] * 3
        + [pl.BlockSpec(memory_space=pl.ANY)],
        scratch_shapes=[
            pltpu.VMEM((shards, chips, rows, cols), bf16),
            pltpu.VMEM((shards, chips, rows, cols), bf16),
            pltpu.VMEM((shards, chips, rows, cols), bf16),
            pltpu.VMEM((shards, rows, cols), bf16),
            pltpu.VMEM((shards, rows, cols), bf16),
            pltpu.VMEM((2, chips, rows, cols), bf16),
            pltpu.VMEM((count,) + extra.shape, bf16),
            pltpu.VMEM(extra.shape, bf16),
            pltpu.VMEM((shards,) + extra.shape, bf16),
            dma((shards,)),
            dma((shards,)),
            dma((shards, chips)),
            dma((shards, chips)),
            dma((shards,)),
            dma((shards,)),
            dma((chips,)),
            dma((chips,)),
            dma((chips,)),
            dma((chips,)),
            dma((count,)),
            dma((count,)),
            dma((shards,)),
            dma((shards,)),
            dma((shards,)),
            dma((shards,)),
            dma((1,)),
        ],
        compiler_params=pltpu.CompilerParams(
            collective_id=2, has_side_effects=True, vmem_limit_bytes=BIG_VMEM
        ),
        name="reduce_grads",
    )(cut, extra, blocks)


def attention_core(stride, expert_count, r):
    rows, width = r.flat.shape
    bf16 = jnp.bfloat16
    mask = same_image(rows, stride, r.x.shape[0])
    low_lanes = lax.broadcasted_iota(jnp.int32, (rows, 128), 1) < HEAD_DIM

    def attend(pair, carry):
        def part(which):
            return r.packed[:, pl.ds(pl.multiple_of(which * width + pair * 128, 128), 128)]

        query, key, value = part(0), part(1), part(2)
        zero = jnp.zeros_like(query)
        weights_low = masked_softmax(jnp.where(low_lanes, query, zero), key, mask).astype(bf16)
        weights_high = masked_softmax(jnp.where(low_lanes, zero, query), key, mask).astype(bf16)
        r.mixed[:, pl.ds(pl.multiple_of(pair * 128, 128), 128)] = jnp.where(
            low_lanes, plain_dot(weights_low, value), plain_dot(weights_high, value)
        ).astype(bf16)
        return carry

    lax.fori_loop(0, HEADS // 2, attend, 0)


def route_core(expert_count, r, proj):
    bf16 = jnp.bfloat16
    residual = r.flat[...] + plain_dot(r.mixed[...], proj) + r.vectors[2:3, :]
    r.residual[...] = residual
    normed_two, _ = norm_stats(residual)
    expert_in = (normed_two * r.vectors[3:4, :] + r.vectors[4:5, :]).astype(bf16)
    r.tokens[...] = expert_in
    r.gates[...] = softmax_gates(expert_in, r.router[...], expert_count)


def softmax_gates(rows, router, expert_count):
    logits = contract_cols(rows, router)
    lanes = lax.broadcasted_iota(jnp.int32, logits.shape, 1)
    logits = jnp.where(lanes < expert_count, logits, -1e30)
    shifted = jnp.exp(logits - jnp.max(logits, axis=-1, keepdims=True))
    return shifted / jnp.sum(shifted, axis=-1, keepdims=True)


FUSED_IN = (
    "live",
    "x",
    "grad",
    "routes",
    "qkv",
    "proj",
    "extra",
    "in_w",
    "out_wt",
    "in_bias",
    "out_bias",
)
FUSED_OUT = (
    "qkv_all",
    "proj_all",
    "vectors",
    "router",
    "packed",
    "mixed",
    "residual",
    "tokens",
    "gates",
    "summed",
    "route",
    "in_grad",
    "out_grad",
    "in_bias_grad",
    "out_bias_grad",
)


def fused_kernel(shards, experts, capacity, expert_count, stride, names, *refs):
    r = types.SimpleNamespace(**dict(zip(names, refs)))
    chips = experts // 2
    place = Place(shards, chips)
    bf16 = jnp.bfloat16
    me, shard = place.expert, place.shard
    row_count, width = r.tokens.shape
    group_rows = r.rows_in.shape[1]
    shard_rows = r.qkv.shape[0]
    seq_length, image_count = r.x.shape[:2]
    first_rows = 2 * capacity // 16 * 16
    second_rows = group_rows - first_rows
    upper = lax.div(shard, 2)
    even = lax.rem(shard, 2) == 0
    place.greet(
        [place.along(j) for j in range(1, shards)]
        + [place.plane(i) for i in range(1, experts)]
    )
    order = (1, 3, 2)
    kinds = ((r.qkv, r.qkv_all), (r.proj, r.proj_all))

    def target(i):
        return lax.rem(me + i, experts)

    def origin(i):
        return lax.rem(me - i + experts, experts)

    def owner(j):
        return lax.rem(shard - j + shards, shards)

    def cut(kind, chip_step):
        source = kinds[kind][0]
        rows = source.shape[0] // chips
        cols = source.shape[1] // 2
        chip = lax.rem(place.chip + chip_step + chips, chips)
        return (
            pl.ds(pl.multiple_of(chip * rows, 16), rows),
            pl.ds(pl.multiple_of(place.core * cols, 128), cols),
        )

    def far_copy(kind, j):
        rows, cols = cut(kind, 0)
        return remote(
            kinds[kind][0].at[rows, cols],
            kinds[kind][1].at[shard, rows, cols],
            r.far_s.at[kind, j],
            r.far_r.at[kind, j],
            place.along(j),
        )

    def to_twin(kind, j, i):
        rows, cols = cut(kind, -i)
        block = kinds[kind][1].at[owner(j), rows, cols]
        return remote(
            block, block, r.twin_s.at[kind, j, i], r.twin_r.at[kind, j, i], place.sibling()
        )

    def to_peer(kind, j, i):
        rows, cols = cut(kind, 0)
        block = kinds[kind][1].at[owner(j), rows, cols]
        return remote(
            block, block, r.peer_s.at[kind, j, i], r.peer_r.at[kind, j, i], place.peer(i)
        )

    def small_copy(which, j):
        src, dst = ((r.extra, r.extra_all), (r.slots, r.slots_all))[which]
        return remote(
            src, dst.at[shard], r.small_s.at[which, j], r.small_r.at[which, j], place.along(j)
        )

    def up_line_copy(j):
        return remote(
            r.up, r.up_line.at[shard], r.upline_s.at[j], r.upline_r.at[j], place.along(j)
        )

    for j in order:
        small_copy(0, j).start()
    for kind in range(2):
        for j in order:
            far_copy(kind, j).start()
    local = [
        pltpu.make_async_copy(r.qkv, r.qkv_all.at[shard], r.here.at[0]),
        pltpu.make_async_copy(r.proj, r.proj_all.at[shard], r.here.at[1]),
    ]
    for copy in local:
        copy.start()
    r.extra_all[shard] = r.extra[...]
    spread_rows(r.flat, r.grad, image_count, seq_length, stride)
    r.slot_col[...] = jnp.zeros_like(r.slot_col) - 1.0
    for image in range(image_count):
        here = slice(image * stride, (image + 1) * stride)
        alive = r.live[image].astype(jnp.float32)
        r.up[here, :] = (r.flat[here, :] * alive).astype(bf16)
        r.turn[...] = jnp.zeros_like(r.turn)
        r.turn[0:2, :seq_length] = r.routes[image].astype(jnp.float32)
        named = r.turn[...].T[:seq_length]
        r.slot_col[image * stride : image * stride + seq_length, 0:8] = (
            named * alive - (1.0 - alive)
        )
    lanes = lax.broadcasted_iota(jnp.int32, (row_count, 128), 1)
    lane_ids = lanes.astype(jnp.float32)
    first, second = (r.slot_col[:row_count, k : k + 1] for k in range(2))
    chosen = (lane_ids == first) | (lane_ids == second)
    earlier = lax.broadcasted_iota(jnp.int32, (row_count, row_count), 0) > (
        lax.broadcasted_iota(jnp.int32, (row_count, row_count), 1)
    )
    place_in = plain_dot(
        jnp.where(earlier, 1.0, 0.0).astype(bf16), jnp.where(chosen, 1.0, 0.0).astype(bf16)
    )
    place_in += lane_ids * group_rows + (shard * capacity).astype(jnp.float32)
    both = jnp.zeros((row_count, 128), jnp.float32)
    for k, named in enumerate((first, second)):
        slot = jnp.sum(jnp.where(lane_ids == named, place_in, 0.0), axis=-1, keepdims=True)
        both += jnp.where(lanes == k, jnp.where(named < 0.0, -1.0, slot), 0.0)
    r.slots[...] = jnp.zeros_like(r.slots)
    r.slots[:, :row_count] = both.T[:8]
    for j in order:
        small_copy(1, j).start()
    r.slots_all[shard] = r.slots[...]
    r.up_line[shard] = r.up[...]
    spread_rows(r.flat, r.x, image_count, seq_length, stride)

    for kind in range(2):
        for j in order:
            far_copy(kind, j).wait_recv()
            for i in range(1, chips):
                to_peer(kind, j, i).start()
            to_twin(kind, j, 0).start()
    for j in order:
        up_line_copy(j).start()

    for j in order:
        small_copy(0, j).wait_recv()
    lane_from = lax.broadcasted_iota(jnp.int32, (r.extra.shape[1], width), 0)
    lane_to = lax.broadcasted_iota(jnp.int32, (r.extra.shape[1], width), 1)

    def placed(source, at):
        hit = (lane_to == lane_from + at * shard_rows) & (lane_from < shard_rows)
        return plain_dot(r.extra_all[source], jnp.where(hit, 1.0, 0.0).astype(bf16))

    whole = placed(0, 0)
    for at in range(1, shards):
        whole += placed(at, at)
    r.vectors[...] = whole[expert_count : expert_count + 8]
    r.router[...] = jnp.zeros_like(r.router)
    r.router[:expert_count, :] = whole[:expert_count].astype(bf16)
    biases = []
    for first in (0, shards // 2):
        total = jnp.zeros((1, width), jnp.float32)
        for at in range(shards):
            row = expert_count + VECTORS - 2 + at % 2
            total += placed(first + at // 2, at)[row : row + 1]
        biases.append(total)
    hit = (lane_to == lane_from + shard * shard_rows) & (lane_from < shard_rows)
    own_bias = plain_dot(
        jnp.broadcast_to(as_float(r.out_bias[...]), (16, shard_rows)).astype(bf16),
        jnp.where(hit, 1.0, 0.0).astype(bf16)[:shard_rows],
    )
    r.own_bias[...] = own_bias[:8]
    normed, _ = norm_stats(r.flat[...])
    r.attn[...] = (normed * r.vectors[0:1, :] + r.vectors[1:2, :]).astype(bf16)

    for kind in range(2):
        for j in order:
            for i in range(1, chips):
                to_peer(kind, j, i).wait_recv()
                to_twin(kind, j, i).start()

    for j in order:
        small_copy(1, j).wait_recv()
    for at in range(shards):
        r.slot_col[at * row_count : (at + 1) * row_count, 0:8] = r.slots_all[at].T[:row_count]

    def table(at, base, size):
        ids = (lax.broadcasted_iota(jnp.int32, (size, row_count), 0) + base).astype(jnp.float32)
        slots = r.slots_all[at]
        hit = (ids == slots[0:1, :row_count]) | (ids == slots[1:2, :row_count])
        return jnp.where(hit, 1.0, 0.0).astype(bf16)

    def up_copy(i):
        return remote(
            r.stage_a.at[target(i)], r.up_in.at[me], r.up_s.at[i], r.up_r.at[i], place.plane(i)
        )

    hidden = r.in_w.shape[1]

    def weight_copy(j):
        cols = pl.ds(
            pl.multiple_of(lax.rem(shard + j, shards) * hidden, 128), hidden
        )
        rows = pl.ds(pl.multiple_of(shard * shard_rows, 16), shard_rows)
        return remote(
            r.out_wt.at[:, cols],
            r.out_w.at[rows],
            r.weight_s.at[j],
            r.weight_r.at[j],
            place.along(j),
        )

    weight_local = pltpu.make_async_copy(
        r.out_wt.at[:, pl.ds(pl.multiple_of(shard * hidden, 128), hidden)],
        r.out_w.at[pl.ds(pl.multiple_of(shard * shard_rows, 16), shard_rows)],
        r.here.at[2],
    )
    weight_local.start()
    for j in order:
        up_line_copy(j).wait_recv()
    for j in order:
        weight_copy(j).start()

    def dispatch_up(i, carry):
        to = target(i)
        picked = plain_dot(table(0, to * group_rows, group_rows), r.up_line[0])
        for at in range(1, shards):
            picked += plain_dot(table(at, to * group_rows, group_rows), r.up_line[at])
        picked = picked.astype(bf16)

        @pl.when(i == 0)
        def _():
            r.up_in[me] = picked

        @pl.when(i > 0)
        def _():
            r.stage_a[to] = picked
            up_copy(i).start()

        return carry

    lax.fori_loop(0, experts, dispatch_up, 0)

    for copy in local:
        copy.wait()
    for j in order:
        for i in range(chips):
            to_twin(0, j, i).wait_recv()

    def project(tile, carry):
        cols = pl.ds(pl.multiple_of(tile * width, 128), width)
        weight = r.qkv_all[:, :, cols].reshape(width, width)
        bias = jnp.where(tile == 0, biases[0], jnp.where(tile == 2, biases[1], 0.0))
        r.packed[:, cols] = (plain_dot(r.attn[...], weight) + bias).astype(bf16)
        return carry

    lax.fori_loop(0, 3, project, 0)
    attention_core(stride, expert_count, r)
    for j in order:
        for i in range(chips):
            to_twin(1, j, i).wait_recv()
    route_core(expert_count, r, r.proj_all[...].reshape(width, width))

    def line_copy(j):
        return remote(
            r.tokens, r.line.at[shard], r.line_s.at[j], r.line_r.at[j], place.along(j)
        )

    def with_pair(act):
        @pl.when(even)
        def _():
            act(3)

        @pl.when(jnp.logical_not(even))
        def _():
            act(1)

    @pl.when(even)
    def _():
        line_copy(1).start()

    @pl.when(jnp.logical_not(even))
    def _():
        line_copy(3).start()

    r.line[shard] = r.tokens[...]

    def row_copy(i, part, start, size):
        here = pl.ds(pl.multiple_of(start, 16), size)
        return remote(
            r.stage_b.at[target(i), here],
            r.rows_in.at[me, here],
            r.row_s.at[i, part],
            r.row_r.at[i, part],
            place.plane(i),
        )

    spans = (
        (upper * second_rows, first_rows),
        ((1 - upper) * first_rows, second_rows),
    )

    def dispatch(part, sources):
        start, size = spans[part]
        here = pl.ds(pl.multiple_of(start, 16), size)

        def one(i, carry):
            to = target(i)
            base = to * group_rows + start
            picked = plain_dot(table(sources[0], base, size), r.line[sources[0]])
            for at in sources[1:]:
                picked += plain_dot(table(at, base, size), r.line[at])
            picked = picked.astype(bf16)

            @pl.when(i == 0)
            def _():
                r.rows_in[me, here, :] = picked

            @pl.when(i > 0)
            def _():
                r.stage_b[to, here, :] = picked
                row_copy(i, part, start, size).start()

            return carry

        lax.fori_loop(0, experts, one, 0)

    with_pair(lambda j: line_copy(j).wait_recv())

    @pl.when(even)
    def _():
        line_copy(3).start()

    @pl.when(jnp.logical_not(even))
    def _():
        line_copy(1).start()

    line_copy(2).start()
    dispatch(0, (2 * upper, 2 * upper + 1))

    @pl.when(even)
    def _():
        line_copy(1).wait_recv()

    @pl.when(jnp.logical_not(even))
    def _():
        line_copy(3).wait_recv()

    line_copy(2).wait_recv()
    dispatch(1, tuple(range(shards)))

    def out_copy(i):
        return remote(
            r.stage_a.at[origin(i)],
            r.out_in.at[me],
            r.out_s.at[i],
            r.out_r.at[i],
            place.plane(experts - i),
        )

    def note_copy(i):
        return remote(
            r.notes.at[origin(i)],
            r.note_in.at[me],
            r.note_s.at[i],
            r.note_r.at[i],
            place.plane(experts - i),
        )

    half = width // 2

    def back_copy(i, part):
        cols = pl.ds(part * half, half)
        return remote(
            r.stage_b.at[origin(i), :, cols],
            r.back_in.at[me, :, cols],
            r.back_s.at[i, part],
            r.back_r.at[i, part],
            place.plane(experts - i),
        )

    weight_local.wait()
    for j in order:
        weight_copy(j).wait_recv()

    def drain_up(i, carry):
        up_copy(i).wait_send()
        return carry

    lax.fori_loop(1, experts, drain_up, 0)
    r.notes[...] = jnp.zeros_like(r.notes)

    def forward(i, carry):
        at = origin(i)

        @pl.when(i > 0)
        def _():
            for part in range(2):
                row_copy(i, part, *spans[part]).wait_recv()

        rows = r.rows_in[at]
        gelu_out, gelu_slope = gelu_parts(
            plain_dot(rows, r.in_w[...]) + as_float(r.in_bias[...])
        )
        r.slope[at] = gelu_slope
        gelu_bf = gelu_out.astype(bf16)
        r.gelu[at] = gelu_bf
        gates = softmax_gates(rows, r.router[...], expert_count)
        gate_lanes = lax.broadcasted_iota(jnp.int32, gates.shape, 1)
        gate = jnp.sum(jnp.where(gate_lanes == me, gates, 0.0), axis=-1, keepdims=True)

        @pl.when(i > 0)
        def _():
            up_copy(i).wait_recv()

        upstream = as_float(r.up_in[at])
        r.sent[at] = (gate * upstream).astype(bf16)
        expert_out = contract_cols(gelu_bf, r.out_w[...]) + r.own_bias[0:1, :]
        gate_grad = jnp.sum(upstream * expert_out, axis=-1, keepdims=True)
        notes = jnp.broadcast_to(gate_grad, (group_rows, 128)).T[:16].astype(bf16)
        gated = (gate * expert_out).astype(bf16)

        @pl.when(i == 0)
        def _():
            r.out_in[me] = gated
            r.note_in[me, :, :group_rows] = notes

        @pl.when(i > 0)
        def _():
            r.stage_a[at] = gated
            r.notes[at, :, :group_rows] = notes
            out_copy(i).start()
            note_copy(i).start()

        return carry

    lax.fori_loop(0, experts, forward, 0)
    r.in_bias_grad[...] = jnp.zeros_like(r.in_bias_grad)
    r.out_bias_grad[...] = jnp.zeros_like(r.out_bias_grad)

    def drain_rows(i, carry):
        for part in range(2):
            row_copy(i, part, *spans[part]).wait_send()
        return carry

    lax.fori_loop(1, experts, drain_rows, 0)

    def backward(i, carry):
        at = origin(i)
        sent = r.sent[at]
        r.out_bias_grad[0:1, :] += jnp.sum(as_float(sent), axis=0, keepdims=True)
        pre_grad = plain_dot(sent, r.out_w[...]) * r.slope[at]
        r.in_bias_grad[0:1, :] += jnp.sum(pre_grad, axis=0, keepdims=True)
        pre_bf = pre_grad.astype(bf16)
        r.pre[at] = pre_bf
        back = contract_cols(pre_bf, r.in_w[...]).astype(bf16)

        @pl.when(i == 0)
        def _():
            r.back_in[me] = back

        @pl.when(i > 0)
        def _():
            r.stage_b[at] = back
            back_copy(i, 0).start()

        return carry

    lax.fori_loop(0, experts, backward, 0)

    def push_rest(i, carry):
        back_copy(i, 1).start()
        return carry

    lax.fori_loop(1, experts, push_rest, 0)

    def hits(source):
        ids = lax.broadcasted_iota(jnp.int32, (shards * row_count, group_rows), 1)
        ids = (ids + source * group_rows).astype(jnp.float32)
        hit = (ids == r.slot_col[:, 0:1]) | (ids == r.slot_col[:, 1:2])
        return jnp.where(hit, 1.0, 0.0).astype(bf16)

    def collect_out(i, carry):
        at = target(i)

        @pl.when(i > 0)
        def _():
            out_copy(i).wait_recv()
            note_copy(i).wait_recv()

        chosen = hits(at)
        r.total[:, :width] += plain_dot(chosen, r.out_in[at])
        rows_at = lax.broadcasted_iota(jnp.int32, (128, group_rows), 0)
        note = as_float(r.note_in[at, 0:1, :group_rows])
        r.total[:, width:] += contract_cols(
            chosen, jnp.where(rows_at == at, note, 0.0).astype(bf16)
        )
        return carry

    columns = ((0, width + 128), (0, half), (half, half))

    def sum_copy(which, j):
        src, dst = ((r.far_out, r.far_out_in), (r.far_back, r.far_back_in))[min(which, 1)]
        to = lax.rem(shard + j, shards)
        cols = pl.ds(*columns[which])
        return remote(
            src.at[to, :, cols],
            dst.at[j, :, cols],
            r.sum_s.at[which, j],
            r.sum_r.at[which, j],
            place.along(j),
        )

    own = pl.ds(pl.multiple_of(shard * row_count, 16), row_count)

    def spread_sums(which):
        far = (r.far_out, r.far_back)[min(which, 1)]
        cols = pl.ds(*columns[which])
        for at in range(shards):
            far[at, :, cols] = r.total[at * row_count : (at + 1) * row_count, cols].astype(bf16)
        for j in order:
            sum_copy(which, j).start()

    r.total[...] = jnp.zeros_like(r.total)
    lax.fori_loop(0, experts, collect_out, 0)
    spread_sums(0)
    r.summed[...] = r.total[own, :]

    tile = 128
    for left, right, grad in ((r.sent, r.gelu, r.out_grad), (r.rows_in, r.pre, r.in_grad)):

        def weigh(at, carry, left=left, right=right, grad=grad):
            cols = pl.ds(pl.multiple_of(at * tile, 128), tile)
            lhs = left[:, :, cols].reshape(experts * group_rows, tile)
            rhs = right[...].reshape(experts * group_rows, right.shape[2])
            grad[cols, :] = contract_rows(lhs, rhs).astype(grad.dtype)
            return carry

        lax.fori_loop(0, left.shape[2] // tile, weigh, 0)

    r.total[...] = jnp.zeros_like(r.total)

    for part in range(2):

        def collect_back(i, carry, part=part):
            at = target(i)
            cols = pl.ds(part * half, half)

            @pl.when(i > 0)
            def _():
                back_copy(i, part).wait_recv()

            r.total[:, cols] += plain_dot(hits(at), r.back_in[at, :, cols])
            return carry

        lax.fori_loop(0, experts, collect_back, 0)
        spread_sums(1 + part)
    for j in order:
        sum_copy(0, j).wait_recv()
        r.summed[...] += as_float(r.far_out_in[j])
    r.route[...] = r.total[own, :width]
    for part in range(2):
        cols = pl.ds(*columns[1 + part])
        for j in order:
            sum_copy(1 + part, j).wait_recv()
            r.route[:, cols] += as_float(r.far_back_in[j, :, cols])

    for j in order:
        for which in range(2):
            far_copy(which, j).wait_send()
            small_copy(which, j).wait_send()
            for i in range(chips):
                to_twin(which, j, i).wait_send()
                if i:
                    to_peer(which, j, i).wait_send()
        for which in range(3):
            sum_copy(which, j).wait_send()
        up_line_copy(j).wait_send()
        line_copy(j).wait_send()
        weight_copy(j).wait_send()

    def finish(i, carry):
        out_copy(i).wait_send()
        note_copy(i).wait_send()
        back_copy(i, 0).wait_send()
        back_copy(i, 1).wait_send()
        return carry

    lax.fori_loop(1, experts, finish, 0)


def fused_pass(shards, experts, capacity, expert_count, stride, inputs):
    x, qkv, proj, extra, in_w = (inputs[at] for at in (1, 4, 5, 6, 7))
    width, hidden = in_w.shape
    row_count = x.shape[1] * stride
    router_pad = round_up(expert_count, 128)
    group_rows = round_up(shards * capacity, 16)
    lanes = round_up(group_rows, 128)
    chips = experts // 2
    bf16, f32, dma = jnp.bfloat16, jnp.float32, pltpu.SemaphoreType.DMA
    vmem, anywhere = pl.BlockSpec(memory_space=pltpu.VMEM), pl.BlockSpec(memory_space=pl.ANY)

    def shape(dims, kind=bf16):
        return jax.ShapeDtypeStruct(dims, kind)

    outs = (
        shape((shards,) + qkv.shape),
        shape((shards,) + proj.shape),
        shape((8, width), f32),
        shape((router_pad, width)),
        shape((row_count, 3 * width)),
        shape((row_count, width)),
        shape((row_count, width), f32),
        shape((row_count, width)),
        shape((row_count, router_pad), f32),
        shape((row_count, width + 128), f32),
        shape((row_count, width), f32),
        shape((width, hidden), f32),
        shape((width, hidden)),
        shape((8, hidden), f32),
        shape((8, width), f32),
    )
    group = (experts, group_rows)
    scratch = {
        "flat": pltpu.VMEM((row_count, width), f32),
        "attn": pltpu.VMEM((row_count, width), bf16),
        "up": pltpu.VMEM((row_count, width), bf16),
        "turn": pltpu.VMEM((8, 128), f32),
        "slots": pltpu.VMEM((8, round_up(row_count, 128)), f32),
        "own_bias": pltpu.VMEM((8, width), f32),
        "extra_all": pltpu.VMEM((shards,) + extra.shape, bf16),
        "slots_all": pltpu.VMEM((shards, 8, round_up(row_count, 128)), f32),
        "slot_col": pltpu.VMEM((shards * row_count, 128), f32),
        "up_line": pltpu.VMEM((shards, row_count, width), bf16),
        "line": pltpu.VMEM((shards, row_count, width), bf16),
        "out_w": pltpu.VMEM((width, hidden), bf16),
        "up_in": pltpu.VMEM(group + (width,), bf16),
        "stage_a": pltpu.VMEM(group + (width,), bf16),
        "stage_b": pltpu.VMEM(group + (width,), bf16),
        "rows_in": pltpu.VMEM(group + (width,), bf16),
        "gelu": pltpu.VMEM(group + (hidden,), bf16),
        "slope": pltpu.VMEM(group + (hidden,), f32),
        "sent": pltpu.VMEM(group + (width,), bf16),
        "pre": pltpu.VMEM(group + (hidden,), bf16),
        "out_in": pltpu.VMEM(group + (width,), bf16),
        "back_in": pltpu.VMEM(group + (width,), bf16),
        "notes": pltpu.VMEM((experts, 16, lanes), bf16),
        "note_in": pltpu.VMEM((experts, 16, lanes), bf16),
        "total": pltpu.VMEM((shards * row_count, width + 128), f32),
        "far_out": pltpu.VMEM((shards, row_count, width + 128), bf16),
        "far_out_in": pltpu.VMEM((shards, row_count, width + 128), bf16),
        "far_back": pltpu.VMEM((shards, row_count, width), bf16),
        "far_back_in": pltpu.VMEM((shards, row_count, width), bf16),
        "here": dma((3,)),
    }
    pairs = {
        "far": (2, shards),
        "twin": (2, shards, chips),
        "peer": (2, shards, chips),
        "small": (2, shards),
        "upline": (shards,),
        "up": (experts,),
        "line": (shards,),
        "weight": (shards,),
        "row": (experts, 2),
        "out": (experts,),
        "note": (experts,),
        "back": (experts, 2),
        "sum": (3, shards),
    }
    for name, dims in pairs.items():
        scratch[name + "_s"] = dma(dims)
        scratch[name + "_r"] = dma(dims)
    names = FUSED_IN + FUSED_OUT + tuple(scratch)
    specs = [anywhere if name in ("qkv", "proj", "out_wt") else vmem for name in FUSED_IN]
    specs[0] = pl.BlockSpec(memory_space=pltpu.SMEM)
    return pl.pallas_call(
        functools.partial(fused_kernel, shards, experts, capacity, expert_count, stride, names),
        out_shape=outs,
        in_specs=specs,
        out_specs=[vmem] * len(outs),
        scratch_shapes=list(scratch.values()),
        compiler_params=pltpu.CompilerParams(
            collective_id=1, has_side_effects=True, vmem_limit_bytes=BIG_VMEM
        ),
        name="front_and_experts",
    )(*inputs)


def expert_slow(
    tokens, gates, route_rows, tables, line_up, up_in, in_slice, out_slice, in_bias, own_bias
):
    row_count, width = tokens.shape
    bf16 = jnp.bfloat16
    table_0, table_1, send_table = tables
    router_pad = gates.shape[1]
    chosen = route_rows[:, :, None] == jnp.arange(router_pad, dtype=jnp.int32)[None, None, :]
    gate_pick = jnp.sum(jnp.where(chosen, gates[:, None, :], 0.0), axis=2)
    gate_high = gate_pick.astype(bf16)
    gate_low = (gate_pick - as_float(gate_high)).astype(bf16)
    gate_notes = jnp.concatenate([gate_high, gate_low], axis=1)
    gate_notes = jnp.pad(gate_notes, ((0, 0), (0, 128 - gate_notes.shape[1])))
    sent_line = jnp.concatenate([tokens, gate_notes], axis=1)
    row_line = lax.all_gather(sent_line, "shard", axis=0, tiled=True)
    line_in = row_line[:, :width]
    gate_line = as_float(row_line[:, width : width + 4])
    line_gate = gate_line[:, 0:2] + gate_line[:, 2:4]
    outgoing = contract_rows(send_table, line_in).astype(bf16)
    slot_gate = jnp.sum(
        jnp.where(table_0, line_gate[:, 0:1], 0.0) + jnp.where(table_1, line_gate[:, 1:2], 0.0),
        axis=0,
    )
    slot_high = slot_gate.astype(bf16)
    slot_low = (slot_gate - as_float(slot_high)).astype(bf16)
    slot_notes = jnp.pad(jnp.stack([slot_high, slot_low], axis=1), ((0, 0), (0, 126)))
    incoming = lax.all_to_all(
        jnp.concatenate([outgoing, slot_notes], axis=1),
        "expert",
        split_axis=0,
        concat_axis=0,
        tiled=True,
    )
    rows_in = incoming[:, :width]
    gate_in = as_float(incoming[:, width : width + 1]) + as_float(
        incoming[:, width + 1 : width + 2]
    )
    grad_in = (as_float(up_in) * gate_in).astype(bf16)
    pre_act = plain_dot(rows_in, in_slice) + in_bias
    gelu_out, gelu_slope = gelu_parts(pre_act)
    gelu_bf = gelu_out.astype(bf16)
    expert_out = (plain_dot(gelu_bf, out_slice) + own_bias).astype(bf16)
    returned = lax.all_to_all(expert_out, "expert", split_axis=0, concat_axis=0, tiled=True)
    pre_grad = contract_cols(grad_in, out_slice) * gelu_slope
    pre_bf = pre_grad.astype(bf16)
    back_rows = contract_cols(pre_bf, in_slice).astype(bf16)
    returned_grad = lax.all_to_all(back_rows, "expert", split_axis=0, concat_axis=0, tiled=True)
    out_0 = plain_dot(table_0.astype(bf16), returned)
    out_1 = plain_dot(table_1.astype(bf16), returned)
    combined = line_gate[:, 0:1] * out_0 + line_gate[:, 1:2] * out_1
    line_up_wide = as_float(line_up)
    gate_grad_line = jnp.stack(
        [jnp.sum(line_up_wide * out_0, axis=1), jnp.sum(line_up_wide * out_1, axis=1)], axis=1
    )
    joined = jnp.concatenate(
        [combined.astype(bf16), jnp.pad(gate_grad_line, ((0, 0), (0, 126))).astype(bf16)], axis=1
    )
    summed = as_float(lax.psum_scatter(joined, "shard", scatter_dimension=0, tiled=True))
    picked = jnp.sum(
        jnp.where(chosen, summed[:, width : width + 2][:, :, None], 0.0), axis=1
    )
    summed = jnp.concatenate([summed[:, :width], picked], axis=1)
    back_line = plain_dot(send_table, returned_grad)
    route_grad = lax.psum_scatter(back_line.astype(bf16), "shard", scatter_dimension=0, tiled=True)
    return (
        summed,
        route_grad,
        contract_rows(rows_in, pre_bf),
        contract_rows(gelu_bf, grad_in).astype(bf16),
        jnp.sum(pre_grad, axis=0)[None],
        jnp.sum(as_float(grad_in), axis=0)[None],
    )


def body(
    block_input,
    image_live,
    expert_routes,
    first_gain,
    first_shift,
    qkv_weight,
    query_value_bias,
    attn_out_weight,
    attn_out_bias,
    second_gain,
    second_shift,
    router_weight,
    expert_in_weight,
    expert_in_bias,
    expert_out_weight,
    expert_out_bias,
    output_grad,
):
    image_count, seq_length, width = block_input.shape
    shards = lax.axis_size("shard")
    experts = lax.axis_size("expert")
    chips = experts // 2
    expert_count = router_weight.shape[1]
    my_shard = lax.axis_index("shard")
    shard_rows = first_gain.shape[0]
    stride = round_up(seq_length, 8)
    row_count = image_count * stride
    capacity = (3 * image_count * seq_length + expert_count - 1) // expert_count
    group_rows = round_up(shards * capacity, 16)
    slot_rows = expert_count * group_rows
    bf16 = jnp.bfloat16
    fast = chips == 4 and shards == 4 and shard_rows % (16 * chips) == 0

    router_pad = round_up(expert_count, 128)
    extra_rows = round_up(VECTORS + expert_count, 16)
    extra_cols = round_up(shard_rows, 128)
    extra = jnp.pad(
        router_weight.T, ((0, extra_rows - expert_count), (0, extra_cols - shard_rows))
    )
    row_ids = lax.broadcasted_iota(jnp.int32, extra.shape, 0)
    for at, vector in enumerate(
        (
            first_gain,
            first_shift,
            attn_out_bias,
            second_gain,
            second_shift,
            query_value_bias[:shard_rows],
            query_value_bias[shard_rows:],
        )
    ):
        padded = jnp.pad(vector, (0, extra_cols - shard_rows))
        extra = jnp.where(row_ids == expert_count + at, padded[None, :], extra)
    turned_in = jnp.transpose(block_input, (1, 0, 2))
    turned_grad = jnp.transpose(output_grad, (1, 0, 2))
    in_slice = expert_in_weight[0]
    out_slice_t = expert_out_weight[0].T
    if fast:
        (
            qkv_full,
            proj_full,
            vectors,
            router_t,
            packed,
            mixed,
            residual,
            expert_in,
            gates,
            summed,
            route_grad,
            in_weight_grad,
            out_weight_grad,
            in_bias_sum,
            out_bias_sum,
        ) = fused_pass(
            shards,
            experts,
            capacity,
            expert_count,
            stride,
            (
                image_live,
                turned_in,
                turned_grad,
                jnp.transpose(expert_routes, (0, 2, 1)),
                qkv_weight,
                attn_out_weight,
                extra,
                in_slice,
                out_slice_t,
                expert_in_bias,
                expert_out_bias,
            ),
        )
        qkv_full = qkv_full.reshape(width, 3 * width)
        proj_full = proj_full.reshape(width, width)
    else:
        tail_rows = stride - seq_length
        live_rows = jnp.repeat(image_live, stride) * jnp.tile(
            (jnp.arange(stride) < seq_length).astype(jnp.int32), image_count
        )
        route_rows = jnp.pad(expert_routes, ((0, 0), (0, tail_rows), (0, 0))).reshape(row_count, 2)
        route_code, position = slot_places(route_rows, live_rows, expert_count)
        up_rows = (
            jnp.pad(output_grad, ((0, 0), (0, tail_rows), (0, 0))).reshape(row_count, width)
            * as_float(live_rows)[:, None]
        )
        own_bias = lax.dynamic_update_slice(
            jnp.zeros((1, width), jnp.float32),
            as_float(expert_out_bias),
            (0, my_shard * shard_rows),
        )
        in_bias = as_float(expert_in_bias)
        notes = jnp.concatenate([route_code.astype(bf16), position.astype(bf16)], axis=1)
        notes = jnp.pad(notes, ((0, 0), (0, 128 - notes.shape[1])))
        up_line = jnp.concatenate([up_rows.astype(bf16), notes], axis=1)
        qkv_all, proj_all, extra_all, line_all = (
            lax.all_gather(each, "shard", axis=0, tiled=False)
            for each in (qkv_weight, attn_out_weight, extra, up_line)
        )
        qkv_full = qkv_all.reshape(width, 3 * width)
        proj_full = proj_all.reshape(width, width)
        extra_t = jnp.transpose(extra_all[:, :, :shard_rows], (1, 0, 2))
        rows_t = extra_t[expert_count:]
        vectors = as_float(rows_t[:8]).reshape(8, width)
        query_value = as_float(rows_t[5:7])
        bias_full = jnp.transpose(query_value, (1, 0, 2)).reshape(2 * width)
        bias_row = jnp.concatenate(
            [bias_full[:width], jnp.zeros((width,), jnp.float32), bias_full[width:]]
        )
        bias_row = jnp.pad(bias_row[None], ((0, 7), (0, 0)))
        router_t = jnp.pad(
            extra_t[:expert_count].reshape(expert_count, width),
            ((0, router_pad - expert_count), (0, 0)),
        )
        line_rows = shards * row_count
        line = line_all.reshape(line_rows, width + 128)
        line_up = line[:, :width]
        line_notes = as_float(line[:, width : width + 4])
        line_ids = jnp.arange(line_rows, dtype=jnp.int32)[:, None]
        line_slot = (
            line_notes[:, 0:2].astype(jnp.int32) * group_rows
            + (line_ids // row_count) * capacity
            + line_notes[:, 2:4].astype(jnp.int32)
        )
        line_slot = jnp.where(line_notes[:, 0:2] >= 0, line_slot, -1)
        slot_ids = jnp.arange(slot_rows, dtype=jnp.int32)
        table_0 = line_slot[:, 0:1] == slot_ids[None, :]
        table_1 = line_slot[:, 1:2] == slot_ids[None, :]
        send_table = (table_0 | table_1).astype(bf16)
        up_out = contract_rows(send_table, line_up).astype(bf16)
        up_in = lax.all_to_all(up_out, "expert", split_axis=0, concat_axis=0, tiled=True)
        out_slice = lax.all_to_all(
            expert_out_weight[0], "shard", split_axis=0, concat_axis=1, tiled=True
        )
        packed, mixed, residual, expert_in, gates = pl.pallas_call(
            functools.partial(forward_kernel, stride, expert_count),
            out_shape=[
                jax.ShapeDtypeStruct((row_count, 3 * width), bf16),
                jax.ShapeDtypeStruct((row_count, width), bf16),
                jax.ShapeDtypeStruct((row_count, width), jnp.float32),
                jax.ShapeDtypeStruct((row_count, width), bf16),
                jax.ShapeDtypeStruct((row_count, router_pad), jnp.float32),
            ],
            in_specs=[pl.BlockSpec(memory_space=pltpu.VMEM)] * 6,
            out_specs=[pl.BlockSpec(memory_space=pltpu.VMEM)] * 5,
            scratch_shapes=[
                pltpu.VMEM((row_count, width), jnp.float32),
                pltpu.VMEM((row_count, width), bf16),
            ],
            compiler_params=pltpu.CompilerParams(vmem_limit_bytes=BIG_VMEM),
            name="attention_forward",
        )(turned_in, qkv_full, proj_full, vectors, bias_row, router_t)
        (
            summed,
            route_grad,
            in_weight_grad,
            out_weight_grad,
            in_bias_sum,
            out_bias_sum,
        ) = expert_slow(
            expert_in,
            gates,
            route_rows,
            (table_0, table_1, send_table),
            line_up,
            up_in,
            in_slice,
            out_slice,
            in_bias,
            own_bias,
        )
        out_weight_grad = out_weight_grad.T
    out_weight_grad = out_weight_grad.reshape(shards, shard_rows, -1)
    in_weight_part = in_weight_grad[None]
    in_bias_part = in_bias_sum[:1]
    out_bias_part = lax.dynamic_slice_in_dim(
        out_bias_sum[0], my_shard * shard_rows, shard_rows
    )[None]

    smem = pl.BlockSpec(memory_space=pltpu.SMEM)
    vmem = pl.BlockSpec(memory_space=pltpu.VMEM)
    wide_rows = pltpu.VMEM((row_count, width), jnp.float32)
    block_output, input_grad, weight_grads, extra_grads = pl.pallas_call(
        functools.partial(backward_kernel, stride),
        out_shape=[
            jax.ShapeDtypeStruct(turned_in.shape, jnp.float32),
            jax.ShapeDtypeStruct(turned_in.shape, jnp.float32),
            jax.ShapeDtypeStruct((2, width, 2 * width), bf16),
            jax.ShapeDtypeStruct((extra_rows, width), jnp.float32),
        ],
        in_specs=[smem] + [vmem] * 13,
        out_specs=[vmem] * 4,
        scratch_shapes=[
            wide_rows,
            wide_rows,
            pltpu.VMEM((width, row_count), bf16),
            pltpu.VMEM((row_count, width), bf16),
            pltpu.VMEM((row_count, 3 * width), bf16),
            wide_rows,
        ],
        compiler_params=pltpu.CompilerParams(vmem_limit_bytes=BIG_VMEM),
        cost_estimate=pl.CostEstimate(
            flops=32 * row_count * width * width,
            bytes_accessed=48 * width * width,
            transcendentals=2 * HEADS * row_count * row_count,
        ),
        name="attention_backward",
    )(
        image_live,
        turned_in,
        turned_grad,
        packed,
        mixed,
        residual,
        expert_in,
        gates,
        summed,
        route_grad,
        qkv_full,
        proj_full,
        vectors,
        router_t,
    )
    qkv_sum, proj_sum, extra_sum, out_weight_blocks = reduce_grads(
        fast, shards, chips, weight_grads, extra_grads.astype(bf16), out_weight_grad
    )
    out_weight_part = (
        jnp.transpose(as_float(out_weight_blocks), (0, 2, 1)).reshape(-1, shard_rows)[None]
    )

    def own(array_in, size, axis=0):
        return lax.dynamic_slice_in_dim(array_in, my_shard * size, size, axis=axis)

    mine = own(extra_sum, shard_rows, axis=1)
    return (
        jnp.transpose(block_output, (1, 0, 2)),
        jnp.transpose(input_grad, (1, 0, 2)),
        mine[0],
        mine[1],
        qkv_sum,
        own(extra_sum[5:7].reshape(2 * width), 2 * shard_rows),
        proj_sum,
        mine[2],
        mine[3],
        mine[4],
        mine[VECTORS : VECTORS + expert_count].T,
        in_weight_part,
        in_bias_part,
        out_weight_part,
        out_bias_part,
    )


def solution(mesh):
    in_specs = (
        P(("expert", "shard"), None, None),
        P(("expert", "shard")),
        P(("expert", "shard"), None, None),
        P("shard"),
        P("shard"),
        P("shard", None),
        P("shard"),
        P("shard", None),
        P("shard"),
        P("shard"),
        P("shard"),
        P("shard", None),
        P("expert", None, "shard"),
        P("expert", "shard"),
        P("expert", None, "shard"),
        P("expert", "shard"),
        P(("expert", "shard"), None, None),
    )
    out_specs = (
        P(("expert", "shard"), None, None),
        P(("expert", "shard"), None, None),
        P("shard"),
        P("shard"),
        P("shard", None),
        P("shard"),
        P("shard", None),
        P("shard"),
        P("shard"),
        P("shard"),
        P("shard", None),
        P("expert", None, "shard"),
        P("expert", "shard"),
        P("expert", None, "shard"),
        P("expert", "shard"),
    )
    return jax.shard_map(body, mesh=mesh, in_specs=in_specs, out_specs=out_specs, check_vma=False)
```

```python
import functools
import math
import types

import jax
import jax.numpy as jnp
from jax import lax
from jax.experimental import pallas as pl
from jax.experimental.pallas import tpu as pltpu
from jax.sharding import PartitionSpec as P

HEADS = 12
HEAD_DIM = 64


EPSILON = 1e-06
PRECISE = lax.Precision.HIGHEST
HALF_ROOT = 0.7071067811865476
DENSITY = 0.3989422804014327


def as_float(array_in):
    return array_in.astype(jnp.float32)


def contract_rows(left_side, right_side):
    return lax.dot_general(
        left_side, right_side, (((0,), (0,)), ((), ())), preferred_element_type=jnp.float32
    )


def contract_cols(left_side, right_side):
    return lax.dot_general(
        left_side, right_side, (((1,), (1,)), ((), ())), preferred_element_type=jnp.float32
    )


def precise_rows(left_side, right_side):
    return lax.dot_general(
        left_side,
        right_side,
        (((0,), (0,)), ((), ())),
        precision=PRECISE,
        preferred_element_type=jnp.float32,
    )


def precise_cols(left_side, right_side):
    return lax.dot_general(
        left_side,
        right_side,
        (((1,), (1,)), ((), ())),
        precision=PRECISE,
        preferred_element_type=jnp.float32,
    )


def layer_norm(values_in, gain_vec, shift_vec):
    center = values_in - jnp.mean(values_in, axis=-1, keepdims=True)
    inv_std = lax.rsqrt(jnp.mean(center * center, axis=-1, keepdims=True) + EPSILON)
    normed = center * inv_std
    return (normed * as_float(gain_vec) + as_float(shift_vec), normed, inv_std)


def norm_back(upstream, normed, inv_std, gain_vec):
    scaled = upstream * as_float(gain_vec)
    return inv_std * (
        scaled
        - jnp.mean(scaled, axis=-1, keepdims=True)
        - normed * jnp.mean(scaled * normed, axis=-1, keepdims=True)
    )


def gelu_parts(pre_act):
    normal_cdf = 0.5 * (1.0 + jax.scipy.special.erf(pre_act * HALF_ROOT))
    return (
        pre_act * normal_cdf,
        normal_cdf + pre_act * DENSITY * jnp.exp(-0.5 * pre_act * pre_act),
    )


BIG_VMEM = 56 * 1024 * 1024
VECTORS = 7


def plain_dot(left_side, right_side):
    return jnp.dot(left_side, right_side, preferred_element_type=jnp.float32)


def exact_dot(left_side, right_side):
    return lax.dot_general(
        left_side,
        right_side,
        (((1,), (0,)), ((), ())),
        precision=PRECISE,
        preferred_element_type=jnp.float32,
    )


def round_up(value, step):
    return -(-value // step) * step


def slot_places(route_rows, live_rows, expert_count):
    row_count = route_rows.shape[0]
    flat_routes = route_rows.reshape(2 * row_count)
    alive_pairs = jnp.repeat(live_rows, 2)
    chosen = (flat_routes[:, None] == jnp.arange(expert_count, dtype=jnp.int32)[None, :]).astype(
        jnp.int32
    )
    live_hits = chosen * alive_pairs[:, None]
    earlier = (
        jnp.arange(2 * row_count, dtype=jnp.int32)[:, None]
        > jnp.arange(2 * row_count, dtype=jnp.int32)[None, :]
    ).astype(jnp.bfloat16)
    counted = jnp.dot(earlier, live_hits.astype(jnp.bfloat16), preferred_element_type=jnp.float32)
    position = jnp.sum(counted * as_float(live_hits), axis=1)
    route_code = jnp.where(alive_pairs > 0, flat_routes, -1).astype(jnp.float32)
    return route_code.reshape(row_count, 2), position.reshape(row_count, 2)


class Place:
    def __init__(self, shards, chips):
        self.shards = shards
        self.chips = chips
        self.expert = lax.axis_index("expert")
        self.shard = lax.axis_index("shard")
        self.core = lax.rem(self.expert, 2)
        self.chip = lax.div(self.expert, 2)

    def along(self, step):
        return {
            "expert": self.expert,
            "shard": lax.rem(self.shard + step + self.shards, self.shards),
        }

    def peer(self, step):
        other = lax.rem(self.chip + step + self.chips, self.chips)
        return {"expert": other * 2 + self.core, "shard": self.shard}

    def sibling(self):
        return {"expert": self.chip * 2 + 1 - self.core, "shard": self.shard}

    def plane(self, step):
        count = 2 * self.chips
        return {"expert": lax.rem(self.expert + step, count), "shard": self.shard}

    def greet(self, others):
        barrier = pltpu.get_barrier_semaphore()
        for other in others:
            pl.semaphore_signal(
                barrier, inc=1, device_id=other, device_id_type=pl.DeviceIdType.MESH
            )
        pl.semaphore_wait(barrier, len(others))


def remote(src, dst, send_sem, recv_sem, device):
    return pltpu.make_async_remote_copy(
        src_ref=src,
        dst_ref=dst,
        send_sem=send_sem,
        recv_sem=recv_sem,
        device_id=device,
        device_id_type=pl.DeviceIdType.MESH,
    )


def norm_stats(values_in):
    center = values_in - jnp.mean(values_in, axis=-1, keepdims=True)
    inv_std = lax.rsqrt(jnp.mean(center * center, axis=-1, keepdims=True) + EPSILON)
    return center * inv_std, inv_std


def spread_rows(dst, src, image_count, seq_length, stride):
    dst[...] = jnp.zeros_like(dst)
    for image in range(image_count):
        dst[image * stride : image * stride + seq_length, :] = src[:, image, :]


def same_image(rows, stride, seq_length):
    row_at = lax.broadcasted_iota(jnp.int32, (rows, rows), 0)
    col_at = lax.broadcasted_iota(jnp.int32, (rows, rows), 1)
    mask = None
    for image in range(rows // stride):
        low = image * stride
        part = (
            (row_at >= low)
            & (row_at < low + stride)
            & (col_at >= low)
            & (col_at < low + seq_length)
        )
        mask = part if mask is None else mask | part
    return mask


def masked_softmax(query_half, keys, mask):
    scores = contract_cols(query_half, keys) * (1.0 / math.sqrt(HEAD_DIM))
    scores = jnp.where(mask, scores, -1e30)
    row_max = jnp.max(scores, axis=-1, keepdims=True)
    log_total = row_max + jnp.log(jnp.sum(jnp.exp(scores - row_max), axis=-1, keepdims=True))
    return jnp.exp(scores - log_total)


def forward_kernel(
    stride,
    expert_count,
    x_ref,
    qkv_ref,
    proj_ref,
    vec_ref,
    bias_ref,
    router_ref,
    packed_ref,
    mixed_ref,
    residual_ref,
    line_ref,
    gates_ref,
    flat_ref,
    attn_ref,
):
    seq_length, image_count, width = x_ref.shape
    rows = flat_ref.shape[0]
    bf16 = jnp.bfloat16
    spread_rows(flat_ref, x_ref, image_count, seq_length, stride)
    normed, _ = norm_stats(flat_ref[...])
    attn_ref[...] = (normed * vec_ref[0:1, :] + vec_ref[1:2, :]).astype(bf16)

    def project(tile, carry):
        cols = pl.ds(pl.multiple_of(tile * width, 128), width)
        packed_ref[:, cols] = (
            plain_dot(attn_ref[...], qkv_ref[:, cols]) + bias_ref[0:1, cols]
        ).astype(bf16)
        return carry

    lax.fori_loop(0, 3, project, 0)
    mask = same_image(rows, stride, seq_length)
    low_lanes = lax.broadcasted_iota(jnp.int32, (rows, 128), 1) < HEAD_DIM

    def attend(pair, carry):
        def part(which):
            return packed_ref[:, pl.ds(pl.multiple_of(which * width + pair * 128, 128), 128)]

        query, key, value = part(0), part(1), part(2)
        zero = jnp.zeros_like(query)
        weights_low = masked_softmax(jnp.where(low_lanes, query, zero), key, mask).astype(bf16)
        weights_high = masked_softmax(jnp.where(low_lanes, zero, query), key, mask).astype(bf16)
        mixed_ref[:, pl.ds(pl.multiple_of(pair * 128, 128), 128)] = jnp.where(
            low_lanes, plain_dot(weights_low, value), plain_dot(weights_high, value)
        ).astype(bf16)
        return carry

    lax.fori_loop(0, HEADS // 2, attend, 0)
    residual = flat_ref[...] + plain_dot(mixed_ref[...], proj_ref[...]) + vec_ref[2:3, :]
    residual_ref[...] = residual
    normed_two, _ = norm_stats(residual)
    expert_in = (normed_two * vec_ref[3:4, :] + vec_ref[4:5, :]).astype(bf16)
    line_ref[...] = expert_in
    logits = contract_cols(expert_in, router_ref[...])
    lanes = lax.broadcasted_iota(jnp.int32, logits.shape, 1)
    logits = jnp.where(lanes < expert_count, logits, -1e30)
    shifted = jnp.exp(logits - jnp.max(logits, axis=-1, keepdims=True))
    gates_ref[...] = shifted / jnp.sum(shifted, axis=-1, keepdims=True)


def backward_kernel(
    stride,
    live_ref,
    x_ref,
    up_ref,
    packed_ref,
    mixed_ref,
    residual_ref,
    expert_ref,
    gates_ref,
    summed_ref,
    back_ref,
    qkv_ref,
    proj_ref,
    vec_ref,
    router_ref,
    block_ref,
    grad_ref,
    weight_ref,
    extra_ref,
    flat_ref,
    upstream_ref,
    attn_t_ref,
    mixed_grad_ref,
    packed_grad_ref,
    res_grad_ref,
):
    seq_length, image_count, width = x_ref.shape
    rows = flat_ref.shape[0]
    bf16 = jnp.bfloat16
    half = 3 * width // 2
    spread_rows(flat_ref, x_ref, image_count, seq_length, stride)
    upstream_ref[...] = jnp.zeros_like(upstream_ref)
    residual = residual_ref[...]
    block = residual + as_float(summed_ref[:, :width])
    for image in range(image_count):
        live = live_ref[image].astype(jnp.float32)
        here = slice(image * stride, image * stride + seq_length)
        upstream_ref[here, :] = up_ref[:, image, :] * live
        block_ref[:, image, :] = block[here, :]

    gates = gates_ref[...]
    picked = as_float(summed_ref[:, width:])
    logit_grad = gates * (picked - jnp.sum(gates * picked, axis=-1, keepdims=True))
    router_rows = extra_ref.shape[0] - VECTORS
    extra_ref[VECTORS:, :] = precise_rows(logit_grad, as_float(expert_ref[...]))[
        :router_rows
    ]
    normed_two_grad = as_float(back_ref[...]) + exact_dot(
        logit_grad, as_float(router_ref[...])
    )
    normed_two, inv_two = norm_stats(residual)
    extra_ref[3:4, :] = jnp.sum(normed_two_grad * normed_two, axis=0, keepdims=True)
    extra_ref[4:5, :] = jnp.sum(normed_two_grad, axis=0, keepdims=True)
    residual_grad = upstream_ref[...] + norm_back(
        normed_two_grad, normed_two, inv_two, vec_ref[3:4, :]
    )
    res_grad_ref[...] = residual_grad
    extra_ref[2:3, :] = jnp.sum(residual_grad, axis=0, keepdims=True)
    residual_bf = residual_grad.astype(bf16)
    proj_grad = contract_rows(mixed_ref[...], residual_bf)
    for core in range(2):
        weight_ref[core, :, half:] = proj_grad[
            :, core * (width // 2) : (core + 1) * (width // 2)
        ].astype(bf16)
    mixed_grad_ref[...] = contract_cols(residual_bf, proj_ref[...]).astype(bf16)

    mask = same_image(rows, stride, seq_length)
    low_lanes = lax.broadcasted_iota(jnp.int32, (rows, 128), 1) < HEAD_DIM

    def attend(pair, carry):
        def part(which):
            return pl.ds(pl.multiple_of(which * width + pair * 128, 128), 128)

        query, key, value = (packed_ref[:, part(which)] for which in range(3))
        mixed_grad = mixed_grad_ref[:, part(0)]
        zero = jnp.zeros_like(query)
        totals = [0.0, 0.0, 0.0]
        for high in range(2):

            def only(array_in):
                return jnp.where(low_lanes, zero if high else array_in, array_in if high else zero)

            query_half, mixed_half = only(query), only(mixed_grad)
            probs = masked_softmax(query_half, key, mask)
            prob_grad = contract_cols(mixed_half, value)
            score_grad = (
                probs
                * (prob_grad - jnp.sum(probs * prob_grad, axis=-1, keepdims=True))
                * (1.0 / math.sqrt(HEAD_DIM))
            ).astype(bf16)
            totals[0] += plain_dot(score_grad, only(key))
            totals[1] += contract_rows(score_grad, query_half)
            totals[2] += contract_rows(probs.astype(bf16), mixed_half)
        for which in range(3):
            packed_grad_ref[:, part(which)] = totals[which].astype(bf16)
        extra_ref[5:6, part(0)] = jnp.sum(totals[0], axis=0, keepdims=True)
        extra_ref[6:7, part(0)] = jnp.sum(totals[2], axis=0, keepdims=True)
        return carry

    lax.fori_loop(0, HEADS // 2, attend, 0)

    normed_one, inv_one = norm_stats(flat_ref[...])
    attn_in = normed_one * vec_ref[0:1, :] + vec_ref[1:2, :]
    attn_t_ref[...] = attn_in.T.astype(bf16)
    tile = half // 3

    def weigh(at, carry):
        src = pl.ds(pl.multiple_of(at * tile, 128), tile)
        dst = pl.ds(pl.multiple_of(lax.rem(at, 3) * tile, 128), tile)
        weight_ref[lax.div(at, 3), :, dst] = plain_dot(
            attn_t_ref[...], packed_grad_ref[:, src]
        ).astype(bf16)
        return carry

    lax.fori_loop(0, 6, weigh, 0)
    upstream_ref[...] = jnp.zeros_like(upstream_ref)

    def push_back(at, carry):
        cols = pl.ds(pl.multiple_of(at * width, 128), width)
        upstream_ref[...] += contract_cols(packed_grad_ref[:, cols], qkv_ref[:, cols])
        return carry

    lax.fori_loop(0, 3, push_back, 0)
    normed_one_grad = upstream_ref[...]
    extra_ref[0:1, :] = jnp.sum(normed_one_grad * normed_one, axis=0, keepdims=True)
    extra_ref[1:2, :] = jnp.sum(normed_one_grad, axis=0, keepdims=True)
    input_grad = res_grad_ref[...] + norm_back(
        normed_one_grad, normed_one, inv_one, vec_ref[0:1, :]
    )
    for image in range(image_count):
        grad_ref[:, image, :] = input_grad[image * stride : image * stride + seq_length, :]


def backward_reduce_kernel(shards, chips, stride, names, *refs):
    r = types.SimpleNamespace(**dict(zip(names, refs)))
    place = Place(shards, chips)
    bf16 = jnp.bfloat16
    core, chip, shard = place.core, place.chip, place.shard
    count = 2 * chips
    seq_length, image_count, width = r.x.shape
    rows = r.flat.shape[0]
    side = width // 2
    groups = 4
    piece = r.whole.shape[3]
    shard_rows = width // shards
    place.greet(
        [place.along(j) for j in range(1, shards)]
        + [place.plane(i) for i in range(1, count)]
    )
    order = (1, 3, 2)
    sent = []

    def send(copy):
        copy.start()
        sent.append(copy)

    def block_copy(j):
        cols = pl.ds(pl.multiple_of(shard * width, 128), width)
        return remote(
            r.blocks.at[lax.rem(shard + j, shards)],
            r.blocks_out.at[:, cols],
            r.block_s.at[j],
            r.block_r.at[j],
            place.along(j),
        )

    for j in order:
        send(block_copy(j))
    block_local = pltpu.make_async_copy(
        r.blocks.at[shard],
        r.blocks_out.at[:, pl.ds(pl.multiple_of(shard * width, 128), width)],
        r.here.at[0],
    )
    block_local.start()

    def twin_copy(g):
        return remote(
            r.weights.at[g, 1 - core],
            r.twin_in.at[g],
            r.twin_s.at[g],
            r.twin_r.at[g],
            place.sibling(),
        )

    def peer_copy(g, i):
        return remote(
            r.plane_sum.at[g, :, lax.rem(chip + i, chips)],
            r.peer_in.at[g, i],
            r.peer_s.at[g, i],
            r.peer_r.at[g, i],
            place.peer(i),
        )

    def far_copy(g, j):
        return remote(
            r.far_out.at[g, lax.rem(shard + j, shards)],
            r.far_in.at[g, j],
            r.far_s.at[g, j],
            r.far_r.at[g, j],
            place.along(j),
        )

    def back_copy(g, i):
        block = r.whole.at[g, core, chip]
        return remote(block, block, r.back_s.at[g, i], r.back_r.at[g, i], place.peer(i))

    def last_copy(g, i):
        block = r.whole.at[g, core, lax.rem(chip - i + chips, chips)]
        return remote(block, block, r.last_s.at[g, i], r.last_r.at[g, i], place.sibling())

    def small_copy(i):
        return remote(
            r.small, r.small_in.at[i], r.small_s.at[i], r.small_r.at[i], place.plane(i)
        )

    def edge_copy(j):
        return remote(
            r.small_sum, r.small_far.at[j], r.edge_s.at[j], r.edge_r.at[j], place.along(j)
        )

    def store_group(g, half, value):
        r.weights[g, half] = value.astype(bf16).reshape(shards, chips, piece, side)

    def to_plane(g):
        twin_copy(g).wait_recv()
        for at in range(shards):
            r.plane_sum[g, at] = (
                as_float(r.weights[g, core, at]) + as_float(r.twin_in[g, at])
            ).astype(bf16)
        for i in range(1, chips):
            send(peer_copy(g, i))

    def to_far(g):
        mine = as_float(r.plane_sum[g, :, chip])
        for i in range(1, chips):
            peer_copy(g, i).wait_recv()
            mine += as_float(r.peer_in[g, i])
        r.far_out[g] = mine.astype(bf16)
        for j in order:
            send(far_copy(g, j))

    def to_back(g):
        mine = as_float(r.far_out[g, shard])
        for j in order:
            far_copy(g, j).wait_recv()
            mine += as_float(r.far_in[g, j])
        r.whole[g, core, chip] = mine.astype(bf16)
        for i in range(1, chips):
            send(back_copy(g, i))
        send(last_copy(g, 0))

    spread_rows(r.flat, r.grad, image_count, seq_length, stride)
    residual = r.residual[...]
    block = residual + r.summed[:, :width]
    for image in range(image_count):
        alive = r.live[image].astype(jnp.float32)
        here = slice(image * stride, image * stride + seq_length)
        r.upstream[image * stride : (image + 1) * stride, :] = (
            r.flat[image * stride : (image + 1) * stride, :] * alive
        )
        r.block_out[:, image, :] = block[here, :]
    gates = r.gates[...]
    picked = r.summed[:, width:]
    logit_grad = gates * (picked - jnp.sum(gates * picked, axis=-1, keepdims=True))
    normed_two_grad = r.route[...] + exact_dot(logit_grad, as_float(r.router[...]))
    normed_two, inv_two = norm_stats(residual)
    residual_grad = r.upstream[...] + norm_back(
        normed_two_grad, normed_two, inv_two, r.vectors[3:4, :]
    )
    r.res_grad[...] = residual_grad
    residual_bf = residual_grad.astype(bf16)
    proj_grad = contract_rows(r.mixed[...], residual_bf)
    for half in range(2):
        store_group(0, half, proj_grad[:, half * side : (half + 1) * side])
    send(twin_copy(0))
    r.mixed_grad[...] = contract_cols(residual_bf, r.proj[...]).astype(bf16)
    router_rows = r.totals.shape[0] - VECTORS
    r.totals[VECTORS:, :] = precise_rows(logit_grad, as_float(r.tokens[...]))[:router_rows]
    r.totals[2:3, :] = jnp.sum(residual_grad, axis=0, keepdims=True)
    r.totals[3:4, :] = jnp.sum(normed_two_grad * normed_two, axis=0, keepdims=True)
    r.totals[4:5, :] = jnp.sum(normed_two_grad, axis=0, keepdims=True)
    spread_rows(r.flat, r.x, image_count, seq_length, stride)
    normed_one, inv_one = norm_stats(r.flat[...])
    attn_in = normed_one * r.vectors[0:1, :] + r.vectors[1:2, :]
    r.attn_t[...] = attn_in.T.astype(bf16)
    r.flat[...] = normed_one

    mask = same_image(rows, stride, seq_length)
    low_lanes = lax.broadcasted_iota(jnp.int32, (rows, 128), 1) < HEAD_DIM

    def attend(pair, carry):
        def part(which):
            return pl.ds(pl.multiple_of(which * width + pair * 128, 128), 128)

        query, key, value = (r.packed[:, part(which)] for which in range(3))
        mixed_grad = r.mixed_grad[:, part(0)]
        zero = jnp.zeros_like(query)
        totals = [0.0, 0.0, 0.0]
        for high in range(2):

            def only(array_in):
                return jnp.where(low_lanes, zero if high else array_in, array_in if high else zero)

            query_half, mixed_half = only(query), only(mixed_grad)
            probs = masked_softmax(query_half, key, mask)
            prob_grad = contract_cols(mixed_half, value)
            score_grad = (
                probs
                * (prob_grad - jnp.sum(probs * prob_grad, axis=-1, keepdims=True))
                * (1.0 / math.sqrt(HEAD_DIM))
            ).astype(bf16)
            totals[0] += plain_dot(score_grad, only(key))
            totals[1] += contract_rows(score_grad, query_half)
            totals[2] += contract_rows(probs.astype(bf16), mixed_half)
        for which in range(3):
            r.packed_grad[:, part(which)] = totals[which].astype(bf16)
        r.totals[5:6, part(0)] = jnp.sum(totals[0], axis=0, keepdims=True)
        r.totals[6:7, part(0)] = jnp.sum(totals[2], axis=0, keepdims=True)
        return carry

    pairs = width // 128
    lax.fori_loop(0, pairs // 2, attend, 0)
    to_plane(0)
    lax.fori_loop(pairs // 2, pairs, attend, 0)
    for g in range(1, groups):
        for half in (1 - core, core):
            cols = pl.ds(pl.multiple_of((g - 1) * width + half * side, 128), side)
            store_group(g, half, plain_dot(r.attn_t[...], r.packed_grad[:, cols]))
            if half is not core:
                send(twin_copy(g))
        if g > 1:
            to_plane(g - 1)
    to_plane(groups - 1)

    r.upstream[...] = jnp.zeros_like(r.upstream)

    def push_back(at, carry):
        cols = pl.ds(pl.multiple_of(at * width, 128), width)
        r.upstream[...] += contract_cols(r.packed_grad[:, cols], r.qkv[:, cols])
        return carry

    lax.fori_loop(0, 3, push_back, 0)
    normed_one_grad = r.upstream[...]
    normed_one = r.flat[...]
    r.totals[0:1, :] = jnp.sum(normed_one_grad * normed_one, axis=0, keepdims=True)
    r.totals[1:2, :] = jnp.sum(normed_one_grad, axis=0, keepdims=True)
    r.small[...] = r.totals[...].astype(bf16)
    for i in range(1, count):
        send(small_copy(i))
    to_far(0)
    input_grad = r.res_grad[...] + norm_back(
        normed_one_grad, normed_one, inv_one, r.vectors[0:1, :]
    )
    for image in range(image_count):
        r.grad_out[:, image, :] = input_grad[image * stride : image * stride + seq_length, :]
    to_far(1)
    to_back(0)
    total = as_float(r.small[...])
    for i in range(1, count):
        small_copy(i).wait_recv()
        total += as_float(r.small_in[i])
    r.small_sum[...] = total.astype(bf16)
    for j in order:
        send(edge_copy(j))
    to_far(2)
    to_back(1)
    to_far(3)
    to_back(2)
    total = as_float(r.small_sum[...])
    for j in order:
        edge_copy(j).wait_recv()
        total += as_float(r.small_far[j])

    def cut(values, start, size):
        lane_from = lax.broadcasted_iota(jnp.int32, (width, size), 0)
        lane_to = lax.broadcasted_iota(jnp.int32, (width, size), 1)
        return exact_dot(values, jnp.where(lane_from == lane_to + start, 1.0, 0.0))

    r.small_out[...] = cut(total, shard * shard_rows, r.small_out.shape[1])
    low = jnp.broadcast_to(total[5:6], (8, width))
    high = jnp.broadcast_to(total[6:7], (8, width))
    which = jnp.where(lax.div(shard, shards // 2) == 0, low, high)
    r.bias_out[...] = cut(which, lax.rem(shard, shards // 2) * side, side)

    def forward_last(g):
        for i in range(1, chips):
            back_copy(g, i).wait_recv()
            send(last_copy(g, i))

    for g in range(groups - 1):
        forward_last(g)
    to_back(groups - 1)
    forward_last(groups - 1)
    for g in range(groups):
        for i in range(chips):
            last_copy(g, i).wait_recv()
        for half in range(2):
            for at in range(chips):
                here = slice(at * piece, (at + 1) * piece)
                cols = slice(half * side, (half + 1) * side)
                if g == 0:
                    r.proj_out[here, cols] = r.whole[g, half, at]
                else:
                    start = (g - 1) * width + half * side
                    r.qkv_out[here, start : start + side] = r.whole[g, half, at]
    block_local.wait()
    for j in order:
        block_copy(j).wait_recv()
    for copy in sent:
        copy.wait_send()


def backward_reduce(shards, chips, stride, inputs):
    x, packed, blocks = inputs[1], inputs[3], inputs[14]
    rows, width = packed.shape[0], x.shape[2]
    shard_rows = width // shards
    piece = shard_rows // chips
    side = width // 2
    expert_count = 2 * chips
    small_rows = round_up(VECTORS + expert_count, 16)
    bf16, f32, dma = jnp.bfloat16, jnp.float32, pltpu.SemaphoreType.DMA
    vmem, anywhere = pl.BlockSpec(memory_space=pltpu.VMEM), pl.BlockSpec(memory_space=pl.ANY)

    def shape(dims, kind=bf16):
        return jax.ShapeDtypeStruct(dims, kind)

    smem = pl.BlockSpec(memory_space=pltpu.SMEM)
    ins = dict(
        live=smem,
        x=vmem,
        grad=vmem,
        packed=vmem,
        mixed=vmem,
        residual=vmem,
        tokens=vmem,
        gates=vmem,
        summed=vmem,
        route=vmem,
        qkv=vmem,
        proj=vmem,
        vectors=vmem,
        router=vmem,
        blocks=anywhere,
    )
    outs = dict(
        block_out=shape(x.shape, f32),
        grad_out=shape(x.shape, f32),
        qkv_out=shape((shard_rows, 3 * width)),
        proj_out=shape((shard_rows, width)),
        small_out=shape((small_rows, round_up(shard_rows, 128)), f32),
        bias_out=shape((8, side), f32),
        blocks_out=shape((shard_rows, shards * width)),
    )
    scratch = dict(
        flat=pltpu.VMEM((rows, width), f32),
        upstream=pltpu.VMEM((rows, width), f32),
        res_grad=pltpu.VMEM((rows, width), f32),
        attn_t=pltpu.VMEM((width, rows), bf16),
        mixed_grad=pltpu.VMEM((rows, width), bf16),
        packed_grad=pltpu.VMEM((rows, 3 * width), bf16),
        totals=pltpu.VMEM((small_rows, width), f32),
        weights=pltpu.VMEM((4, 2, shards, chips, piece, side), bf16),
        twin_in=pltpu.VMEM((4, shards, chips, piece, side), bf16),
        plane_sum=pltpu.VMEM((4, shards, chips, piece, side), bf16),
        peer_in=pltpu.VMEM((4, chips, shards, piece, side), bf16),
        far_out=pltpu.VMEM((4, shards, piece, side), bf16),
        far_in=pltpu.VMEM((4, shards, piece, side), bf16),
        whole=pltpu.VMEM((4, 2, chips, piece, side), bf16),
        small=pltpu.VMEM((small_rows, width), bf16),
        small_in=pltpu.VMEM((2 * chips, small_rows, width), bf16),
        small_sum=pltpu.VMEM((small_rows, width), bf16),
        small_far=pltpu.VMEM((shards, small_rows, width), bf16),
        here=dma((1,)),
    )
    pairs = dict(
        block=(shards,),
        twin=(4,),
        peer=(4, chips),
        far=(4, shards),
        back=(4, chips),
        last=(4, chips),
        small=(2 * chips,),
        edge=(shards,),
    )
    for name, dims in pairs.items():
        scratch[name + "_s"] = dma(dims)
        scratch[name + "_r"] = dma(dims)
    names = tuple(ins) + tuple(outs) + tuple(scratch)
    return pl.pallas_call(
        functools.partial(backward_reduce_kernel, shards, chips, stride, names),
        out_shape=list(outs.values()),
        in_specs=list(ins.values()),
        out_specs=[vmem] * 6 + [anywhere],
        scratch_shapes=list(scratch.values()),
        compiler_params=pltpu.CompilerParams(
            collective_id=2, has_side_effects=True, vmem_limit_bytes=BIG_VMEM
        ),
        name="backward_and_reduce",
    )(*inputs)


def reduce_slow(grads, extra, blocks):
    width = grads.shape[2] // 2
    wide = 3 * width // 2
    joined = jnp.concatenate(
        [grads[0, :, :wide], grads[1, :, :wide], grads[0, :, wide:], grads[1, :, wide:]],
        axis=1,
    )
    mine = lax.psum_scatter(joined, "shard", scatter_dimension=0, tiled=True)
    mine = as_float(lax.psum(mine, "expert"))
    extra_sum = as_float(lax.psum(extra, ("shard", "expert")))
    moved = lax.all_to_all(blocks, "shard", split_axis=0, concat_axis=0, tiled=True)
    return mine[:, : 3 * width], mine[:, 3 * width :], extra_sum, moved


def attention_core(stride, expert_count, r):
    rows, width = r.flat.shape
    bf16 = jnp.bfloat16
    mask = same_image(rows, stride, r.x.shape[0])
    low_lanes = lax.broadcasted_iota(jnp.int32, (rows, 128), 1) < HEAD_DIM

    def attend(pair, carry):
        def part(which):
            return r.packed[:, pl.ds(pl.multiple_of(which * width + pair * 128, 128), 128)]

        query, key, value = part(0), part(1), part(2)
        zero = jnp.zeros_like(query)
        weights_low = masked_softmax(jnp.where(low_lanes, query, zero), key, mask).astype(bf16)
        weights_high = masked_softmax(jnp.where(low_lanes, zero, query), key, mask).astype(bf16)
        r.mixed[:, pl.ds(pl.multiple_of(pair * 128, 128), 128)] = jnp.where(
            low_lanes, plain_dot(weights_low, value), plain_dot(weights_high, value)
        ).astype(bf16)
        return carry

    lax.fori_loop(0, HEADS // 2, attend, 0)


def route_core(expert_count, r, proj):
    bf16 = jnp.bfloat16
    residual = r.flat[...] + plain_dot(r.mixed[...], proj) + r.vectors[2:3, :]
    r.residual[...] = residual
    normed_two, _ = norm_stats(residual)
    expert_in = (normed_two * r.vectors[3:4, :] + r.vectors[4:5, :]).astype(bf16)
    r.tokens[...] = expert_in
    r.gates[...] = softmax_gates(expert_in, r.router[...], expert_count)


def softmax_gates(rows, router, expert_count):
    logits = contract_cols(rows, router)
    lanes = lax.broadcasted_iota(jnp.int32, logits.shape, 1)
    logits = jnp.where(lanes < expert_count, logits, -1e30)
    shifted = jnp.exp(logits - jnp.max(logits, axis=-1, keepdims=True))
    return shifted / jnp.sum(shifted, axis=-1, keepdims=True)


def fused_kernel(shards, experts, capacity, expert_count, stride, names, *refs):
    r = types.SimpleNamespace(**dict(zip(names, refs)))
    chips = experts // 2
    place = Place(shards, chips)
    bf16 = jnp.bfloat16
    me, shard = place.expert, place.shard
    row_count, width = r.tokens.shape
    group_rows = r.rows_in.shape[1]
    shard_rows = r.qkv.shape[0]
    seq_length, image_count = r.x.shape[:2]
    first_rows = 2 * capacity // 16 * 16
    second_rows = group_rows - first_rows
    upper = lax.div(shard, 2)
    even = lax.rem(shard, 2) == 0
    place.greet(
        [place.along(j) for j in range(1, shards)]
        + [place.plane(i) for i in range(1, experts)]
    )
    order = (1, 3, 2)
    spans = (
        (upper * second_rows, first_rows),
        ((1 - upper) * first_rows, second_rows),
    )

    def with_pair(act):
        @pl.when(even)
        def _():
            act(3)

        @pl.when(jnp.logical_not(even))
        def _():
            act(1)

    def push_pair(copy):
        @pl.when(even)
        def _():
            copy(1).start()

        @pl.when(jnp.logical_not(even))
        def _():
            copy(3).start()

    def push_others(copy):
        with_pair(lambda j: copy(j).start())
        copy(2).start()

    def wait_others(copy):
        @pl.when(even)
        def _():
            copy(1).wait_recv()

        @pl.when(jnp.logical_not(even))
        def _():
            copy(3).wait_recv()

        copy(2).wait_recv()

    kinds = ((r.qkv, r.qkv_all), (r.proj, r.proj_all))

    def target(i):
        return lax.rem(me + i, experts)

    def origin(i):
        return lax.rem(me - i + experts, experts)

    def owner(j):
        return lax.rem(shard - j + shards, shards)

    def cut(kind, chip_step):
        source = kinds[kind][0]
        rows = source.shape[0] // chips
        cols = source.shape[1] // 2
        chip = lax.rem(place.chip + chip_step + chips, chips)
        return (
            pl.ds(pl.multiple_of(chip * rows, 16), rows),
            pl.ds(pl.multiple_of(place.core * cols, 128), cols),
        )

    def far_copy(kind, j):
        rows, cols = cut(kind, 0)
        return remote(
            kinds[kind][0].at[rows, cols],
            kinds[kind][1].at[shard, rows, cols],
            r.far_s.at[kind, j],
            r.far_r.at[kind, j],
            place.along(j),
        )

    def to_twin(kind, j, i):
        rows, cols = cut(kind, -i)
        block = kinds[kind][1].at[owner(j), rows, cols]
        return remote(
            block, block, r.twin_s.at[kind, j, i], r.twin_r.at[kind, j, i], place.sibling()
        )

    def to_peer(kind, j, i):
        rows, cols = cut(kind, 0)
        block = kinds[kind][1].at[owner(j), rows, cols]
        return remote(
            block, block, r.peer_s.at[kind, j, i], r.peer_r.at[kind, j, i], place.peer(i)
        )

    def small_copy(which, j):
        src, dst = ((r.extra, r.extra_all), (r.slots, r.slots_all))[which]
        return remote(
            src, dst.at[shard], r.small_s.at[which, j], r.small_r.at[which, j], place.along(j)
        )

    def up_line_copy(j):
        return remote(
            r.up, r.up_line.at[shard], r.upline_s.at[j], r.upline_r.at[j], place.along(j)
        )

    r.extra[...] = jnp.zeros_like(r.extra)
    r.extra[:expert_count, :shard_rows] = r.router_part[...]
    r.extra[expert_count : expert_count + VECTORS, :shard_rows] = r.rows7[...]
    for j in order:
        small_copy(0, j).start()
    for kind in range(2):
        for j in order:
            far_copy(kind, j).start()
    local = [
        pltpu.make_async_copy(r.qkv, r.qkv_all.at[shard], r.here.at[0]),
        pltpu.make_async_copy(r.proj, r.proj_all.at[shard], r.here.at[1]),
    ]
    for copy in local:
        copy.start()
    r.extra_all[shard] = r.extra[...]
    spread_rows(r.flat, r.grad, image_count, seq_length, stride)
    r.slot_col[...] = jnp.zeros_like(r.slot_col) - 1.0
    for image in range(image_count):
        here = slice(image * stride, (image + 1) * stride)
        alive = r.live[image].astype(jnp.float32)
        r.up[here, :] = (r.flat[here, :] * alive).astype(bf16)
        r.turn[...] = jnp.zeros_like(r.turn)
        r.turn[0:2, :seq_length] = r.routes[image].astype(jnp.float32)
        named = r.turn[...].T[:seq_length]
        r.slot_col[image * stride : image * stride + seq_length, 0:8] = (
            named * alive - (1.0 - alive)
        )
    lanes = lax.broadcasted_iota(jnp.int32, (row_count, 128), 1)
    lane_ids = lanes.astype(jnp.float32)
    first, second = (r.slot_col[:row_count, k : k + 1] for k in range(2))
    chosen = (lane_ids == first) | (lane_ids == second)
    earlier = lax.broadcasted_iota(jnp.int32, (row_count, row_count), 0) > (
        lax.broadcasted_iota(jnp.int32, (row_count, row_count), 1)
    )
    place_in = plain_dot(
        jnp.where(earlier, 1.0, 0.0).astype(bf16), jnp.where(chosen, 1.0, 0.0).astype(bf16)
    )
    place_in += lane_ids * group_rows + (shard * capacity).astype(jnp.float32)
    both = jnp.zeros((row_count, 128), jnp.float32)
    for k, named in enumerate((first, second)):
        slot = jnp.sum(jnp.where(lane_ids == named, place_in, 0.0), axis=-1, keepdims=True)
        both += jnp.where(lanes == k, jnp.where(named < 0.0, -1.0, slot), 0.0)
    r.slots[...] = jnp.zeros_like(r.slots)
    r.slots[:, :row_count] = both.T[:8]
    for j in order:
        small_copy(1, j).start()
    r.slots_all[shard] = r.slots[...]
    r.up_line[shard] = r.up[...]
    spread_rows(r.flat, r.x, image_count, seq_length, stride)

    for kind in range(2):
        for j in order:
            far_copy(kind, j).wait_recv()
            for i in range(1, chips):
                to_peer(kind, j, i).start()
            to_twin(kind, j, 0).start()
    push_pair(up_line_copy)

    for j in order:
        small_copy(0, j).wait_recv()
    lane_from = lax.broadcasted_iota(jnp.int32, (r.extra.shape[1], width), 0)
    lane_to = lax.broadcasted_iota(jnp.int32, (r.extra.shape[1], width), 1)

    def placed(source, at):
        hit = (lane_to == lane_from + at * shard_rows) & (lane_from < shard_rows)
        return plain_dot(r.extra_all[source], jnp.where(hit, 1.0, 0.0).astype(bf16))

    whole = placed(0, 0)
    for at in range(1, shards):
        whole += placed(at, at)
    r.vectors[...] = whole[expert_count : expert_count + 8]
    r.router[...] = jnp.zeros_like(r.router)
    r.router[:expert_count, :] = whole[:expert_count].astype(bf16)
    biases = []
    for first in (0, shards // 2):
        total = jnp.zeros((1, width), jnp.float32)
        for at in range(shards):
            row = expert_count + VECTORS - 2 + at % 2
            total += placed(first + at // 2, at)[row : row + 1]
        biases.append(total)
    hit = (lane_to == lane_from + shard * shard_rows) & (lane_from < shard_rows)
    own_bias = plain_dot(
        jnp.broadcast_to(as_float(r.out_bias[...]), (16, shard_rows)).astype(bf16),
        jnp.where(hit, 1.0, 0.0).astype(bf16)[:shard_rows],
    )
    r.own_bias[...] = own_bias[:8]
    normed, _ = norm_stats(r.flat[...])
    r.attn[...] = (normed * r.vectors[0:1, :] + r.vectors[1:2, :]).astype(bf16)

    push_others(up_line_copy)
    for kind in range(2):
        for j in order:
            for i in range(1, chips):
                to_peer(kind, j, i).wait_recv()
                to_twin(kind, j, i).start()

    for j in order:
        small_copy(1, j).wait_recv()
    for at in range(shards):
        r.slot_col[at * row_count : (at + 1) * row_count, 0:8] = r.slots_all[at].T[:row_count]

    def table(at, base, size):
        ids = (lax.broadcasted_iota(jnp.int32, (size, row_count), 0) + base).astype(jnp.float32)
        slots = r.slots_all[at]
        hit = (ids == slots[0:1, :row_count]) | (ids == slots[1:2, :row_count])
        return jnp.where(hit, 1.0, 0.0).astype(bf16)

    def slot_copy(stage, landing, send_sems, recv_sems, i, part):
        start, size = spans[part]
        here = pl.ds(pl.multiple_of(start, 16), size)
        return remote(
            stage.at[target(i), here],
            landing.at[me, here],
            send_sems.at[i, part],
            recv_sems.at[i, part],
            place.plane(i),
        )

    def up_copy(i, part):
        return slot_copy(r.stage_a, r.up_in, r.up_s, r.up_r, i, part)

    def row_copy(i, part):
        return slot_copy(r.stage_b, r.rows_in, r.row_s, r.row_r, i, part)

    def dispatch(part, sources, line, stage, landing, copy):
        start, size = spans[part]
        here = pl.ds(pl.multiple_of(start, 16), size)

        def one(i, carry):
            to = target(i)
            base = to * group_rows + start
            picked = plain_dot(table(sources[0], base, size), line[sources[0]])
            for at in sources[1:]:
                picked += plain_dot(table(at, base, size), line[at])
            picked = picked.astype(bf16)

            @pl.when(i == 0)
            def _():
                landing[me, here, :] = picked

            @pl.when(i > 0)
            def _():
                stage[to, here, :] = picked
                copy(i, part).start()

            return carry

        lax.fori_loop(0, experts, one, 0)

    pair_planes = (2 * upper, 2 * upper + 1)
    all_planes = tuple(range(shards))
    with_pair(lambda j: up_line_copy(j).wait_recv())
    dispatch(0, pair_planes, r.up_line, r.stage_a, r.up_in, up_copy)

    hidden = r.in_w.shape[1]

    def weight_copy(j):
        cols = pl.ds(
            pl.multiple_of(lax.rem(shard + j, shards) * hidden, 128), hidden
        )
        rows = pl.ds(pl.multiple_of(shard * shard_rows, 16), shard_rows)
        return remote(
            r.out_wt.at[:, cols],
            r.out_w.at[rows],
            r.weight_s.at[j],
            r.weight_r.at[j],
            place.along(j),
        )

    weight_local = pltpu.make_async_copy(
        r.out_wt.at[:, pl.ds(pl.multiple_of(shard * hidden, 128), hidden)],
        r.out_w.at[pl.ds(pl.multiple_of(shard * shard_rows, 16), shard_rows)],
        r.here.at[2],
    )
    weight_local.start()
    for copy in local:
        copy.wait()
    for j in order:
        for i in range(chips):
            to_twin(0, j, i).wait_recv()

    def project(tile, carry):
        cols = pl.ds(pl.multiple_of(tile * width, 128), width)
        weight = r.qkv_all[:, :, cols].reshape(width, width)
        bias = jnp.where(tile == 0, biases[0], jnp.where(tile == 2, biases[1], 0.0))
        r.packed[:, cols] = (plain_dot(r.attn[...], weight) + bias).astype(bf16)
        return carry

    lax.fori_loop(0, 3, project, 0)
    wait_others(up_line_copy)
    for j in order:
        weight_copy(j).start()
    dispatch(1, all_planes, r.up_line, r.stage_a, r.up_in, up_copy)
    attention_core(stride, expert_count, r)
    for j in order:
        for i in range(chips):
            to_twin(1, j, i).wait_recv()
    route_core(expert_count, r, r.proj_all[...].reshape(width, width))

    def line_copy(j):
        return remote(
            r.tokens, r.line.at[shard], r.line_s.at[j], r.line_r.at[j], place.along(j)
        )

    push_pair(line_copy)
    r.line[shard] = r.tokens[...]

    with_pair(lambda j: line_copy(j).wait_recv())
    push_others(line_copy)
    dispatch(0, pair_planes, r.line, r.stage_b, r.rows_in, row_copy)
    wait_others(line_copy)
    dispatch(1, all_planes, r.line, r.stage_b, r.rows_in, row_copy)

    def keep_table(at, carry):
        ids = lax.broadcasted_iota(jnp.int32, (shards * row_count, group_rows), 1)
        ids = (ids + at * group_rows).astype(jnp.float32)
        hit = (ids == r.slot_col[:, 0:1]) | (ids == r.slot_col[:, 1:2])
        r.tables[at] = jnp.where(hit, 1.0, 0.0).astype(bf16)
        return carry

    lax.fori_loop(0, experts, keep_table, 0)

    half, third = width // 2, width // 3

    def out_copy(i, part):
        cols = pl.ds(part * half, half)
        return remote(
            r.stage_a.at[origin(i), :, cols],
            r.out_in.at[me, :, cols],
            r.out_s.at[i, part],
            r.out_r.at[i, part],
            place.plane(experts - i),
        )

    def note_copy(i):
        return remote(
            r.notes.at[origin(i)],
            r.note_in.at[me],
            r.note_s.at[i],
            r.note_r.at[i],
            place.plane(experts - i),
        )

    def back_copy(i, part):
        cols = pl.ds(part * third, third)
        return remote(
            r.stage_b.at[origin(i), :, cols],
            r.back_in.at[me, :, cols],
            r.back_s.at[i, part],
            r.back_r.at[i, part],
            place.plane(experts - i),
        )

    weight_local.wait()
    for j in order:
        weight_copy(j).wait_recv()

    def drain_up(i, carry):
        for part in range(2):
            up_copy(i, part).wait_send()
        return carry

    lax.fori_loop(1, experts, drain_up, 0)
    r.notes[...] = jnp.zeros_like(r.notes)

    def forward(i, carry):
        at = origin(i)

        @pl.when(i > 0)
        def _():
            for part in range(2):
                row_copy(i, part).wait_recv()

        rows = r.rows_in[at]
        gelu_out, gelu_slope = gelu_parts(
            plain_dot(rows, r.in_w[...]) + as_float(r.in_bias[...])
        )
        r.slope[at] = gelu_slope
        gelu_bf = gelu_out.astype(bf16)
        r.gelu[at] = gelu_bf
        gates = softmax_gates(rows, r.router[...], expert_count)
        gate_lanes = lax.broadcasted_iota(jnp.int32, gates.shape, 1)
        gate = jnp.sum(jnp.where(gate_lanes == me, gates, 0.0), axis=-1, keepdims=True)

        @pl.when(i > 0)
        def _():
            for part in range(2):
                up_copy(i, part).wait_recv()

        upstream = as_float(r.up_in[at])
        r.sent[at] = (gate * upstream).astype(bf16)
        expert_out = contract_cols(gelu_bf, r.out_w[...]) + r.own_bias[0:1, :]
        gate_grad = jnp.sum(upstream * expert_out, axis=-1, keepdims=True)
        notes = jnp.broadcast_to(gate_grad, (group_rows, 128)).T[:16].astype(bf16)
        gated = (gate * expert_out).astype(bf16)

        @pl.when(i == 0)
        def _():
            r.out_in[me] = gated
            r.note_in[me, :, :group_rows] = notes

        @pl.when(i > 0)
        def _():
            r.stage_a[at] = gated
            r.notes[at, :, :group_rows] = notes
            out_copy(i, 0).start()
            note_copy(i).start()

        return carry

    lax.fori_loop(0, experts, forward, 0)

    def push_out(i, carry):
        out_copy(i, 1).start()
        return carry

    lax.fori_loop(1, experts, push_out, 0)
    r.in_bias_grad[...] = jnp.zeros_like(r.in_bias_grad)
    r.out_bias_grad[...] = jnp.zeros_like(r.out_bias_grad)

    def drain_rows(i, carry):
        for part in range(2):
            row_copy(i, part).wait_send()
        return carry

    lax.fori_loop(1, experts, drain_rows, 0)

    def backward(i, carry):
        at = origin(i)
        sent = r.sent[at]
        r.out_bias_grad[0:1, :] += jnp.sum(as_float(sent), axis=0, keepdims=True)
        pre_grad = plain_dot(sent, r.out_w[...]) * r.slope[at]
        r.in_bias_grad[0:1, :] += jnp.sum(pre_grad, axis=0, keepdims=True)
        pre_bf = pre_grad.astype(bf16)
        r.pre[at] = pre_bf
        back = contract_cols(pre_bf, r.in_w[...]).astype(bf16)

        @pl.when(i == 0)
        def _():
            r.back_in[me] = back

        @pl.when(i > 0)
        def _():
            r.stage_b[at] = back
            back_copy(i, 0).start()

        return carry

    lax.fori_loop(0, experts, backward, 0)

    for part in range(1, 3):

        def push_rest(i, carry, part=part):
            back_copy(i, part).start()
            return carry

        lax.fori_loop(1, experts, push_rest, 0)

    def collect(landing, copy, part, size):
        cols = pl.ds(part * size, size)

        def one(i, carry):
            at = target(i)

            @pl.when(i > 0)
            def _():
                copy(i, part).wait_recv()

            r.total[:, cols] += plain_dot(r.tables[at], landing[at, :, cols])
            return carry

        lax.fori_loop(0, experts, one, 0)

    def collect_notes(i, carry):
        at = target(i)

        @pl.when(i > 0)
        def _():
            note_copy(i).wait_recv()

        rows_at = lax.broadcasted_iota(jnp.int32, (128, group_rows), 0)
        note = as_float(r.note_in[at, 0:1, :group_rows])
        r.total[:, width:] += contract_cols(
            r.tables[at], jnp.where(rows_at == at, note, 0.0).astype(bf16)
        )
        return carry

    columns = ((0, half), (half, half)) + tuple((at * third, third) for at in range(3))

    def sum_copy(which, j):
        src, dst = (r.far_out, r.far_out_in) if which < 2 else (r.far_back, r.far_back_in)
        to = lax.rem(shard + j, shards)
        cols = pl.ds(*columns[which])
        return remote(
            src.at[to, :, cols],
            dst.at[j, :, cols],
            r.sum_s.at[which, j],
            r.sum_r.at[which, j],
            place.along(j),
        )

    def note_sum_copy(j):
        return remote(
            r.note_far.at[lax.rem(shard + j, shards)],
            r.note_far_in.at[j],
            r.notesum_s.at[j],
            r.notesum_r.at[j],
            place.along(j),
        )

    own = pl.ds(pl.multiple_of(shard * row_count, 16), row_count)

    def spread_sums(which):
        far = r.far_out if which < 2 else r.far_back
        cols = pl.ds(*columns[which])
        for at in range(shards):
            far[at, :, cols] = r.total[at * row_count : (at + 1) * row_count, cols].astype(bf16)
        for j in order:
            sum_copy(which, j).start()

    def weigh(left, right, grad):
        tile = 128

        def one(at, carry):
            cols = pl.ds(pl.multiple_of(at * tile, 128), tile)
            lhs = left[:, :, cols].reshape(experts * group_rows, tile)
            rhs = right[...].reshape(experts * group_rows, right.shape[2])
            grad[cols, :] = contract_rows(lhs, rhs).astype(grad.dtype)
            return carry

        lax.fori_loop(0, left.shape[2] // tile, one, 0)

    r.total[...] = jnp.zeros_like(r.total)
    collect(r.out_in, out_copy, 0, half)
    spread_sums(0)
    lax.fori_loop(0, experts, collect_notes, 0)
    r.note_far[...] = jnp.zeros_like(r.note_far)
    for at in range(shards):
        notes = r.total[at * row_count : (at + 1) * row_count, width:].T
        r.note_far[at, :, :row_count] = notes[: r.note_far.shape[1]].astype(bf16)
    for j in order:
        note_sum_copy(j).start()
    weigh(r.sent, r.gelu, r.out_grad)
    collect(r.out_in, out_copy, 1, half)
    spread_sums(1)
    r.summed[...] = r.total[own, :]
    weigh(r.rows_in, r.pre, r.in_grad)
    r.total[...] = jnp.zeros_like(r.total)
    for part in range(3):
        collect(r.back_in, back_copy, part, third)
        spread_sums(2 + part)
    r.route[...] = r.total[own, :width]
    for j in order:
        note_sum_copy(j).wait_recv()
        notes = as_float(r.note_far_in[j]).T
        lanes_in = notes.shape[1]
        r.summed[:, width : width + lanes_in] += notes[:row_count]
    for which in range(5):
        cols = pl.ds(*columns[which])
        for j in order:
            sum_copy(which, j).wait_recv()
            if which < 2:
                r.summed[:, cols] += as_float(r.far_out_in[j, :, cols])
            else:
                r.route[:, cols] += as_float(r.far_back_in[j, :, cols])

    for j in order:
        for which in range(2):
            far_copy(which, j).wait_send()
            small_copy(which, j).wait_send()
            for i in range(chips):
                to_twin(which, j, i).wait_send()
                if i:
                    to_peer(which, j, i).wait_send()
        for which in range(5):
            sum_copy(which, j).wait_send()
        note_sum_copy(j).wait_send()
        up_line_copy(j).wait_send()
        line_copy(j).wait_send()
        weight_copy(j).wait_send()

    def finish(i, carry):
        out_copy(i, 0).wait_send()
        out_copy(i, 1).wait_send()
        note_copy(i).wait_send()
        for part in range(3):
            back_copy(i, part).wait_send()
        return carry

    lax.fori_loop(1, experts, finish, 0)


def fused_pass(shards, experts, capacity, expert_count, stride, inputs):
    x, qkv, proj, in_w = (inputs[at] for at in (1, 4, 5, 8))
    extra_shape = (round_up(VECTORS + expert_count, 16), round_up(qkv.shape[0], 128))
    width, hidden = in_w.shape
    row_count = x.shape[1] * stride
    router_pad = round_up(expert_count, 128)
    group_rows = round_up(shards * capacity, 16)
    lanes = round_up(group_rows, 128)
    chips = experts // 2
    bf16, f32, dma = jnp.bfloat16, jnp.float32, pltpu.SemaphoreType.DMA
    vmem, anywhere = pl.BlockSpec(memory_space=pltpu.VMEM), pl.BlockSpec(memory_space=pl.ANY)

    def shape(dims, kind=bf16):
        return jax.ShapeDtypeStruct(dims, kind)

    smem = pl.BlockSpec(memory_space=pltpu.SMEM)
    ins = dict(
        live=smem,
        x=vmem,
        grad=vmem,
        routes=vmem,
        qkv=anywhere,
        proj=anywhere,
        rows7=vmem,
        router_part=vmem,
        in_w=vmem,
        out_wt=anywhere,
        in_bias=vmem,
        out_bias=vmem,
    )
    outs = dict(
        qkv_all=shape((shards,) + qkv.shape),
        proj_all=shape((shards,) + proj.shape),
        vectors=shape((8, width), f32),
        router=shape((router_pad, width)),
        packed=shape((row_count, 3 * width)),
        mixed=shape((row_count, width)),
        residual=shape((row_count, width), f32),
        tokens=shape((row_count, width)),
        gates=shape((row_count, router_pad), f32),
        summed=shape((row_count, width + 128), f32),
        route=shape((row_count, width), f32),
        in_grad=shape((width, hidden), f32),
        out_grad=shape((width, hidden)),
        in_bias_grad=shape((8, hidden), f32),
        out_bias_grad=shape((8, width), f32),
    )
    group = (experts, group_rows)
    note_rows = round_up(expert_count, 16)
    scratch = dict(
        flat=pltpu.VMEM((row_count, width), f32),
        attn=pltpu.VMEM((row_count, width), bf16),
        up=pltpu.VMEM((row_count, width), bf16),
        turn=pltpu.VMEM((8, 128), f32),
        slots=pltpu.VMEM((8, round_up(row_count, 128)), f32),
        own_bias=pltpu.VMEM((8, width), f32),
        extra=pltpu.VMEM(extra_shape, bf16),
        extra_all=pltpu.VMEM((shards,) + extra_shape, bf16),
        slots_all=pltpu.VMEM((shards, 8, round_up(row_count, 128)), f32),
        slot_col=pltpu.VMEM((shards * row_count, 128), f32),
        up_line=pltpu.VMEM((shards, row_count, width), bf16),
        line=pltpu.VMEM((shards, row_count, width), bf16),
        out_w=pltpu.VMEM((width, hidden), bf16),
        up_in=pltpu.VMEM(group + (width,), bf16),
        stage_a=pltpu.VMEM(group + (width,), bf16),
        stage_b=pltpu.VMEM(group + (width,), bf16),
        rows_in=pltpu.VMEM(group + (width,), bf16),
        gelu=pltpu.VMEM(group + (hidden,), bf16),
        slope=pltpu.VMEM(group + (hidden,), f32),
        sent=pltpu.VMEM(group + (width,), bf16),
        pre=pltpu.VMEM(group + (hidden,), bf16),
        out_in=pltpu.VMEM(group + (width,), bf16),
        back_in=pltpu.VMEM(group + (width,), bf16),
        notes=pltpu.VMEM((experts, 16, lanes), bf16),
        note_in=pltpu.VMEM((experts, 16, lanes), bf16),
        total=pltpu.VMEM((shards * row_count, width + 128), f32),
        far_out=pltpu.VMEM((shards, row_count, width), bf16),
        far_out_in=pltpu.VMEM((shards, row_count, width), bf16),
        note_far=pltpu.VMEM((shards, note_rows, round_up(row_count, 128)), bf16),
        note_far_in=pltpu.VMEM((shards, note_rows, round_up(row_count, 128)), bf16),
        tables=pltpu.VMEM((experts, shards * row_count, group_rows), bf16),
        far_back=pltpu.VMEM((shards, row_count, width), bf16),
        far_back_in=pltpu.VMEM((shards, row_count, width), bf16),
        here=dma((3,)),
    )
    pairs = dict(
        far=(2, shards),
        twin=(2, shards, chips),
        peer=(2, shards, chips),
        small=(2, shards),
        upline=(shards,),
        up=(experts, 2),
        line=(shards,),
        weight=(shards,),
        row=(experts, 2),
        out=(experts, 2),
        note=(experts,),
        back=(experts, 3),
        sum=(5, shards),
        notesum=(shards,),
    )
    for name, dims in pairs.items():
        scratch[name + "_s"] = dma(dims)
        scratch[name + "_r"] = dma(dims)
    names = tuple(ins) + tuple(outs) + tuple(scratch)
    return pl.pallas_call(
        functools.partial(fused_kernel, shards, experts, capacity, expert_count, stride, names),
        out_shape=list(outs.values()),
        in_specs=list(ins.values()),
        out_specs=[vmem] * len(outs),
        scratch_shapes=list(scratch.values()),
        compiler_params=pltpu.CompilerParams(
            collective_id=1, has_side_effects=True, vmem_limit_bytes=BIG_VMEM
        ),
        name="front_and_experts",
    )(*inputs)


def expert_slow(
    tokens, gates, route_rows, tables, line_up, up_in, in_slice, out_slice, in_bias, own_bias
):
    row_count, width = tokens.shape
    bf16 = jnp.bfloat16
    table_0, table_1, send_table = tables
    router_pad = gates.shape[1]
    chosen = route_rows[:, :, None] == jnp.arange(router_pad, dtype=jnp.int32)[None, None, :]
    gate_pick = jnp.sum(jnp.where(chosen, gates[:, None, :], 0.0), axis=2)
    gate_high = gate_pick.astype(bf16)
    gate_low = (gate_pick - as_float(gate_high)).astype(bf16)
    gate_notes = jnp.concatenate([gate_high, gate_low], axis=1)
    gate_notes = jnp.pad(gate_notes, ((0, 0), (0, 128 - gate_notes.shape[1])))
    sent_line = jnp.concatenate([tokens, gate_notes], axis=1)
    row_line = lax.all_gather(sent_line, "shard", axis=0, tiled=True)
    line_in = row_line[:, :width]
    gate_line = as_float(row_line[:, width : width + 4])
    line_gate = gate_line[:, 0:2] + gate_line[:, 2:4]
    outgoing = contract_rows(send_table, line_in).astype(bf16)
    slot_gate = jnp.sum(
        jnp.where(table_0, line_gate[:, 0:1], 0.0) + jnp.where(table_1, line_gate[:, 1:2], 0.0),
        axis=0,
    )
    slot_high = slot_gate.astype(bf16)
    slot_low = (slot_gate - as_float(slot_high)).astype(bf16)
    slot_notes = jnp.pad(jnp.stack([slot_high, slot_low], axis=1), ((0, 0), (0, 126)))
    incoming = lax.all_to_all(
        jnp.concatenate([outgoing, slot_notes], axis=1),
        "expert",
        split_axis=0,
        concat_axis=0,
        tiled=True,
    )
    rows_in = incoming[:, :width]
    gate_in = as_float(incoming[:, width : width + 1]) + as_float(
        incoming[:, width + 1 : width + 2]
    )
    grad_in = (as_float(up_in) * gate_in).astype(bf16)
    pre_act = plain_dot(rows_in, in_slice) + in_bias
    gelu_out, gelu_slope = gelu_parts(pre_act)
    gelu_bf = gelu_out.astype(bf16)
    expert_out = (plain_dot(gelu_bf, out_slice) + own_bias).astype(bf16)
    returned = lax.all_to_all(expert_out, "expert", split_axis=0, concat_axis=0, tiled=True)
    pre_grad = contract_cols(grad_in, out_slice) * gelu_slope
    pre_bf = pre_grad.astype(bf16)
    back_rows = contract_cols(pre_bf, in_slice).astype(bf16)
    returned_grad = lax.all_to_all(back_rows, "expert", split_axis=0, concat_axis=0, tiled=True)
    out_0 = plain_dot(table_0.astype(bf16), returned)
    out_1 = plain_dot(table_1.astype(bf16), returned)
    combined = line_gate[:, 0:1] * out_0 + line_gate[:, 1:2] * out_1
    line_up_wide = as_float(line_up)
    gate_grad_line = jnp.stack(
        [jnp.sum(line_up_wide * out_0, axis=1), jnp.sum(line_up_wide * out_1, axis=1)], axis=1
    )
    joined = jnp.concatenate(
        [combined.astype(bf16), jnp.pad(gate_grad_line, ((0, 0), (0, 126))).astype(bf16)], axis=1
    )
    summed = as_float(lax.psum_scatter(joined, "shard", scatter_dimension=0, tiled=True))
    picked = jnp.sum(
        jnp.where(chosen, summed[:, width : width + 2][:, :, None], 0.0), axis=1
    )
    summed = jnp.concatenate([summed[:, :width], picked], axis=1)
    back_line = plain_dot(send_table, returned_grad)
    route_grad = lax.psum_scatter(back_line.astype(bf16), "shard", scatter_dimension=0, tiled=True)
    return (
        summed,
        route_grad,
        contract_rows(rows_in, pre_bf),
        contract_rows(gelu_bf, grad_in).astype(bf16),
        jnp.sum(pre_grad, axis=0)[None],
        jnp.sum(as_float(grad_in), axis=0)[None],
    )


def body(
    block_input,
    image_live,
    expert_routes,
    first_gain,
    first_shift,
    qkv_weight,
    query_value_bias,
    attn_out_weight,
    attn_out_bias,
    second_gain,
    second_shift,
    router_weight,
    expert_in_weight,
    expert_in_bias,
    expert_out_weight,
    expert_out_bias,
    output_grad,
):
    image_count, seq_length, width = block_input.shape
    shards = lax.axis_size("shard")
    experts = lax.axis_size("expert")
    chips = experts // 2
    expert_count = router_weight.shape[1]
    my_shard = lax.axis_index("shard")
    shard_rows = first_gain.shape[0]
    stride = round_up(seq_length, 8)
    row_count = image_count * stride
    capacity = (3 * image_count * seq_length + expert_count - 1) // expert_count
    group_rows = round_up(shards * capacity, 16)
    slot_rows = expert_count * group_rows
    bf16 = jnp.bfloat16
    fast = chips == 4 and shards == 4 and shard_rows % (16 * chips) == 0

    router_pad = round_up(expert_count, 128)
    extra_rows = round_up(VECTORS + expert_count, 16)
    extra_cols = round_up(shard_rows, 128)
    vector_rows = jnp.concatenate(
        [
            first_gain,
            first_shift,
            attn_out_bias,
            second_gain,
            second_shift,
            query_value_bias,
        ]
    ).reshape(VECTORS, shard_rows)
    turned_in = jnp.transpose(block_input, (1, 0, 2))
    turned_grad = jnp.transpose(output_grad, (1, 0, 2))
    in_slice = expert_in_weight[0]
    out_slice_t = expert_out_weight[0].T
    if fast:
        (
            qkv_full,
            proj_full,
            vectors,
            router_t,
            packed,
            mixed,
            residual,
            expert_in,
            gates,
            summed,
            route_grad,
            in_weight_grad,
            out_weight_grad,
            in_bias_sum,
            out_bias_sum,
        ) = fused_pass(
            shards,
            experts,
            capacity,
            expert_count,
            stride,
            (
                image_live,
                turned_in,
                turned_grad,
                jnp.transpose(expert_routes, (0, 2, 1)),
                qkv_weight,
                attn_out_weight,
                vector_rows,
                router_weight.T,
                in_slice,
                out_slice_t,
                expert_in_bias,
                expert_out_bias,
            ),
        )
        qkv_full = qkv_full.reshape(width, 3 * width)
        proj_full = proj_full.reshape(width, width)
    else:
        tail_rows = stride - seq_length
        live_rows = jnp.repeat(image_live, stride) * jnp.tile(
            (jnp.arange(stride) < seq_length).astype(jnp.int32), image_count
        )
        route_rows = jnp.pad(expert_routes, ((0, 0), (0, tail_rows), (0, 0))).reshape(row_count, 2)
        route_code, position = slot_places(route_rows, live_rows, expert_count)
        up_rows = (
            jnp.pad(output_grad, ((0, 0), (0, tail_rows), (0, 0))).reshape(row_count, width)
            * as_float(live_rows)[:, None]
        )
        own_bias = lax.dynamic_update_slice(
            jnp.zeros((1, width), jnp.float32),
            as_float(expert_out_bias),
            (0, my_shard * shard_rows),
        )
        in_bias = as_float(expert_in_bias)
        notes = jnp.concatenate([route_code.astype(bf16), position.astype(bf16)], axis=1)
        notes = jnp.pad(notes, ((0, 0), (0, 128 - notes.shape[1])))
        up_line = jnp.concatenate([up_rows.astype(bf16), notes], axis=1)
        extra = jnp.pad(
            jnp.concatenate([router_weight.T, vector_rows]),
            ((0, extra_rows - expert_count - VECTORS), (0, extra_cols - shard_rows)),
        )
        qkv_all, proj_all, extra_all, line_all = (
            lax.all_gather(each, "shard", axis=0, tiled=False)
            for each in (qkv_weight, attn_out_weight, extra, up_line)
        )
        qkv_full = qkv_all.reshape(width, 3 * width)
        proj_full = proj_all.reshape(width, width)
        extra_t = jnp.transpose(extra_all[:, :, :shard_rows], (1, 0, 2))
        rows_t = extra_t[expert_count:]
        vectors = as_float(rows_t[:8]).reshape(8, width)
        query_value = as_float(rows_t[5:7])
        bias_full = jnp.transpose(query_value, (1, 0, 2)).reshape(2 * width)
        bias_row = jnp.concatenate(
            [bias_full[:width], jnp.zeros((width,), jnp.float32), bias_full[width:]]
        )
        bias_row = jnp.pad(bias_row[None], ((0, 7), (0, 0)))
        router_t = jnp.pad(
            extra_t[:expert_count].reshape(expert_count, width),
            ((0, router_pad - expert_count), (0, 0)),
        )
        line_rows = shards * row_count
        line = line_all.reshape(line_rows, width + 128)
        line_up = line[:, :width]
        line_notes = as_float(line[:, width : width + 4])
        line_ids = jnp.arange(line_rows, dtype=jnp.int32)[:, None]
        line_slot = (
            line_notes[:, 0:2].astype(jnp.int32) * group_rows
            + (line_ids // row_count) * capacity
            + line_notes[:, 2:4].astype(jnp.int32)
        )
        line_slot = jnp.where(line_notes[:, 0:2] >= 0, line_slot, -1)
        slot_ids = jnp.arange(slot_rows, dtype=jnp.int32)
        table_0 = line_slot[:, 0:1] == slot_ids[None, :]
        table_1 = line_slot[:, 1:2] == slot_ids[None, :]
        send_table = (table_0 | table_1).astype(bf16)
        up_out = contract_rows(send_table, line_up).astype(bf16)
        up_in = lax.all_to_all(up_out, "expert", split_axis=0, concat_axis=0, tiled=True)
        out_slice = lax.all_to_all(
            expert_out_weight[0], "shard", split_axis=0, concat_axis=1, tiled=True
        )
        packed, mixed, residual, expert_in, gates = pl.pallas_call(
            functools.partial(forward_kernel, stride, expert_count),
            out_shape=[
                jax.ShapeDtypeStruct((row_count, 3 * width), bf16),
                jax.ShapeDtypeStruct((row_count, width), bf16),
                jax.ShapeDtypeStruct((row_count, width), jnp.float32),
                jax.ShapeDtypeStruct((row_count, width), bf16),
                jax.ShapeDtypeStruct((row_count, router_pad), jnp.float32),
            ],
            in_specs=[pl.BlockSpec(memory_space=pltpu.VMEM)] * 6,
            out_specs=[pl.BlockSpec(memory_space=pltpu.VMEM)] * 5,
            scratch_shapes=[
                pltpu.VMEM((row_count, width), jnp.float32),
                pltpu.VMEM((row_count, width), bf16),
            ],
            compiler_params=pltpu.CompilerParams(vmem_limit_bytes=BIG_VMEM),
            name="attention_forward",
        )(turned_in, qkv_full, proj_full, vectors, bias_row, router_t)
        (
            summed,
            route_grad,
            in_weight_grad,
            out_weight_grad,
            in_bias_sum,
            out_bias_sum,
        ) = expert_slow(
            expert_in,
            gates,
            route_rows,
            (table_0, table_1, send_table),
            line_up,
            up_in,
            in_slice,
            out_slice,
            in_bias,
            own_bias,
        )
        out_weight_grad = out_weight_grad.T
    out_weight_grad = out_weight_grad.reshape(shards, shard_rows, -1)
    in_weight_part = in_weight_grad[None]
    in_bias_part = in_bias_sum[:1]
    out_bias_part = lax.dynamic_slice_in_dim(
        out_bias_sum[0], my_shard * shard_rows, shard_rows
    )[None]

    if fast:
        (
            block_output,
            input_grad,
            qkv_sum,
            proj_sum,
            mine,
            bias_part,
            out_weight_rows,
        ) = backward_reduce(
            shards,
            chips,
            stride,
            (
                image_live,
                turned_in,
                turned_grad,
                packed,
                mixed,
                residual,
                expert_in,
                gates,
                summed,
                route_grad,
                qkv_full,
                proj_full,
                vectors,
                router_t,
                out_weight_grad,
            ),
        )
        out_weight_part = as_float(out_weight_rows).T[None]
        mine = mine[:, :shard_rows]
        bias_part = bias_part[0]
    else:
        smem = pl.BlockSpec(memory_space=pltpu.SMEM)
        vmem = pl.BlockSpec(memory_space=pltpu.VMEM)
        wide_rows = pltpu.VMEM((row_count, width), jnp.float32)
        block_output, input_grad, weight_grads, extra_grads = pl.pallas_call(
            functools.partial(backward_kernel, stride),
            out_shape=[
                jax.ShapeDtypeStruct(turned_in.shape, jnp.float32),
                jax.ShapeDtypeStruct(turned_in.shape, jnp.float32),
                jax.ShapeDtypeStruct((2, width, 2 * width), bf16),
                jax.ShapeDtypeStruct((extra_rows, width), jnp.float32),
            ],
            in_specs=[smem] + [vmem] * 13,
            out_specs=[vmem] * 4,
            scratch_shapes=[
                wide_rows,
                wide_rows,
                pltpu.VMEM((width, row_count), bf16),
                pltpu.VMEM((row_count, width), bf16),
                pltpu.VMEM((row_count, 3 * width), bf16),
                wide_rows,
            ],
            compiler_params=pltpu.CompilerParams(vmem_limit_bytes=BIG_VMEM),
            cost_estimate=pl.CostEstimate(
                flops=32 * row_count * width * width,
                bytes_accessed=48 * width * width,
                transcendentals=2 * HEADS * row_count * row_count,
            ),
            name="attention_backward",
        )(
            image_live,
            turned_in,
            turned_grad,
            packed,
            mixed,
            residual,
            expert_in,
            gates,
            summed,
            route_grad,
            qkv_full,
            proj_full,
            vectors,
            router_t,
        )
        qkv_sum, proj_sum, extra_sum, out_weight_blocks = reduce_slow(
            weight_grads, extra_grads.astype(bf16), out_weight_grad
        )
        out_weight_part = (
            jnp.transpose(as_float(out_weight_blocks), (0, 2, 1)).reshape(-1, shard_rows)[None]
        )

        def own(array_in, size, axis=0):
            return lax.dynamic_slice_in_dim(array_in, my_shard * size, size, axis=axis)

        mine = own(extra_sum, shard_rows, axis=1)
        bias_part = own(extra_sum[5:7].reshape(2 * width), 2 * shard_rows)
    return (
        jnp.transpose(block_output, (1, 0, 2)),
        jnp.transpose(input_grad, (1, 0, 2)),
        mine[0],
        mine[1],
        as_float(qkv_sum),
        bias_part,
        as_float(proj_sum),
        mine[2],
        mine[3],
        mine[4],
        mine[VECTORS : VECTORS + expert_count].T,
        in_weight_part,
        in_bias_part,
        out_weight_part,
        out_bias_part,
    )


def solution(mesh):
    in_specs = (
        P(("expert", "shard"), None, None),
        P(("expert", "shard")),
        P(("expert", "shard"), None, None),
        P("shard"),
        P("shard"),
        P("shard", None),
        P("shard"),
        P("shard", None),
        P("shard"),
        P("shard"),
        P("shard"),
        P("shard", None),
        P("expert", None, "shard"),
        P("expert", "shard"),
        P("expert", None, "shard"),
        P("expert", "shard"),
        P(("expert", "shard"), None, None),
    )
    out_specs = (
        P(("expert", "shard"), None, None),
        P(("expert", "shard"), None, None),
        P("shard"),
        P("shard"),
        P("shard", None),
        P("shard"),
        P("shard", None),
        P("shard"),
        P("shard"),
        P("shard"),
        P("shard", None),
        P("expert", None, "shard"),
        P("expert", "shard"),
        P("expert", None, "shard"),
        P("expert", "shard"),
    )
    return jax.shard_map(body, mesh=mesh, in_specs=in_specs, out_specs=out_specs, check_vma=False)
```

```python
import functools
import math
import types

import jax
import jax.numpy as jnp
from jax import lax
from jax.experimental import pallas as pl
from jax.experimental.pallas import tpu as pltpu
from jax.sharding import PartitionSpec as P

HEADS = 12
HEAD_DIM = 64


EPSILON = 1e-06
PRECISE = lax.Precision.HIGHEST
HALF_ROOT = 0.7071067811865476
DENSITY = 0.3989422804014327


def as_float(array_in):
    return array_in.astype(jnp.float32)


def contract_rows(left_side, right_side):
    return lax.dot_general(
        left_side, right_side, (((0,), (0,)), ((), ())), preferred_element_type=jnp.float32
    )


def contract_cols(left_side, right_side):
    return lax.dot_general(
        left_side, right_side, (((1,), (1,)), ((), ())), preferred_element_type=jnp.float32
    )


def precise_rows(left_side, right_side):
    return lax.dot_general(
        left_side,
        right_side,
        (((0,), (0,)), ((), ())),
        precision=PRECISE,
        preferred_element_type=jnp.float32,
    )


def precise_cols(left_side, right_side):
    return lax.dot_general(
        left_side,
        right_side,
        (((1,), (1,)), ((), ())),
        precision=PRECISE,
        preferred_element_type=jnp.float32,
    )


def layer_norm(values_in, gain_vec, shift_vec):
    center = values_in - jnp.mean(values_in, axis=-1, keepdims=True)
    inv_std = lax.rsqrt(jnp.mean(center * center, axis=-1, keepdims=True) + EPSILON)
    normed = center * inv_std
    return (normed * as_float(gain_vec) + as_float(shift_vec), normed, inv_std)


def norm_back(upstream, normed, inv_std, gain_vec):
    scaled = upstream * as_float(gain_vec)
    return inv_std * (
        scaled
        - jnp.mean(scaled, axis=-1, keepdims=True)
        - normed * jnp.mean(scaled * normed, axis=-1, keepdims=True)
    )


def gelu_parts(pre_act):
    normal_cdf = 0.5 * (1.0 + jax.scipy.special.erf(pre_act * HALF_ROOT))
    return (
        pre_act * normal_cdf,
        normal_cdf + pre_act * DENSITY * jnp.exp(-0.5 * pre_act * pre_act),
    )


BIG_VMEM = 56 * 1024 * 1024
VECTORS = 7


def plain_dot(left_side, right_side):
    return jnp.dot(left_side, right_side, preferred_element_type=jnp.float32)


def exact_dot(left_side, right_side):
    return lax.dot_general(
        left_side,
        right_side,
        (((1,), (0,)), ((), ())),
        precision=PRECISE,
        preferred_element_type=jnp.float32,
    )


def round_up(value, step):
    return -(-value // step) * step


def slot_places(route_rows, live_rows, expert_count):
    row_count = route_rows.shape[0]
    flat_routes = route_rows.reshape(2 * row_count)
    alive_pairs = jnp.repeat(live_rows, 2)
    chosen = (flat_routes[:, None] == jnp.arange(expert_count, dtype=jnp.int32)[None, :]).astype(
        jnp.int32
    )
    live_hits = chosen * alive_pairs[:, None]
    earlier = (
        jnp.arange(2 * row_count, dtype=jnp.int32)[:, None]
        > jnp.arange(2 * row_count, dtype=jnp.int32)[None, :]
    ).astype(jnp.bfloat16)
    counted = jnp.dot(earlier, live_hits.astype(jnp.bfloat16), preferred_element_type=jnp.float32)
    position = jnp.sum(counted * as_float(live_hits), axis=1)
    route_code = jnp.where(alive_pairs > 0, flat_routes, -1).astype(jnp.float32)
    return route_code.reshape(row_count, 2), position.reshape(row_count, 2)


class Place:
    def __init__(self, shards, chips):
        self.shards = shards
        self.chips = chips
        self.expert = lax.axis_index("expert")
        self.shard = lax.axis_index("shard")
        self.core = lax.rem(self.expert, 2)
        self.chip = lax.div(self.expert, 2)

    def along(self, step):
        return {
            "expert": self.expert,
            "shard": lax.rem(self.shard + step + self.shards, self.shards),
        }

    def peer(self, step):
        other = lax.rem(self.chip + step + self.chips, self.chips)
        return {"expert": other * 2 + self.core, "shard": self.shard}

    def sibling(self):
        return {"expert": self.chip * 2 + 1 - self.core, "shard": self.shard}

    def plane(self, step):
        count = 2 * self.chips
        return {"expert": lax.rem(self.expert + step, count), "shard": self.shard}

    def greet(self, others):
        barrier = pltpu.get_barrier_semaphore()
        for other in others:
            pl.semaphore_signal(
                barrier, inc=1, device_id=other, device_id_type=pl.DeviceIdType.MESH
            )
        pl.semaphore_wait(barrier, len(others))


def remote(src, dst, send_sem, recv_sem, device):
    return pltpu.make_async_remote_copy(
        src_ref=src,
        dst_ref=dst,
        send_sem=send_sem,
        recv_sem=recv_sem,
        device_id=device,
        device_id_type=pl.DeviceIdType.MESH,
    )


def norm_stats(values_in):
    center = values_in - jnp.mean(values_in, axis=-1, keepdims=True)
    inv_std = lax.rsqrt(jnp.mean(center * center, axis=-1, keepdims=True) + EPSILON)
    return center * inv_std, inv_std


def spread_rows(dst, src, image_count, seq_length, stride):
    dst[...] = jnp.zeros_like(dst)
    for image in range(image_count):
        dst[image * stride : image * stride + seq_length, :] = src[:, image, :]


def same_image(rows, stride, seq_length):
    row_at = lax.broadcasted_iota(jnp.int32, (rows, rows), 0)
    col_at = lax.broadcasted_iota(jnp.int32, (rows, rows), 1)
    mask = None
    for image in range(rows // stride):
        low = image * stride
        part = (
            (row_at >= low)
            & (row_at < low + stride)
            & (col_at >= low)
            & (col_at < low + seq_length)
        )
        mask = part if mask is None else mask | part
    return mask


def masked_softmax(query_half, keys, mask):
    scores = contract_cols(query_half, keys) * (1.0 / math.sqrt(HEAD_DIM))
    scores = jnp.where(mask, scores, -1e30)
    row_max = jnp.max(scores, axis=-1, keepdims=True)
    log_total = row_max + jnp.log(jnp.sum(jnp.exp(scores - row_max), axis=-1, keepdims=True))
    return jnp.exp(scores - log_total)


def forward_kernel(
    stride,
    expert_count,
    x_ref,
    qkv_ref,
    proj_ref,
    vec_ref,
    bias_ref,
    router_ref,
    packed_ref,
    mixed_ref,
    residual_ref,
    line_ref,
    gates_ref,
    flat_ref,
    attn_ref,
):
    seq_length, image_count, width = x_ref.shape
    rows = flat_ref.shape[0]
    bf16 = jnp.bfloat16
    spread_rows(flat_ref, x_ref, image_count, seq_length, stride)
    normed, _ = norm_stats(flat_ref[...])
    attn_ref[...] = (normed * vec_ref[0:1, :] + vec_ref[1:2, :]).astype(bf16)

    def project(tile, carry):
        cols = pl.ds(pl.multiple_of(tile * width, 128), width)
        packed_ref[:, cols] = (
            plain_dot(attn_ref[...], qkv_ref[:, cols]) + bias_ref[0:1, cols]
        ).astype(bf16)
        return carry

    lax.fori_loop(0, 3, project, 0)
    mask = same_image(rows, stride, seq_length)
    low_lanes = lax.broadcasted_iota(jnp.int32, (rows, 128), 1) < HEAD_DIM

    def attend(pair, carry):
        def part(which):
            return packed_ref[:, pl.ds(pl.multiple_of(which * width + pair * 128, 128), 128)]

        query, key, value = part(0), part(1), part(2)
        zero = jnp.zeros_like(query)
        weights_low = masked_softmax(jnp.where(low_lanes, query, zero), key, mask).astype(bf16)
        weights_high = masked_softmax(jnp.where(low_lanes, zero, query), key, mask).astype(bf16)
        mixed_ref[:, pl.ds(pl.multiple_of(pair * 128, 128), 128)] = jnp.where(
            low_lanes, plain_dot(weights_low, value), plain_dot(weights_high, value)
        ).astype(bf16)
        return carry

    lax.fori_loop(0, HEADS // 2, attend, 0)
    residual = flat_ref[...] + plain_dot(mixed_ref[...], proj_ref[...]) + vec_ref[2:3, :]
    residual_ref[...] = residual
    normed_two, _ = norm_stats(residual)
    expert_in = (normed_two * vec_ref[3:4, :] + vec_ref[4:5, :]).astype(bf16)
    line_ref[...] = expert_in
    logits = contract_cols(expert_in, router_ref[...])
    lanes = lax.broadcasted_iota(jnp.int32, logits.shape, 1)
    logits = jnp.where(lanes < expert_count, logits, -1e30)
    shifted = jnp.exp(logits - jnp.max(logits, axis=-1, keepdims=True))
    gates_ref[...] = shifted / jnp.sum(shifted, axis=-1, keepdims=True)


def backward_kernel(
    stride,
    live_ref,
    x_ref,
    up_ref,
    packed_ref,
    mixed_ref,
    residual_ref,
    expert_ref,
    gates_ref,
    summed_ref,
    back_ref,
    qkv_ref,
    proj_ref,
    vec_ref,
    router_ref,
    block_ref,
    grad_ref,
    weight_ref,
    extra_ref,
    flat_ref,
    upstream_ref,
    attn_t_ref,
    mixed_grad_ref,
    packed_grad_ref,
    res_grad_ref,
):
    seq_length, image_count, width = x_ref.shape
    rows = flat_ref.shape[0]
    bf16 = jnp.bfloat16
    half = 3 * width // 2
    spread_rows(flat_ref, x_ref, image_count, seq_length, stride)
    upstream_ref[...] = jnp.zeros_like(upstream_ref)
    residual = residual_ref[...]
    block = residual + as_float(summed_ref[:, :width])
    for image in range(image_count):
        live = live_ref[image].astype(jnp.float32)
        here = slice(image * stride, image * stride + seq_length)
        upstream_ref[here, :] = up_ref[:, image, :] * live
        block_ref[:, image, :] = block[here, :]

    gates = gates_ref[...]
    picked = as_float(summed_ref[:, width:])
    logit_grad = gates * (picked - jnp.sum(gates * picked, axis=-1, keepdims=True))
    router_rows = extra_ref.shape[0] - VECTORS
    extra_ref[VECTORS:, :] = precise_rows(logit_grad, as_float(expert_ref[...]))[
        :router_rows
    ]
    normed_two_grad = as_float(back_ref[...]) + exact_dot(
        logit_grad, as_float(router_ref[...])
    )
    normed_two, inv_two = norm_stats(residual)
    extra_ref[3:4, :] = jnp.sum(normed_two_grad * normed_two, axis=0, keepdims=True)
    extra_ref[4:5, :] = jnp.sum(normed_two_grad, axis=0, keepdims=True)
    residual_grad = upstream_ref[...] + norm_back(
        normed_two_grad, normed_two, inv_two, vec_ref[3:4, :]
    )
    res_grad_ref[...] = residual_grad
    extra_ref[2:3, :] = jnp.sum(residual_grad, axis=0, keepdims=True)
    residual_bf = residual_grad.astype(bf16)
    proj_grad = contract_rows(mixed_ref[...], residual_bf)
    for core in range(2):
        weight_ref[core, :, half:] = proj_grad[
            :, core * (width // 2) : (core + 1) * (width // 2)
        ].astype(bf16)
    mixed_grad_ref[...] = contract_cols(residual_bf, proj_ref[...]).astype(bf16)

    mask = same_image(rows, stride, seq_length)
    low_lanes = lax.broadcasted_iota(jnp.int32, (rows, 128), 1) < HEAD_DIM

    def attend(pair, carry):
        def part(which):
            return pl.ds(pl.multiple_of(which * width + pair * 128, 128), 128)

        query, key, value = (packed_ref[:, part(which)] for which in range(3))
        mixed_grad = mixed_grad_ref[:, part(0)]
        zero = jnp.zeros_like(query)
        totals = [0.0, 0.0, 0.0]
        for high in range(2):

            def only(array_in):
                return jnp.where(low_lanes, zero if high else array_in, array_in if high else zero)

            query_half, mixed_half = only(query), only(mixed_grad)
            probs = masked_softmax(query_half, key, mask)
            prob_grad = contract_cols(mixed_half, value)
            score_grad = (
                probs
                * (prob_grad - jnp.sum(probs * prob_grad, axis=-1, keepdims=True))
                * (1.0 / math.sqrt(HEAD_DIM))
            ).astype(bf16)
            totals[0] += plain_dot(score_grad, only(key))
            totals[1] += contract_rows(score_grad, query_half)
            totals[2] += contract_rows(probs.astype(bf16), mixed_half)
        for which in range(3):
            packed_grad_ref[:, part(which)] = totals[which].astype(bf16)
        extra_ref[5:6, part(0)] = jnp.sum(totals[0], axis=0, keepdims=True)
        extra_ref[6:7, part(0)] = jnp.sum(totals[2], axis=0, keepdims=True)
        return carry

    lax.fori_loop(0, HEADS // 2, attend, 0)

    normed_one, inv_one = norm_stats(flat_ref[...])
    attn_in = normed_one * vec_ref[0:1, :] + vec_ref[1:2, :]
    attn_t_ref[...] = attn_in.T.astype(bf16)
    tile = half // 3

    def weigh(at, carry):
        src = pl.ds(pl.multiple_of(at * tile, 128), tile)
        dst = pl.ds(pl.multiple_of(lax.rem(at, 3) * tile, 128), tile)
        weight_ref[lax.div(at, 3), :, dst] = plain_dot(
            attn_t_ref[...], packed_grad_ref[:, src]
        ).astype(bf16)
        return carry

    lax.fori_loop(0, 6, weigh, 0)
    upstream_ref[...] = jnp.zeros_like(upstream_ref)

    def push_back(at, carry):
        cols = pl.ds(pl.multiple_of(at * width, 128), width)
        upstream_ref[...] += contract_cols(packed_grad_ref[:, cols], qkv_ref[:, cols])
        return carry

    lax.fori_loop(0, 3, push_back, 0)
    normed_one_grad = upstream_ref[...]
    extra_ref[0:1, :] = jnp.sum(normed_one_grad * normed_one, axis=0, keepdims=True)
    extra_ref[1:2, :] = jnp.sum(normed_one_grad, axis=0, keepdims=True)
    input_grad = res_grad_ref[...] + norm_back(
        normed_one_grad, normed_one, inv_one, vec_ref[0:1, :]
    )
    for image in range(image_count):
        grad_ref[:, image, :] = input_grad[image * stride : image * stride + seq_length, :]


def backward_reduce_kernel(shards, chips, stride, names, *refs):
    r = types.SimpleNamespace(**dict(zip(names, refs)))
    place = Place(shards, chips)
    bf16 = jnp.bfloat16
    core, chip, shard = place.core, place.chip, place.shard
    count = 2 * chips
    seq_length, image_count, width = r.x.shape
    rows = r.flat.shape[0]
    side = width // 2
    groups = 4
    piece = r.whole.shape[3]
    shard_rows = width // shards
    place.greet(
        [place.along(j) for j in range(1, shards)]
        + [place.plane(i) for i in range(1, count)]
    )
    order = (1, 3, 2)
    sent = []

    def send(copy):
        copy.start()
        sent.append(copy)

    def block_copy(j):
        cols = pl.ds(pl.multiple_of(shard * width, 128), width)
        return remote(
            r.blocks.at[lax.rem(shard + j, shards)],
            r.blocks_out.at[:, cols],
            r.block_s.at[j],
            r.block_r.at[j],
            place.along(j),
        )

    for j in order:
        send(block_copy(j))
    block_local = pltpu.make_async_copy(
        r.blocks.at[shard],
        r.blocks_out.at[:, pl.ds(pl.multiple_of(shard * width, 128), width)],
        r.here.at[0],
    )
    block_local.start()

    def twin_copy(g):
        return remote(
            r.weights.at[g, 1 - core],
            r.twin_in.at[g],
            r.twin_s.at[g],
            r.twin_r.at[g],
            place.sibling(),
        )

    def peer_copy(g, i):
        return remote(
            r.plane_sum.at[g, :, lax.rem(chip + i, chips)],
            r.peer_in.at[g, i],
            r.peer_s.at[g, i],
            r.peer_r.at[g, i],
            place.peer(i),
        )

    def far_copy(g, j):
        return remote(
            r.far_out.at[g, lax.rem(shard + j, shards)],
            r.far_in.at[g, j],
            r.far_s.at[g, j],
            r.far_r.at[g, j],
            place.along(j),
        )

    def back_copy(g, i):
        block = r.whole.at[g, core, chip]
        return remote(block, block, r.back_s.at[g, i], r.back_r.at[g, i], place.peer(i))

    def last_copy(g, i):
        block = r.whole.at[g, core, lax.rem(chip - i + chips, chips)]
        return remote(block, block, r.last_s.at[g, i], r.last_r.at[g, i], place.sibling())

    def small_copy(i):
        return remote(
            r.small, r.small_in.at[i], r.small_s.at[i], r.small_r.at[i], place.plane(i)
        )

    def edge_copy(j):
        return remote(
            r.small_sum, r.small_far.at[j], r.edge_s.at[j], r.edge_r.at[j], place.along(j)
        )

    def store_group(g, half, value):
        r.weights[g, half] = value.astype(bf16).reshape(shards, chips, piece, side)

    def to_plane(g):
        twin_copy(g).wait_recv()
        for at in range(shards):
            r.plane_sum[g, at] = (
                as_float(r.weights[g, core, at]) + as_float(r.twin_in[g, at])
            ).astype(bf16)
        for i in range(1, chips):
            send(peer_copy(g, i))

    def to_far(g):
        mine = as_float(r.plane_sum[g, :, chip])
        for i in range(1, chips):
            peer_copy(g, i).wait_recv()
            mine += as_float(r.peer_in[g, i])
        r.far_out[g] = mine.astype(bf16)
        for j in order:
            send(far_copy(g, j))

    def to_back(g):
        mine = as_float(r.far_out[g, shard])
        for j in order:
            far_copy(g, j).wait_recv()
            mine += as_float(r.far_in[g, j])
        r.whole[g, core, chip] = mine.astype(bf16)
        for i in range(1, chips):
            send(back_copy(g, i))
        send(last_copy(g, 0))

    spread_rows(r.flat, r.grad, image_count, seq_length, stride)
    residual = r.residual[...]
    block = residual + r.summed[:, :width]
    for image in range(image_count):
        alive = r.live[image].astype(jnp.float32)
        here = slice(image * stride, image * stride + seq_length)
        r.upstream[image * stride : (image + 1) * stride, :] = (
            r.flat[image * stride : (image + 1) * stride, :] * alive
        )
        r.block_out[:, image, :] = block[here, :]
    gates = r.gates[...]
    picked = r.summed[:, width:]
    logit_grad = gates * (picked - jnp.sum(gates * picked, axis=-1, keepdims=True))
    normed_two_grad = r.route[...] + exact_dot(logit_grad, as_float(r.router[...]))
    normed_two, inv_two = norm_stats(residual)
    residual_grad = r.upstream[...] + norm_back(
        normed_two_grad, normed_two, inv_two, r.vectors[3:4, :]
    )
    r.res_grad[...] = residual_grad
    residual_bf = residual_grad.astype(bf16)
    proj_grad = contract_rows(r.mixed[...], residual_bf)
    for half in range(2):
        store_group(0, half, proj_grad[:, half * side : (half + 1) * side])
    send(twin_copy(0))
    r.mixed_grad[...] = contract_cols(residual_bf, r.proj[...]).astype(bf16)
    router_rows = r.totals.shape[0] - VECTORS
    r.totals[VECTORS:, :] = precise_rows(logit_grad, as_float(r.tokens[...]))[:router_rows]
    r.totals[2:3, :] = jnp.sum(residual_grad, axis=0, keepdims=True)
    r.totals[3:4, :] = jnp.sum(normed_two_grad * normed_two, axis=0, keepdims=True)
    r.totals[4:5, :] = jnp.sum(normed_two_grad, axis=0, keepdims=True)
    spread_rows(r.flat, r.x, image_count, seq_length, stride)
    normed_one, inv_one = norm_stats(r.flat[...])
    attn_in = normed_one * r.vectors[0:1, :] + r.vectors[1:2, :]
    r.attn_t[...] = attn_in.T.astype(bf16)
    r.flat[...] = normed_one

    mask = same_image(rows, stride, seq_length)
    low_lanes = lax.broadcasted_iota(jnp.int32, (rows, 128), 1) < HEAD_DIM

    def attend(pair, carry):
        def part(which):
            return pl.ds(pl.multiple_of(which * width + pair * 128, 128), 128)

        query, key, value = (r.packed[:, part(which)] for which in range(3))
        mixed_grad = r.mixed_grad[:, part(0)]
        zero = jnp.zeros_like(query)
        totals = [0.0, 0.0, 0.0]
        for high in range(2):

            def only(array_in):
                return jnp.where(low_lanes, zero if high else array_in, array_in if high else zero)

            query_half, mixed_half = only(query), only(mixed_grad)
            probs = masked_softmax(query_half, key, mask)
            prob_grad = contract_cols(mixed_half, value)
            score_grad = (
                probs
                * (prob_grad - jnp.sum(probs * prob_grad, axis=-1, keepdims=True))
                * (1.0 / math.sqrt(HEAD_DIM))
            ).astype(bf16)
            totals[0] += plain_dot(score_grad, only(key))
            totals[1] += contract_rows(score_grad, query_half)
            totals[2] += contract_rows(probs.astype(bf16), mixed_half)
        for which in range(3):
            r.packed_grad[:, part(which)] = totals[which].astype(bf16)
        r.totals[5:6, part(0)] = jnp.sum(totals[0], axis=0, keepdims=True)
        r.totals[6:7, part(0)] = jnp.sum(totals[2], axis=0, keepdims=True)
        return carry

    pairs = width // 128
    lax.fori_loop(0, pairs // 2, attend, 0)
    to_plane(0)
    lax.fori_loop(pairs // 2, pairs, attend, 0)
    for g in range(1, groups):
        for half in (1 - core, core):
            cols = pl.ds(pl.multiple_of((g - 1) * width + half * side, 128), side)
            store_group(g, half, plain_dot(r.attn_t[...], r.packed_grad[:, cols]))
            if half is not core:
                send(twin_copy(g))
        if g > 1:
            to_plane(g - 1)
    to_plane(groups - 1)

    r.upstream[...] = jnp.zeros_like(r.upstream)

    def push_back(at, carry):
        cols = pl.ds(pl.multiple_of(at * width, 128), width)
        r.upstream[...] += contract_cols(r.packed_grad[:, cols], r.qkv[:, cols])
        return carry

    lax.fori_loop(0, 3, push_back, 0)
    normed_one_grad = r.upstream[...]
    normed_one = r.flat[...]
    r.totals[0:1, :] = jnp.sum(normed_one_grad * normed_one, axis=0, keepdims=True)
    r.totals[1:2, :] = jnp.sum(normed_one_grad, axis=0, keepdims=True)
    r.small[...] = r.totals[...].astype(bf16)
    for i in range(1, count):
        send(small_copy(i))
    to_far(0)
    input_grad = r.res_grad[...] + norm_back(
        normed_one_grad, normed_one, inv_one, r.vectors[0:1, :]
    )
    for image in range(image_count):
        r.grad_out[:, image, :] = input_grad[image * stride : image * stride + seq_length, :]
    to_far(1)
    to_back(0)
    total = as_float(r.small[...])
    for i in range(1, count):
        small_copy(i).wait_recv()
        total += as_float(r.small_in[i])
    r.small_sum[...] = total.astype(bf16)
    for j in order:
        send(edge_copy(j))
    to_far(2)
    to_back(1)
    to_far(3)
    to_back(2)
    total = as_float(r.small_sum[...])
    for j in order:
        edge_copy(j).wait_recv()
        total += as_float(r.small_far[j])

    def cut(values, start, size):
        lane_from = lax.broadcasted_iota(jnp.int32, (width, size), 0)
        lane_to = lax.broadcasted_iota(jnp.int32, (width, size), 1)
        return exact_dot(values, jnp.where(lane_from == lane_to + start, 1.0, 0.0))

    r.small_out[...] = cut(total, shard * shard_rows, r.small_out.shape[1])
    low = jnp.broadcast_to(total[5:6], (8, width))
    high = jnp.broadcast_to(total[6:7], (8, width))
    which = jnp.where(lax.div(shard, shards // 2) == 0, low, high)
    r.bias_out[...] = cut(which, lax.rem(shard, shards // 2) * side, side)[:1]

    def forward_last(g):
        for i in range(1, chips):
            back_copy(g, i).wait_recv()
            send(last_copy(g, i))

    for g in range(groups - 1):
        forward_last(g)
    to_back(groups - 1)
    forward_last(groups - 1)
    for g in range(groups):
        for i in range(chips):
            last_copy(g, i).wait_recv()
        for half in range(2):
            for at in range(chips):
                here = slice(at * piece, (at + 1) * piece)
                cols = slice(half * side, (half + 1) * side)
                if g == 0:
                    r.proj_out[here, cols] = r.whole[g, half, at]
                else:
                    start = (g - 1) * width + half * side
                    r.qkv_out[here, start : start + side] = r.whole[g, half, at]
    block_local.wait()
    for j in order:
        block_copy(j).wait_recv()
    for copy in sent:
        copy.wait_send()


def backward_reduce(shards, chips, stride, inputs):
    x, packed, blocks = inputs[1], inputs[3], inputs[14]
    rows, width = packed.shape[0], x.shape[2]
    shard_rows = width // shards
    piece = shard_rows // chips
    side = width // 2
    expert_count = 2 * chips
    small_rows = round_up(VECTORS + expert_count, 16)
    bf16, f32, dma = jnp.bfloat16, jnp.float32, pltpu.SemaphoreType.DMA
    vmem, anywhere = pl.BlockSpec(memory_space=pltpu.VMEM), pl.BlockSpec(memory_space=pl.ANY)

    def shape(dims, kind=bf16):
        return jax.ShapeDtypeStruct(dims, kind)

    smem = pl.BlockSpec(memory_space=pltpu.SMEM)
    ins = dict(
        live=smem,
        x=vmem,
        grad=vmem,
        packed=vmem,
        mixed=vmem,
        residual=vmem,
        tokens=vmem,
        gates=vmem,
        summed=vmem,
        route=vmem,
        qkv=vmem,
        proj=vmem,
        vectors=vmem,
        router=vmem,
        blocks=anywhere,
    )
    outs = dict(
        block_out=shape(x.shape, f32),
        grad_out=shape(x.shape, f32),
        qkv_out=shape((shard_rows, 3 * width)),
        proj_out=shape((shard_rows, width)),
        small_out=shape((small_rows, round_up(shard_rows, 128)), f32),
        bias_out=shape((1, side), f32),
        blocks_out=shape((shard_rows, shards * width)),
    )
    scratch = dict(
        flat=pltpu.VMEM((rows, width), f32),
        upstream=pltpu.VMEM((rows, width), f32),
        res_grad=pltpu.VMEM((rows, width), f32),
        attn_t=pltpu.VMEM((width, rows), bf16),
        mixed_grad=pltpu.VMEM((rows, width), bf16),
        packed_grad=pltpu.VMEM((rows, 3 * width), bf16),
        totals=pltpu.VMEM((small_rows, width), f32),
        weights=pltpu.VMEM((4, 2, shards, chips, piece, side), bf16),
        twin_in=pltpu.VMEM((4, shards, chips, piece, side), bf16),
        plane_sum=pltpu.VMEM((4, shards, chips, piece, side), bf16),
        peer_in=pltpu.VMEM((4, chips, shards, piece, side), bf16),
        far_out=pltpu.VMEM((4, shards, piece, side), bf16),
        far_in=pltpu.VMEM((4, shards, piece, side), bf16),
        whole=pltpu.VMEM((4, 2, chips, piece, side), bf16),
        small=pltpu.VMEM((small_rows, width), bf16),
        small_in=pltpu.VMEM((2 * chips, small_rows, width), bf16),
        small_sum=pltpu.VMEM((small_rows, width), bf16),
        small_far=pltpu.VMEM((shards, small_rows, width), bf16),
        here=dma((1,)),
    )
    pairs = dict(
        block=(shards,),
        twin=(4,),
        peer=(4, chips),
        far=(4, shards),
        back=(4, chips),
        last=(4, chips),
        small=(2 * chips,),
        edge=(shards,),
    )
    for name, dims in pairs.items():
        scratch[name + "_s"] = dma(dims)
        scratch[name + "_r"] = dma(dims)
    names = tuple(ins) + tuple(outs) + tuple(scratch)
    return pl.pallas_call(
        functools.partial(backward_reduce_kernel, shards, chips, stride, names),
        out_shape=list(outs.values()),
        in_specs=list(ins.values()),
        out_specs=[vmem] * 6 + [anywhere],
        scratch_shapes=list(scratch.values()),
        compiler_params=pltpu.CompilerParams(
            collective_id=2, has_side_effects=True, vmem_limit_bytes=BIG_VMEM
        ),
        name="backward_and_reduce",
    )(*inputs)


def reduce_slow(grads, extra, blocks):
    width = grads.shape[2] // 2
    wide = 3 * width // 2
    joined = jnp.concatenate(
        [grads[0, :, :wide], grads[1, :, :wide], grads[0, :, wide:], grads[1, :, wide:]],
        axis=1,
    )
    mine = lax.psum_scatter(joined, "shard", scatter_dimension=0, tiled=True)
    mine = as_float(lax.psum(mine, "expert"))
    extra_sum = as_float(lax.psum(extra, ("shard", "expert")))
    moved = lax.all_to_all(blocks, "shard", split_axis=0, concat_axis=0, tiled=True)
    return mine[:, : 3 * width], mine[:, 3 * width :], extra_sum, moved


def attention_core(stride, expert_count, r):
    rows, width = r.flat.shape
    bf16 = jnp.bfloat16
    mask = same_image(rows, stride, r.x.shape[0])
    low_lanes = lax.broadcasted_iota(jnp.int32, (rows, 128), 1) < HEAD_DIM

    def attend(pair, carry):
        def part(which):
            return r.packed[:, pl.ds(pl.multiple_of(which * width + pair * 128, 128), 128)]

        query, key, value = part(0), part(1), part(2)
        zero = jnp.zeros_like(query)
        weights_low = masked_softmax(jnp.where(low_lanes, query, zero), key, mask).astype(bf16)
        weights_high = masked_softmax(jnp.where(low_lanes, zero, query), key, mask).astype(bf16)
        r.mixed[:, pl.ds(pl.multiple_of(pair * 128, 128), 128)] = jnp.where(
            low_lanes, plain_dot(weights_low, value), plain_dot(weights_high, value)
        ).astype(bf16)
        return carry

    lax.fori_loop(0, HEADS // 2, attend, 0)


def route_core(expert_count, r, proj):
    bf16 = jnp.bfloat16
    residual = r.flat[...] + plain_dot(r.mixed[...], proj) + r.vectors[2:3, :]
    r.residual[...] = residual
    normed_two, _ = norm_stats(residual)
    expert_in = (normed_two * r.vectors[3:4, :] + r.vectors[4:5, :]).astype(bf16)
    r.tokens[...] = expert_in
    r.gates[...] = softmax_gates(expert_in, r.router[...], expert_count)


def softmax_gates(rows, router, expert_count):
    logits = contract_cols(rows, router)
    lanes = lax.broadcasted_iota(jnp.int32, logits.shape, 1)
    logits = jnp.where(lanes < expert_count, logits, -1e30)
    shifted = jnp.exp(logits - jnp.max(logits, axis=-1, keepdims=True))
    return shifted / jnp.sum(shifted, axis=-1, keepdims=True)


def fused_kernel(shards, experts, capacity, expert_count, stride, names, *refs):
    r = types.SimpleNamespace(**dict(zip(names, refs)))
    chips = experts // 2
    place = Place(shards, chips)
    bf16 = jnp.bfloat16
    me, shard = place.expert, place.shard
    row_count, width = r.tokens.shape
    group_rows = r.rows_in.shape[1]
    shard_rows = r.qkv.shape[0]
    seq_length, image_count = r.x.shape[:2]
    first_rows = 2 * capacity // 16 * 16
    second_rows = group_rows - first_rows
    upper = lax.div(shard, 2)
    even = lax.rem(shard, 2) == 0
    place.greet(
        [place.along(j) for j in range(1, shards)]
        + [place.plane(i) for i in range(1, experts)]
    )
    order = (1, 3, 2)
    spans = (
        (upper * second_rows, first_rows),
        ((1 - upper) * first_rows, second_rows),
    )

    def with_pair(act):
        @pl.when(even)
        def _():
            act(3)

        @pl.when(jnp.logical_not(even))
        def _():
            act(1)

    def push_pair(copy):
        @pl.when(even)
        def _():
            copy(1).start()

        @pl.when(jnp.logical_not(even))
        def _():
            copy(3).start()

    def push_others(copy):
        with_pair(lambda j: copy(j).start())
        copy(2).start()

    def wait_others(copy):
        @pl.when(even)
        def _():
            copy(1).wait_recv()

        @pl.when(jnp.logical_not(even))
        def _():
            copy(3).wait_recv()

        copy(2).wait_recv()

    kinds = ((r.qkv, r.qkv_all), (r.proj, r.proj_all))

    def target(i):
        return lax.rem(me + i, experts)

    def origin(i):
        return lax.rem(me - i + experts, experts)

    def owner(j):
        return lax.rem(shard - j + shards, shards)

    def cut(kind, chip_step):
        source = kinds[kind][0]
        rows = source.shape[0] // chips
        cols = source.shape[1] // 2
        chip = lax.rem(place.chip + chip_step + chips, chips)
        return (
            pl.ds(pl.multiple_of(chip * rows, 16), rows),
            pl.ds(pl.multiple_of(place.core * cols, 128), cols),
        )

    def far_copy(kind, j):
        rows, cols = cut(kind, 0)
        return remote(
            kinds[kind][0].at[rows, cols],
            kinds[kind][1].at[shard, rows, cols],
            r.far_s.at[kind, j],
            r.far_r.at[kind, j],
            place.along(j),
        )

    def to_twin(kind, j, i):
        rows, cols = cut(kind, -i)
        block = kinds[kind][1].at[owner(j), rows, cols]
        return remote(
            block, block, r.twin_s.at[kind, j, i], r.twin_r.at[kind, j, i], place.sibling()
        )

    def to_peer(kind, j, i):
        rows, cols = cut(kind, 0)
        block = kinds[kind][1].at[owner(j), rows, cols]
        return remote(
            block, block, r.peer_s.at[kind, j, i], r.peer_r.at[kind, j, i], place.peer(i)
        )

    def small_copy(which, j):
        src, dst = ((r.extra, r.extra_all), (r.slots, r.slots_all))[which]
        return remote(
            src, dst.at[shard], r.small_s.at[which, j], r.small_r.at[which, j], place.along(j)
        )

    def up_line_copy(j):
        return remote(
            r.up, r.up_line.at[shard], r.upline_s.at[j], r.upline_r.at[j], place.along(j)
        )

    r.extra[...] = jnp.zeros_like(r.extra)
    r.extra[:expert_count, :shard_rows] = r.router_part[...]
    r.extra[expert_count : expert_count + VECTORS, :shard_rows] = r.rows7[...]
    for j in order:
        small_copy(0, j).start()
    for kind in range(2):
        for j in order:
            far_copy(kind, j).start()
    local = [
        pltpu.make_async_copy(r.qkv, r.qkv_all.at[shard], r.here.at[0]),
        pltpu.make_async_copy(r.proj, r.proj_all.at[shard], r.here.at[1]),
    ]
    for copy in local:
        copy.start()
    r.extra_all[shard] = r.extra[...]
    spread_rows(r.flat, r.grad, image_count, seq_length, stride)
    r.slot_col[...] = jnp.zeros_like(r.slot_col) - 1.0
    for image in range(image_count):
        here = slice(image * stride, (image + 1) * stride)
        alive = r.live[image].astype(jnp.float32)
        r.up[here, :] = (r.flat[here, :] * alive).astype(bf16)
        r.turn[...] = jnp.zeros_like(r.turn)
        r.turn[0:2, :seq_length] = r.routes[image].astype(jnp.float32)
        named = r.turn[...].T[:seq_length]
        r.slot_col[image * stride : image * stride + seq_length, 0:8] = (
            named * alive - (1.0 - alive)
        )
    lanes = lax.broadcasted_iota(jnp.int32, (row_count, 128), 1)
    lane_ids = lanes.astype(jnp.float32)
    first, second = (r.slot_col[:row_count, k : k + 1] for k in range(2))
    chosen = (lane_ids == first) | (lane_ids == second)
    earlier = lax.broadcasted_iota(jnp.int32, (row_count, row_count), 0) > (
        lax.broadcasted_iota(jnp.int32, (row_count, row_count), 1)
    )
    place_in = plain_dot(
        jnp.where(earlier, 1.0, 0.0).astype(bf16), jnp.where(chosen, 1.0, 0.0).astype(bf16)
    )
    place_in += lane_ids * group_rows + (shard * capacity).astype(jnp.float32)
    both = jnp.zeros((row_count, 128), jnp.float32)
    for k, named in enumerate((first, second)):
        slot = jnp.sum(jnp.where(lane_ids == named, place_in, 0.0), axis=-1, keepdims=True)
        both += jnp.where(lanes == k, jnp.where(named < 0.0, -1.0, slot), 0.0)
    r.slots[...] = jnp.zeros_like(r.slots)
    r.slots[:, :row_count] = both.T[:8]
    for j in order:
        small_copy(1, j).start()
    r.slots_all[shard] = r.slots[...]
    r.up_line[shard] = r.up[...]
    spread_rows(r.flat, r.x, image_count, seq_length, stride)

    for kind in range(2):
        for j in order:
            far_copy(kind, j).wait_recv()
            for i in range(1, chips):
                to_peer(kind, j, i).start()
            to_twin(kind, j, 0).start()
    push_pair(up_line_copy)

    for j in order:
        small_copy(0, j).wait_recv()
    lane_from = lax.broadcasted_iota(jnp.int32, (r.extra.shape[1], width), 0)
    lane_to = lax.broadcasted_iota(jnp.int32, (r.extra.shape[1], width), 1)

    def placed(source, at):
        hit = (lane_to == lane_from + at * shard_rows) & (lane_from < shard_rows)
        return plain_dot(r.extra_all[source], jnp.where(hit, 1.0, 0.0).astype(bf16))

    whole = placed(0, 0)
    for at in range(1, shards):
        whole += placed(at, at)
    r.vectors[...] = whole[expert_count : expert_count + 8]
    r.router[...] = jnp.zeros_like(r.router)
    r.router[:expert_count, :] = whole[:expert_count].astype(bf16)
    biases = []
    for first in (0, shards // 2):
        total = jnp.zeros((1, width), jnp.float32)
        for at in range(shards):
            row = expert_count + VECTORS - 2 + at % 2
            total += placed(first + at // 2, at)[row : row + 1]
        biases.append(total)
    hit = (lane_to == lane_from + shard * shard_rows) & (lane_from < shard_rows)
    own_bias = plain_dot(
        jnp.broadcast_to(as_float(r.out_bias[...]), (16, shard_rows)).astype(bf16),
        jnp.where(hit, 1.0, 0.0).astype(bf16)[:shard_rows],
    )
    r.own_bias[...] = own_bias[:8]
    normed, _ = norm_stats(r.flat[...])
    r.attn[...] = (normed * r.vectors[0:1, :] + r.vectors[1:2, :]).astype(bf16)

    push_others(up_line_copy)
    for kind in range(2):
        for j in order:
            for i in range(1, chips):
                to_peer(kind, j, i).wait_recv()
                to_twin(kind, j, i).start()

    for j in order:
        small_copy(1, j).wait_recv()
    for at in range(shards):
        r.slot_col[at * row_count : (at + 1) * row_count, 0:8] = r.slots_all[at].T[:row_count]

    def table(at, base, size):
        ids = (lax.broadcasted_iota(jnp.int32, (size, row_count), 0) + base).astype(jnp.float32)
        slots = r.slots_all[at]
        hit = (ids == slots[0:1, :row_count]) | (ids == slots[1:2, :row_count])
        return jnp.where(hit, 1.0, 0.0).astype(bf16)

    def slot_copy(stage, landing, send_sems, recv_sems, i, part):
        start, size = spans[part]
        here = pl.ds(pl.multiple_of(start, 16), size)
        return remote(
            stage.at[target(i), here],
            landing.at[me, here],
            send_sems.at[i, part],
            recv_sems.at[i, part],
            place.plane(i),
        )

    def up_copy(i, part):
        return slot_copy(r.stage_a, r.up_in, r.up_s, r.up_r, i, part)

    def row_copy(i, part):
        return slot_copy(r.stage_b, r.rows_in, r.row_s, r.row_r, i, part)

    def dispatch(part, sources, line, stage, landing, copy):
        start, size = spans[part]
        here = pl.ds(pl.multiple_of(start, 16), size)

        def one(i, carry):
            to = target(i)
            base = to * group_rows + start
            picked = plain_dot(table(sources[0], base, size), line[sources[0]])
            for at in sources[1:]:
                picked += plain_dot(table(at, base, size), line[at])
            picked = picked.astype(bf16)

            @pl.when(i == 0)
            def _():
                landing[me, here, :] = picked

            @pl.when(i > 0)
            def _():
                stage[to, here, :] = picked
                copy(i, part).start()

            return carry

        lax.fori_loop(0, experts, one, 0)

    pair_planes = (2 * upper, 2 * upper + 1)
    all_planes = tuple(range(shards))
    with_pair(lambda j: up_line_copy(j).wait_recv())
    dispatch(0, pair_planes, r.up_line, r.stage_a, r.up_in, up_copy)

    hidden = r.in_w.shape[1]

    def weight_copy(j, part):
        part_cols = hidden // 2
        start = lax.rem(shard + j, shards) * hidden + part * part_cols
        rows = pl.ds(pl.multiple_of(shard * shard_rows, 16), shard_rows)
        return remote(
            r.out_wt.at[:, pl.ds(pl.multiple_of(start, 128), part_cols)],
            r.out_w.at[rows, pl.ds(part * part_cols, part_cols)],
            r.weight_s.at[j, part],
            r.weight_r.at[j, part],
            place.along(j),
        )

    weight_local = pltpu.make_async_copy(
        r.out_wt.at[:, pl.ds(pl.multiple_of(shard * hidden, 128), hidden)],
        r.out_w.at[pl.ds(pl.multiple_of(shard * shard_rows, 16), shard_rows)],
        r.here.at[2],
    )
    weight_local.start()
    for copy in local:
        copy.wait()
    for j in order:
        for i in range(chips):
            to_twin(0, j, i).wait_recv()

    def project(tile, carry):
        cols = pl.ds(pl.multiple_of(tile * width, 128), width)
        weight = r.qkv_all[:, :, cols].reshape(width, width)
        bias = jnp.where(tile == 0, biases[0], jnp.where(tile == 2, biases[1], 0.0))
        r.packed[:, cols] = (plain_dot(r.attn[...], weight) + bias).astype(bf16)
        return carry

    lax.fori_loop(0, 3, project, 0)
    wait_others(up_line_copy)
    for j in order:
        weight_copy(j, 0).start()
    dispatch(1, all_planes, r.up_line, r.stage_a, r.up_in, up_copy)
    attention_core(stride, expert_count, r)
    for j in order:
        for i in range(chips):
            to_twin(1, j, i).wait_recv()
    route_core(expert_count, r, r.proj_all[...].reshape(width, width))

    def line_copy(j):
        return remote(
            r.tokens, r.line.at[shard], r.line_s.at[j], r.line_r.at[j], place.along(j)
        )

    push_pair(line_copy)
    r.line[shard] = r.tokens[...]

    with_pair(lambda j: line_copy(j).wait_recv())
    push_others(line_copy)
    dispatch(0, pair_planes, r.line, r.stage_b, r.rows_in, row_copy)
    wait_others(line_copy)
    for j in order:
        weight_copy(j, 1).start()
    dispatch(1, all_planes, r.line, r.stage_b, r.rows_in, row_copy)

    def keep_table(at, carry):
        ids = lax.broadcasted_iota(jnp.int32, (shards * row_count, group_rows), 1)
        ids = (ids + at * group_rows).astype(jnp.float32)
        hit = (ids == r.slot_col[:, 0:1]) | (ids == r.slot_col[:, 1:2])
        r.tables[at] = jnp.where(hit, 1.0, 0.0).astype(bf16)
        return carry

    lax.fori_loop(0, experts, keep_table, 0)

    half, third = width // 2, width // 3

    def out_copy(i, part):
        cols = pl.ds(part * half, half)
        return remote(
            r.stage_a.at[origin(i), :, cols],
            r.out_in.at[me, :, cols],
            r.out_s.at[i, part],
            r.out_r.at[i, part],
            place.plane(experts - i),
        )

    def note_copy(i):
        return remote(
            r.notes.at[origin(i)],
            r.note_in.at[me],
            r.note_s.at[i],
            r.note_r.at[i],
            place.plane(experts - i),
        )

    def back_copy(i, part):
        cols = pl.ds(part * third, third)
        return remote(
            r.stage_b.at[origin(i), :, cols],
            r.back_in.at[me, :, cols],
            r.back_s.at[i, part],
            r.back_r.at[i, part],
            place.plane(experts - i),
        )

    weight_local.wait()
    for j in order:
        for part in range(2):
            weight_copy(j, part).wait_recv()

    def drain_up(i, carry):
        for part in range(2):
            up_copy(i, part).wait_send()
        return carry

    lax.fori_loop(1, experts, drain_up, 0)
    r.notes[...] = jnp.zeros_like(r.notes)

    def forward(i, carry):
        at = origin(i)

        @pl.when(i > 0)
        def _():
            for part in range(2):
                row_copy(i, part).wait_recv()

        rows = r.rows_in[at]
        gelu_out, gelu_slope = gelu_parts(
            plain_dot(rows, r.in_w[...]) + as_float(r.in_bias[...])
        )
        r.slope[at] = gelu_slope
        gelu_bf = gelu_out.astype(bf16)
        r.gelu[at] = gelu_bf
        gates = softmax_gates(rows, r.router[...], expert_count)
        gate_lanes = lax.broadcasted_iota(jnp.int32, gates.shape, 1)
        gate = jnp.sum(jnp.where(gate_lanes == me, gates, 0.0), axis=-1, keepdims=True)

        @pl.when(i > 0)
        def _():
            for part in range(2):
                up_copy(i, part).wait_recv()

        upstream = as_float(r.up_in[at])
        r.sent[at] = (gate * upstream).astype(bf16)
        expert_out = contract_cols(gelu_bf, r.out_w[...]) + r.own_bias[0:1, :]
        gate_grad = jnp.sum(upstream * expert_out, axis=-1, keepdims=True)
        notes = jnp.broadcast_to(gate_grad, (group_rows, 128)).T[:16].astype(bf16)
        gated = (gate * expert_out).astype(bf16)

        @pl.when(i == 0)
        def _():
            r.out_in[me] = gated
            r.note_in[me, :, :group_rows] = notes

        @pl.when(i > 0)
        def _():
            r.stage_a[at] = gated
            r.notes[at, :, :group_rows] = notes
            out_copy(i, 0).start()
            note_copy(i).start()

        return carry

    lax.fori_loop(0, experts, forward, 0)

    def push_out(i, carry):
        out_copy(i, 1).start()
        return carry

    lax.fori_loop(1, experts, push_out, 0)
    r.in_bias_grad[...] = jnp.zeros_like(r.in_bias_grad)
    r.out_bias_grad[...] = jnp.zeros_like(r.out_bias_grad)

    def drain_rows(i, carry):
        for part in range(2):
            row_copy(i, part).wait_send()
        return carry

    lax.fori_loop(1, experts, drain_rows, 0)

    def backward(i, carry):
        at = origin(i)
        sent = r.sent[at]
        r.out_bias_grad[0:1, :] += jnp.sum(as_float(sent), axis=0, keepdims=True)
        pre_grad = plain_dot(sent, r.out_w[...]) * r.slope[at]
        r.in_bias_grad[0:1, :] += jnp.sum(pre_grad, axis=0, keepdims=True)
        pre_bf = pre_grad.astype(bf16)
        r.pre[at] = pre_bf
        back = contract_cols(pre_bf, r.in_w[...]).astype(bf16)

        @pl.when(i == 0)
        def _():
            r.back_in[me] = back

        @pl.when(i > 0)
        def _():
            r.stage_b[at] = back
            back_copy(i, 0).start()

        return carry

    lax.fori_loop(0, experts, backward, 0)

    for part in range(1, 3):

        def push_rest(i, carry, part=part):
            back_copy(i, part).start()
            return carry

        lax.fori_loop(1, experts, push_rest, 0)

    def collect(landing, copy, part, size):
        cols = pl.ds(part * size, size)

        def one(i, carry):
            at = target(i)

            @pl.when(i > 0)
            def _():
                copy(i, part).wait_recv()

            r.total[:, cols] += plain_dot(r.tables[at], landing[at, :, cols])
            return carry

        lax.fori_loop(0, experts, one, 0)

    def collect_notes(i, carry):
        at = target(i)

        @pl.when(i > 0)
        def _():
            note_copy(i).wait_recv()

        rows_at = lax.broadcasted_iota(jnp.int32, (128, group_rows), 0)
        note = as_float(r.note_in[at, 0:1, :group_rows])
        r.total[:, width:] += contract_cols(
            r.tables[at], jnp.where(rows_at == at, note, 0.0).astype(bf16)
        )
        return carry

    columns = ((0, half), (half, half)) + tuple((at * third, third) for at in range(3))

    def sum_copy(which, j):
        src, dst = (r.far_out, r.far_out_in) if which < 2 else (r.far_back, r.far_back_in)
        to = lax.rem(shard + j, shards)
        cols = pl.ds(*columns[which])
        return remote(
            src.at[to, :, cols],
            dst.at[j, :, cols],
            r.sum_s.at[which, j],
            r.sum_r.at[which, j],
            place.along(j),
        )

    def note_sum_copy(j):
        return remote(
            r.note_far.at[lax.rem(shard + j, shards)],
            r.note_far_in.at[j],
            r.notesum_s.at[j],
            r.notesum_r.at[j],
            place.along(j),
        )

    own = pl.ds(pl.multiple_of(shard * row_count, 16), row_count)

    def spread_sums(which):
        far = r.far_out if which < 2 else r.far_back
        cols = pl.ds(*columns[which])
        for at in range(shards):
            far[at, :, cols] = r.total[at * row_count : (at + 1) * row_count, cols].astype(bf16)
        for j in order:
            sum_copy(which, j).start()

    def weigh(left, right, grad):
        tile = 128

        def one(at, carry):
            cols = pl.ds(pl.multiple_of(at * tile, 128), tile)
            lhs = left[:, :, cols].reshape(experts * group_rows, tile)
            rhs = right[...].reshape(experts * group_rows, right.shape[2])
            grad[cols, :] = contract_rows(lhs, rhs).astype(grad.dtype)
            return carry

        lax.fori_loop(0, left.shape[2] // tile, one, 0)

    r.total[...] = jnp.zeros_like(r.total)
    collect(r.out_in, out_copy, 0, half)
    spread_sums(0)
    lax.fori_loop(0, experts, collect_notes, 0)
    r.note_far[...] = jnp.zeros_like(r.note_far)
    for at in range(shards):
        notes = r.total[at * row_count : (at + 1) * row_count, width:].T
        r.note_far[at, :, :row_count] = notes[: r.note_far.shape[1]].astype(bf16)
    for j in order:
        note_sum_copy(j).start()
    weigh(r.sent, r.gelu, r.out_grad)
    collect(r.out_in, out_copy, 1, half)
    spread_sums(1)
    r.summed[...] = r.total[own, :]
    weigh(r.rows_in, r.pre, r.in_grad)
    r.total[...] = jnp.zeros_like(r.total)
    for part in range(3):
        collect(r.back_in, back_copy, part, third)
        spread_sums(2 + part)
    r.route[...] = r.total[own, :width]
    for j in order:
        note_sum_copy(j).wait_recv()
        notes = as_float(r.note_far_in[j]).T
        lanes_in = notes.shape[1]
        r.summed[:, width : width + lanes_in] += notes[:row_count]
    for which in range(5):
        cols = pl.ds(*columns[which])
        for j in order:
            sum_copy(which, j).wait_recv()
            if which < 2:
                r.summed[:, cols] += as_float(r.far_out_in[j, :, cols])
            else:
                r.route[:, cols] += as_float(r.far_back_in[j, :, cols])

    for j in order:
        for which in range(2):
            far_copy(which, j).wait_send()
            small_copy(which, j).wait_send()
            for i in range(chips):
                to_twin(which, j, i).wait_send()
                if i:
                    to_peer(which, j, i).wait_send()
        for which in range(5):
            sum_copy(which, j).wait_send()
        note_sum_copy(j).wait_send()
        up_line_copy(j).wait_send()
        line_copy(j).wait_send()
        for part in range(2):
            weight_copy(j, part).wait_send()

    def finish(i, carry):
        out_copy(i, 0).wait_send()
        out_copy(i, 1).wait_send()
        note_copy(i).wait_send()
        for part in range(3):
            back_copy(i, part).wait_send()
        return carry

    lax.fori_loop(1, experts, finish, 0)


def fused_pass(shards, experts, capacity, expert_count, stride, inputs):
    x, qkv, proj, in_w = (inputs[at] for at in (1, 4, 5, 8))
    extra_shape = (round_up(VECTORS + expert_count, 16), round_up(qkv.shape[0], 128))
    width, hidden = in_w.shape
    row_count = x.shape[1] * stride
    router_pad = round_up(expert_count, 128)
    group_rows = round_up(shards * capacity, 16)
    lanes = round_up(group_rows, 128)
    chips = experts // 2
    bf16, f32, dma = jnp.bfloat16, jnp.float32, pltpu.SemaphoreType.DMA
    vmem, anywhere = pl.BlockSpec(memory_space=pltpu.VMEM), pl.BlockSpec(memory_space=pl.ANY)

    def shape(dims, kind=bf16):
        return jax.ShapeDtypeStruct(dims, kind)

    smem = pl.BlockSpec(memory_space=pltpu.SMEM)
    ins = dict(
        live=smem,
        x=vmem,
        grad=vmem,
        routes=vmem,
        qkv=anywhere,
        proj=anywhere,
        rows7=vmem,
        router_part=vmem,
        in_w=vmem,
        out_wt=anywhere,
        in_bias=vmem,
        out_bias=vmem,
    )
    outs = dict(
        qkv_all=shape((shards,) + qkv.shape),
        proj_all=shape((shards,) + proj.shape),
        vectors=shape((8, width), f32),
        router=shape((router_pad, width)),
        packed=shape((row_count, 3 * width)),
        mixed=shape((row_count, width)),
        residual=shape((row_count, width), f32),
        tokens=shape((row_count, width)),
        gates=shape((row_count, router_pad), f32),
        summed=shape((row_count, width + 128), f32),
        route=shape((row_count, width), f32),
        in_grad=shape((width, hidden), f32),
        out_grad=shape((width, hidden)),
        in_bias_grad=shape((1, hidden), f32),
        out_bias_grad=shape((1, width), f32),
    )
    group = (experts, group_rows)
    note_rows = round_up(expert_count, 16)
    scratch = dict(
        flat=pltpu.VMEM((row_count, width), f32),
        attn=pltpu.VMEM((row_count, width), bf16),
        up=pltpu.VMEM((row_count, width), bf16),
        turn=pltpu.VMEM((8, 128), f32),
        slots=pltpu.VMEM((8, round_up(row_count, 128)), f32),
        own_bias=pltpu.VMEM((8, width), f32),
        extra=pltpu.VMEM(extra_shape, bf16),
        extra_all=pltpu.VMEM((shards,) + extra_shape, bf16),
        slots_all=pltpu.VMEM((shards, 8, round_up(row_count, 128)), f32),
        slot_col=pltpu.VMEM((shards * row_count, 128), f32),
        up_line=pltpu.VMEM((shards, row_count, width), bf16),
        line=pltpu.VMEM((shards, row_count, width), bf16),
        out_w=pltpu.VMEM((width, hidden), bf16),
        up_in=pltpu.VMEM(group + (width,), bf16),
        stage_a=pltpu.VMEM(group + (width,), bf16),
        stage_b=pltpu.VMEM(group + (width,), bf16),
        rows_in=pltpu.VMEM(group + (width,), bf16),
        gelu=pltpu.VMEM(group + (hidden,), bf16),
        slope=pltpu.VMEM(group + (hidden,), f32),
        sent=pltpu.VMEM(group + (width,), bf16),
        pre=pltpu.VMEM(group + (hidden,), bf16),
        out_in=pltpu.VMEM(group + (width,), bf16),
        back_in=pltpu.VMEM(group + (width,), bf16),
        notes=pltpu.VMEM((experts, 16, lanes), bf16),
        note_in=pltpu.VMEM((experts, 16, lanes), bf16),
        total=pltpu.VMEM((shards * row_count, width + 128), f32),
        far_out=pltpu.VMEM((shards, row_count, width), bf16),
        far_out_in=pltpu.VMEM((shards, row_count, width), bf16),
        note_far=pltpu.VMEM((shards, note_rows, round_up(row_count, 128)), bf16),
        note_far_in=pltpu.VMEM((shards, note_rows, round_up(row_count, 128)), bf16),
        tables=pltpu.VMEM((experts, shards * row_count, group_rows), bf16),
        far_back=pltpu.VMEM((shards, row_count, width), bf16),
        far_back_in=pltpu.VMEM((shards, row_count, width), bf16),
        here=dma((3,)),
    )
    pairs = dict(
        far=(2, shards),
        twin=(2, shards, chips),
        peer=(2, shards, chips),
        small=(2, shards),
        upline=(shards,),
        up=(experts, 2),
        line=(shards,),
        weight=(shards, 2),
        row=(experts, 2),
        out=(experts, 2),
        note=(experts,),
        back=(experts, 3),
        sum=(5, shards),
        notesum=(shards,),
    )
    for name, dims in pairs.items():
        scratch[name + "_s"] = dma(dims)
        scratch[name + "_r"] = dma(dims)
    names = tuple(ins) + tuple(outs) + tuple(scratch)
    return pl.pallas_call(
        functools.partial(fused_kernel, shards, experts, capacity, expert_count, stride, names),
        out_shape=list(outs.values()),
        in_specs=list(ins.values()),
        out_specs=[vmem] * len(outs),
        scratch_shapes=list(scratch.values()),
        compiler_params=pltpu.CompilerParams(
            collective_id=1, has_side_effects=True, vmem_limit_bytes=BIG_VMEM
        ),
        name="front_and_experts",
    )(*inputs)


def expert_slow(
    tokens, gates, route_rows, tables, line_up, up_in, in_slice, out_slice, in_bias, own_bias
):
    row_count, width = tokens.shape
    bf16 = jnp.bfloat16
    table_0, table_1, send_table = tables
    router_pad = gates.shape[1]
    chosen = route_rows[:, :, None] == jnp.arange(router_pad, dtype=jnp.int32)[None, None, :]
    gate_pick = jnp.sum(jnp.where(chosen, gates[:, None, :], 0.0), axis=2)
    gate_high = gate_pick.astype(bf16)
    gate_low = (gate_pick - as_float(gate_high)).astype(bf16)
    gate_notes = jnp.concatenate([gate_high, gate_low], axis=1)
    gate_notes = jnp.pad(gate_notes, ((0, 0), (0, 128 - gate_notes.shape[1])))
    sent_line = jnp.concatenate([tokens, gate_notes], axis=1)
    row_line = lax.all_gather(sent_line, "shard", axis=0, tiled=True)
    line_in = row_line[:, :width]
    gate_line = as_float(row_line[:, width : width + 4])
    line_gate = gate_line[:, 0:2] + gate_line[:, 2:4]
    outgoing = contract_rows(send_table, line_in).astype(bf16)
    slot_gate = jnp.sum(
        jnp.where(table_0, line_gate[:, 0:1], 0.0) + jnp.where(table_1, line_gate[:, 1:2], 0.0),
        axis=0,
    )
    slot_high = slot_gate.astype(bf16)
    slot_low = (slot_gate - as_float(slot_high)).astype(bf16)
    slot_notes = jnp.pad(jnp.stack([slot_high, slot_low], axis=1), ((0, 0), (0, 126)))
    incoming = lax.all_to_all(
        jnp.concatenate([outgoing, slot_notes], axis=1),
        "expert",
        split_axis=0,
        concat_axis=0,
        tiled=True,
    )
    rows_in = incoming[:, :width]
    gate_in = as_float(incoming[:, width : width + 1]) + as_float(
        incoming[:, width + 1 : width + 2]
    )
    grad_in = (as_float(up_in) * gate_in).astype(bf16)
    pre_act = plain_dot(rows_in, in_slice) + in_bias
    gelu_out, gelu_slope = gelu_parts(pre_act)
    gelu_bf = gelu_out.astype(bf16)
    expert_out = (plain_dot(gelu_bf, out_slice) + own_bias).astype(bf16)
    returned = lax.all_to_all(expert_out, "expert", split_axis=0, concat_axis=0, tiled=True)
    pre_grad = contract_cols(grad_in, out_slice) * gelu_slope
    pre_bf = pre_grad.astype(bf16)
    back_rows = contract_cols(pre_bf, in_slice).astype(bf16)
    returned_grad = lax.all_to_all(back_rows, "expert", split_axis=0, concat_axis=0, tiled=True)
    out_0 = plain_dot(table_0.astype(bf16), returned)
    out_1 = plain_dot(table_1.astype(bf16), returned)
    combined = line_gate[:, 0:1] * out_0 + line_gate[:, 1:2] * out_1
    line_up_wide = as_float(line_up)
    gate_grad_line = jnp.stack(
        [jnp.sum(line_up_wide * out_0, axis=1), jnp.sum(line_up_wide * out_1, axis=1)], axis=1
    )
    joined = jnp.concatenate(
        [combined.astype(bf16), jnp.pad(gate_grad_line, ((0, 0), (0, 126))).astype(bf16)], axis=1
    )
    summed = as_float(lax.psum_scatter(joined, "shard", scatter_dimension=0, tiled=True))
    picked = jnp.sum(
        jnp.where(chosen, summed[:, width : width + 2][:, :, None], 0.0), axis=1
    )
    summed = jnp.concatenate([summed[:, :width], picked], axis=1)
    back_line = plain_dot(send_table, returned_grad)
    route_grad = lax.psum_scatter(back_line.astype(bf16), "shard", scatter_dimension=0, tiled=True)
    return (
        summed,
        route_grad,
        contract_rows(rows_in, pre_bf),
        contract_rows(gelu_bf, grad_in).astype(bf16),
        jnp.sum(pre_grad, axis=0)[None],
        jnp.sum(as_float(grad_in), axis=0)[None],
    )


def body(
    block_input,
    image_live,
    expert_routes,
    first_gain,
    first_shift,
    qkv_weight,
    query_value_bias,
    attn_out_weight,
    attn_out_bias,
    second_gain,
    second_shift,
    router_weight,
    expert_in_weight,
    expert_in_bias,
    expert_out_weight,
    expert_out_bias,
    output_grad,
):
    image_count, seq_length, width = block_input.shape
    shards = lax.axis_size("shard")
    experts = lax.axis_size("expert")
    chips = experts // 2
    expert_count = router_weight.shape[1]
    my_shard = lax.axis_index("shard")
    shard_rows = first_gain.shape[0]
    stride = round_up(seq_length, 8)
    row_count = image_count * stride
    capacity = (3 * image_count * seq_length + expert_count - 1) // expert_count
    group_rows = round_up(shards * capacity, 16)
    slot_rows = expert_count * group_rows
    bf16 = jnp.bfloat16
    fast = chips == 4 and shards == 4 and shard_rows % (16 * chips) == 0

    router_pad = round_up(expert_count, 128)
    extra_rows = round_up(VECTORS + expert_count, 16)
    extra_cols = round_up(shard_rows, 128)
    vector_rows = jnp.concatenate(
        [
            first_gain,
            first_shift,
            attn_out_bias,
            second_gain,
            second_shift,
            query_value_bias,
        ]
    ).reshape(VECTORS, shard_rows)
    turned_in = jnp.transpose(block_input, (1, 0, 2))
    turned_grad = jnp.transpose(output_grad, (1, 0, 2))
    in_slice = expert_in_weight[0]
    out_slice_t = expert_out_weight[0].T
    if fast:
        (
            qkv_full,
            proj_full,
            vectors,
            router_t,
            packed,
            mixed,
            residual,
            expert_in,
            gates,
            summed,
            route_grad,
            in_weight_grad,
            out_weight_grad,
            in_bias_sum,
            out_bias_sum,
        ) = fused_pass(
            shards,
            experts,
            capacity,
            expert_count,
            stride,
            (
                image_live,
                turned_in,
                turned_grad,
                jnp.transpose(expert_routes, (0, 2, 1)),
                qkv_weight,
                attn_out_weight,
                vector_rows,
                router_weight.T,
                in_slice,
                out_slice_t,
                expert_in_bias,
                expert_out_bias,
            ),
        )
        qkv_full = qkv_full.reshape(width, 3 * width)
        proj_full = proj_full.reshape(width, width)
    else:
        tail_rows = stride - seq_length
        live_rows = jnp.repeat(image_live, stride) * jnp.tile(
            (jnp.arange(stride) < seq_length).astype(jnp.int32), image_count
        )
        route_rows = jnp.pad(expert_routes, ((0, 0), (0, tail_rows), (0, 0))).reshape(row_count, 2)
        route_code, position = slot_places(route_rows, live_rows, expert_count)
        up_rows = (
            jnp.pad(output_grad, ((0, 0), (0, tail_rows), (0, 0))).reshape(row_count, width)
            * as_float(live_rows)[:, None]
        )
        own_bias = lax.dynamic_update_slice(
            jnp.zeros((1, width), jnp.float32),
            as_float(expert_out_bias),
            (0, my_shard * shard_rows),
        )
        in_bias = as_float(expert_in_bias)
        notes = jnp.concatenate([route_code.astype(bf16), position.astype(bf16)], axis=1)
        notes = jnp.pad(notes, ((0, 0), (0, 128 - notes.shape[1])))
        up_line = jnp.concatenate([up_rows.astype(bf16), notes], axis=1)
        extra = jnp.pad(
            jnp.concatenate([router_weight.T, vector_rows]),
            ((0, extra_rows - expert_count - VECTORS), (0, extra_cols - shard_rows)),
        )
        qkv_all, proj_all, extra_all, line_all = (
            lax.all_gather(each, "shard", axis=0, tiled=False)
            for each in (qkv_weight, attn_out_weight, extra, up_line)
        )
        qkv_full = qkv_all.reshape(width, 3 * width)
        proj_full = proj_all.reshape(width, width)
        extra_t = jnp.transpose(extra_all[:, :, :shard_rows], (1, 0, 2))
        rows_t = extra_t[expert_count:]
        vectors = as_float(rows_t[:8]).reshape(8, width)
        query_value = as_float(rows_t[5:7])
        bias_full = jnp.transpose(query_value, (1, 0, 2)).reshape(2 * width)
        bias_row = jnp.concatenate(
            [bias_full[:width], jnp.zeros((width,), jnp.float32), bias_full[width:]]
        )
        bias_row = jnp.pad(bias_row[None], ((0, 7), (0, 0)))
        router_t = jnp.pad(
            extra_t[:expert_count].reshape(expert_count, width),
            ((0, router_pad - expert_count), (0, 0)),
        )
        line_rows = shards * row_count
        line = line_all.reshape(line_rows, width + 128)
        line_up = line[:, :width]
        line_notes = as_float(line[:, width : width + 4])
        line_ids = jnp.arange(line_rows, dtype=jnp.int32)[:, None]
        line_slot = (
            line_notes[:, 0:2].astype(jnp.int32) * group_rows
            + (line_ids // row_count) * capacity
            + line_notes[:, 2:4].astype(jnp.int32)
        )
        line_slot = jnp.where(line_notes[:, 0:2] >= 0, line_slot, -1)
        slot_ids = jnp.arange(slot_rows, dtype=jnp.int32)
        table_0 = line_slot[:, 0:1] == slot_ids[None, :]
        table_1 = line_slot[:, 1:2] == slot_ids[None, :]
        send_table = (table_0 | table_1).astype(bf16)
        up_out = contract_rows(send_table, line_up).astype(bf16)
        up_in = lax.all_to_all(up_out, "expert", split_axis=0, concat_axis=0, tiled=True)
        out_slice = lax.all_to_all(
            expert_out_weight[0], "shard", split_axis=0, concat_axis=1, tiled=True
        )
        packed, mixed, residual, expert_in, gates = pl.pallas_call(
            functools.partial(forward_kernel, stride, expert_count),
            out_shape=[
                jax.ShapeDtypeStruct((row_count, 3 * width), bf16),
                jax.ShapeDtypeStruct((row_count, width), bf16),
                jax.ShapeDtypeStruct((row_count, width), jnp.float32),
                jax.ShapeDtypeStruct((row_count, width), bf16),
                jax.ShapeDtypeStruct((row_count, router_pad), jnp.float32),
            ],
            in_specs=[pl.BlockSpec(memory_space=pltpu.VMEM)] * 6,
            out_specs=[pl.BlockSpec(memory_space=pltpu.VMEM)] * 5,
            scratch_shapes=[
                pltpu.VMEM((row_count, width), jnp.float32),
                pltpu.VMEM((row_count, width), bf16),
            ],
            compiler_params=pltpu.CompilerParams(vmem_limit_bytes=BIG_VMEM),
            name="attention_forward",
        )(turned_in, qkv_full, proj_full, vectors, bias_row, router_t)
        (
            summed,
            route_grad,
            in_weight_grad,
            out_weight_grad,
            in_bias_sum,
            out_bias_sum,
        ) = expert_slow(
            expert_in,
            gates,
            route_rows,
            (table_0, table_1, send_table),
            line_up,
            up_in,
            in_slice,
            out_slice,
            in_bias,
            own_bias,
        )
        out_weight_grad = out_weight_grad.T
    out_weight_grad = out_weight_grad.reshape(shards, shard_rows, -1)
    in_weight_part = in_weight_grad[None]
    in_bias_part = in_bias_sum[:1]
    out_bias_part = lax.dynamic_slice_in_dim(
        out_bias_sum[0], my_shard * shard_rows, shard_rows
    )[None]

    if fast:
        (
            block_output,
            input_grad,
            qkv_sum,
            proj_sum,
            mine,
            bias_part,
            out_weight_rows,
        ) = backward_reduce(
            shards,
            chips,
            stride,
            (
                image_live,
                turned_in,
                turned_grad,
                packed,
                mixed,
                residual,
                expert_in,
                gates,
                summed,
                route_grad,
                qkv_full,
                proj_full,
                vectors,
                router_t,
                out_weight_grad,
            ),
        )
        out_weight_part = as_float(out_weight_rows).T[None]
        mine = mine[:, :shard_rows]
        bias_part = bias_part[0]
    else:
        smem = pl.BlockSpec(memory_space=pltpu.SMEM)
        vmem = pl.BlockSpec(memory_space=pltpu.VMEM)
        wide_rows = pltpu.VMEM((row_count, width), jnp.float32)
        block_output, input_grad, weight_grads, extra_grads = pl.pallas_call(
            functools.partial(backward_kernel, stride),
            out_shape=[
                jax.ShapeDtypeStruct(turned_in.shape, jnp.float32),
                jax.ShapeDtypeStruct(turned_in.shape, jnp.float32),
                jax.ShapeDtypeStruct((2, width, 2 * width), bf16),
                jax.ShapeDtypeStruct((extra_rows, width), jnp.float32),
            ],
            in_specs=[smem] + [vmem] * 13,
            out_specs=[vmem] * 4,
            scratch_shapes=[
                wide_rows,
                wide_rows,
                pltpu.VMEM((width, row_count), bf16),
                pltpu.VMEM((row_count, width), bf16),
                pltpu.VMEM((row_count, 3 * width), bf16),
                wide_rows,
            ],
            compiler_params=pltpu.CompilerParams(vmem_limit_bytes=BIG_VMEM),
            cost_estimate=pl.CostEstimate(
                flops=32 * row_count * width * width,
                bytes_accessed=48 * width * width,
                transcendentals=2 * HEADS * row_count * row_count,
            ),
            name="attention_backward",
        )(
            image_live,
            turned_in,
            turned_grad,
            packed,
            mixed,
            residual,
            expert_in,
            gates,
            summed,
            route_grad,
            qkv_full,
            proj_full,
            vectors,
            router_t,
        )
        qkv_sum, proj_sum, extra_sum, out_weight_blocks = reduce_slow(
            weight_grads, extra_grads.astype(bf16), out_weight_grad
        )
        out_weight_part = (
            jnp.transpose(as_float(out_weight_blocks), (0, 2, 1)).reshape(-1, shard_rows)[None]
        )

        def own(array_in, size, axis=0):
            return lax.dynamic_slice_in_dim(array_in, my_shard * size, size, axis=axis)

        mine = own(extra_sum, shard_rows, axis=1)
        bias_part = own(extra_sum[5:7].reshape(2 * width), 2 * shard_rows)
    return (
        jnp.transpose(block_output, (1, 0, 2)),
        jnp.transpose(input_grad, (1, 0, 2)),
        mine[0],
        mine[1],
        as_float(qkv_sum),
        bias_part,
        as_float(proj_sum),
        mine[2],
        mine[3],
        mine[4],
        mine[VECTORS : VECTORS + expert_count].T,
        in_weight_part,
        in_bias_part,
        out_weight_part,
        out_bias_part,
    )


def solution(mesh):
    in_specs = (
        P(("expert", "shard"), None, None),
        P(("expert", "shard")),
        P(("expert", "shard"), None, None),
        P("shard"),
        P("shard"),
        P("shard", None),
        P("shard"),
        P("shard", None),
        P("shard"),
        P("shard"),
        P("shard"),
        P("shard", None),
        P("expert", None, "shard"),
        P("expert", "shard"),
        P("expert", None, "shard"),
        P("expert", "shard"),
        P(("expert", "shard"), None, None),
    )
    out_specs = (
        P(("expert", "shard"), None, None),
        P(("expert", "shard"), None, None),
        P("shard"),
        P("shard"),
        P("shard", None),
        P("shard"),
        P("shard", None),
        P("shard"),
        P("shard"),
        P("shard"),
        P("shard", None),
        P("expert", None, "shard"),
        P("expert", "shard"),
        P("expert", None, "shard"),
        P("expert", "shard"),
    )
    return jax.shard_map(body, mesh=mesh, in_specs=in_specs, out_specs=out_specs, check_vma=False)
```

```python
import functools
import math
import types

import jax
import jax.numpy as jnp
from jax import lax
from jax.experimental import pallas as pl
from jax.experimental.pallas import tpu as pltpu
from jax.sharding import PartitionSpec as P

HEADS = 12
HEAD_DIM = 64


EPSILON = 1e-06
PRECISE = lax.Precision.HIGHEST
HALF_ROOT = 0.7071067811865476
DENSITY = 0.3989422804014327


def as_float(array_in):
    return array_in.astype(jnp.float32)


def contract_rows(left_side, right_side):
    return lax.dot_general(
        left_side, right_side, (((0,), (0,)), ((), ())), preferred_element_type=jnp.float32
    )


def contract_cols(left_side, right_side):
    return lax.dot_general(
        left_side, right_side, (((1,), (1,)), ((), ())), preferred_element_type=jnp.float32
    )


def precise_rows(left_side, right_side):
    return lax.dot_general(
        left_side,
        right_side,
        (((0,), (0,)), ((), ())),
        precision=PRECISE,
        preferred_element_type=jnp.float32,
    )


def precise_cols(left_side, right_side):
    return lax.dot_general(
        left_side,
        right_side,
        (((1,), (1,)), ((), ())),
        precision=PRECISE,
        preferred_element_type=jnp.float32,
    )


def layer_norm(values_in, gain_vec, shift_vec):
    center = values_in - jnp.mean(values_in, axis=-1, keepdims=True)
    inv_std = lax.rsqrt(jnp.mean(center * center, axis=-1, keepdims=True) + EPSILON)
    normed = center * inv_std
    return (normed * as_float(gain_vec) + as_float(shift_vec), normed, inv_std)


def norm_back(upstream, normed, inv_std, gain_vec):
    scaled = upstream * as_float(gain_vec)
    return inv_std * (
        scaled
        - jnp.mean(scaled, axis=-1, keepdims=True)
        - normed * jnp.mean(scaled * normed, axis=-1, keepdims=True)
    )


def gelu_parts(pre_act):
    normal_cdf = 0.5 * (1.0 + jax.scipy.special.erf(pre_act * HALF_ROOT))
    return (
        pre_act * normal_cdf,
        normal_cdf + pre_act * DENSITY * jnp.exp(-0.5 * pre_act * pre_act),
    )


BIG_VMEM = 56 * 1024 * 1024
VECTORS = 7


def plain_dot(left_side, right_side):
    return jnp.dot(left_side, right_side, preferred_element_type=jnp.float32)


def exact_dot(left_side, right_side):
    return lax.dot_general(
        left_side,
        right_side,
        (((1,), (0,)), ((), ())),
        precision=PRECISE,
        preferred_element_type=jnp.float32,
    )


def round_up(value, step):
    return -(-value // step) * step


def slot_places(route_rows, live_rows, expert_count):
    row_count = route_rows.shape[0]
    flat_routes = route_rows.reshape(2 * row_count)
    alive_pairs = jnp.repeat(live_rows, 2)
    chosen = (flat_routes[:, None] == jnp.arange(expert_count, dtype=jnp.int32)[None, :]).astype(
        jnp.int32
    )
    live_hits = chosen * alive_pairs[:, None]
    earlier = (
        jnp.arange(2 * row_count, dtype=jnp.int32)[:, None]
        > jnp.arange(2 * row_count, dtype=jnp.int32)[None, :]
    ).astype(jnp.bfloat16)
    counted = jnp.dot(earlier, live_hits.astype(jnp.bfloat16), preferred_element_type=jnp.float32)
    position = jnp.sum(counted * as_float(live_hits), axis=1)
    route_code = jnp.where(alive_pairs > 0, flat_routes, -1).astype(jnp.float32)
    return route_code.reshape(row_count, 2), position.reshape(row_count, 2)


class Place:
    def __init__(self, shards, chips):
        self.shards = shards
        self.chips = chips
        self.expert = lax.axis_index("expert")
        self.shard = lax.axis_index("shard")
        self.core = lax.rem(self.expert, 2)
        self.chip = lax.div(self.expert, 2)

    def along(self, step):
        return {
            "expert": self.expert,
            "shard": lax.rem(self.shard + step + self.shards, self.shards),
        }

    def peer(self, step):
        other = lax.rem(self.chip + step + self.chips, self.chips)
        return {"expert": other * 2 + self.core, "shard": self.shard}

    def sibling(self):
        return {"expert": self.chip * 2 + 1 - self.core, "shard": self.shard}

    def plane(self, step):
        count = 2 * self.chips
        return {"expert": lax.rem(self.expert + step, count), "shard": self.shard}

    def greet(self, others):
        barrier = pltpu.get_barrier_semaphore()
        for other in others:
            pl.semaphore_signal(
                barrier, inc=1, device_id=other, device_id_type=pl.DeviceIdType.MESH
            )
        pl.semaphore_wait(barrier, len(others))


def remote(src, dst, send_sem, recv_sem, device):
    return pltpu.make_async_remote_copy(
        src_ref=src,
        dst_ref=dst,
        send_sem=send_sem,
        recv_sem=recv_sem,
        device_id=device,
        device_id_type=pl.DeviceIdType.MESH,
    )


def norm_stats(values_in):
    center = values_in - jnp.mean(values_in, axis=-1, keepdims=True)
    inv_std = lax.rsqrt(jnp.mean(center * center, axis=-1, keepdims=True) + EPSILON)
    return center * inv_std, inv_std


def spread_rows(dst, src, image_count, seq_length, stride):
    dst[...] = jnp.zeros_like(dst)
    for image in range(image_count):
        dst[image * stride : image * stride + seq_length, :] = src[:, image, :]


def same_image(rows, stride, seq_length):
    row_at = lax.broadcasted_iota(jnp.int32, (rows, rows), 0)
    col_at = lax.broadcasted_iota(jnp.int32, (rows, rows), 1)
    mask = None
    for image in range(rows // stride):
        low = image * stride
        part = (
            (row_at >= low)
            & (row_at < low + stride)
            & (col_at >= low)
            & (col_at < low + seq_length)
        )
        mask = part if mask is None else mask | part
    return mask


def masked_softmax(query_half, keys, mask):
    scores = contract_cols(query_half, keys) * (1.0 / math.sqrt(HEAD_DIM))
    scores = jnp.where(mask, scores, -1e30)
    row_max = jnp.max(scores, axis=-1, keepdims=True)
    log_total = row_max + jnp.log(jnp.sum(jnp.exp(scores - row_max), axis=-1, keepdims=True))
    return jnp.exp(scores - log_total)


def forward_kernel(
    stride,
    expert_count,
    x_ref,
    qkv_ref,
    proj_ref,
    vec_ref,
    bias_ref,
    router_ref,
    packed_ref,
    mixed_ref,
    residual_ref,
    line_ref,
    gates_ref,
    flat_ref,
    attn_ref,
):
    seq_length, image_count, width = x_ref.shape
    rows = flat_ref.shape[0]
    bf16 = jnp.bfloat16
    spread_rows(flat_ref, x_ref, image_count, seq_length, stride)
    normed, _ = norm_stats(flat_ref[...])
    attn_ref[...] = (normed * vec_ref[0:1, :] + vec_ref[1:2, :]).astype(bf16)

    def project(tile, carry):
        cols = pl.ds(pl.multiple_of(tile * width, 128), width)
        packed_ref[:, cols] = (
            plain_dot(attn_ref[...], qkv_ref[:, cols]) + bias_ref[0:1, cols]
        ).astype(bf16)
        return carry

    lax.fori_loop(0, 3, project, 0)
    mask = same_image(rows, stride, seq_length)
    low_lanes = lax.broadcasted_iota(jnp.int32, (rows, 128), 1) < HEAD_DIM

    def attend(pair, carry):
        def part(which):
            return packed_ref[:, pl.ds(pl.multiple_of(which * width + pair * 128, 128), 128)]

        query, key, value = part(0), part(1), part(2)
        zero = jnp.zeros_like(query)
        weights_low = masked_softmax(jnp.where(low_lanes, query, zero), key, mask).astype(bf16)
        weights_high = masked_softmax(jnp.where(low_lanes, zero, query), key, mask).astype(bf16)
        mixed_ref[:, pl.ds(pl.multiple_of(pair * 128, 128), 128)] = jnp.where(
            low_lanes, plain_dot(weights_low, value), plain_dot(weights_high, value)
        ).astype(bf16)
        return carry

    lax.fori_loop(0, HEADS // 2, attend, 0)
    residual = flat_ref[...] + plain_dot(mixed_ref[...], proj_ref[...]) + vec_ref[2:3, :]
    residual_ref[...] = residual
    normed_two, _ = norm_stats(residual)
    expert_in = (normed_two * vec_ref[3:4, :] + vec_ref[4:5, :]).astype(bf16)
    line_ref[...] = expert_in
    logits = contract_cols(expert_in, router_ref[...])
    lanes = lax.broadcasted_iota(jnp.int32, logits.shape, 1)
    logits = jnp.where(lanes < expert_count, logits, -1e30)
    shifted = jnp.exp(logits - jnp.max(logits, axis=-1, keepdims=True))
    gates_ref[...] = shifted / jnp.sum(shifted, axis=-1, keepdims=True)


def backward_kernel(
    stride,
    live_ref,
    x_ref,
    up_ref,
    packed_ref,
    mixed_ref,
    residual_ref,
    expert_ref,
    gates_ref,
    summed_ref,
    back_ref,
    qkv_ref,
    proj_ref,
    vec_ref,
    router_ref,
    block_ref,
    grad_ref,
    weight_ref,
    extra_ref,
    flat_ref,
    upstream_ref,
    attn_t_ref,
    mixed_grad_ref,
    packed_grad_ref,
    res_grad_ref,
):
    seq_length, image_count, width = x_ref.shape
    rows = flat_ref.shape[0]
    bf16 = jnp.bfloat16
    half = 3 * width // 2
    spread_rows(flat_ref, x_ref, image_count, seq_length, stride)
    upstream_ref[...] = jnp.zeros_like(upstream_ref)
    residual = residual_ref[...]
    block = residual + as_float(summed_ref[:, :width])
    for image in range(image_count):
        live = live_ref[image].astype(jnp.float32)
        here = slice(image * stride, image * stride + seq_length)
        upstream_ref[here, :] = up_ref[:, image, :] * live
        block_ref[:, image, :] = block[here, :]

    gates = gates_ref[...]
    picked = as_float(summed_ref[:, width:])
    logit_grad = gates * (picked - jnp.sum(gates * picked, axis=-1, keepdims=True))
    router_rows = extra_ref.shape[0] - VECTORS
    extra_ref[VECTORS:, :] = precise_rows(logit_grad, as_float(expert_ref[...]))[
        :router_rows
    ]
    normed_two_grad = as_float(back_ref[...]) + exact_dot(
        logit_grad, as_float(router_ref[...])
    )
    normed_two, inv_two = norm_stats(residual)
    extra_ref[3:4, :] = jnp.sum(normed_two_grad * normed_two, axis=0, keepdims=True)
    extra_ref[4:5, :] = jnp.sum(normed_two_grad, axis=0, keepdims=True)
    residual_grad = upstream_ref[...] + norm_back(
        normed_two_grad, normed_two, inv_two, vec_ref[3:4, :]
    )
    res_grad_ref[...] = residual_grad
    extra_ref[2:3, :] = jnp.sum(residual_grad, axis=0, keepdims=True)
    residual_bf = residual_grad.astype(bf16)
    proj_grad = contract_rows(mixed_ref[...], residual_bf)
    for core in range(2):
        weight_ref[core, :, half:] = proj_grad[
            :, core * (width // 2) : (core + 1) * (width // 2)
        ].astype(bf16)
    mixed_grad_ref[...] = contract_cols(residual_bf, proj_ref[...]).astype(bf16)

    mask = same_image(rows, stride, seq_length)
    low_lanes = lax.broadcasted_iota(jnp.int32, (rows, 128), 1) < HEAD_DIM

    def attend(pair, carry):
        def part(which):
            return pl.ds(pl.multiple_of(which * width + pair * 128, 128), 128)

        query, key, value = (packed_ref[:, part(which)] for which in range(3))
        mixed_grad = mixed_grad_ref[:, part(0)]
        zero = jnp.zeros_like(query)
        totals = [0.0, 0.0, 0.0]
        for high in range(2):

            def only(array_in):
                return jnp.where(low_lanes, zero if high else array_in, array_in if high else zero)

            query_half, mixed_half = only(query), only(mixed_grad)
            probs = masked_softmax(query_half, key, mask)
            prob_grad = contract_cols(mixed_half, value)
            score_grad = (
                probs
                * (prob_grad - jnp.sum(probs * prob_grad, axis=-1, keepdims=True))
                * (1.0 / math.sqrt(HEAD_DIM))
            ).astype(bf16)
            totals[0] += plain_dot(score_grad, only(key))
            totals[1] += contract_rows(score_grad, query_half)
            totals[2] += contract_rows(probs.astype(bf16), mixed_half)
        for which in range(3):
            packed_grad_ref[:, part(which)] = totals[which].astype(bf16)
        extra_ref[5:6, part(0)] = jnp.sum(totals[0], axis=0, keepdims=True)
        extra_ref[6:7, part(0)] = jnp.sum(totals[2], axis=0, keepdims=True)
        return carry

    lax.fori_loop(0, HEADS // 2, attend, 0)

    normed_one, inv_one = norm_stats(flat_ref[...])
    attn_in = normed_one * vec_ref[0:1, :] + vec_ref[1:2, :]
    attn_t_ref[...] = attn_in.T.astype(bf16)
    tile = half // 3

    def weigh(at, carry):
        src = pl.ds(pl.multiple_of(at * tile, 128), tile)
        dst = pl.ds(pl.multiple_of(lax.rem(at, 3) * tile, 128), tile)
        weight_ref[lax.div(at, 3), :, dst] = plain_dot(
            attn_t_ref[...], packed_grad_ref[:, src]
        ).astype(bf16)
        return carry

    lax.fori_loop(0, 6, weigh, 0)
    upstream_ref[...] = jnp.zeros_like(upstream_ref)

    def push_back(at, carry):
        cols = pl.ds(pl.multiple_of(at * width, 128), width)
        upstream_ref[...] += contract_cols(packed_grad_ref[:, cols], qkv_ref[:, cols])
        return carry

    lax.fori_loop(0, 3, push_back, 0)
    normed_one_grad = upstream_ref[...]
    extra_ref[0:1, :] = jnp.sum(normed_one_grad * normed_one, axis=0, keepdims=True)
    extra_ref[1:2, :] = jnp.sum(normed_one_grad, axis=0, keepdims=True)
    input_grad = res_grad_ref[...] + norm_back(
        normed_one_grad, normed_one, inv_one, vec_ref[0:1, :]
    )
    for image in range(image_count):
        grad_ref[:, image, :] = input_grad[image * stride : image * stride + seq_length, :]


def backward_reduce_kernel(shards, chips, stride, names, *refs):
    r = types.SimpleNamespace(**dict(zip(names, refs)))
    place = Place(shards, chips)
    bf16 = jnp.bfloat16
    core, chip, shard = place.core, place.chip, place.shard
    count = 2 * chips
    seq_length, image_count, width = r.x.shape
    rows = r.flat.shape[0]
    side = width // 2
    groups = 4
    piece = r.whole.shape[3]
    shard_rows = width // shards
    place.greet(
        [place.along(j) for j in range(1, shards)]
        + [place.plane(i) for i in range(1, count)]
    )
    order = (1, 3, 2)
    sent = []

    def send(copy):
        copy.start()
        sent.append(copy)

    def block_copy(j):
        cols = pl.ds(pl.multiple_of(shard * width, 128), width)
        return remote(
            r.blocks.at[lax.rem(shard + j, shards)],
            r.blocks_out.at[:, cols],
            r.block_s.at[j],
            r.block_r.at[j],
            place.along(j),
        )

    for j in order:
        send(block_copy(j))
    block_local = pltpu.make_async_copy(
        r.blocks.at[shard],
        r.blocks_out.at[:, pl.ds(pl.multiple_of(shard * width, 128), width)],
        r.here.at[0],
    )
    block_local.start()

    def twin_copy(g):
        return remote(
            r.weights.at[g, 1 - core],
            r.twin_in.at[g],
            r.twin_s.at[g],
            r.twin_r.at[g],
            place.sibling(),
        )

    def peer_copy(g, i):
        return remote(
            r.plane_sum.at[g, :, lax.rem(chip + i, chips)],
            r.peer_in.at[g, i],
            r.peer_s.at[g, i],
            r.peer_r.at[g, i],
            place.peer(i),
        )

    def far_copy(g, j):
        return remote(
            r.far_out.at[g, lax.rem(shard + j, shards)],
            r.far_in.at[g, j],
            r.far_s.at[g, j],
            r.far_r.at[g, j],
            place.along(j),
        )

    def back_copy(g, i):
        block = r.whole.at[g, core, chip]
        return remote(block, block, r.back_s.at[g, i], r.back_r.at[g, i], place.peer(i))

    def last_copy(g, i):
        block = r.whole.at[g, core, lax.rem(chip - i + chips, chips)]
        return remote(block, block, r.last_s.at[g, i], r.last_r.at[g, i], place.sibling())

    def small_copy(i):
        return remote(
            r.small, r.small_in.at[i], r.small_s.at[i], r.small_r.at[i], place.plane(i)
        )

    def edge_copy(j):
        return remote(
            r.small_sum, r.small_far.at[j], r.edge_s.at[j], r.edge_r.at[j], place.along(j)
        )

    def store_group(g, half, value):
        r.weights[g, half] = value.astype(bf16).reshape(shards, chips, piece, side)

    def to_plane(g):
        twin_copy(g).wait_recv()
        for at in range(shards):
            r.plane_sum[g, at] = (
                as_float(r.weights[g, core, at]) + as_float(r.twin_in[g, at])
            ).astype(bf16)
        for i in range(1, chips):
            send(peer_copy(g, i))

    def to_far(g):
        mine = as_float(r.plane_sum[g, :, chip])
        for i in range(1, chips):
            peer_copy(g, i).wait_recv()
            mine += as_float(r.peer_in[g, i])
        r.far_out[g] = mine.astype(bf16)
        for j in order:
            send(far_copy(g, j))

    def to_back(g):
        mine = as_float(r.far_out[g, shard])
        for j in order:
            far_copy(g, j).wait_recv()
            mine += as_float(r.far_in[g, j])
        r.whole[g, core, chip] = mine.astype(bf16)
        for i in range(1, chips):
            send(back_copy(g, i))
        send(last_copy(g, 0))

    spread_rows(r.flat, r.grad, image_count, seq_length, stride)
    residual = r.residual[...]
    block = residual + r.summed[:, :width]
    for image in range(image_count):
        alive = r.live[image].astype(jnp.float32)
        here = slice(image * stride, image * stride + seq_length)
        r.upstream[image * stride : (image + 1) * stride, :] = (
            r.flat[image * stride : (image + 1) * stride, :] * alive
        )
        r.block_out[:, image, :] = block[here, :]
    gates = r.gates[...]
    picked = r.summed[:, width:]
    logit_grad = gates * (picked - jnp.sum(gates * picked, axis=-1, keepdims=True))
    normed_two_grad = r.route[...] + exact_dot(logit_grad, as_float(r.router[...]))
    normed_two, inv_two = norm_stats(residual)
    residual_grad = r.upstream[...] + norm_back(
        normed_two_grad, normed_two, inv_two, r.vectors[3:4, :]
    )
    r.res_grad[...] = residual_grad
    residual_bf = residual_grad.astype(bf16)
    proj_grad = contract_rows(r.mixed[...], residual_bf)
    for half in range(2):
        store_group(0, half, proj_grad[:, half * side : (half + 1) * side])
    send(twin_copy(0))
    r.mixed_grad[...] = contract_cols(residual_bf, r.proj[...]).astype(bf16)
    router_rows = r.totals.shape[0] - VECTORS
    r.totals[VECTORS:, :] = precise_rows(logit_grad, as_float(r.tokens[...]))[:router_rows]
    r.totals[2:3, :] = jnp.sum(residual_grad, axis=0, keepdims=True)
    r.totals[3:4, :] = jnp.sum(normed_two_grad * normed_two, axis=0, keepdims=True)
    r.totals[4:5, :] = jnp.sum(normed_two_grad, axis=0, keepdims=True)
    spread_rows(r.flat, r.x, image_count, seq_length, stride)
    normed_one, inv_one = norm_stats(r.flat[...])
    attn_in = normed_one * r.vectors[0:1, :] + r.vectors[1:2, :]
    r.attn_t[...] = attn_in.T.astype(bf16)
    r.flat[...] = normed_one

    mask = same_image(rows, stride, seq_length)
    low_lanes = lax.broadcasted_iota(jnp.int32, (rows, 128), 1) < HEAD_DIM

    def attend(pair, carry):
        def part(which):
            return pl.ds(pl.multiple_of(which * width + pair * 128, 128), 128)

        query, key, value = (r.packed[:, part(which)] for which in range(3))
        mixed_grad = r.mixed_grad[:, part(0)]
        zero = jnp.zeros_like(query)
        totals = [0.0, 0.0, 0.0]
        for high in range(2):

            def only(array_in):
                return jnp.where(low_lanes, zero if high else array_in, array_in if high else zero)

            query_half, mixed_half = only(query), only(mixed_grad)
            probs = masked_softmax(query_half, key, mask)
            prob_grad = contract_cols(mixed_half, value)
            score_grad = (
                probs
                * (prob_grad - jnp.sum(probs * prob_grad, axis=-1, keepdims=True))
                * (1.0 / math.sqrt(HEAD_DIM))
            ).astype(bf16)
            totals[0] += plain_dot(score_grad, only(key))
            totals[1] += contract_rows(score_grad, query_half)
            totals[2] += contract_rows(probs.astype(bf16), mixed_half)
        for which in range(3):
            r.packed_grad[:, part(which)] = totals[which].astype(bf16)
        r.totals[5:6, part(0)] = jnp.sum(totals[0], axis=0, keepdims=True)
        r.totals[6:7, part(0)] = jnp.sum(totals[2], axis=0, keepdims=True)
        return carry

    pairs = width // 128
    lax.fori_loop(0, pairs // 2, attend, 0)
    to_plane(0)
    lax.fori_loop(pairs // 2, pairs, attend, 0)
    for g in range(1, groups):
        for half in (1 - core, core):
            cols = pl.ds(pl.multiple_of((g - 1) * width + half * side, 128), side)
            store_group(g, half, plain_dot(r.attn_t[...], r.packed_grad[:, cols]))
            if half is not core:
                send(twin_copy(g))
        if g > 1:
            to_plane(g - 1)
    to_plane(groups - 1)

    r.upstream[...] = jnp.zeros_like(r.upstream)

    def push_back(at, carry):
        cols = pl.ds(pl.multiple_of(at * width, 128), width)
        r.upstream[...] += contract_cols(r.packed_grad[:, cols], r.qkv[:, cols])
        return carry

    lax.fori_loop(0, 3, push_back, 0)
    normed_one_grad = r.upstream[...]
    normed_one = r.flat[...]
    r.totals[0:1, :] = jnp.sum(normed_one_grad * normed_one, axis=0, keepdims=True)
    r.totals[1:2, :] = jnp.sum(normed_one_grad, axis=0, keepdims=True)
    r.small[...] = r.totals[...].astype(bf16)
    for i in range(1, count):
        send(small_copy(i))
    to_far(0)
    input_grad = r.res_grad[...] + norm_back(
        normed_one_grad, normed_one, inv_one, r.vectors[0:1, :]
    )
    for image in range(image_count):
        r.grad_out[:, image, :] = input_grad[image * stride : image * stride + seq_length, :]
    to_far(1)
    to_back(0)
    total = as_float(r.small[...])
    for i in range(1, count):
        small_copy(i).wait_recv()
        total += as_float(r.small_in[i])
    r.small_sum[...] = total.astype(bf16)
    for j in order:
        send(edge_copy(j))
    to_far(2)
    to_back(1)
    to_far(3)
    to_back(2)
    total = as_float(r.small_sum[...])
    for j in order:
        edge_copy(j).wait_recv()
        total += as_float(r.small_far[j])

    def cut(values, start, size):
        lane_from = lax.broadcasted_iota(jnp.int32, (width, size), 0)
        lane_to = lax.broadcasted_iota(jnp.int32, (width, size), 1)
        return exact_dot(values, jnp.where(lane_from == lane_to + start, 1.0, 0.0))

    r.small_out[...] = cut(total, shard * shard_rows, r.small_out.shape[1])
    low = jnp.broadcast_to(total[5:6], (8, width))
    high = jnp.broadcast_to(total[6:7], (8, width))
    which = jnp.where(lax.div(shard, shards // 2) == 0, low, high)
    r.bias_out[...] = cut(which, lax.rem(shard, shards // 2) * side, side)[:1]

    def forward_last(g):
        for i in range(1, chips):
            back_copy(g, i).wait_recv()
            send(last_copy(g, i))

    for g in range(groups - 1):
        forward_last(g)
    to_back(groups - 1)
    forward_last(groups - 1)
    for g in range(groups):
        for i in range(chips):
            last_copy(g, i).wait_recv()
        for half in range(2):
            for at in range(chips):
                here = slice(at * piece, (at + 1) * piece)
                cols = slice(half * side, (half + 1) * side)
                if g == 0:
                    r.proj_out[here, cols] = r.whole[g, half, at]
                else:
                    start = (g - 1) * width + half * side
                    r.qkv_out[here, start : start + side] = r.whole[g, half, at]
    block_local.wait()
    for j in order:
        block_copy(j).wait_recv()
    for copy in sent:
        copy.wait_send()


def backward_reduce(shards, chips, stride, inputs):
    x, packed, blocks = inputs[1], inputs[3], inputs[14]
    rows, width = packed.shape[0], x.shape[2]
    shard_rows = width // shards
    piece = shard_rows // chips
    side = width // 2
    expert_count = 2 * chips
    small_rows = round_up(VECTORS + expert_count, 16)
    bf16, f32, dma = jnp.bfloat16, jnp.float32, pltpu.SemaphoreType.DMA
    vmem, anywhere = pl.BlockSpec(memory_space=pltpu.VMEM), pl.BlockSpec(memory_space=pl.ANY)

    def shape(dims, kind=bf16):
        return jax.ShapeDtypeStruct(dims, kind)

    smem = pl.BlockSpec(memory_space=pltpu.SMEM)
    ins = dict(
        live=smem,
        x=vmem,
        grad=vmem,
        packed=vmem,
        mixed=vmem,
        residual=vmem,
        tokens=vmem,
        gates=vmem,
        summed=vmem,
        route=vmem,
        qkv=vmem,
        proj=vmem,
        vectors=vmem,
        router=vmem,
        blocks=anywhere,
    )
    outs = dict(
        block_out=shape(x.shape, f32),
        grad_out=shape(x.shape, f32),
        qkv_out=shape((shard_rows, 3 * width)),
        proj_out=shape((shard_rows, width)),
        small_out=shape((small_rows, round_up(shard_rows, 128)), f32),
        bias_out=shape((1, side), f32),
        blocks_out=shape((shard_rows, shards * width)),
    )
    scratch = dict(
        flat=pltpu.VMEM((rows, width), f32),
        upstream=pltpu.VMEM((rows, width), f32),
        res_grad=pltpu.VMEM((rows, width), f32),
        attn_t=pltpu.VMEM((width, rows), bf16),
        mixed_grad=pltpu.VMEM((rows, width), bf16),
        packed_grad=pltpu.VMEM((rows, 3 * width), bf16),
        totals=pltpu.VMEM((small_rows, width), f32),
        weights=pltpu.VMEM((4, 2, shards, chips, piece, side), bf16),
        twin_in=pltpu.VMEM((4, shards, chips, piece, side), bf16),
        plane_sum=pltpu.VMEM((4, shards, chips, piece, side), bf16),
        peer_in=pltpu.VMEM((4, chips, shards, piece, side), bf16),
        far_out=pltpu.VMEM((4, shards, piece, side), bf16),
        far_in=pltpu.VMEM((4, shards, piece, side), bf16),
        whole=pltpu.VMEM((4, 2, chips, piece, side), bf16),
        small=pltpu.VMEM((small_rows, width), bf16),
        small_in=pltpu.VMEM((2 * chips, small_rows, width), bf16),
        small_sum=pltpu.VMEM((small_rows, width), bf16),
        small_far=pltpu.VMEM((shards, small_rows, width), bf16),
        here=dma((1,)),
    )
    pairs = dict(
        block=(shards,),
        twin=(4,),
        peer=(4, chips),
        far=(4, shards),
        back=(4, chips),
        last=(4, chips),
        small=(2 * chips,),
        edge=(shards,),
    )
    for name, dims in pairs.items():
        scratch[name + "_s"] = dma(dims)
        scratch[name + "_r"] = dma(dims)
    names = tuple(ins) + tuple(outs) + tuple(scratch)
    return pl.pallas_call(
        functools.partial(backward_reduce_kernel, shards, chips, stride, names),
        out_shape=list(outs.values()),
        in_specs=list(ins.values()),
        out_specs=[vmem] * 6 + [anywhere],
        scratch_shapes=list(scratch.values()),
        compiler_params=pltpu.CompilerParams(
            collective_id=2, has_side_effects=True, vmem_limit_bytes=BIG_VMEM
        ),
        name="backward_and_reduce",
    )(*inputs)


def reduce_slow(grads, extra, blocks):
    width = grads.shape[2] // 2
    wide = 3 * width // 2
    joined = jnp.concatenate(
        [grads[0, :, :wide], grads[1, :, :wide], grads[0, :, wide:], grads[1, :, wide:]],
        axis=1,
    )
    mine = lax.psum_scatter(joined, "shard", scatter_dimension=0, tiled=True)
    mine = as_float(lax.psum(mine, "expert"))
    extra_sum = as_float(lax.psum(extra, ("shard", "expert")))
    moved = lax.all_to_all(blocks, "shard", split_axis=0, concat_axis=0, tiled=True)
    return mine[:, : 3 * width], mine[:, 3 * width :], extra_sum, moved


def attention_core(stride, expert_count, r):
    rows, width = r.flat.shape
    bf16 = jnp.bfloat16
    mask = same_image(rows, stride, r.x.shape[0])
    low_lanes = lax.broadcasted_iota(jnp.int32, (rows, 128), 1) < HEAD_DIM

    def attend(pair, carry):
        def part(which):
            return r.packed[:, pl.ds(pl.multiple_of(which * width + pair * 128, 128), 128)]

        query, key, value = part(0), part(1), part(2)
        zero = jnp.zeros_like(query)
        weights_low = masked_softmax(jnp.where(low_lanes, query, zero), key, mask).astype(bf16)
        weights_high = masked_softmax(jnp.where(low_lanes, zero, query), key, mask).astype(bf16)
        r.mixed[:, pl.ds(pl.multiple_of(pair * 128, 128), 128)] = jnp.where(
            low_lanes, plain_dot(weights_low, value), plain_dot(weights_high, value)
        ).astype(bf16)
        return carry

    lax.fori_loop(0, HEADS // 2, attend, 0)


def route_core(expert_count, r, proj):
    bf16 = jnp.bfloat16
    residual = r.flat[...] + plain_dot(r.mixed[...], proj) + r.vectors[2:3, :]
    r.residual[...] = residual
    normed_two, _ = norm_stats(residual)
    expert_in = (normed_two * r.vectors[3:4, :] + r.vectors[4:5, :]).astype(bf16)
    r.tokens[...] = expert_in
    r.gates[...] = softmax_gates(expert_in, r.router[...], expert_count)


def softmax_gates(rows, router, expert_count):
    logits = contract_cols(rows, router)
    lanes = lax.broadcasted_iota(jnp.int32, logits.shape, 1)
    logits = jnp.where(lanes < expert_count, logits, -1e30)
    shifted = jnp.exp(logits - jnp.max(logits, axis=-1, keepdims=True))
    return shifted / jnp.sum(shifted, axis=-1, keepdims=True)


def fused_kernel(shards, experts, capacity, expert_count, stride, names, *refs):
    r = types.SimpleNamespace(**dict(zip(names, refs)))
    chips = experts // 2
    place = Place(shards, chips)
    bf16 = jnp.bfloat16
    me, shard = place.expert, place.shard
    row_count, width = r.tokens.shape
    group_rows = r.rows_in.shape[1]
    shard_rows = r.qkv.shape[0]
    seq_length, image_count = r.x.shape[:2]
    first_rows = 2 * capacity // 16 * 16
    second_rows = group_rows - first_rows
    upper = lax.div(shard, 2)
    even = lax.rem(shard, 2) == 0
    place.greet(
        [place.along(j) for j in range(1, shards)]
        + [place.plane(i) for i in range(1, experts)]
    )
    order = (1, 3, 2)
    spans = (
        (upper * second_rows, first_rows),
        ((1 - upper) * first_rows, second_rows),
    )

    def with_pair(act):
        @pl.when(even)
        def _():
            act(3)

        @pl.when(jnp.logical_not(even))
        def _():
            act(1)

    def push_pair(copy):
        @pl.when(even)
        def _():
            copy(1).start()

        @pl.when(jnp.logical_not(even))
        def _():
            copy(3).start()

    def push_others(copy):
        with_pair(lambda j: copy(j).start())
        copy(2).start()

    def wait_others(copy):
        @pl.when(even)
        def _():
            copy(1).wait_recv()

        @pl.when(jnp.logical_not(even))
        def _():
            copy(3).wait_recv()

        copy(2).wait_recv()

    kinds = ((r.qkv, r.qkv_all), (r.proj, r.proj_all))

    def target(i):
        return lax.rem(me + i, experts)

    def origin(i):
        return lax.rem(me - i + experts, experts)

    def owner(j):
        return lax.rem(shard - j + shards, shards)

    def cut(kind, chip_step):
        source = kinds[kind][0]
        rows = source.shape[0] // chips
        cols = source.shape[1] // 2
        chip = lax.rem(place.chip + chip_step + chips, chips)
        return (
            pl.ds(pl.multiple_of(chip * rows, 16), rows),
            pl.ds(pl.multiple_of(place.core * cols, 128), cols),
        )

    def far_copy(kind, j):
        rows, cols = cut(kind, 0)
        return remote(
            kinds[kind][0].at[rows, cols],
            kinds[kind][1].at[shard, rows, cols],
            r.far_s.at[kind, j],
            r.far_r.at[kind, j],
            place.along(j),
        )

    def to_twin(kind, j, i):
        rows, cols = cut(kind, -i)
        block = kinds[kind][1].at[owner(j), rows, cols]
        return remote(
            block, block, r.twin_s.at[kind, j, i], r.twin_r.at[kind, j, i], place.sibling()
        )

    def to_peer(kind, j, i):
        rows, cols = cut(kind, 0)
        block = kinds[kind][1].at[owner(j), rows, cols]
        return remote(
            block, block, r.peer_s.at[kind, j, i], r.peer_r.at[kind, j, i], place.peer(i)
        )

    def small_copy(which, j):
        src, dst = ((r.extra, r.extra_all), (r.slots, r.slots_all))[which]
        return remote(
            src, dst.at[shard], r.small_s.at[which, j], r.small_r.at[which, j], place.along(j)
        )

    def up_line_copy(j):
        return remote(
            r.up, r.up_line.at[shard], r.upline_s.at[j], r.upline_r.at[j], place.along(j)
        )

    r.extra[...] = jnp.zeros_like(r.extra)
    r.extra[:expert_count, :shard_rows] = r.router_part[...]
    r.extra[expert_count : expert_count + VECTORS, :shard_rows] = r.rows7[...]
    for j in order:
        small_copy(0, j).start()
    for kind in range(2):
        for j in order:
            far_copy(kind, j).start()
    local = [
        pltpu.make_async_copy(r.qkv, r.qkv_all.at[shard], r.here.at[0]),
        pltpu.make_async_copy(r.proj, r.proj_all.at[shard], r.here.at[1]),
    ]
    for copy in local:
        copy.start()
    r.extra_all[shard] = r.extra[...]
    spread_rows(r.flat, r.grad, image_count, seq_length, stride)
    r.slot_col[...] = jnp.zeros_like(r.slot_col) - 1.0
    for image in range(image_count):
        here = slice(image * stride, (image + 1) * stride)
        alive = r.live[image].astype(jnp.float32)
        r.up[here, :] = (r.flat[here, :] * alive).astype(bf16)
        r.turn[...] = jnp.zeros_like(r.turn)
        r.turn[0:2, :seq_length] = r.routes[image].astype(jnp.float32)
        named = r.turn[...].T[:seq_length]
        r.slot_col[image * stride : image * stride + seq_length, 0:8] = (
            named * alive - (1.0 - alive)
        )
    lanes = lax.broadcasted_iota(jnp.int32, (row_count, 128), 1)
    lane_ids = lanes.astype(jnp.float32)
    first, second = (r.slot_col[:row_count, k : k + 1] for k in range(2))
    chosen = (lane_ids == first) | (lane_ids == second)
    earlier = lax.broadcasted_iota(jnp.int32, (row_count, row_count), 0) > (
        lax.broadcasted_iota(jnp.int32, (row_count, row_count), 1)
    )
    place_in = plain_dot(
        jnp.where(earlier, 1.0, 0.0).astype(bf16), jnp.where(chosen, 1.0, 0.0).astype(bf16)
    )
    place_in += lane_ids * group_rows + (shard * capacity).astype(jnp.float32)
    both = jnp.zeros((row_count, 128), jnp.float32)
    for k, named in enumerate((first, second)):
        slot = jnp.sum(jnp.where(lane_ids == named, place_in, 0.0), axis=-1, keepdims=True)
        both += jnp.where(lanes == k, jnp.where(named < 0.0, -1.0, slot), 0.0)
    r.slots[...] = jnp.zeros_like(r.slots)
    r.slots[:, :row_count] = both.T[:8]
    for j in order:
        small_copy(1, j).start()
    r.slots_all[shard] = r.slots[...]
    r.up_line[shard] = r.up[...]
    spread_rows(r.flat, r.x, image_count, seq_length, stride)

    for kind in range(2):
        for j in order:
            far_copy(kind, j).wait_recv()
            for i in range(1, chips):
                to_peer(kind, j, i).start()
            to_twin(kind, j, 0).start()
    push_pair(up_line_copy)

    for j in order:
        small_copy(0, j).wait_recv()
    lane_from = lax.broadcasted_iota(jnp.int32, (r.extra.shape[1], width), 0)
    lane_to = lax.broadcasted_iota(jnp.int32, (r.extra.shape[1], width), 1)

    def placed(source, at):
        hit = (lane_to == lane_from + at * shard_rows) & (lane_from < shard_rows)
        return plain_dot(r.extra_all[source], jnp.where(hit, 1.0, 0.0).astype(bf16))

    whole = placed(0, 0)
    for at in range(1, shards):
        whole += placed(at, at)
    r.vectors[...] = whole[expert_count : expert_count + 8]
    r.router[...] = jnp.zeros_like(r.router)
    r.router[:expert_count, :] = whole[:expert_count].astype(bf16)
    biases = []
    for first in (0, shards // 2):
        total = jnp.zeros((1, width), jnp.float32)
        for at in range(shards):
            row = expert_count + VECTORS - 2 + at % 2
            total += placed(first + at // 2, at)[row : row + 1]
        biases.append(total)
    hit = (lane_to == lane_from + shard * shard_rows) & (lane_from < shard_rows)
    own_bias = plain_dot(
        jnp.broadcast_to(as_float(r.out_bias[...]), (16, shard_rows)).astype(bf16),
        jnp.where(hit, 1.0, 0.0).astype(bf16)[:shard_rows],
    )
    r.own_bias[...] = own_bias[:8]
    normed, _ = norm_stats(r.flat[...])
    r.attn[...] = (normed * r.vectors[0:1, :] + r.vectors[1:2, :]).astype(bf16)

    push_others(up_line_copy)
    for kind in range(2):
        for j in order:
            for i in range(1, chips):
                to_peer(kind, j, i).wait_recv()
                to_twin(kind, j, i).start()

    for j in order:
        small_copy(1, j).wait_recv()
    for at in range(shards):
        r.slot_col[at * row_count : (at + 1) * row_count, 0:8] = r.slots_all[at].T[:row_count]

    def table(at, base, size):
        ids = (lax.broadcasted_iota(jnp.int32, (size, row_count), 0) + base).astype(jnp.float32)
        slots = r.slots_all[at]
        hit = (ids == slots[0:1, :row_count]) | (ids == slots[1:2, :row_count])
        return jnp.where(hit, 1.0, 0.0).astype(bf16)

    def slot_copy(stage, landing, send_sems, recv_sems, i, part):
        start, size = spans[part]
        here = pl.ds(pl.multiple_of(start, 16), size)
        return remote(
            stage.at[target(i), here],
            landing.at[me, here],
            send_sems.at[i, part],
            recv_sems.at[i, part],
            place.plane(i),
        )

    def up_copy(i, part):
        return slot_copy(r.stage_a, r.up_in, r.up_s, r.up_r, i, part)

    def row_copy(i, part):
        return slot_copy(r.stage_b, r.rows_in, r.row_s, r.row_r, i, part)

    def dispatch(part, sources, line, stage, landing, copy):
        start, size = spans[part]
        here = pl.ds(pl.multiple_of(start, 16), size)

        def one(i, carry):
            to = target(i)
            base = to * group_rows + start
            picked = plain_dot(table(sources[0], base, size), line[sources[0]])
            for at in sources[1:]:
                picked += plain_dot(table(at, base, size), line[at])
            picked = picked.astype(bf16)

            @pl.when(i == 0)
            def _():
                landing[me, here, :] = picked

            @pl.when(i > 0)
            def _():
                stage[to, here, :] = picked
                copy(i, part).start()

            return carry

        lax.fori_loop(0, experts, one, 0)

    pair_planes = (2 * upper, 2 * upper + 1)
    all_planes = tuple(range(shards))
    with_pair(lambda j: up_line_copy(j).wait_recv())
    dispatch(0, pair_planes, r.up_line, r.stage_a, r.up_in, up_copy)

    hidden = r.in_w.shape[1]

    def weight_copy(j, part):
        part_cols = hidden // 2
        start = lax.rem(shard + j, shards) * hidden + part * part_cols
        rows = pl.ds(pl.multiple_of(shard * shard_rows, 16), shard_rows)
        return remote(
            r.out_wt.at[:, pl.ds(pl.multiple_of(start, 128), part_cols)],
            r.out_w.at[rows, pl.ds(part * part_cols, part_cols)],
            r.weight_s.at[j, part],
            r.weight_r.at[j, part],
            place.along(j),
        )

    weight_local = pltpu.make_async_copy(
        r.out_wt.at[:, pl.ds(pl.multiple_of(shard * hidden, 128), hidden)],
        r.out_w.at[pl.ds(pl.multiple_of(shard * shard_rows, 16), shard_rows)],
        r.here.at[2],
    )
    weight_local.start()
    for copy in local:
        copy.wait()
    for j in order:
        for i in range(chips):
            to_twin(0, j, i).wait_recv()

    def project(tile, carry):
        cols = pl.ds(pl.multiple_of(tile * width, 128), width)
        weight = r.qkv_all[:, :, cols].reshape(width, width)
        bias = jnp.where(tile == 0, biases[0], jnp.where(tile == 2, biases[1], 0.0))
        r.packed[:, cols] = (plain_dot(r.attn[...], weight) + bias).astype(bf16)
        return carry

    lax.fori_loop(0, 3, project, 0)
    attention_core(stride, expert_count, r)
    wait_others(up_line_copy)
    for j in order:
        weight_copy(j, 0).start()
    dispatch(1, all_planes, r.up_line, r.stage_a, r.up_in, up_copy)
    for j in order:
        for i in range(chips):
            to_twin(1, j, i).wait_recv()
    route_core(expert_count, r, r.proj_all[...].reshape(width, width))

    def line_copy(j):
        return remote(
            r.tokens, r.line.at[shard], r.line_s.at[j], r.line_r.at[j], place.along(j)
        )

    push_pair(line_copy)
    r.line[shard] = r.tokens[...]

    with_pair(lambda j: line_copy(j).wait_recv())
    push_others(line_copy)
    dispatch(0, pair_planes, r.line, r.stage_b, r.rows_in, row_copy)
    wait_others(line_copy)
    for j in order:
        weight_copy(j, 1).start()
    dispatch(1, all_planes, r.line, r.stage_b, r.rows_in, row_copy)

    def keep_table(at, carry):
        ids = lax.broadcasted_iota(jnp.int32, (shards * row_count, group_rows), 1)
        ids = (ids + at * group_rows).astype(jnp.float32)
        hit = (ids == r.slot_col[:, 0:1]) | (ids == r.slot_col[:, 1:2])
        r.tables[at] = jnp.where(hit, 1.0, 0.0).astype(bf16)
        return carry

    lax.fori_loop(0, experts, keep_table, 0)

    half, third = width // 2, width // 3

    def out_copy(i, part):
        cols = pl.ds(part * half, half)
        return remote(
            r.stage_a.at[origin(i), :, cols],
            r.out_in.at[me, :, cols],
            r.out_s.at[i, part],
            r.out_r.at[i, part],
            place.plane(experts - i),
        )

    def note_copy(i):
        return remote(
            r.notes.at[origin(i)],
            r.note_in.at[me],
            r.note_s.at[i],
            r.note_r.at[i],
            place.plane(experts - i),
        )

    def back_copy(i, part):
        cols = pl.ds(part * third, third)
        return remote(
            r.stage_b.at[origin(i), :, cols],
            r.back_in.at[me, :, cols],
            r.back_s.at[i, part],
            r.back_r.at[i, part],
            place.plane(experts - i),
        )

    weight_local.wait()
    for j in order:
        for part in range(2):
            weight_copy(j, part).wait_recv()

    def drain_up(i, carry):
        for part in range(2):
            up_copy(i, part).wait_send()
        return carry

    lax.fori_loop(1, experts, drain_up, 0)
    r.notes[...] = jnp.zeros_like(r.notes)

    def forward(i, carry):
        at = origin(i)

        @pl.when(i > 0)
        def _():
            for part in range(2):
                row_copy(i, part).wait_recv()

        rows = r.rows_in[at]
        gelu_out, gelu_slope = gelu_parts(
            plain_dot(rows, r.in_w[...]) + as_float(r.in_bias[...])
        )
        r.slope[at] = gelu_slope
        gelu_bf = gelu_out.astype(bf16)
        r.gelu[at] = gelu_bf
        gates = softmax_gates(rows, r.router[...], expert_count)
        gate_lanes = lax.broadcasted_iota(jnp.int32, gates.shape, 1)
        gate = jnp.sum(jnp.where(gate_lanes == me, gates, 0.0), axis=-1, keepdims=True)

        @pl.when(i > 0)
        def _():
            for part in range(2):
                up_copy(i, part).wait_recv()

        upstream = as_float(r.up_in[at])
        r.sent[at] = (gate * upstream).astype(bf16)
        expert_out = contract_cols(gelu_bf, r.out_w[...]) + r.own_bias[0:1, :]
        gate_grad = jnp.sum(upstream * expert_out, axis=-1, keepdims=True)
        notes = jnp.broadcast_to(gate_grad, (group_rows, 128)).T[:16].astype(bf16)
        gated = (gate * expert_out).astype(bf16)

        @pl.when(i == 0)
        def _():
            r.out_in[me] = gated
            r.note_in[me, :, :group_rows] = notes

        @pl.when(i > 0)
        def _():
            r.stage_a[at] = gated
            r.notes[at, :, :group_rows] = notes
            out_copy(i, 0).start()
            note_copy(i).start()

        return carry

    lax.fori_loop(0, experts, forward, 0)

    def push_out(i, carry):
        out_copy(i, 1).start()
        return carry

    lax.fori_loop(1, experts, push_out, 0)
    r.in_bias_grad[...] = jnp.zeros_like(r.in_bias_grad)
    r.out_bias_grad[...] = jnp.zeros_like(r.out_bias_grad)

    def drain_rows(i, carry):
        for part in range(2):
            row_copy(i, part).wait_send()
        return carry

    lax.fori_loop(1, experts, drain_rows, 0)

    def backward(i, carry):
        at = origin(i)
        sent = r.sent[at]
        r.out_bias_grad[0:1, :] += jnp.sum(as_float(sent), axis=0, keepdims=True)
        pre_grad = plain_dot(sent, r.out_w[...]) * r.slope[at]
        r.in_bias_grad[0:1, :] += jnp.sum(pre_grad, axis=0, keepdims=True)
        pre_bf = pre_grad.astype(bf16)
        r.pre[at] = pre_bf
        back = contract_cols(pre_bf, r.in_w[...]).astype(bf16)

        @pl.when(i == 0)
        def _():
            r.back_in[me] = back

        @pl.when(i > 0)
        def _():
            r.stage_b[at] = back
            back_copy(i, 0).start()

        return carry

    lax.fori_loop(0, experts, backward, 0)

    for part in range(1, 3):

        def push_rest(i, carry, part=part):
            back_copy(i, part).start()
            return carry

        lax.fori_loop(1, experts, push_rest, 0)

    def collect(landing, copy, part, size):
        cols = pl.ds(part * size, size)

        def one(i, carry):
            at = target(i)

            @pl.when(i > 0)
            def _():
                copy(i, part).wait_recv()

            r.total[:, cols] += plain_dot(r.tables[at], landing[at, :, cols])
            return carry

        lax.fori_loop(0, experts, one, 0)

    def collect_notes(i, carry):
        at = target(i)

        @pl.when(i > 0)
        def _():
            note_copy(i).wait_recv()

        rows_at = lax.broadcasted_iota(jnp.int32, (128, group_rows), 0)
        note = as_float(r.note_in[at, 0:1, :group_rows])
        r.total[:, width:] += contract_cols(
            r.tables[at], jnp.where(rows_at == at, note, 0.0).astype(bf16)
        )
        return carry

    columns = ((0, half), (half, half)) + tuple((at * third, third) for at in range(3))

    def sum_copy(which, j):
        src, dst = (r.far_out, r.far_out_in) if which < 2 else (r.far_back, r.far_back_in)
        to = lax.rem(shard + j, shards)
        cols = pl.ds(*columns[which])
        return remote(
            src.at[to, :, cols],
            dst.at[j, :, cols],
            r.sum_s.at[which, j],
            r.sum_r.at[which, j],
            place.along(j),
        )

    def note_sum_copy(j):
        return remote(
            r.note_far.at[lax.rem(shard + j, shards)],
            r.note_far_in.at[j],
            r.notesum_s.at[j],
            r.notesum_r.at[j],
            place.along(j),
        )

    own = pl.ds(pl.multiple_of(shard * row_count, 16), row_count)

    def spread_sums(which):
        far = r.far_out if which < 2 else r.far_back
        cols = pl.ds(*columns[which])
        for at in range(shards):
            far[at, :, cols] = r.total[at * row_count : (at + 1) * row_count, cols].astype(bf16)
        for j in order:
            sum_copy(which, j).start()

    def weigh(left, right, grad):
        tile = 128

        def one(at, carry):
            cols = pl.ds(pl.multiple_of(at * tile, 128), tile)
            lhs = left[:, :, cols].reshape(experts * group_rows, tile)
            rhs = right[...].reshape(experts * group_rows, right.shape[2])
            grad[cols, :] = contract_rows(lhs, rhs).astype(grad.dtype)
            return carry

        lax.fori_loop(0, left.shape[2] // tile, one, 0)

    r.total[...] = jnp.zeros_like(r.total)
    collect(r.out_in, out_copy, 0, half)
    spread_sums(0)
    lax.fori_loop(0, experts, collect_notes, 0)
    r.note_far[...] = jnp.zeros_like(r.note_far)
    for at in range(shards):
        notes = r.total[at * row_count : (at + 1) * row_count, width:].T
        r.note_far[at, :, :row_count] = notes[: r.note_far.shape[1]].astype(bf16)
    for j in order:
        note_sum_copy(j).start()
    weigh(r.sent, r.gelu, r.out_grad)
    collect(r.out_in, out_copy, 1, half)
    spread_sums(1)
    r.summed[...] = r.total[own, :]
    weigh(r.rows_in, r.pre, r.in_grad)
    r.total[...] = jnp.zeros_like(r.total)
    for part in range(3):
        collect(r.back_in, back_copy, part, third)
        spread_sums(2 + part)
    r.route[...] = r.total[own, :width]
    for j in order:
        note_sum_copy(j).wait_recv()
        notes = as_float(r.note_far_in[j]).T
        lanes_in = notes.shape[1]
        r.summed[:, width : width + lanes_in] += notes[:row_count]
    for which in range(5):
        cols = pl.ds(*columns[which])
        for j in order:
            sum_copy(which, j).wait_recv()
            if which < 2:
                r.summed[:, cols] += as_float(r.far_out_in[j, :, cols])
            else:
                r.route[:, cols] += as_float(r.far_back_in[j, :, cols])

    for j in order:
        for which in range(2):
            far_copy(which, j).wait_send()
            small_copy(which, j).wait_send()
            for i in range(chips):
                to_twin(which, j, i).wait_send()
                if i:
                    to_peer(which, j, i).wait_send()
        for which in range(5):
            sum_copy(which, j).wait_send()
        note_sum_copy(j).wait_send()
        up_line_copy(j).wait_send()
        line_copy(j).wait_send()
        for part in range(2):
            weight_copy(j, part).wait_send()

    def finish(i, carry):
        out_copy(i, 0).wait_send()
        out_copy(i, 1).wait_send()
        note_copy(i).wait_send()
        for part in range(3):
            back_copy(i, part).wait_send()
        return carry

    lax.fori_loop(1, experts, finish, 0)


def fused_pass(shards, experts, capacity, expert_count, stride, inputs):
    x, qkv, proj, in_w = (inputs[at] for at in (1, 4, 5, 8))
    extra_shape = (round_up(VECTORS + expert_count, 16), round_up(qkv.shape[0], 128))
    width, hidden = in_w.shape
    row_count = x.shape[1] * stride
    router_pad = round_up(expert_count, 128)
    group_rows = round_up(shards * capacity, 16)
    lanes = round_up(group_rows, 128)
    chips = experts // 2
    bf16, f32, dma = jnp.bfloat16, jnp.float32, pltpu.SemaphoreType.DMA
    vmem, anywhere = pl.BlockSpec(memory_space=pltpu.VMEM), pl.BlockSpec(memory_space=pl.ANY)

    def shape(dims, kind=bf16):
        return jax.ShapeDtypeStruct(dims, kind)

    smem = pl.BlockSpec(memory_space=pltpu.SMEM)
    ins = dict(
        live=smem,
        x=vmem,
        grad=vmem,
        routes=vmem,
        qkv=anywhere,
        proj=anywhere,
        rows7=vmem,
        router_part=vmem,
        in_w=vmem,
        out_wt=anywhere,
        in_bias=vmem,
        out_bias=vmem,
    )
    outs = dict(
        qkv_all=shape((shards,) + qkv.shape),
        proj_all=shape((shards,) + proj.shape),
        vectors=shape((8, width), f32),
        router=shape((router_pad, width)),
        packed=shape((row_count, 3 * width)),
        mixed=shape((row_count, width)),
        residual=shape((row_count, width), f32),
        tokens=shape((row_count, width)),
        gates=shape((row_count, router_pad), f32),
        summed=shape((row_count, width + 128), f32),
        route=shape((row_count, width), f32),
        in_grad=shape((width, hidden), f32),
        out_grad=shape((width, hidden)),
        in_bias_grad=shape((1, hidden), f32),
        out_bias_grad=shape((1, width), f32),
    )
    group = (experts, group_rows)
    note_rows = round_up(expert_count, 16)
    scratch = dict(
        flat=pltpu.VMEM((row_count, width), f32),
        attn=pltpu.VMEM((row_count, width), bf16),
        up=pltpu.VMEM((row_count, width), bf16),
        turn=pltpu.VMEM((8, 128), f32),
        slots=pltpu.VMEM((8, round_up(row_count, 128)), f32),
        own_bias=pltpu.VMEM((8, width), f32),
        extra=pltpu.VMEM(extra_shape, bf16),
        extra_all=pltpu.VMEM((shards,) + extra_shape, bf16),
        slots_all=pltpu.VMEM((shards, 8, round_up(row_count, 128)), f32),
        slot_col=pltpu.VMEM((shards * row_count, 128), f32),
        up_line=pltpu.VMEM((shards, row_count, width), bf16),
        line=pltpu.VMEM((shards, row_count, width), bf16),
        out_w=pltpu.VMEM((width, hidden), bf16),
        up_in=pltpu.VMEM(group + (width,), bf16),
        stage_a=pltpu.VMEM(group + (width,), bf16),
        stage_b=pltpu.VMEM(group + (width,), bf16),
        rows_in=pltpu.VMEM(group + (width,), bf16),
        gelu=pltpu.VMEM(group + (hidden,), bf16),
        slope=pltpu.VMEM(group + (hidden,), f32),
        sent=pltpu.VMEM(group + (width,), bf16),
        pre=pltpu.VMEM(group + (hidden,), bf16),
        out_in=pltpu.VMEM(group + (width,), bf16),
        back_in=pltpu.VMEM(group + (width,), bf16),
        notes=pltpu.VMEM((experts, 16, lanes), bf16),
        note_in=pltpu.VMEM((experts, 16, lanes), bf16),
        total=pltpu.VMEM((shards * row_count, width + 128), f32),
        far_out=pltpu.VMEM((shards, row_count, width), bf16),
        far_out_in=pltpu.VMEM((shards, row_count, width), bf16),
        note_far=pltpu.VMEM((shards, note_rows, round_up(row_count, 128)), bf16),
        note_far_in=pltpu.VMEM((shards, note_rows, round_up(row_count, 128)), bf16),
        tables=pltpu.VMEM((experts, shards * row_count, group_rows), bf16),
        far_back=pltpu.VMEM((shards, row_count, width), bf16),
        far_back_in=pltpu.VMEM((shards, row_count, width), bf16),
        here=dma((3,)),
    )
    pairs = dict(
        far=(2, shards),
        twin=(2, shards, chips),
        peer=(2, shards, chips),
        small=(2, shards),
        upline=(shards,),
        up=(experts, 2),
        line=(shards,),
        weight=(shards, 2),
        row=(experts, 2),
        out=(experts, 2),
        note=(experts,),
        back=(experts, 3),
        sum=(5, shards),
        notesum=(shards,),
    )
    for name, dims in pairs.items():
        scratch[name + "_s"] = dma(dims)
        scratch[name + "_r"] = dma(dims)
    names = tuple(ins) + tuple(outs) + tuple(scratch)
    return pl.pallas_call(
        functools.partial(fused_kernel, shards, experts, capacity, expert_count, stride, names),
        out_shape=list(outs.values()),
        in_specs=list(ins.values()),
        out_specs=[vmem] * len(outs),
        scratch_shapes=list(scratch.values()),
        compiler_params=pltpu.CompilerParams(
            collective_id=1, has_side_effects=True, vmem_limit_bytes=BIG_VMEM
        ),
        name="front_and_experts",
    )(*inputs)


def expert_slow(
    tokens, gates, route_rows, tables, line_up, up_in, in_slice, out_slice, in_bias, own_bias
):
    row_count, width = tokens.shape
    bf16 = jnp.bfloat16
    table_0, table_1, send_table = tables
    router_pad = gates.shape[1]
    chosen = route_rows[:, :, None] == jnp.arange(router_pad, dtype=jnp.int32)[None, None, :]
    gate_pick = jnp.sum(jnp.where(chosen, gates[:, None, :], 0.0), axis=2)
    gate_high = gate_pick.astype(bf16)
    gate_low = (gate_pick - as_float(gate_high)).astype(bf16)
    gate_notes = jnp.concatenate([gate_high, gate_low], axis=1)
    gate_notes = jnp.pad(gate_notes, ((0, 0), (0, 128 - gate_notes.shape[1])))
    sent_line = jnp.concatenate([tokens, gate_notes], axis=1)
    row_line = lax.all_gather(sent_line, "shard", axis=0, tiled=True)
    line_in = row_line[:, :width]
    gate_line = as_float(row_line[:, width : width + 4])
    line_gate = gate_line[:, 0:2] + gate_line[:, 2:4]
    outgoing = contract_rows(send_table, line_in).astype(bf16)
    slot_gate = jnp.sum(
        jnp.where(table_0, line_gate[:, 0:1], 0.0) + jnp.where(table_1, line_gate[:, 1:2], 0.0),
        axis=0,
    )
    slot_high = slot_gate.astype(bf16)
    slot_low = (slot_gate - as_float(slot_high)).astype(bf16)
    slot_notes = jnp.pad(jnp.stack([slot_high, slot_low], axis=1), ((0, 0), (0, 126)))
    incoming = lax.all_to_all(
        jnp.concatenate([outgoing, slot_notes], axis=1),
        "expert",
        split_axis=0,
        concat_axis=0,
        tiled=True,
    )
    rows_in = incoming[:, :width]
    gate_in = as_float(incoming[:, width : width + 1]) + as_float(
        incoming[:, width + 1 : width + 2]
    )
    grad_in = (as_float(up_in) * gate_in).astype(bf16)
    pre_act = plain_dot(rows_in, in_slice) + in_bias
    gelu_out, gelu_slope = gelu_parts(pre_act)
    gelu_bf = gelu_out.astype(bf16)
    expert_out = (plain_dot(gelu_bf, out_slice) + own_bias).astype(bf16)
    returned = lax.all_to_all(expert_out, "expert", split_axis=0, concat_axis=0, tiled=True)
    pre_grad = contract_cols(grad_in, out_slice) * gelu_slope
    pre_bf = pre_grad.astype(bf16)
    back_rows = contract_cols(pre_bf, in_slice).astype(bf16)
    returned_grad = lax.all_to_all(back_rows, "expert", split_axis=0, concat_axis=0, tiled=True)
    out_0 = plain_dot(table_0.astype(bf16), returned)
    out_1 = plain_dot(table_1.astype(bf16), returned)
    combined = line_gate[:, 0:1] * out_0 + line_gate[:, 1:2] * out_1
    line_up_wide = as_float(line_up)
    gate_grad_line = jnp.stack(
        [jnp.sum(line_up_wide * out_0, axis=1), jnp.sum(line_up_wide * out_1, axis=1)], axis=1
    )
    joined = jnp.concatenate(
        [combined.astype(bf16), jnp.pad(gate_grad_line, ((0, 0), (0, 126))).astype(bf16)], axis=1
    )
    summed = as_float(lax.psum_scatter(joined, "shard", scatter_dimension=0, tiled=True))
    picked = jnp.sum(
        jnp.where(chosen, summed[:, width : width + 2][:, :, None], 0.0), axis=1
    )
    summed = jnp.concatenate([summed[:, :width], picked], axis=1)
    back_line = plain_dot(send_table, returned_grad)
    route_grad = lax.psum_scatter(back_line.astype(bf16), "shard", scatter_dimension=0, tiled=True)
    return (
        summed,
        route_grad,
        contract_rows(rows_in, pre_bf),
        contract_rows(gelu_bf, grad_in).astype(bf16),
        jnp.sum(pre_grad, axis=0)[None],
        jnp.sum(as_float(grad_in), axis=0)[None],
    )


def body(
    block_input,
    image_live,
    expert_routes,
    first_gain,
    first_shift,
    qkv_weight,
    query_value_bias,
    attn_out_weight,
    attn_out_bias,
    second_gain,
    second_shift,
    router_weight,
    expert_in_weight,
    expert_in_bias,
    expert_out_weight,
    expert_out_bias,
    output_grad,
):
    image_count, seq_length, width = block_input.shape
    shards = lax.axis_size("shard")
    experts = lax.axis_size("expert")
    chips = experts // 2
    expert_count = router_weight.shape[1]
    my_shard = lax.axis_index("shard")
    shard_rows = first_gain.shape[0]
    stride = round_up(seq_length, 8)
    row_count = image_count * stride
    capacity = (3 * image_count * seq_length + expert_count - 1) // expert_count
    group_rows = round_up(shards * capacity, 16)
    slot_rows = expert_count * group_rows
    bf16 = jnp.bfloat16
    fast = chips == 4 and shards == 4 and shard_rows % (16 * chips) == 0

    router_pad = round_up(expert_count, 128)
    extra_rows = round_up(VECTORS + expert_count, 16)
    extra_cols = round_up(shard_rows, 128)
    vector_rows = jnp.concatenate(
        [
            first_gain,
            first_shift,
            attn_out_bias,
            second_gain,
            second_shift,
            query_value_bias,
        ]
    ).reshape(VECTORS, shard_rows)
    turned_in = jnp.transpose(block_input, (1, 0, 2))
    turned_grad = jnp.transpose(output_grad, (1, 0, 2))
    in_slice = expert_in_weight[0]
    out_slice_t = expert_out_weight[0].T
    if fast:
        (
            qkv_full,
            proj_full,
            vectors,
            router_t,
            packed,
            mixed,
            residual,
            expert_in,
            gates,
            summed,
            route_grad,
            in_weight_grad,
            out_weight_grad,
            in_bias_sum,
            out_bias_sum,
        ) = fused_pass(
            shards,
            experts,
            capacity,
            expert_count,
            stride,
            (
                image_live,
                turned_in,
                turned_grad,
                jnp.transpose(expert_routes, (0, 2, 1)),
                qkv_weight,
                attn_out_weight,
                vector_rows,
                router_weight.T,
                in_slice,
                out_slice_t,
                expert_in_bias,
                expert_out_bias,
            ),
        )
        qkv_full = qkv_full.reshape(width, 3 * width)
        proj_full = proj_full.reshape(width, width)
    else:
        tail_rows = stride - seq_length
        live_rows = jnp.repeat(image_live, stride) * jnp.tile(
            (jnp.arange(stride) < seq_length).astype(jnp.int32), image_count
        )
        route_rows = jnp.pad(expert_routes, ((0, 0), (0, tail_rows), (0, 0))).reshape(row_count, 2)
        route_code, position = slot_places(route_rows, live_rows, expert_count)
        up_rows = (
            jnp.pad(output_grad, ((0, 0), (0, tail_rows), (0, 0))).reshape(row_count, width)
            * as_float(live_rows)[:, None]
        )
        own_bias = lax.dynamic_update_slice(
            jnp.zeros((1, width), jnp.float32),
            as_float(expert_out_bias),
            (0, my_shard * shard_rows),
        )
        in_bias = as_float(expert_in_bias)
        notes = jnp.concatenate([route_code.astype(bf16), position.astype(bf16)], axis=1)
        notes = jnp.pad(notes, ((0, 0), (0, 128 - notes.shape[1])))
        up_line = jnp.concatenate([up_rows.astype(bf16), notes], axis=1)
        extra = jnp.pad(
            jnp.concatenate([router_weight.T, vector_rows]),
            ((0, extra_rows - expert_count - VECTORS), (0, extra_cols - shard_rows)),
        )
        qkv_all, proj_all, extra_all, line_all = (
            lax.all_gather(each, "shard", axis=0, tiled=False)
            for each in (qkv_weight, attn_out_weight, extra, up_line)
        )
        qkv_full = qkv_all.reshape(width, 3 * width)
        proj_full = proj_all.reshape(width, width)
        extra_t = jnp.transpose(extra_all[:, :, :shard_rows], (1, 0, 2))
        rows_t = extra_t[expert_count:]
        vectors = as_float(rows_t[:8]).reshape(8, width)
        query_value = as_float(rows_t[5:7])
        bias_full = jnp.transpose(query_value, (1, 0, 2)).reshape(2 * width)
        bias_row = jnp.concatenate(
            [bias_full[:width], jnp.zeros((width,), jnp.float32), bias_full[width:]]
        )
        bias_row = jnp.pad(bias_row[None], ((0, 7), (0, 0)))
        router_t = jnp.pad(
            extra_t[:expert_count].reshape(expert_count, width),
            ((0, router_pad - expert_count), (0, 0)),
        )
        line_rows = shards * row_count
        line = line_all.reshape(line_rows, width + 128)
        line_up = line[:, :width]
        line_notes = as_float(line[:, width : width + 4])
        line_ids = jnp.arange(line_rows, dtype=jnp.int32)[:, None]
        line_slot = (
            line_notes[:, 0:2].astype(jnp.int32) * group_rows
            + (line_ids // row_count) * capacity
            + line_notes[:, 2:4].astype(jnp.int32)
        )
        line_slot = jnp.where(line_notes[:, 0:2] >= 0, line_slot, -1)
        slot_ids = jnp.arange(slot_rows, dtype=jnp.int32)
        table_0 = line_slot[:, 0:1] == slot_ids[None, :]
        table_1 = line_slot[:, 1:2] == slot_ids[None, :]
        send_table = (table_0 | table_1).astype(bf16)
        up_out = contract_rows(send_table, line_up).astype(bf16)
        up_in = lax.all_to_all(up_out, "expert", split_axis=0, concat_axis=0, tiled=True)
        out_slice = lax.all_to_all(
            expert_out_weight[0], "shard", split_axis=0, concat_axis=1, tiled=True
        )
        packed, mixed, residual, expert_in, gates = pl.pallas_call(
            functools.partial(forward_kernel, stride, expert_count),
            out_shape=[
                jax.ShapeDtypeStruct((row_count, 3 * width), bf16),
                jax.ShapeDtypeStruct((row_count, width), bf16),
                jax.ShapeDtypeStruct((row_count, width), jnp.float32),
                jax.ShapeDtypeStruct((row_count, width), bf16),
                jax.ShapeDtypeStruct((row_count, router_pad), jnp.float32),
            ],
            in_specs=[pl.BlockSpec(memory_space=pltpu.VMEM)] * 6,
            out_specs=[pl.BlockSpec(memory_space=pltpu.VMEM)] * 5,
            scratch_shapes=[
                pltpu.VMEM((row_count, width), jnp.float32),
                pltpu.VMEM((row_count, width), bf16),
            ],
            compiler_params=pltpu.CompilerParams(vmem_limit_bytes=BIG_VMEM),
            name="attention_forward",
        )(turned_in, qkv_full, proj_full, vectors, bias_row, router_t)
        (
            summed,
            route_grad,
            in_weight_grad,
            out_weight_grad,
            in_bias_sum,
            out_bias_sum,
        ) = expert_slow(
            expert_in,
            gates,
            route_rows,
            (table_0, table_1, send_table),
            line_up,
            up_in,
            in_slice,
            out_slice,
            in_bias,
            own_bias,
        )
        out_weight_grad = out_weight_grad.T
    out_weight_grad = out_weight_grad.reshape(shards, shard_rows, -1)
    in_weight_part = in_weight_grad[None]
    in_bias_part = in_bias_sum[:1]
    out_bias_part = lax.dynamic_slice_in_dim(
        out_bias_sum[0], my_shard * shard_rows, shard_rows
    )[None]

    if fast:
        (
            block_output,
            input_grad,
            qkv_sum,
            proj_sum,
            mine,
            bias_part,
            out_weight_rows,
        ) = backward_reduce(
            shards,
            chips,
            stride,
            (
                image_live,
                turned_in,
                turned_grad,
                packed,
                mixed,
                residual,
                expert_in,
                gates,
                summed,
                route_grad,
                qkv_full,
                proj_full,
                vectors,
                router_t,
                out_weight_grad,
            ),
        )
        out_weight_part = as_float(out_weight_rows).T[None]
        mine = mine[:, :shard_rows]
        bias_part = bias_part[0]
    else:
        smem = pl.BlockSpec(memory_space=pltpu.SMEM)
        vmem = pl.BlockSpec(memory_space=pltpu.VMEM)
        wide_rows = pltpu.VMEM((row_count, width), jnp.float32)
        block_output, input_grad, weight_grads, extra_grads = pl.pallas_call(
            functools.partial(backward_kernel, stride),
            out_shape=[
                jax.ShapeDtypeStruct(turned_in.shape, jnp.float32),
                jax.ShapeDtypeStruct(turned_in.shape, jnp.float32),
                jax.ShapeDtypeStruct((2, width, 2 * width), bf16),
                jax.ShapeDtypeStruct((extra_rows, width), jnp.float32),
            ],
            in_specs=[smem] + [vmem] * 13,
            out_specs=[vmem] * 4,
            scratch_shapes=[
                wide_rows,
                wide_rows,
                pltpu.VMEM((width, row_count), bf16),
                pltpu.VMEM((row_count, width), bf16),
                pltpu.VMEM((row_count, 3 * width), bf16),
                wide_rows,
            ],
            compiler_params=pltpu.CompilerParams(vmem_limit_bytes=BIG_VMEM),
            cost_estimate=pl.CostEstimate(
                flops=32 * row_count * width * width,
                bytes_accessed=48 * width * width,
                transcendentals=2 * HEADS * row_count * row_count,
            ),
            name="attention_backward",
        )(
            image_live,
            turned_in,
            turned_grad,
            packed,
            mixed,
            residual,
            expert_in,
            gates,
            summed,
            route_grad,
            qkv_full,
            proj_full,
            vectors,
            router_t,
        )
        qkv_sum, proj_sum, extra_sum, out_weight_blocks = reduce_slow(
            weight_grads, extra_grads.astype(bf16), out_weight_grad
        )
        out_weight_part = (
            jnp.transpose(as_float(out_weight_blocks), (0, 2, 1)).reshape(-1, shard_rows)[None]
        )

        def own(array_in, size, axis=0):
            return lax.dynamic_slice_in_dim(array_in, my_shard * size, size, axis=axis)

        mine = own(extra_sum, shard_rows, axis=1)
        bias_part = own(extra_sum[5:7].reshape(2 * width), 2 * shard_rows)
    return (
        jnp.transpose(block_output, (1, 0, 2)),
        jnp.transpose(input_grad, (1, 0, 2)),
        mine[0],
        mine[1],
        as_float(qkv_sum),
        bias_part,
        as_float(proj_sum),
        mine[2],
        mine[3],
        mine[4],
        mine[VECTORS : VECTORS + expert_count].T,
        in_weight_part,
        in_bias_part,
        out_weight_part,
        out_bias_part,
    )


def solution(mesh):
    in_specs = (
        P(("expert", "shard"), None, None),
        P(("expert", "shard")),
        P(("expert", "shard"), None, None),
        P("shard"),
        P("shard"),
        P("shard", None),
        P("shard"),
        P("shard", None),
        P("shard"),
        P("shard"),
        P("shard"),
        P("shard", None),
        P("expert", None, "shard"),
        P("expert", "shard"),
        P("expert", None, "shard"),
        P("expert", "shard"),
        P(("expert", "shard"), None, None),
    )
    out_specs = (
        P(("expert", "shard"), None, None),
        P(("expert", "shard"), None, None),
        P("shard"),
        P("shard"),
        P("shard", None),
        P("shard"),
        P("shard", None),
        P("shard"),
        P("shard"),
        P("shard"),
        P("shard", None),
        P("expert", None, "shard"),
        P("expert", "shard"),
        P("expert", None, "shard"),
        P("expert", "shard"),
    )
    return jax.shard_map(body, mesh=mesh, in_specs=in_specs, out_specs=out_specs, check_vma=False)
```
